32 devices in a mesh: rec: 4 (over y, core), tm: 8 (over z, x).
Axes of the slice: x: 2, y: 2, z: 4, core: 2. Of those that a mesh axis runs over, the one named last changes fastest.
Arguments:
- frames: bfloat16 [4, 4096, 1024], P('rec', 'tm'), may hold values from -6 to 6
- lengths: int32 [4], P('rec'), may hold values from 1024 to 4096, as said below
- norm_gain: float32 [1024], replicated, may hold values from 0.1 to 1.9
- memory_gain: float32 [1024], replicated, may hold values from 0.1 to 1.9
- qkv_weight: bfloat16 [3, 1024, 1024], P(None, None, 'tm'), may hold values from -3.75 to 3.75
- out_weight: bfloat16 [1024, 1024], P(None, 'tm'), may hold values from -0.1875 to 0.1875
- segment_ids: int32 [4, 8, 512], P('rec', 'tm'), may hold values from 0 to 127, never falling along the last dimension, each value on 1 to 12 neighbouring positions
- owners: int32 [4, 8, 128, 1], P('rec', 'tm'), may hold values from 0 to 7; in each aligned block of 128 rows (0 to 127, 128 to 255, ..., all dimensions but the last counted through in order) at most 32 rows name the same one
- language_weight: bfloat16 [1024, 2048], P(None, 'rec'), may hold values from -0.1875 to 0.1875
Outputs:
- encoded: bfloat16 [4, 4096, 1024], P('rec', 'tm')
- lm_rows: bfloat16 [4, 8, 256, 2048], P('rec', 'tm')
The draws below stay inside these ranges and needn't reach their ends.
Inputs may be any that keep to these rules, and one draw needn't show every extreme that they name: `lengths`: one recording has exactly 4096 live frames. `segment_ids`: in each block, token numbers never fall and each of the 128 tokens has 1 to 12 frames, one exactly 12. `owners`: within the 128 tokens of one block no owner is named more than 32 times, a bound that some block reaches.
All inputs are finite; a program needn't handle non-finite values.
Results may differ from the reference program's by a relative error of at most 0.035.
Values may be sent and summed in bfloat16 or wider, within the bound.
No kernel may reach another device: no remote copies, remote signals or barrier semaphores. Data moves between devices by JAX's collectives and lax.ppermute only.
A program may use at most 64 MiB of HBM per device.

```python
import math
import jax
import jax.numpy as jnp
import numpy as np
from jax import lax

D = 1024
H = 16
DL = 2048
C = 32
RC = 8
SEG_MOST = 12
F_DEV = 512
TOK_DEV = 128
CAP = 32
SLOTS = 256
REC = 4
FRAMES = 4096
N_TM = 8


def draw_lengths(key, part):
    first_key, second_key = jax.random.split(key)
    drawn = jax.random.randint(first_key, (REC,), FRAMES // 4, FRAMES + 1)
    picked = jax.random.randint(second_key, (), 0, REC)
    return jnp.where(jnp.arange(REC) == picked, FRAMES, drawn).astype(jnp.int32)


def draw_qkv_weight(key, part):
    base_draw = jax.random.normal(key, (3, D, D), jnp.float32)
    base_draw = jnp.clip(base_draw, -6.0, 6.0) * D ** (-0.5)
    base_draw = jnp.clip(base_draw, -3.75, 3.75)
    return base_draw.astype(jnp.bfloat16)


def steps_of(own_key, shape, cuts, low, largest):
    loudness = 1.0
    for axis_at, parts in cuts:
        steps = jax.random.uniform(jax.random.fold_in(jax.random.fold_in(own_key, 6), axis_at), (parts,), jnp.float32, low / len(cuts), largest / len(cuts))
        loudness = loudness * jnp.repeat(jnp.exp(steps), shape[axis_at] // parts).reshape((-1,) + (1,) * (len(shape) - 1 - axis_at))
    return loudness


def length_profile(count, total, bound, lean):
    portions = [(1 << 20) // math.isqrt(grade ** lean) + 1 for grade in range(2, count + 1)]
    surplus, given = total - bound - (count - 1), [1] * (count - 1)
    while surplus > 0:
        free = [i for i in range(count - 1) if given[i] < bound]
        pool, left = sum([portions[i] for i in free]), surplus
        for i in free:
            extra = min(bound - given[i], max(1, left * portions[i] // pool), surplus)
            given[i] = given[i] + extra
            surplus = surplus - extra
    return np.array([bound] + given)


def uneven_parts(key, amount, total, bound, skew):
    if amount == 2:
        one = jax.random.randint(key, (), max(1, total - bound), min(bound, total - 1) + 1)
        return jnp.stack([one, total - one])
    sizes = jnp.asarray(length_profile(amount, total, bound, skew), jnp.int32)
    couples = (amount - 1) // 2
    donor, sink = sizes[1:1 + 2 * couples:2], sizes[2:2 + 2 * couples:2]
    room = jnp.minimum(donor - 1, bound - sink)
    moved = jax.random.randint(jax.random.fold_in(key, 1), (couples,), 0, 1 << 20) % (room + 1)
    sizes = sizes.at[1:1 + 2 * couples:2].set(donor - moved).at[2:2 + 2 * couples:2].set(sink + moved)
    return sizes[jax.random.permutation(jax.random.fold_in(key, 2), amount)]


def routed_block(rng, own, number, rows, number_of, top, most, slope):
    order = jax.random.permutation(rng, number_of)
    heavy_load, ordinary = load_shares(number_of, rows * top, most, slope, True), load_shares(number_of, rows * top, most, slope, False)
    places = jnp.arange(number_of)

    def named(sizes, offset_by):
        used = int((sizes > 0).sum())
        fixed = max(1, used // 4)
        shifted = fixed + (places - fixed + offset_by * (used - fixed)) % max(1, number_of - fixed)
        return jnp.zeros((number_of,), jnp.int32).at[order[jnp.where(places < fixed, places, shifted)]].set(jnp.asarray(sizes, jnp.int32))

    sizes = jnp.where(number % 4 == 0, named(heavy_load, number // 4), named(ordinary, number - number // 4 - 1))
    mixed = jax.random.permutation(jax.random.fold_in(own, 3), number_of)
    giver, taker = mixed[0:number_of // 2 * 2:2], mixed[1:number_of // 2 * 2:2]
    room = jnp.minimum(sizes[giver] - 1, most - sizes[taker]) // 2
    room = jnp.where((giver == order[0]) | (taker == order[0]) | (sizes[taker] == 0), 0, jnp.maximum(room, 0))
    shifted = jax.random.randint(jax.random.fold_in(own, 4), (number_of // 2,), 0, 1 << 20) % (room + 1)
    sizes = sizes.at[giver].add(-shifted).at[taker].add(shifted)
    labels = jnp.searchsorted(jnp.cumsum(sizes), jnp.arange(rows * top), side="right").astype(jnp.int32)
    grid = labels.reshape(top, rows).T
    grid = grid[jax.random.permutation(jax.random.fold_in(own, 1), rows)]
    offset_by = jax.random.randint(jax.random.fold_in(own, 2), (rows, 1), 0, top)
    return jnp.take_along_axis(grid, (jnp.arange(top)[None, :] + offset_by) % top, axis=1)


def load_shares(count, total, reach, slope, full):
    portions = [(1 << 20) // math.isqrt(standing ** slope) + 1 for standing in range(1, count + 1)]
    largest = reach if full else min(reach, max(-(-total // count), total * portions[0] // sum(portions)))
    least = 1 if total - largest >= count - 1 else 0
    holding, surplus = [largest] + [least] * (count - 1), total - largest - least * (count - 1)
    while surplus > 0:
        movable = [i for i in range(1, count) if holding[i] < largest] or [i for i in range(1, count) if holding[i] < reach]
        mass, budget = sum([portions[i] for i in movable]), surplus
        for i in movable:
            extra = min(reach - holding[i], max(1, budget * portions[i] // mass), surplus)
            holding[i] = holding[i] + extra
            surplus = surplus - extra
    return np.array(holding)


def scatter_about(stream_key, extent, width, most, pieces=(), held_as=jnp.bfloat16):
    factor_of = steps_of(stream_key, extent, pieces, -0.22, 0.18) if pieces else 1.0
    values = jax.random.normal(stream_key, extent, jnp.float32) * width * factor_of
    return jnp.minimum(jnp.maximum(values, -most), most).astype(held_as)


def setup_inputs(seed: int = 0) -> dict:
    splits = jax.random.split(jax.random.key(seed), 10)
    frames = scatter_about(splits[0], (REC, FRAMES, D), 1.0, 6.0, ((0, 4), (1, 8)))
    lengths = draw_lengths(jax.random.fold_in(splits[9], 71), 0)
    norm_gain = jnp.clip(1.0 + 0.18 * jax.random.normal(splits[2], (D,), jnp.float32), 0.1, 1.9)
    memory_gain = jnp.clip(1.0 + 0.18 * jax.random.normal(splits[3], (D,), jnp.float32), 0.1, 1.9)
    qkv_weight = draw_qkv_weight(jax.random.fold_in(splits[9], 71), 0)
    out_weight = scatter_about(splits[5], (D, D), D ** -0.5, 0.1875, ((1, 8),))
    segment_ids = jax.vmap(lambda own: jnp.searchsorted(jnp.cumsum(uneven_parts(own, TOK_DEV, F_DEV, SEG_MOST, 2)), jnp.arange(F_DEV), side="right"))(jax.random.split(splits[6], REC * N_TM)).reshape((REC, N_TM, F_DEV)).astype(jnp.int32)
    owners_keys = jax.random.split(jax.random.fold_in(splits[7], 1), REC * N_TM * TOK_DEV // TOK_DEV)
    owners_turns = jax.random.permutation(jax.random.fold_in(splits[7], 3), REC * N_TM * TOK_DEV // TOK_DEV)
    owners = jax.vmap(lambda own, number: routed_block(jax.random.fold_in(splits[7], 2), own, number, TOK_DEV, N_TM, 1, CAP, 2))(owners_keys, owners_turns).reshape((REC, N_TM, TOK_DEV, 1))
    language_weight = scatter_about(splits[8], (D, DL), D ** -0.5, 0.1875, ((1, 4),))
    return dict(frames=frames, lengths=lengths, norm_gain=norm_gain, memory_gain=memory_gain, qkv_weight=qkv_weight, out_weight=out_weight, segment_ids=segment_ids, owners=owners, language_weight=language_weight)


EPS_NORM = 1e-05
EPS_MEMORY = 1e-06
NEG_BIG = -1e+30

def layer_norm(values_in, gain):
    values_in = values_in.astype(jnp.float32)
    centre = lax.optimization_barrier(jnp.mean(values_in, axis=-1, keepdims=True))
    centred = values_in - centre
    spread = lax.optimization_barrier(jnp.mean(centred * centred, axis=-1, keepdims=True))
    return centred * lax.rsqrt(spread + EPS_NORM) * gain

def span_memory(normed, live_mask, gain, span_len):
    model_width = normed.shape[1]
    masked = jnp.where(live_mask[:, None], normed.astype(jnp.float32), jnp.float32(0.0))
    owner_sums = masked.reshape(-1, span_len, model_width).sum(axis=1)
    counts = live_mask.reshape(-1, span_len).astype(jnp.float32).sum(axis=1)
    means = owner_sums / jnp.maximum(counts, 1.0)[:, None]
    power = lax.optimization_barrier(jnp.mean(means * means, axis=-1, keepdims=True))
    return (means * lax.rsqrt(power + EPS_MEMORY) * gain).astype(jnp.bfloat16)

def block_size(frame_count):
    return 256 if frame_count % 256 == 0 else 128

def local_part(query, keys, values, first_frame, length, head_count, span_len, right_len):
    frame_count, model_width = query.shape
    head_size = model_width // head_count
    group_rows = 4 * span_len
    group_count = frame_count // group_rows
    block_rows = block_size(frame_count)
    query_blocks = query.reshape(group_count, group_rows, head_count, head_size).astype(jnp.float32)
    key_blocks = keys[:frame_count].reshape(group_count, group_rows, head_count, head_size)
    value_blocks = values[:frame_count].reshape(group_count, group_rows, head_count, head_size)
    key_tail = keys[frame_count:].reshape(1, right_len, head_count, head_size)
    value_tail = values[frame_count:].reshape(1, right_len, head_count, head_size)
    key_all = jnp.concatenate([key_blocks, jnp.concatenate([key_blocks[1:, :right_len], key_tail], axis=0)], axis=1)
    value_all = jnp.concatenate([value_blocks, jnp.concatenate([value_blocks[1:, :right_len], value_tail], axis=0)], axis=1)
    start_offsets = jnp.arange(group_count, dtype=jnp.int32)[:, None] * group_rows
    query_pos = first_frame + start_offsets + jnp.arange(group_rows, dtype=jnp.int32)[None, :]
    key_pos = first_frame + jnp.concatenate([start_offsets + jnp.arange(group_rows, dtype=jnp.int32)[None, :], start_offsets + group_rows + jnp.arange(right_len, dtype=jnp.int32)[None, :]], axis=1)
    query_span = query_pos // span_len
    span_end = (query_span + 1) * span_len
    same = (key_pos // span_len)[:, None, :] == query_span[:, :, None]
    ahead = (key_pos[:, None, :] >= span_end[:, :, None]) & (key_pos[:, None, :] < span_end[:, :, None] + right_len)
    allowed = (same | ahead) & (key_pos < length)[:, None, :]
    scores = jnp.einsum('gqhd,gkhd->ghqk', query_blocks, key_all.astype(jnp.float32)) * head_size ** (-0.5)
    scores = jnp.where(allowed[:, None], scores, NEG_BIG)
    row_peak = lax.optimization_barrier(jnp.max(scores, axis=-1))
    weights = jnp.where(allowed[:, None], jnp.exp(scores - row_peak[..., None]), jnp.float32(0.0))
    row_total = lax.optimization_barrier(jnp.sum(weights, axis=-1))
    accum = jnp.einsum('ghqk,gkhd->ghqd', weights.astype(jnp.bfloat16).astype(jnp.float32), value_all.astype(jnp.float32))
    block_count = frame_count // block_rows
    row_peak = row_peak.transpose(1, 0, 2).reshape(head_count, block_count, block_rows).transpose(1, 0, 2)
    row_total = row_total.transpose(1, 0, 2).reshape(head_count, block_count, block_rows).transpose(1, 0, 2)
    accum = accum.transpose(1, 0, 2, 3).reshape(head_count, block_count, block_rows, head_size).transpose(1, 0, 2, 3)
    return (row_peak, row_total, accum)

def memory_update(carry, memory_keys, memory_values, start, query, first_frame, length, head_count, span_len):
    row_peak, row_total, accum = carry
    block_count, _, block_rows = row_peak.shape
    row_count, model_width = memory_keys.shape
    head_size = model_width // head_count
    mem_keys = memory_keys.reshape(row_count, head_count, head_size).astype(jnp.float32)
    mem_values = memory_values.reshape(row_count, head_count, head_size).astype(jnp.float32)
    mem_index = start + jnp.arange(row_count, dtype=jnp.int32)
    mem_live = mem_index * span_len < length
    query_blocks = query.reshape(block_count, block_rows, head_count, head_size)
    positions = first_frame + jnp.arange(block_count * block_rows, dtype=jnp.int32).reshape(block_count, block_rows)

    def one_block(packed):
        query_now, pos_now, peak_now, total_now, accum_now = packed
        scores = jnp.einsum('qhd,khd->hqk', query_now.astype(jnp.float32), mem_keys) * head_size ** (-0.5)
        allowed = (mem_index[None, :] < (pos_now // span_len)[:, None]) & mem_live[None, :]
        scores = jnp.where(allowed[None], scores, NEG_BIG)
        new_peak = jnp.maximum(peak_now, lax.optimization_barrier(jnp.max(scores, axis=-1)))
        weights = jnp.where(allowed[None], jnp.exp(scores - new_peak[..., None]), jnp.float32(0.0))
        factor = jnp.exp(peak_now - new_peak)
        total_next = total_now * factor + lax.optimization_barrier(jnp.sum(weights, axis=-1))
        accum_next = accum_now * factor[..., None] + jnp.einsum('hqk,khd->hqd', weights.astype(jnp.bfloat16).astype(jnp.float32), mem_values)
        return (new_peak, total_next, accum_next)
    return lax.map(one_block, (query_blocks, positions, row_peak, row_total, accum))

def finish(carry, frame_count, model_width):
    row_peak, row_total, accum = carry
    result = accum / row_total[..., None]
    return result.transpose(0, 2, 1, 3).reshape(frame_count, model_width).astype(jnp.bfloat16)

def dispatch_matrix(owner_ids, owner_count, capacity):
    choose = (owner_ids[:, None] == jnp.arange(owner_count, dtype=jnp.int32)[None, :]).astype(jnp.int32)
    before = jnp.cumsum(choose, axis=0) - choose
    slot_index = lax.optimization_barrier(jnp.sum(before * choose, axis=1))
    target = owner_ids * capacity + slot_index
    slot_rows = jnp.arange(owner_count * capacity, dtype=jnp.int32)
    return (slot_rows[:, None] == target[None, :]).astype(jnp.bfloat16)

def reference(frames, lengths, norm_gain, memory_gain, qkv_weight, out_weight, segment_ids, owners, language_weight):

    def one_recording(packed):
        rec_frames, length, rec_segments, rec_owners = packed
        normed = layer_norm(rec_frames, norm_gain).astype(jnp.bfloat16)
        live_mask = jnp.arange(FRAMES, dtype=jnp.int32) < length
        memory = span_memory(normed, live_mask, memory_gain, C)
        query = jnp.dot(normed, qkv_weight[0], preferred_element_type=jnp.float32).astype(jnp.bfloat16)
        keys = jnp.dot(normed, qkv_weight[1], preferred_element_type=jnp.float32).astype(jnp.bfloat16)
        values = jnp.dot(normed, qkv_weight[2], preferred_element_type=jnp.float32).astype(jnp.bfloat16)
        memory_keys = jnp.dot(memory, qkv_weight[1], preferred_element_type=jnp.float32).astype(jnp.bfloat16)
        memory_values = jnp.dot(memory, qkv_weight[2], preferred_element_type=jnp.float32).astype(jnp.bfloat16)
        padding = jnp.zeros((RC, D), jnp.bfloat16)
        keys_padded = jnp.concatenate([keys, padding], axis=0)
        values_padded = jnp.concatenate([values, padding], axis=0)

        def one_block(block_id):
            first_frame = (block_id * F_DEV).astype(jnp.int32)
            query_now = lax.dynamic_slice_in_dim(query, first_frame, F_DEV, 0)
            keys_now = lax.dynamic_slice_in_dim(keys_padded, first_frame, F_DEV + RC, 0)
            values_now = lax.dynamic_slice_in_dim(values_padded, first_frame, F_DEV + RC, 0)
            carry = local_part(query_now, keys_now, values_now, first_frame, length, H, C, RC)
            carry = memory_update(carry, memory_keys, memory_values, 0, query_now, first_frame, length, H, C)
            return finish(carry, F_DEV, D)
        attended = lax.map(one_block, jnp.arange(N_TM, dtype=jnp.int32)).reshape(FRAMES, D)
        projected = jnp.dot(attended, out_weight, preferred_element_type=jnp.float32)
        encoded = jnp.where(live_mask[:, None], rec_frames.astype(jnp.float32) + projected, jnp.float32(0.0)).astype(jnp.bfloat16)
        encoder_blocks = encoded.reshape(N_TM, F_DEV, D)
        owner_indicator = (rec_segments[:, None, :] == jnp.arange(TOK_DEV, dtype=jnp.int32)[None, :, None]).astype(jnp.float32)
        owner_sums = jnp.einsum('xqe,xem->xqm', owner_indicator, encoder_blocks.astype(jnp.float32))
        counts = lax.optimization_barrier(jnp.sum(owner_indicator, axis=-1))
        pooled_rows = (owner_sums / counts[..., None]).astype(jnp.bfloat16)
        route_matrix = jax.vmap(lambda owner_ids: dispatch_matrix(owner_ids, N_TM, CAP))(rec_owners[:, :, 0])
        sent_rows = jnp.einsum('hag,hgw->haw', route_matrix.astype(jnp.float32), pooled_rows.astype(jnp.float32)).astype(jnp.bfloat16)
        received = sent_rows.reshape(N_TM, N_TM, CAP, D).transpose(1, 0, 2, 3).reshape(N_TM * SLOTS, D)
        lm_out = jnp.dot(received, language_weight, preferred_element_type=jnp.float32).astype(jnp.bfloat16)
        return (encoded, lm_out.reshape(N_TM, SLOTS, DL))
    encoded, lm_rows = lax.map(one_recording, (frames, lengths, segment_ids, owners))
    return (encoded, lm_rows)
```

```python
import functools

import jax
import jax.numpy as jnp
from jax import lax
from jax.experimental import pallas as pl
from jax.experimental.pallas import tpu as pltpu
from jax.sharding import PartitionSpec as P

H = 16
C = 32
RC = 8


EPS_NORM = 1e-05
EPS_MEMORY = 1e-06
NEG_BIG = -1e30
LANES = 128


def shifted(block, axis, distance):
    devices = range(lax.axis_size(axis))
    route = [(i - distance, i) for i in devices if i - distance in devices]
    return lax.ppermute(block, axis, route)


def layer_norm(values_in, gain):
    values_in = values_in.astype(jnp.float32)
    centre = jnp.mean(values_in, axis=-1, keepdims=True)
    centred = values_in - centre
    spread = jnp.mean(centred * centred, axis=-1, keepdims=True)
    return centred * lax.rsqrt(spread + EPS_NORM) * gain


def span_memory(normed, live_mask, gain, span_len):
    model_width = normed.shape[1]
    masked = jnp.where(live_mask[:, None], normed.astype(jnp.float32), jnp.float32(0.0))
    owner_sums = masked.reshape(-1, span_len, model_width).sum(axis=1)
    counts = live_mask.reshape(-1, span_len).astype(jnp.float32).sum(axis=1)
    means = owner_sums / jnp.maximum(counts, 1.0)[:, None]
    power = jnp.mean(means * means, axis=-1, keepdims=True)
    return (means * lax.rsqrt(power + EPS_MEMORY) * gain).astype(jnp.bfloat16)


def block_size():
    return 256


def local_part(query, keys, values, first_frame, length, head_count, span_len, right_len):
    frame_count, model_width = query.shape
    head_size = model_width // head_count
    group_rows = 4 * span_len
    group_count = frame_count // group_rows
    block_rows = block_size()
    query_blocks = query.reshape(group_count, group_rows, head_count, head_size)
    key_blocks = keys[:frame_count].reshape(group_count, group_rows, head_count, head_size)
    value_blocks = values[:frame_count].reshape(group_count, group_rows, head_count, head_size)
    key_tail = keys[frame_count:].reshape(1, right_len, head_count, head_size)
    value_tail = values[frame_count:].reshape(1, right_len, head_count, head_size)
    key_all = jnp.concatenate(
        [key_blocks, jnp.concatenate([key_blocks[1:, :right_len], key_tail], axis=0)], axis=1
    )
    value_all = jnp.concatenate(
        [value_blocks, jnp.concatenate([value_blocks[1:, :right_len], value_tail], axis=0)], axis=1
    )
    start_offsets = jnp.arange(group_count, dtype=jnp.int32)[:, None] * group_rows
    query_pos = first_frame + start_offsets + jnp.arange(group_rows, dtype=jnp.int32)[None, :]
    key_pos = first_frame + jnp.concatenate(
        [
            start_offsets + jnp.arange(group_rows, dtype=jnp.int32)[None, :],
            start_offsets + group_rows + jnp.arange(right_len, dtype=jnp.int32)[None, :],
        ],
        axis=1,
    )
    query_span = query_pos // span_len
    span_end = (query_span + 1) * span_len
    same = (key_pos // span_len)[:, None, :] == query_span[:, :, None]
    ahead = (key_pos[:, None, :] >= span_end[:, :, None]) & (
        key_pos[:, None, :] < span_end[:, :, None] + right_len
    )
    allowed = (same | ahead) & (key_pos < length)[:, None, :]
    scores = jnp.einsum(
        "gqhd,gkhd->ghqk", query_blocks, key_all, preferred_element_type=jnp.float32
    ) * head_size ** (-0.5)
    scores = jnp.where(allowed[:, None], scores, NEG_BIG)
    row_peak = jnp.max(scores, axis=-1)
    weights = jnp.where(allowed[:, None], jnp.exp(scores - row_peak[..., None]), jnp.float32(0.0))
    row_total = jnp.sum(weights, axis=-1)
    accum = jnp.einsum(
        "ghqk,gkhd->ghqd",
        weights.astype(jnp.bfloat16),
        value_all,
        preferred_element_type=jnp.float32,
    )
    block_count = frame_count // block_rows
    row_peak = (
        row_peak.transpose(1, 0, 2).reshape(head_count, block_count, block_rows).transpose(1, 0, 2)
    )
    row_total = (
        row_total.transpose(1, 0, 2).reshape(head_count, block_count, block_rows).transpose(1, 0, 2)
    )
    accum = (
        accum.transpose(1, 0, 2, 3)
        .reshape(head_count, block_count, block_rows, head_size)
        .transpose(1, 0, 2, 3)
    )
    return (row_peak, row_total, accum)


def memory_update(
    carry, memory_keys, memory_values, query, first_frame, length, head_count, span_len
):
    row_peak, row_total, accum = carry
    block_count, _, block_rows = row_peak.shape
    row_count, model_width = memory_keys.shape
    head_size = model_width // head_count
    mem_keys = memory_keys.reshape(row_count, head_count, head_size)
    mem_values = memory_values.reshape(row_count, head_count, head_size)
    mem_index = jnp.arange(row_count, dtype=jnp.int32)
    mem_live = mem_index * span_len < length
    query_blocks = query.reshape(block_count, block_rows, head_count, head_size)
    positions = first_frame + jnp.arange(block_count * block_rows, dtype=jnp.int32).reshape(
        block_count, block_rows
    )

    def one_block(packed):
        query_now, pos_now, peak_now, total_now, accum_now = packed
        scores = jnp.einsum(
            "qhd,khd->hqk", query_now, mem_keys, preferred_element_type=jnp.float32
        ) * head_size ** (-0.5)
        allowed = (mem_index[None, :] < (pos_now // span_len)[:, None]) & mem_live[None, :]
        scores = jnp.where(allowed[None], scores, NEG_BIG)
        new_peak = jnp.maximum(peak_now, jnp.max(scores, axis=-1))
        weights = jnp.where(allowed[None], jnp.exp(scores - new_peak[..., None]), jnp.float32(0.0))
        factor = jnp.exp(peak_now - new_peak)
        total_next = total_now * factor + jnp.sum(weights, axis=-1)
        accum_next = accum_now * factor[..., None] + jnp.einsum(
            "hqk,khd->hqd",
            weights.astype(jnp.bfloat16),
            mem_values,
            preferred_element_type=jnp.float32,
        )
        return (new_peak, total_next, accum_next)

    return lax.map(one_block, (query_blocks, positions, row_peak, row_total, accum))


def finish(carry, frame_count, model_width):
    row_peak, row_total, accum = carry
    result = accum / row_total[..., None]
    return result.transpose(0, 2, 1, 3).reshape(frame_count, model_width).astype(jnp.bfloat16)


def dispatch_matrix(owner_ids, owner_count, capacity):
    choose = (owner_ids[:, None] == jnp.arange(owner_count, dtype=jnp.int32)[None, :]).astype(
        jnp.int32
    )
    before = jnp.cumsum(choose, axis=0) - choose
    slot_index = jnp.sum(before * choose, axis=1)
    target = owner_ids * capacity + slot_index
    slot_rows = jnp.arange(owner_count * capacity, dtype=jnp.int32)
    return (slot_rows[:, None] == target[None, :]).astype(jnp.bfloat16)


def plain_device(
    frames,
    lengths,
    norm_gain,
    memory_gain,
    qkv_weight,
    out_weight,
    segment_ids,
    owners,
    language_weight,
):
    local_frames = frames[0]
    frame_count, model_width = local_frames.shape
    head_count = H
    time_count = lax.axis_size("tm")
    first_frame = lax.axis_index("tm") * frame_count
    length = lengths[0]
    live_mask = first_frame + jnp.arange(frame_count, dtype=jnp.int32) < length
    right_frames = shifted(local_frames[:RC], "tm", -1)
    normed = layer_norm(local_frames, norm_gain).astype(jnp.bfloat16)
    normed_right = layer_norm(right_frames, norm_gain).astype(jnp.bfloat16)
    memory = span_memory(normed, live_mask, memory_gain, C)
    stacked_rows = jnp.concatenate([normed, normed_right, memory], axis=0)
    projected = jnp.einsum(
        "fd,kdw->kfw",
        stacked_rows,
        lax.all_gather(qkv_weight, "tm", axis=2, tiled=True),
        preferred_element_type=jnp.float32,
    ).astype(jnp.bfloat16)
    split_at = frame_count + RC
    query = projected[0, :frame_count]
    keys = projected[1, :split_at]
    values = projected[2, :split_at]
    memory_keys = projected[1, split_at:]
    memory_values = projected[2, split_at:]
    carry = local_part(query, keys, values, first_frame, length, head_count, C, RC)
    carry = memory_update(
        carry,
        lax.all_gather(memory_keys, "tm", axis=0, tiled=True),
        lax.all_gather(memory_values, "tm", axis=0, tiled=True),
        query,
        first_frame,
        length,
        head_count,
        C,
    )
    attended = finish(carry, frame_count, model_width)
    output_proj = jnp.dot(
        attended,
        lax.all_gather(out_weight, "tm", axis=1, tiled=True),
        preferred_element_type=jnp.float32,
    )
    encoded = jnp.where(
        live_mask[:, None], local_frames.astype(jnp.float32) + output_proj, jnp.float32(0.0)
    ).astype(jnp.bfloat16)
    token_count = owners.shape[2]
    segments = segment_ids[0, 0]
    owner_indicator = (
        segments[None, :] == jnp.arange(token_count, dtype=jnp.int32)[:, None]
    ).astype(jnp.bfloat16)
    owner_sums = jnp.dot(owner_indicator, encoded, preferred_element_type=jnp.float32)
    counts = jnp.sum(owner_indicator.astype(jnp.float32), axis=1)
    pooled_rows = (owner_sums / counts[:, None]).astype(jnp.bfloat16)
    slot_count = 2 * token_count
    capacity = slot_count // time_count
    route_matrix = dispatch_matrix(owners[0, 0, :, 0], time_count, capacity)
    sent_rows = jnp.dot(route_matrix, pooled_rows, preferred_element_type=jnp.float32).astype(
        jnp.bfloat16
    )
    received = lax.all_to_all(
        sent_rows.reshape(time_count, capacity, model_width),
        "tm",
        split_axis=0,
        concat_axis=0,
        tiled=True,
    )
    received = received.reshape(slot_count, model_width)
    lm_out = jnp.dot(
        received,
        lax.all_gather(language_weight, "rec", axis=1, tiled=True),
        preferred_element_type=jnp.float32,
    ).astype(jnp.bfloat16)
    return (encoded[None], lm_out[None, None])


def vmem_spec():
    return pl.BlockSpec(memory_space=pltpu.VMEM)


def smem_spec():
    return pl.BlockSpec(memory_space=pltpu.SMEM)


def local_call(kernel, name, out_shapes, operands, scratch=(), flops=0, moved=0):
    return pl.pallas_call(
        kernel,
        name=name,
        out_shape=out_shapes,
        in_specs=[smem_spec()] + [vmem_spec()] * (len(operands) - 1),
        out_specs=jax.tree.map(lambda _: vmem_spec(), out_shapes),
        scratch_shapes=list(scratch),
        cost_estimate=pl.CostEstimate(flops=flops, bytes_accessed=moved, transcendentals=0),
    )(*operands)


def shape_of(*dims, dtype=jnp.bfloat16):
    return jax.ShapeDtypeStruct(dims, dtype)


def normalise_kernel(span_len, scalars, frames, gain, memory_gain, normed_out, memory_out):
    first_frame, length = scalars[0], scalars[1]
    frame_count, model_width = frames.shape
    span_count = frame_count // span_len
    values = frames[...].astype(jnp.float32)
    centre = jnp.mean(values, axis=-1, keepdims=True)
    centred = values - centre
    spread = jnp.mean(centred * centred, axis=-1, keepdims=True)
    normed = (centred * lax.rsqrt(spread + EPS_NORM) * gain[...]).astype(jnp.bfloat16)
    normed_out[...] = normed
    spans = lax.broadcasted_iota(jnp.int32, (span_count, frame_count), 0)
    places = lax.broadcasted_iota(jnp.int32, (span_count, frame_count), 1)
    member = (places >= spans * span_len) & (places < (spans + 1) * span_len)
    member = member & (places < length - first_frame)
    sums = jnp.dot(
        member.astype(jnp.bfloat16), normed, preferred_element_type=jnp.float32
    )
    counts = jnp.sum(member.astype(jnp.float32), axis=-1, keepdims=True)
    means = sums / jnp.maximum(counts, 1.0)
    power = jnp.mean(means * means, axis=-1, keepdims=True)
    memory_out[...] = (
        means * lax.rsqrt(power + EPS_MEMORY) * memory_gain[...]
    ).astype(jnp.bfloat16)


def attend_kernel(span_len, right_len, head_size, scalars, *refs):
    (rows_0, extra_0, rows_1, extra_1) = refs[:4]
    pieces = refs[4:12]
    out_0, out_1, weight, query, key, value, bias = refs[12:]
    first_frame, core, y_half = scalars[0], scalars[3], scalars[4]
    frame_count, model_width = rows_0.shape
    half = model_width // 2
    width = out_0.shape[1]
    heads = width // head_size
    block = 2 * span_len
    pad = key.shape[0] - frame_count
    near = block + pad
    memory_count = extra_0.shape[0] - pad
    lanes = heads * block

    places = (y_half * half, (1 - y_half) * half)
    for side in range(2):
        place = pl.multiple_of(places[side], half)
        for part in range(3):
            for shard in range(2):
                mine_0, mine_1 = pieces[4 * shard + 2 * side], pieces[4 * shard + 2 * side + 1]
                shard_width = mine_0.shape[2]
                weight[part, pl.ds(place, half), shard * shard_width : (shard + 1) * shard_width] = (
                    jnp.where(core == 0, mine_0[part], mine_1[part])
                )

    rows = lax.broadcasted_iota(jnp.int32, (near, lanes), 0)
    spans = (lax.broadcasted_iota(jnp.int32, (near, lanes), 1) % block) // span_len
    same = (rows >= spans * span_len) & (rows < (spans + 1) * span_len + right_len)
    bias[...] = jnp.where(same, jnp.float32(0.0), jnp.float32(NEG_BIG))
    lane_spans = (lax.broadcasted_iota(jnp.int32, (1, lanes), 1) % block) // span_len
    memory_rows = lax.broadcasted_iota(jnp.int32, (memory_count, lanes), 0)
    feature_head = lax.broadcasted_iota(jnp.int32, (1, width), 1) // head_size
    head_masks = [(feature_head == h).astype(jnp.float32) for h in range(heads)]
    head_masks_16 = [m.astype(jnp.bfloat16) for m in head_masks]

    for rec, (own, extra, out) in enumerate(((rows_0, extra_0, out_0), (rows_1, extra_1, out_1))):
        length = scalars[1 + rec]
        scale = head_size ** (-0.5)
        query[...] = (
            jnp.dot(own[...], weight[0], preferred_element_type=jnp.float32) * scale
        ).astype(jnp.bfloat16)
        key[:frame_count] = jnp.dot(
            own[...], weight[1], preferred_element_type=jnp.float32
        ).astype(jnp.bfloat16)
        value[:frame_count] = jnp.dot(
            own[...], weight[2], preferred_element_type=jnp.float32
        ).astype(jnp.bfloat16)
        extra_key = jnp.dot(extra[...], weight[1], preferred_element_type=jnp.float32).astype(
            jnp.bfloat16
        )
        extra_value = jnp.dot(extra[...], weight[2], preferred_element_type=jnp.float32).astype(
            jnp.bfloat16
        )
        key[frame_count:] = extra_key[:pad]
        value[frame_count:] = extra_value[:pad]
        memory_key, memory_value = extra_key[pad:], extra_value[pad:]
        live_spans = (length + span_len - 1) // span_len

        def one_block(b, _):
            start = pl.multiple_of(b * block, block)
            q_now = query[pl.ds(start, block), :]
            stacked = jnp.concatenate([q_now * m for m in head_masks_16], axis=0)
            keys = jnp.concatenate([key[pl.ds(start, near), :], memory_key], axis=0)
            values = jnp.concatenate([value[pl.ds(start, near), :], memory_value], axis=0)
            scores = lax.dot_general(
                keys, stacked, (((1,), (1,)), ((), ())), preferred_element_type=jnp.float32
            )
            limit = length - first_frame - start
            local = jnp.where(rows < limit, scores[:near] + bias[...], NEG_BIG)
            span_limit = jnp.minimum(first_frame // span_len + 2 * b + lane_spans, live_spans)
            memory = jnp.where(memory_rows < span_limit, scores[near:], NEG_BIG)
            peak = jnp.maximum(
                jnp.max(local, axis=0, keepdims=True), jnp.max(memory, axis=0, keepdims=True)
            )
            local = jnp.exp(local - peak)
            memory = jnp.exp(memory - peak)
            total = jnp.sum(local, axis=0, keepdims=True) + jnp.sum(memory, axis=0, keepdims=True)
            inverse = 1.0 / total
            weights = jnp.concatenate([local * inverse, memory * inverse], axis=0).astype(
                jnp.bfloat16
            )
            mixed = lax.dot_general(
                weights, values, (((0,), (0,)), ((), ())), preferred_element_type=jnp.float32
            )
            picked = mixed[:block] * head_masks[0]
            for h in range(1, heads):
                picked = picked + mixed[h * block : (h + 1) * block] * head_masks[h]
            out[pl.ds(start, block), :] = picked.astype(jnp.bfloat16)
            return 0

        lax.fori_loop(0, frame_count // block, one_block, 0, unroll=2)


def encode_kernel(scalars, *refs):
    attended = refs[:4]
    projections = refs[4:8]
    frames, segments, owners_row, owners_col = refs[8:12]
    encoded_out, sent_out, gathered = refs[12:]
    first_frame, length, y_half, capacity = (scalars[i] for i in range(4))
    frame_count, model_width = frames.shape
    half = model_width // 2
    token_count = owners_row.shape[1]
    offsets = [
        [pl.multiple_of(scalars[4 + 2 * i + s], LANES) for s in range(2)] for i in range(4)
    ]
    shard = attended[0].shape[1] // 2
    for i in range(4):
        for s in range(2):
            gathered[:, pl.ds(offsets[i][s], shard)] = attended[i][:, s * shard : (s + 1) * shard]
    tokens = lax.broadcasted_iota(jnp.int32, (token_count, frame_count), 0)
    indicator = segments[...] == tokens
    counts = jnp.sum(indicator.astype(jnp.float32), axis=1, keepdims=True)
    indicator = indicator.astype(jnp.bfloat16)
    earlier = lax.broadcasted_iota(jnp.int32, (token_count, token_count), 0)
    later = lax.broadcasted_iota(jnp.int32, (token_count, token_count), 1)
    clash = (owners_col[...] == owners_row[...]) & (earlier < later)
    slot = jnp.sum(clash.astype(jnp.int32), axis=0, keepdims=True)
    target = owners_row[...] * capacity + slot
    slots = lax.broadcasted_iota(jnp.int32, (sent_out.shape[0], token_count), 0)
    route = (slots == target).astype(jnp.bfloat16)
    live = (
        first_frame + lax.broadcasted_iota(jnp.int32, (frame_count, 1), 0) < length
    )
    left = gathered[:, pl.ds(pl.multiple_of(y_half * half, half), half)]
    right = gathered[:, pl.ds(pl.multiple_of((1 - y_half) * half, half), half)]
    for i in range(4):
        w = projections[i]
        mixed = jnp.dot(
            left, jnp.concatenate([w[0], w[2]], axis=1), preferred_element_type=jnp.float32
        ) + jnp.dot(
            right, jnp.concatenate([w[1], w[3]], axis=1), preferred_element_type=jnp.float32
        )
        base = jnp.concatenate(
            [frames[:, pl.ds(offsets[i][s], shard)] for s in range(2)], axis=1
        ).astype(jnp.float32)
        encoded = jnp.where(live, base + mixed, 0.0).astype(jnp.bfloat16)
        pooled = (
            jnp.dot(indicator, encoded, preferred_element_type=jnp.float32) / counts
        ).astype(jnp.bfloat16)
        sent = jnp.dot(route, pooled, preferred_element_type=jnp.float32).astype(jnp.bfloat16)
        for s in range(2):
            encoded_out[:, pl.ds(offsets[i][s], shard)] = encoded[:, s * shard : (s + 1) * shard]
            sent_out[:, pl.ds(offsets[i][s], shard)] = sent[:, s * shard : (s + 1) * shard]


def language_kernel(scalars, received, *refs):
    weights, out = refs[:-1], refs[-1]
    for i, w in enumerate(weights):
        width = w.shape[1]
        place = pl.multiple_of(scalars[i], LANES)
        out[:, pl.ds(place, width)] = jnp.dot(
            received[...], w[...], preferred_element_type=jnp.float32
        ).astype(jnp.bfloat16)


def along_x(r, j, _):
    return r, j ^ 1


def along_y(r, j, _):
    return r ^ 2, j


def other_core(r, j, _):
    return r ^ 1, j


def z_up(r, j, count):
    return r, (j + 2) % count


def z_down(r, j, count):
    return r, (j - 2) % count


def relocate(value, core_0, core_1):
    rec_count, time_count = lax.axis_size("rec"), lax.axis_size("tm")
    pairs = []
    for r in range(rec_count):
        for j in range(time_count):
            route = (core_0, core_1)[r % 2]
            if route is not None:
                to_r, to_j = route(r, j, time_count)
                pairs.append((r * time_count + j, to_r * time_count + to_j))
    return lax.ppermute(value, ("rec", "tm"), pairs)


def swap_cores(value):
    return relocate(value, other_core, other_core)


def per_device(
    frames,
    lengths,
    norm_gain,
    memory_gain,
    qkv_weight,
    out_weight,
    segment_ids,
    owners,
    language_weight,
):
    local_frames = frames[0]
    frame_count, model_width = local_frames.shape
    shard = out_weight.shape[1]
    half = model_width // 2
    time_count = lax.axis_size("tm")
    rec_count = lax.axis_size("rec")
    rec, time = lax.axis_index("rec"), lax.axis_index("tm")
    core, y_half = rec % 2, (rec // 2) % 2
    x, z = time % 2, time // 2
    z_count = time_count // 2
    first_frame = time * frame_count
    length = lengths[0]
    head_size = model_width // H
    bf16 = jnp.bfloat16

    own = jnp.concatenate([qkv_weight, out_weight[None]], axis=0)
    own_a = lax.dynamic_slice_in_dim(own, y_half * half, half, 1)
    own_b = lax.dynamic_slice_in_dim(own, (1 - y_half) * half, half, 1)

    def pick(for_core_0, for_core_1):
        return jnp.where(core == 0, for_core_0, for_core_1)

    m1 = relocate(own_a, along_x, z_up)
    m2 = relocate(pick(own_a, own_b), z_down, z_up)

    normed, memory = local_call(
        functools.partial(normalise_kernel, C),
        "normalise",
        (shape_of(frame_count, model_width), shape_of(frame_count // C, model_width)),
        (
            jnp.stack([first_frame, length]).astype(jnp.int32),
            local_frames,
            norm_gain[None],
            memory_gain[None],
        ),
        flops=10 * frame_count * model_width,
        moved=4 * frame_count * model_width,
    )
    other_length = swap_cores(lengths)[0]
    other_normed = swap_cores(normed)
    ahead = shifted(normed[:RC], "tm", -1)
    memories = lax.all_to_all(
        jnp.broadcast_to(memory[None], (time_count,) + memory.shape),
        "tm",
        split_axis=0,
        concat_axis=0,
        tiled=True,
    ).reshape(-1, model_width)
    extra = jnp.concatenate([ahead, jnp.zeros_like(ahead), memories], axis=0)
    other_extra = swap_cores(extra)

    m3 = relocate(m1, along_y, along_x)
    m4 = relocate(pick(own_b, m3), z_down, along_y)
    m5 = relocate(pick(m2, m1), along_x, z_up)
    m6 = relocate(pick(m5, m2), along_y, z_up)
    m7 = relocate(m5, None, along_x)
    m8 = relocate(m7, None, along_y)

    l1 = relocate(language_weight, along_y, along_y)
    l2 = swap_cores(language_weight)
    l3 = swap_cores(l1)

    slot_pieces = (
        ((own_a, m1), (own_b, m2), (m1, m3), (m3, m4)),
        ((m2, m5), (m4, m6), (m5, m7), (m6, m8)),
    )
    scalars = jnp.stack([first_frame, length, other_length, core, y_half]).astype(jnp.int32)
    pad = 2 * RC
    block = 2 * C
    width = 2 * shard
    attended, outs = [], []
    for pieces in slot_pieces:
        flat = [p for pair in pieces for p in pair]
        attended.append(
            local_call(
                functools.partial(attend_kernel, C, RC, head_size),
                "attend",
                (shape_of(frame_count, width), shape_of(frame_count, width)),
                (scalars, normed, extra, other_normed, other_extra, *flat),
                scratch=(
                    pltpu.VMEM((3, model_width, width), bf16),
                    pltpu.VMEM((frame_count, width), bf16),
                    pltpu.VMEM((frame_count + pad, width), bf16),
                    pltpu.VMEM((frame_count + pad, width), bf16),
                    pltpu.VMEM((block + pad, width // head_size * block), jnp.float32),
                ),
                flops=12 * frame_count * model_width * width,
                moved=8 * frame_count * model_width,
            )
        )
        outs.append(jnp.stack([pick(a[3], b[3]) for a, b in pieces]))
    other_outs = [swap_cores(w) for w in outs]
    other_attended = [swap_cores(mine_other) for _, mine_other in attended]

    def group_of(of_core, slot):
        return jnp.where(of_core == 0, z + slot, z - slot - 1) % z_count

    offsets = []
    for of_core in (core, 1 - core):
        for slot in range(2):
            group = group_of(of_core, slot)
            offsets += [(2 * group + x) * shard, (2 * group + 1 - x) * shard]
    token_count = owners.shape[2]
    slot_count = 2 * token_count
    capacity = slot_count // time_count
    owners_col = owners[0, 0]
    encoded, sent_rows = local_call(
        encode_kernel,
        "encode",
        (shape_of(frame_count, model_width), shape_of(slot_count, model_width)),
        (
            jnp.stack([first_frame, length, y_half, capacity] + offsets).astype(jnp.int32),
            attended[0][0],
            attended[1][0],
            *other_attended,
            *outs,
            *other_outs,
            local_frames,
            segment_ids[0],
            owners_col.reshape(1, token_count),
            owners_col,
        ),
        scratch=(pltpu.VMEM((frame_count, model_width), bf16),),
        flops=2 * frame_count * model_width * model_width,
        moved=6 * frame_count * model_width,
    )
    received = lax.all_to_all(
        sent_rows.reshape(time_count, capacity, model_width),
        "tm",
        split_axis=0,
        concat_axis=0,
        tiled=True,
    ).reshape(slot_count, model_width)
    language_shard = language_weight.shape[1]
    places = [(rec ^ i) * language_shard for i in range(rec_count)]
    lm_out = local_call(
        language_kernel,
        "language",
        shape_of(slot_count, rec_count * language_shard),
        (jnp.stack(places).astype(jnp.int32), received, language_weight, l2, l1, l3),
        flops=2 * slot_count * model_width * rec_count * language_shard,
        moved=2 * model_width * rec_count * language_shard,
    )
    return (encoded[None], lm_out[None, None])


def solution(mesh):
    in_specs = (
        P("rec", "tm", None),
        P("rec"),
        P(),
        P(),
        P(None, None, "tm"),
        P(None, "tm"),
        P("rec", "tm", None),
        P("rec", "tm", None, None),
        P(None, "rec"),
    )
    out_specs = (P("rec", "tm", None), P("rec", "tm", None, None))
    rec_count, time_count = mesh.shape["rec"], mesh.shape["tm"]
    paired = shard_map_of(mesh, in_specs, out_specs, per_device)
    plain = shard_map_of(mesh, in_specs, out_specs, plain_device)

    def run(*arrays):
        shard = arrays[5].shape[1] // time_count
        fits = rec_count == 4 and time_count == 8 and shard % LANES == 0
        return (paired if fits else plain)(*arrays)

    return run


def shard_map_of(mesh, in_specs, out_specs, body):
    return jax.shard_map(
        body, mesh=mesh, in_specs=in_specs, out_specs=out_specs, check_vma=False
    )
```

```python
import functools

import jax
import jax.numpy as jnp
from jax import lax
from jax.experimental import pallas as pl
from jax.experimental.pallas import tpu as pltpu
from jax.sharding import PartitionSpec as P


H = 16
C = 32
RC = 8


EPS_NORM = 1e-05
EPS_MEMORY = 1e-06
NEG_BIG = -1e30
LANES = 128


def shifted(block, axis, distance):
    devices = range(lax.axis_size(axis))
    route = [(i - distance, i) for i in devices if i - distance in devices]
    return lax.ppermute(block, axis, route)


def layer_norm(values_in, gain):
    values_in = values_in.astype(jnp.float32)
    centre = jnp.mean(values_in, axis=-1, keepdims=True)
    centred = values_in - centre
    spread = jnp.mean(centred * centred, axis=-1, keepdims=True)
    return centred * lax.rsqrt(spread + EPS_NORM) * gain


def span_memory(normed, live_mask, gain, span_len):
    model_width = normed.shape[1]
    masked = jnp.where(live_mask[:, None], normed.astype(jnp.float32), jnp.float32(0.0))
    owner_sums = masked.reshape(-1, span_len, model_width).sum(axis=1)
    counts = live_mask.reshape(-1, span_len).astype(jnp.float32).sum(axis=1)
    means = owner_sums / jnp.maximum(counts, 1.0)[:, None]
    power = jnp.mean(means * means, axis=-1, keepdims=True)
    return (means * lax.rsqrt(power + EPS_MEMORY) * gain).astype(jnp.bfloat16)


def block_size():
    return 256


def local_part(query, keys, values, first_frame, length, head_count, span_len, right_len):
    frame_count, model_width = query.shape
    head_size = model_width // head_count
    group_rows = 4 * span_len
    group_count = frame_count // group_rows
    block_rows = block_size()
    query_blocks = query.reshape(group_count, group_rows, head_count, head_size)
    key_blocks = keys[:frame_count].reshape(group_count, group_rows, head_count, head_size)
    value_blocks = values[:frame_count].reshape(group_count, group_rows, head_count, head_size)
    key_tail = keys[frame_count:].reshape(1, right_len, head_count, head_size)
    value_tail = values[frame_count:].reshape(1, right_len, head_count, head_size)
    key_all = jnp.concatenate(
        [key_blocks, jnp.concatenate([key_blocks[1:, :right_len], key_tail], axis=0)], axis=1
    )
    value_all = jnp.concatenate(
        [value_blocks, jnp.concatenate([value_blocks[1:, :right_len], value_tail], axis=0)], axis=1
    )
    start_offsets = jnp.arange(group_count, dtype=jnp.int32)[:, None] * group_rows
    query_pos = first_frame + start_offsets + jnp.arange(group_rows, dtype=jnp.int32)[None, :]
    key_pos = first_frame + jnp.concatenate(
        [
            start_offsets + jnp.arange(group_rows, dtype=jnp.int32)[None, :],
            start_offsets + group_rows + jnp.arange(right_len, dtype=jnp.int32)[None, :],
        ],
        axis=1,
    )
    query_span = query_pos // span_len
    span_end = (query_span + 1) * span_len
    same = (key_pos // span_len)[:, None, :] == query_span[:, :, None]
    ahead = (key_pos[:, None, :] >= span_end[:, :, None]) & (
        key_pos[:, None, :] < span_end[:, :, None] + right_len
    )
    allowed = (same | ahead) & (key_pos < length)[:, None, :]
    scores = jnp.einsum(
        "gqhd,gkhd->ghqk", query_blocks, key_all, preferred_element_type=jnp.float32
    ) * head_size ** (-0.5)
    scores = jnp.where(allowed[:, None], scores, NEG_BIG)
    row_peak = jnp.max(scores, axis=-1)
    weights = jnp.where(allowed[:, None], jnp.exp(scores - row_peak[..., None]), jnp.float32(0.0))
    row_total = jnp.sum(weights, axis=-1)
    accum = jnp.einsum(
        "ghqk,gkhd->ghqd",
        weights.astype(jnp.bfloat16),
        value_all,
        preferred_element_type=jnp.float32,
    )
    block_count = frame_count // block_rows
    row_peak = (
        row_peak.transpose(1, 0, 2).reshape(head_count, block_count, block_rows).transpose(1, 0, 2)
    )
    row_total = (
        row_total.transpose(1, 0, 2).reshape(head_count, block_count, block_rows).transpose(1, 0, 2)
    )
    accum = (
        accum.transpose(1, 0, 2, 3)
        .reshape(head_count, block_count, block_rows, head_size)
        .transpose(1, 0, 2, 3)
    )
    return (row_peak, row_total, accum)


def memory_update(
    carry, memory_keys, memory_values, query, first_frame, length, head_count, span_len
):
    row_peak, row_total, accum = carry
    block_count, _, block_rows = row_peak.shape
    row_count, model_width = memory_keys.shape
    head_size = model_width // head_count
    mem_keys = memory_keys.reshape(row_count, head_count, head_size)
    mem_values = memory_values.reshape(row_count, head_count, head_size)
    mem_index = jnp.arange(row_count, dtype=jnp.int32)
    mem_live = mem_index * span_len < length
    query_blocks = query.reshape(block_count, block_rows, head_count, head_size)
    positions = first_frame + jnp.arange(block_count * block_rows, dtype=jnp.int32).reshape(
        block_count, block_rows
    )

    def one_block(packed):
        query_now, pos_now, peak_now, total_now, accum_now = packed
        scores = jnp.einsum(
            "qhd,khd->hqk", query_now, mem_keys, preferred_element_type=jnp.float32
        ) * head_size ** (-0.5)
        allowed = (mem_index[None, :] < (pos_now // span_len)[:, None]) & mem_live[None, :]
        scores = jnp.where(allowed[None], scores, NEG_BIG)
        new_peak = jnp.maximum(peak_now, jnp.max(scores, axis=-1))
        weights = jnp.where(allowed[None], jnp.exp(scores - new_peak[..., None]), jnp.float32(0.0))
        factor = jnp.exp(peak_now - new_peak)
        total_next = total_now * factor + jnp.sum(weights, axis=-1)
        accum_next = accum_now * factor[..., None] + jnp.einsum(
            "hqk,khd->hqd",
            weights.astype(jnp.bfloat16),
            mem_values,
            preferred_element_type=jnp.float32,
        )
        return (new_peak, total_next, accum_next)

    return lax.map(one_block, (query_blocks, positions, row_peak, row_total, accum))


def finish(carry, frame_count, model_width):
    _, row_total, accum = carry
    result = accum / row_total[..., None]
    return result.transpose(0, 2, 1, 3).reshape(frame_count, model_width).astype(jnp.bfloat16)


def dispatch_matrix(owner_ids, owner_count, capacity):
    choose = (owner_ids[:, None] == jnp.arange(owner_count, dtype=jnp.int32)[None, :]).astype(
        jnp.int32
    )
    before = jnp.cumsum(choose, axis=0) - choose
    slot_index = jnp.sum(before * choose, axis=1)
    target = owner_ids * capacity + slot_index
    slot_rows = jnp.arange(owner_count * capacity, dtype=jnp.int32)
    return (slot_rows[:, None] == target[None, :]).astype(jnp.bfloat16)


def plain_device(
    frames,
    lengths,
    norm_gain,
    memory_gain,
    qkv_weight,
    out_weight,
    segment_ids,
    owners,
    language_weight,
):
    local_frames = frames[0]
    frame_count, model_width = local_frames.shape
    head_count = H
    time_count = lax.axis_size("tm")
    first_frame = lax.axis_index("tm") * frame_count
    length = lengths[0]
    live_mask = first_frame + jnp.arange(frame_count, dtype=jnp.int32) < length
    right_frames = shifted(local_frames[:RC], "tm", -1)
    normed = layer_norm(local_frames, norm_gain).astype(jnp.bfloat16)
    normed_right = layer_norm(right_frames, norm_gain).astype(jnp.bfloat16)
    memory = span_memory(normed, live_mask, memory_gain, C)
    stacked_rows = jnp.concatenate([normed, normed_right, memory], axis=0)
    projected = jnp.einsum(
        "fd,kdw->kfw",
        stacked_rows,
        lax.all_gather(qkv_weight, "tm", axis=2, tiled=True),
        preferred_element_type=jnp.float32,
    ).astype(jnp.bfloat16)
    split_at = frame_count + RC
    query = projected[0, :frame_count]
    keys = projected[1, :split_at]
    values = projected[2, :split_at]
    memory_keys = projected[1, split_at:]
    memory_values = projected[2, split_at:]
    carry = local_part(query, keys, values, first_frame, length, head_count, C, RC)
    carry = memory_update(
        carry,
        lax.all_gather(memory_keys, "tm", axis=0, tiled=True),
        lax.all_gather(memory_values, "tm", axis=0, tiled=True),
        query,
        first_frame,
        length,
        head_count,
        C,
    )
    attended = finish(carry, frame_count, model_width)
    output_proj = jnp.dot(
        attended,
        lax.all_gather(out_weight, "tm", axis=1, tiled=True),
        preferred_element_type=jnp.float32,
    )
    encoded = jnp.where(
        live_mask[:, None], local_frames.astype(jnp.float32) + output_proj, jnp.float32(0.0)
    ).astype(jnp.bfloat16)
    token_count = owners.shape[2]
    segments = segment_ids[0, 0]
    owner_indicator = (
        segments[None, :] == jnp.arange(token_count, dtype=jnp.int32)[:, None]
    ).astype(jnp.bfloat16)
    owner_sums = jnp.dot(owner_indicator, encoded, preferred_element_type=jnp.float32)
    counts = jnp.sum(owner_indicator.astype(jnp.float32), axis=1)
    pooled_rows = (owner_sums / counts[:, None]).astype(jnp.bfloat16)
    slot_count = 2 * token_count
    capacity = slot_count // time_count
    route_matrix = dispatch_matrix(owners[0, 0, :, 0], time_count, capacity)
    sent_rows = jnp.dot(route_matrix, pooled_rows, preferred_element_type=jnp.float32).astype(
        jnp.bfloat16
    )
    received = lax.all_to_all(
        sent_rows.reshape(time_count, capacity, model_width),
        "tm",
        split_axis=0,
        concat_axis=0,
        tiled=True,
    )
    received = received.reshape(slot_count, model_width)
    lm_out = jnp.dot(
        received,
        lax.all_gather(language_weight, "rec", axis=1, tiled=True),
        preferred_element_type=jnp.float32,
    ).astype(jnp.bfloat16)
    return (encoded[None], lm_out[None, None])


def vmem_spec():
    return pl.BlockSpec(memory_space=pltpu.VMEM)


def smem_spec():
    return pl.BlockSpec(memory_space=pltpu.SMEM)


def local_call(kernel, out_shapes, operands, scratch=(), flops=0, moved=0):
    return pl.pallas_call(
        kernel,
        out_shape=out_shapes,
        in_specs=[smem_spec()] + [vmem_spec()] * (len(operands) - 1),
        out_specs=jax.tree.map(lambda _: vmem_spec(), out_shapes),
        scratch_shapes=list(scratch),
        cost_estimate=pl.CostEstimate(flops=flops, bytes_accessed=moved, transcendentals=0),
    )(*operands)


def shape_of(*dims, dtype=jnp.bfloat16):
    return jax.ShapeDtypeStruct(dims, dtype)


def normalise_kernel(span_len, scalars, frames, gain, memory_gain, normed_out, memory_out):
    first_frame, length = scalars[0], scalars[1]
    frame_count, _ = frames.shape
    span_count = frame_count // span_len
    values = frames[...].astype(jnp.float32)
    centre = jnp.mean(values, axis=-1, keepdims=True)
    centred = values - centre
    spread = jnp.mean(centred * centred, axis=-1, keepdims=True)
    normed = (centred * lax.rsqrt(spread + EPS_NORM) * gain[...]).astype(jnp.bfloat16)
    normed_out[...] = normed
    spans = lax.broadcasted_iota(jnp.int32, (span_count, frame_count), 0)
    places = lax.broadcasted_iota(jnp.int32, (span_count, frame_count), 1)
    member = (places >= spans * span_len) & (places < (spans + 1) * span_len)
    member = member & (places < length - first_frame)
    sums = jnp.dot(
        member.astype(jnp.bfloat16), normed, preferred_element_type=jnp.float32
    )
    counts = jnp.sum(member.astype(jnp.float32), axis=-1, keepdims=True)
    means = sums / jnp.maximum(counts, 1.0)
    power = jnp.mean(means * means, axis=-1, keepdims=True)
    memory_out[...] = (
        means * lax.rsqrt(power + EPS_MEMORY) * memory_gain[...]
    ).astype(jnp.bfloat16)


def attend_kernel(span_len, right_len, head_size, scalars, *refs):
    (rows_0, extra_0, rows_1, extra_1) = refs[:4]
    pieces = refs[4:12]
    out_0, out_1, projection, weight, query, key, value, bias = refs[12:]
    first_frame, core, y_half = scalars[0], scalars[3], scalars[4]
    frame_count, model_width = rows_0.shape
    half = model_width // 2
    width = out_0.shape[1]
    heads = width // head_size
    block = 2 * span_len
    pad = key.shape[0] - frame_count
    near = block + pad
    memory_count = extra_0.shape[0] - pad
    lanes = heads * block

    places = (y_half * half, (1 - y_half) * half)
    for side in range(2):
        place = pl.ds(pl.multiple_of(places[side], half), half)
        for shard in range(2):
            mine_0, mine_1 = pieces[4 * shard + 2 * side], pieces[4 * shard + 2 * side + 1]
            shard_width = mine_0.shape[2]
            columns = slice(shard * shard_width, (shard + 1) * shard_width)
            for part in range(4):
                chosen = jnp.where(core == 0, mine_0[part], mine_1[part])
                if part < 3:
                    weight[part, place, columns] = chosen
                else:
                    projection[place, columns] = chosen

    rows = lax.broadcasted_iota(jnp.int32, (near, lanes), 0)
    spans = (lax.broadcasted_iota(jnp.int32, (near, lanes), 1) % block) // span_len
    same = (rows >= spans * span_len) & (rows < (spans + 1) * span_len + right_len)
    bias[...] = jnp.where(same, jnp.float32(0.0), jnp.float32(NEG_BIG))
    lane_spans = (lax.broadcasted_iota(jnp.int32, (1, lanes), 1) % block) // span_len
    memory_rows = lax.broadcasted_iota(jnp.int32, (memory_count, lanes), 0)
    feature_head = lax.broadcasted_iota(jnp.int32, (1, width), 1) // head_size
    head_masks = [(feature_head == h).astype(jnp.float32) for h in range(heads)]
    head_masks_16 = [m.astype(jnp.bfloat16) for m in head_masks]

    for rec, (own, extra, out) in enumerate(((rows_0, extra_0, out_0), (rows_1, extra_1, out_1))):
        length = scalars[1 + rec]
        scale = head_size ** (-0.5)
        query[...] = (
            jnp.dot(own[...], weight[0], preferred_element_type=jnp.float32) * scale
        ).astype(jnp.bfloat16)
        key[:frame_count] = jnp.dot(
            own[...], weight[1], preferred_element_type=jnp.float32
        ).astype(jnp.bfloat16)
        value[:frame_count] = jnp.dot(
            own[...], weight[2], preferred_element_type=jnp.float32
        ).astype(jnp.bfloat16)
        extra_key = jnp.dot(extra[...], weight[1], preferred_element_type=jnp.float32).astype(
            jnp.bfloat16
        )
        extra_value = jnp.dot(extra[...], weight[2], preferred_element_type=jnp.float32).astype(
            jnp.bfloat16
        )
        key[frame_count:] = extra_key[:pad]
        value[frame_count:] = extra_value[:pad]
        memory_key, memory_value = extra_key[pad:], extra_value[pad:]
        live_spans = (length + span_len - 1) // span_len

        def one_block(b, _):
            start = pl.multiple_of(b * block, block)
            q_now = query[pl.ds(start, block), :]
            stacked = jnp.concatenate([q_now * m for m in head_masks_16], axis=0)
            keys = jnp.concatenate([key[pl.ds(start, near), :], memory_key], axis=0)
            values = jnp.concatenate([value[pl.ds(start, near), :], memory_value], axis=0)
            scores = lax.dot_general(
                keys, stacked, (((1,), (1,)), ((), ())), preferred_element_type=jnp.float32
            )
            limit = length - first_frame - start
            local = jnp.where(rows < limit, scores[:near] + bias[...], NEG_BIG)
            span_limit = jnp.minimum(first_frame // span_len + 2 * b + lane_spans, live_spans)
            memory = jnp.where(memory_rows < span_limit, scores[near:], NEG_BIG)
            peak = jnp.maximum(
                jnp.max(local, axis=0, keepdims=True), jnp.max(memory, axis=0, keepdims=True)
            )
            local = jnp.exp(local - peak)
            memory = jnp.exp(memory - peak)
            total = jnp.sum(local, axis=0, keepdims=True) + jnp.sum(memory, axis=0, keepdims=True)
            inverse = 1.0 / total
            weights = jnp.concatenate([local * inverse, memory * inverse], axis=0).astype(
                jnp.bfloat16
            )
            mixed = lax.dot_general(
                weights, values, (((0,), (0,)), ((), ())), preferred_element_type=jnp.float32
            )
            picked = mixed[:block] * head_masks[0]
            for h in range(1, heads):
                picked = picked + mixed[h * block : (h + 1) * block] * head_masks[h]
            out[pl.ds(start, block), :] = picked.astype(jnp.bfloat16)
            return 0

        lax.fori_loop(0, frame_count // block, one_block, 0, unroll=2)


def encode_kernel(scalars, *refs):
    attended = refs[:4]
    projections = refs[4:8]
    frames, segments, owners_row, owners_col = refs[8:12]
    encoded_out, sent_out, gathered = refs[12:]
    first_frame, length, capacity = (scalars[i] for i in range(3))
    frame_count, _ = frames.shape
    token_count = owners_row.shape[1]
    offsets = [
        [pl.multiple_of(scalars[3 + 2 * i + s], LANES) for s in range(2)] for i in range(4)
    ]
    shard = attended[0].shape[1] // 2
    for i in range(4):
        for s in range(2):
            gathered[:, pl.ds(offsets[i][s], shard)] = attended[i][:, s * shard : (s + 1) * shard]
    tokens = lax.broadcasted_iota(jnp.int32, (token_count, frame_count), 0)
    indicator = segments[...] == tokens
    counts = jnp.sum(indicator.astype(jnp.float32), axis=1, keepdims=True)
    indicator = indicator.astype(jnp.bfloat16)
    earlier = lax.broadcasted_iota(jnp.int32, (token_count, token_count), 0)
    later = lax.broadcasted_iota(jnp.int32, (token_count, token_count), 1)
    clash = (owners_col[...] == owners_row[...]) & (earlier < later)
    slot = jnp.sum(clash.astype(jnp.int32), axis=0, keepdims=True)
    target = owners_row[...] * capacity + slot
    slots = lax.broadcasted_iota(jnp.int32, (sent_out.shape[0], token_count), 0)
    route = (slots == target).astype(jnp.bfloat16)
    live = (
        first_frame + lax.broadcasted_iota(jnp.int32, (frame_count, 1), 0) < length
    )
    for i in range(4):
        mixed = jnp.dot(
            gathered[...], projections[i][...], preferred_element_type=jnp.float32
        )
        base = jnp.concatenate(
            [frames[:, pl.ds(offsets[i][s], shard)] for s in range(2)], axis=1
        ).astype(jnp.float32)
        encoded = jnp.where(live, base + mixed, 0.0).astype(jnp.bfloat16)
        pooled = (
            jnp.dot(indicator, encoded, preferred_element_type=jnp.float32) / counts
        ).astype(jnp.bfloat16)
        sent = jnp.dot(route, pooled, preferred_element_type=jnp.float32).astype(jnp.bfloat16)
        for s in range(2):
            encoded_out[:, pl.ds(offsets[i][s], shard)] = encoded[:, s * shard : (s + 1) * shard]
            sent_out[:, pl.ds(offsets[i][s], shard)] = sent[:, s * shard : (s + 1) * shard]


def language_kernel(scalars, received, *refs):
    weights, out = refs[:-1], refs[-1]
    half = received.shape[1] // 2
    for i in range(len(weights) // 2):
        upper, lower = weights[2 * i], weights[2 * i + 1]
        width = upper.shape[1]
        place = pl.multiple_of(scalars[i], LANES)
        out[:, pl.ds(place, width)] = (
            jnp.dot(received[:, :half], upper[...], preferred_element_type=jnp.float32)
            + jnp.dot(received[:, half:], lower[...], preferred_element_type=jnp.float32)
        ).astype(jnp.bfloat16)


def along_x(r, j, _):
    return r, j ^ 1


def along_y(r, j, _):
    return r ^ 2, j


def other_core(r, j, _):
    return r ^ 1, j


def z_up(r, j, count):
    return r, (j + 2) % count


def z_down(r, j, count):
    return r, (j - 2) % count


def relocate(value, core_0, core_1):
    rec_count, time_count = lax.axis_size("rec"), lax.axis_size("tm")
    pairs = []
    for r in range(rec_count):
        for j in range(time_count):
            route = (core_0, core_1)[r % 2]
            if route is not None:
                to_r, to_j = route(r, j, time_count)
                pairs.append((r * time_count + j, to_r * time_count + to_j))
    return lax.ppermute(value, ("rec", "tm"), pairs)


def swap_cores(value):
    return relocate(value, other_core, other_core)


def exchange_blocks(blocks):
    return lax.all_to_all(blocks, "tm", split_axis=0, concat_axis=0, tiled=True)


def per_device(
    frames,
    lengths,
    norm_gain,
    memory_gain,
    qkv_weight,
    out_weight,
    segment_ids,
    owners,
    language_weight,
):
    local_frames = frames[0]
    frame_count, model_width = local_frames.shape
    shard = out_weight.shape[1]
    half = model_width // 2
    time_count = lax.axis_size("tm")
    rec_count = lax.axis_size("rec")
    rec, time = lax.axis_index("rec"), lax.axis_index("tm")
    core, y_half = rec % 2, (rec // 2) % 2
    x, z = time % 2, time // 2
    z_count = time_count // 2
    first_frame = time * frame_count
    length = lengths[0]
    head_size = model_width // H
    bf16 = jnp.bfloat16

    own = jnp.concatenate([qkv_weight, out_weight[None]], axis=0)
    own_a = lax.dynamic_slice_in_dim(own, y_half * half, half, 1)
    own_b = lax.dynamic_slice_in_dim(own, (1 - y_half) * half, half, 1)

    def pick(for_core_0, for_core_1):
        return jnp.where(core == 0, for_core_0, for_core_1)

    m1 = relocate(own_a, along_x, z_up)
    m2 = relocate(pick(own_a, own_b), z_down, z_up)
    language_half = language_weight.shape[0] // 2
    l1a = relocate(language_weight[:language_half], along_y, along_y)
    l1b = relocate(language_weight[language_half:], along_y, along_y)

    normed, memory = local_call(
        functools.partial(normalise_kernel, C),
        (shape_of(frame_count, model_width), shape_of(frame_count // C, model_width)),
        (
            jnp.stack([first_frame, length]).astype(jnp.int32),
            local_frames,
            norm_gain[None],
            memory_gain[None],
        ),
        flops=10 * frame_count * model_width,
        moved=4 * frame_count * model_width,
    )
    other_length = swap_cores(lengths)[0]
    other_normed = swap_cores(normed)
    ahead = shifted(normed[:RC], "tm", -1)
    memories = exchange_blocks(
        jnp.broadcast_to(memory[None], (time_count,) + memory.shape)
    ).reshape(-1, model_width)
    extra = jnp.concatenate([ahead, jnp.zeros_like(ahead), memories], axis=0)
    other_extra = swap_cores(extra)

    m3 = relocate(m1, along_y, along_x)
    m4 = relocate(m1, None, z_up)
    m5 = relocate(m2, along_x, z_up)
    m6 = relocate(pick(m2, m3), along_y, along_y)
    m7 = relocate(m4, None, along_x)
    m8 = relocate(m5, along_y, along_x)

    slot_pieces = (
        ((own_a, m1), (own_b, m2), (m1, m3), (m3, m6)),
        ((m2, m4), (m6, m5), (m5, m7), (m8, m8)),
    )
    scalars = jnp.stack([first_frame, length, other_length, core, y_half]).astype(jnp.int32)
    pad = 2 * RC
    block = 2 * C
    width = 2 * shard
    attended, outs = [], []
    for pieces in slot_pieces:
        flat = [p for pair in pieces for p in pair]
        *pair, out_piece = local_call(
            functools.partial(attend_kernel, C, RC, head_size),
            (
                shape_of(frame_count, width),
                shape_of(frame_count, width),
                shape_of(model_width, width),
            ),
            (scalars, normed, extra, other_normed, other_extra, *flat),
            scratch=(
                pltpu.VMEM((3, model_width, width), bf16),
                pltpu.VMEM((frame_count, width), bf16),
                pltpu.VMEM((frame_count + pad, width), bf16),
                pltpu.VMEM((frame_count + pad, width), bf16),
                pltpu.VMEM((block + pad, width // head_size * block), jnp.float32),
            ),
            flops=12 * frame_count * model_width * width,
            moved=8 * frame_count * model_width,
        )
        attended.append(pair)
        outs.append(out_piece)
    other_outs = [swap_cores(w) for w in outs]
    other_attended = [swap_cores(for_other) for _, for_other in attended]

    def group_of(of_core, slot):
        return jnp.where(of_core == 0, z + slot, z - slot - 1) % z_count

    offsets = []
    for of_core in (core, 1 - core):
        for slot in range(2):
            group = group_of(of_core, slot)
            offsets += [(2 * group + x) * shard, (2 * group + 1 - x) * shard]
    token_count = owners.shape[2]
    slot_count = 2 * token_count
    capacity = slot_count // time_count
    owners_col = owners[0, 0]
    encoded, sent_rows = local_call(
        encode_kernel,
        (shape_of(frame_count, model_width), shape_of(slot_count, model_width)),
        (
            jnp.stack([first_frame, length, capacity] + offsets).astype(jnp.int32),
            attended[0][0],
            attended[1][0],
            *other_attended,
            *outs,
            *other_outs,
            local_frames,
            segment_ids[0],
            owners_col.reshape(1, token_count),
            owners_col,
        ),
        scratch=(pltpu.VMEM((frame_count, model_width), bf16),),
        flops=2 * frame_count * model_width * model_width,
        moved=6 * frame_count * model_width,
    )
    received = exchange_blocks(
        sent_rows.reshape(time_count, capacity, model_width)
    ).reshape(slot_count, model_width)
    language_shard = language_weight.shape[1]
    places = [(rec ^ i) * language_shard for i in range(rec_count)]
    lm_out = local_call(
        language_kernel,
        shape_of(slot_count, rec_count * language_shard),
        (
            jnp.stack(places).astype(jnp.int32),
            received,
            *[language_weight[:language_half], language_weight[language_half:]],
            *[swap_cores(language_weight[:language_half])],
            *[swap_cores(language_weight[language_half:])],
            *[l1a, l1b],
            *[swap_cores(l1a), swap_cores(l1b)],
        ),
        flops=2 * slot_count * model_width * rec_count * language_shard,
        moved=2 * model_width * rec_count * language_shard,
    )
    return (encoded[None], lm_out[None, None])


def solution(mesh):
    in_specs = (
        P("rec", "tm", None),
        P("rec"),
        P(),
        P(),
        P(None, None, "tm"),
        P(None, "tm"),
        P("rec", "tm", None),
        P("rec", "tm", None, None),
        P(None, "rec"),
    )
    out_specs = (P("rec", "tm", None), P("rec", "tm", None, None))
    rec_count, time_count = mesh.shape["rec"], mesh.shape["tm"]
    paired = shard_map_of(mesh, in_specs, out_specs, per_device)
    plain = shard_map_of(mesh, in_specs, out_specs, plain_device)

    def run(*arrays):
        shard = arrays[5].shape[1] // time_count
        fits = rec_count == 4 and time_count == 8 and shard % LANES == 0
        return (paired if fits else plain)(*arrays)

    return run


def shard_map_of(mesh, in_specs, out_specs, body):
    return jax.shard_map(
        body, mesh=mesh, in_specs=in_specs, out_specs=out_specs, check_vma=False
    )
```

```python
import functools

import jax
import jax.numpy as jnp
from jax import lax
from jax.experimental import pallas as pl
from jax.experimental.pallas import tpu as pltpu
from jax.sharding import PartitionSpec as P


H = 16
C = 32
RC = 8


EPS_NORM = 1e-05
EPS_MEMORY = 1e-06
NEG_BIG = -1e30
LANES = 128
LOG2_E = 1.4426950408889634


def shifted(block, axis, distance):
    devices = range(lax.axis_size(axis))
    route = [(i - distance, i) for i in devices if i - distance in devices]
    return lax.ppermute(block, axis, route)


def layer_norm(values_in, gain):
    values_in = values_in.astype(jnp.float32)
    centre = jnp.mean(values_in, axis=-1, keepdims=True)
    centred = values_in - centre
    spread = jnp.mean(centred * centred, axis=-1, keepdims=True)
    return centred * lax.rsqrt(spread + EPS_NORM) * gain


def span_memory(normed, live_mask, gain, span_len):
    model_width = normed.shape[1]
    masked = jnp.where(live_mask[:, None], normed.astype(jnp.float32), jnp.float32(0.0))
    owner_sums = masked.reshape(-1, span_len, model_width).sum(axis=1)
    counts = live_mask.reshape(-1, span_len).astype(jnp.float32).sum(axis=1)
    means = owner_sums / jnp.maximum(counts, 1.0)[:, None]
    power = jnp.mean(means * means, axis=-1, keepdims=True)
    return (means * lax.rsqrt(power + EPS_MEMORY) * gain).astype(jnp.bfloat16)


def block_size():
    return 256


def local_part(query, keys, values, first_frame, length, head_count, span_len, right_len):
    frame_count, model_width = query.shape
    head_size = model_width // head_count
    group_rows = 4 * span_len
    group_count = frame_count // group_rows
    block_rows = block_size()
    query_blocks = query.reshape(group_count, group_rows, head_count, head_size)
    key_blocks = keys[:frame_count].reshape(group_count, group_rows, head_count, head_size)
    value_blocks = values[:frame_count].reshape(group_count, group_rows, head_count, head_size)
    key_tail = keys[frame_count:].reshape(1, right_len, head_count, head_size)
    value_tail = values[frame_count:].reshape(1, right_len, head_count, head_size)
    key_all = jnp.concatenate(
        [key_blocks, jnp.concatenate([key_blocks[1:, :right_len], key_tail], axis=0)], axis=1
    )
    value_all = jnp.concatenate(
        [value_blocks, jnp.concatenate([value_blocks[1:, :right_len], value_tail], axis=0)], axis=1
    )
    start_offsets = jnp.arange(group_count, dtype=jnp.int32)[:, None] * group_rows
    query_pos = first_frame + start_offsets + jnp.arange(group_rows, dtype=jnp.int32)[None, :]
    key_pos = first_frame + jnp.concatenate(
        [
            start_offsets + jnp.arange(group_rows, dtype=jnp.int32)[None, :],
            start_offsets + group_rows + jnp.arange(right_len, dtype=jnp.int32)[None, :],
        ],
        axis=1,
    )
    query_span = query_pos // span_len
    span_end = (query_span + 1) * span_len
    same = (key_pos // span_len)[:, None, :] == query_span[:, :, None]
    ahead = (key_pos[:, None, :] >= span_end[:, :, None]) & (
        key_pos[:, None, :] < span_end[:, :, None] + right_len
    )
    allowed = (same | ahead) & (key_pos < length)[:, None, :]
    scores = jnp.einsum(
        "gqhd,gkhd->ghqk", query_blocks, key_all, preferred_element_type=jnp.float32
    ) * head_size ** (-0.5)
    scores = jnp.where(allowed[:, None], scores, NEG_BIG)
    row_peak = jnp.max(scores, axis=-1)
    weights = jnp.where(allowed[:, None], jnp.exp(scores - row_peak[..., None]), jnp.float32(0.0))
    row_total = jnp.sum(weights, axis=-1)
    accum = jnp.einsum(
        "ghqk,gkhd->ghqd",
        weights.astype(jnp.bfloat16),
        value_all,
        preferred_element_type=jnp.float32,
    )
    block_count = frame_count // block_rows
    row_peak = (
        row_peak.transpose(1, 0, 2).reshape(head_count, block_count, block_rows).transpose(1, 0, 2)
    )
    row_total = (
        row_total.transpose(1, 0, 2).reshape(head_count, block_count, block_rows).transpose(1, 0, 2)
    )
    accum = (
        accum.transpose(1, 0, 2, 3)
        .reshape(head_count, block_count, block_rows, head_size)
        .transpose(1, 0, 2, 3)
    )
    return (row_peak, row_total, accum)


def memory_update(
    carry, memory_keys, memory_values, query, first_frame, length, head_count, span_len
):
    row_peak, row_total, accum = carry
    block_count, _, block_rows = row_peak.shape
    row_count, model_width = memory_keys.shape
    head_size = model_width // head_count
    mem_keys = memory_keys.reshape(row_count, head_count, head_size)
    mem_values = memory_values.reshape(row_count, head_count, head_size)
    mem_index = jnp.arange(row_count, dtype=jnp.int32)
    mem_live = mem_index * span_len < length
    query_blocks = query.reshape(block_count, block_rows, head_count, head_size)
    positions = first_frame + jnp.arange(block_count * block_rows, dtype=jnp.int32).reshape(
        block_count, block_rows
    )

    def one_block(packed):
        query_now, pos_now, peak_now, total_now, accum_now = packed
        scores = jnp.einsum(
            "qhd,khd->hqk", query_now, mem_keys, preferred_element_type=jnp.float32
        ) * head_size ** (-0.5)
        allowed = (mem_index[None, :] < (pos_now // span_len)[:, None]) & mem_live[None, :]
        scores = jnp.where(allowed[None], scores, NEG_BIG)
        new_peak = jnp.maximum(peak_now, jnp.max(scores, axis=-1))
        weights = jnp.where(allowed[None], jnp.exp(scores - new_peak[..., None]), jnp.float32(0.0))
        factor = jnp.exp(peak_now - new_peak)
        total_next = total_now * factor + jnp.sum(weights, axis=-1)
        accum_next = accum_now * factor[..., None] + jnp.einsum(
            "hqk,khd->hqd",
            weights.astype(jnp.bfloat16),
            mem_values,
            preferred_element_type=jnp.float32,
        )
        return (new_peak, total_next, accum_next)

    return lax.map(one_block, (query_blocks, positions, row_peak, row_total, accum))


def finish(carry, frame_count, model_width):
    _, row_total, accum = carry
    result = accum / row_total[..., None]
    return result.transpose(0, 2, 1, 3).reshape(frame_count, model_width).astype(jnp.bfloat16)


def dispatch_matrix(owner_ids, owner_count, capacity):
    choose = (owner_ids[:, None] == jnp.arange(owner_count, dtype=jnp.int32)[None, :]).astype(
        jnp.int32
    )
    before = jnp.cumsum(choose, axis=0) - choose
    slot_index = jnp.sum(before * choose, axis=1)
    target = owner_ids * capacity + slot_index
    slot_rows = jnp.arange(owner_count * capacity, dtype=jnp.int32)
    return (slot_rows[:, None] == target[None, :]).astype(jnp.bfloat16)


def plain_device(
    frames,
    lengths,
    norm_gain,
    memory_gain,
    qkv_weight,
    out_weight,
    segment_ids,
    owners,
    language_weight,
):
    local_frames = frames[0]
    frame_count, model_width = local_frames.shape
    head_count = H
    time_count = lax.axis_size("tm")
    first_frame = lax.axis_index("tm") * frame_count
    length = lengths[0]
    live_mask = first_frame + jnp.arange(frame_count, dtype=jnp.int32) < length
    right_frames = shifted(local_frames[:RC], "tm", -1)
    normed = layer_norm(local_frames, norm_gain).astype(jnp.bfloat16)
    normed_right = layer_norm(right_frames, norm_gain).astype(jnp.bfloat16)
    memory = span_memory(normed, live_mask, memory_gain, C)
    stacked_rows = jnp.concatenate([normed, normed_right, memory], axis=0)
    projected = jnp.einsum(
        "fd,kdw->kfw",
        stacked_rows,
        lax.all_gather(qkv_weight, "tm", axis=2, tiled=True),
        preferred_element_type=jnp.float32,
    ).astype(jnp.bfloat16)
    split_at = frame_count + RC
    query = projected[0, :frame_count]
    keys = projected[1, :split_at]
    values = projected[2, :split_at]
    memory_keys = projected[1, split_at:]
    memory_values = projected[2, split_at:]
    carry = local_part(query, keys, values, first_frame, length, head_count, C, RC)
    carry = memory_update(
        carry,
        lax.all_gather(memory_keys, "tm", axis=0, tiled=True),
        lax.all_gather(memory_values, "tm", axis=0, tiled=True),
        query,
        first_frame,
        length,
        head_count,
        C,
    )
    attended = finish(carry, frame_count, model_width)
    output_proj = jnp.dot(
        attended,
        lax.all_gather(out_weight, "tm", axis=1, tiled=True),
        preferred_element_type=jnp.float32,
    )
    encoded = jnp.where(
        live_mask[:, None], local_frames.astype(jnp.float32) + output_proj, jnp.float32(0.0)
    ).astype(jnp.bfloat16)
    token_count = owners.shape[2]
    segments = segment_ids[0, 0]
    owner_indicator = (
        segments[None, :] == jnp.arange(token_count, dtype=jnp.int32)[:, None]
    ).astype(jnp.bfloat16)
    owner_sums = jnp.dot(owner_indicator, encoded, preferred_element_type=jnp.float32)
    counts = jnp.sum(owner_indicator.astype(jnp.float32), axis=1)
    pooled_rows = (owner_sums / counts[:, None]).astype(jnp.bfloat16)
    slot_count = 2 * token_count
    capacity = slot_count // time_count
    route_matrix = dispatch_matrix(owners[0, 0, :, 0], time_count, capacity)
    sent_rows = jnp.dot(route_matrix, pooled_rows, preferred_element_type=jnp.float32).astype(
        jnp.bfloat16
    )
    received = lax.all_to_all(
        sent_rows.reshape(time_count, capacity, model_width),
        "tm",
        split_axis=0,
        concat_axis=0,
        tiled=True,
    )
    received = received.reshape(slot_count, model_width)
    lm_out = jnp.dot(
        received,
        lax.all_gather(language_weight, "rec", axis=1, tiled=True),
        preferred_element_type=jnp.float32,
    ).astype(jnp.bfloat16)
    return (encoded[None], lm_out[None, None])


def vmem_spec():
    return pl.BlockSpec(memory_space=pltpu.VMEM)


def smem_spec():
    return pl.BlockSpec(memory_space=pltpu.SMEM)


def local_call(kernel, out_shapes, scalars, operands, scratch=(), in_place=0, flops=0, moved=0):
    whole = len(operands) - in_place
    return pl.pallas_call(
        kernel,
        out_shape=out_shapes,
        in_specs=[smem_spec()] * len(scalars)
        + [vmem_spec()] * whole
        + [pl.BlockSpec(memory_space=pl.ANY)] * in_place,
        out_specs=jax.tree.map(lambda _: vmem_spec(), out_shapes),
        scratch_shapes=list(scratch),
        cost_estimate=pl.CostEstimate(flops=flops, bytes_accessed=moved, transcendentals=0),
    )(*scalars, *operands)


def shape_of(*dims, dtype=jnp.bfloat16):
    return jax.ShapeDtypeStruct(dims, dtype)


def normalise_kernel(span_len, scalars, frames, gain, memory_gain, normed_out, memory_out):
    first_frame, length = scalars[0], scalars[1]
    frame_count, _ = frames.shape
    span_count = frame_count // span_len
    values = frames[...].astype(jnp.float32)
    centre = jnp.mean(values, axis=-1, keepdims=True)
    centred = values - centre
    spread = jnp.mean(centred * centred, axis=-1, keepdims=True)
    normed = (centred * lax.rsqrt(spread + EPS_NORM) * gain[...]).astype(jnp.bfloat16)
    normed_out[...] = normed
    spans = lax.broadcasted_iota(jnp.int32, (span_count, frame_count), 0)
    places = lax.broadcasted_iota(jnp.int32, (span_count, frame_count), 1)
    member = (places >= spans * span_len) & (places < (spans + 1) * span_len)
    member = member & (places < length - first_frame)
    sums = jnp.dot(
        member.astype(jnp.bfloat16), normed, preferred_element_type=jnp.float32
    )
    counts = jnp.sum(member.astype(jnp.float32), axis=-1, keepdims=True)
    means = sums / jnp.maximum(counts, 1.0)
    power = jnp.mean(means * means, axis=-1, keepdims=True)
    memory_out[...] = (
        means * lax.rsqrt(power + EPS_MEMORY) * memory_gain[...]
    ).astype(jnp.bfloat16)


def attend_kernel(span_len, right_len, head_size, scalars, other_length, *refs):
    sources, pieces = refs[:4], refs[4:12]
    out_0, out_1, projection = refs[12:15]
    rows_in, weight, query, key, value, bias, scores, peaks, weights, sems = refs[15:]
    first_frame, core, y_half = scalars[0], scalars[2], scalars[3]
    frame_count, model_width = sources[0].shape
    half = model_width // 2
    width = out_0.shape[1]
    heads = width // head_size
    block = 2 * span_len
    blocks = frame_count // block
    near = bias.shape[0]
    pad = near - block
    row_count = rows_in.shape[1]
    memory_count = row_count - frame_count - pad
    memory_at = frame_count + pad
    lanes = heads * block

    def piece_copies(of_core, projected):
        places = (y_half * half, (1 - y_half) * half)
        copies = []
        for side in range(2):
            place = pl.ds(pl.multiple_of(places[side], half), half)
            for shard in range(2):
                piece = pieces[4 * shard + 2 * side + of_core]
                columns = pl.ds(shard * piece.shape[2], piece.shape[2])
                index = 2 * side + shard
                if projected:
                    ends = piece.at[3], projection.at[place, columns], sems.at[4 + index]
                else:
                    ends = piece.at[0:3], weight.at[:, place, columns], sems.at[index]
                copies.append(pltpu.make_async_copy(*ends))
        return copies

    row_copies = []
    for rec in range(2):
        row_copies.append(
            [
                pltpu.make_async_copy(
                    sources[2 * rec], rows_in.at[rec, 0:frame_count], sems.at[8 + 2 * rec]
                ),
                pltpu.make_async_copy(
                    sources[2 * rec + 1],
                    rows_in.at[rec, frame_count:row_count],
                    sems.at[9 + 2 * rec],
                ),
            ]
        )

    for of_core in range(2):

        @pl.when(core == of_core)
        def _():
            for copy in piece_copies(of_core, False):
                copy.start()

    for copies in row_copies:
        for copy in copies:
            copy.start()

    for of_core in range(2):

        @pl.when(core == of_core)
        def _():
            for copy in piece_copies(of_core, True):
                copy.start()

    rows = lax.broadcasted_iota(jnp.int32, (near, lanes), 0)
    spans = (lax.broadcasted_iota(jnp.int32, (near, lanes), 1) % block) // span_len
    same = (rows >= spans * span_len) & (rows < (spans + 1) * span_len + right_len)
    bias[...] = jnp.where(same, jnp.float32(0.0), jnp.float32(NEG_BIG))
    lane_spans = (lax.broadcasted_iota(jnp.int32, (1, lanes), 1) % block) // span_len
    memory_rows = lax.broadcasted_iota(jnp.int32, (memory_count, lanes), 0)
    feature_head = lax.broadcasted_iota(jnp.int32, (1, width), 1) // head_size
    head_masks = [(feature_head == h).astype(jnp.bfloat16) for h in range(heads)]
    scale = head_size ** (-0.5) * LOG2_E

    for copy in piece_copies(0, False):
        copy.wait()
    for rec in range(2):
        for copy in row_copies[rec]:
            copy.wait()
        query[rec] = (
            jnp.dot(
                rows_in[rec, 0:frame_count], weight[0], preferred_element_type=jnp.float32
            )
            * scale
        ).astype(jnp.bfloat16)
        key[rec] = jnp.dot(
            rows_in[rec], weight[1], preferred_element_type=jnp.float32
        ).astype(jnp.bfloat16)
        value[rec] = jnp.dot(
            rows_in[rec], weight[2], preferred_element_type=jnp.float32
        ).astype(jnp.bfloat16)

    def score_block(i, _):
        rec = i // blocks
        b = i - rec * blocks
        length = jnp.where(rec == 0, scalars[1], other_length[0])
        start = pl.multiple_of(b * block, block)
        q_now = query[rec, pl.ds(start, block), :]
        stacked = jnp.concatenate([q_now * m for m in head_masks], axis=0)
        keys = jnp.concatenate(
            [key[rec, pl.ds(start, near), :], key[rec, memory_at:row_count, :]], axis=0
        )
        raw = lax.dot_general(
            keys, stacked, (((1,), (1,)), ((), ())), preferred_element_type=jnp.float32
        )
        limit = length - first_frame - start
        local = jnp.where(rows < limit, raw[:near] + bias[...], NEG_BIG)
        live_spans = (length + span_len - 1) // span_len
        span_limit = jnp.minimum(first_frame // span_len + 2 * b + lane_spans, live_spans)
        memory = jnp.where(memory_rows < span_limit, raw[near:], NEG_BIG)
        scores[i, 0:near, :] = local
        scores[i, near:, :] = memory
        peaks[i] = jnp.maximum(
            jnp.max(local, axis=0, keepdims=True), jnp.max(memory, axis=0, keepdims=True)
        )
        return 0

    def weigh_block(i, _):
        weights[i] = jnp.exp2(scores[i] - peaks[i]).astype(jnp.bfloat16)
        return 0

    ones = jnp.ones((near + memory_count, LANES), jnp.bfloat16)
    first_of_pair = lax.broadcasted_iota(jnp.int32, (1, 2 * LANES), 1) % LANES < head_size

    def mix_block(rec, out):
        def body(b, _):
            start = pl.multiple_of(b * block, block)
            values = jnp.concatenate(
                [value[rec, pl.ds(start, near), :], value[rec, memory_at:row_count, :]], axis=0
            )
            for pair in range(width // LANES):
                columns = slice(pair * LANES, (pair + 1) * LANES)
                pair_rows = slice(pair * 2 * block, (pair + 1) * 2 * block)
                mixed = lax.dot_general(
                    weights[rec * blocks + b, :, pair_rows],
                    jnp.concatenate([values[:, columns], ones], axis=1),
                    (((0,), (0,)), ((), ())),
                    preferred_element_type=jnp.float32,
                )
                picked = jnp.where(first_of_pair, mixed[:block], mixed[block:])
                out[pl.ds(start, block), columns] = (
                    picked[:, :LANES] / picked[:, LANES:]
                ).astype(jnp.bfloat16)
            return 0

        return body

    lax.fori_loop(0, 2 * blocks, score_block, 0, unroll=2)
    lax.fori_loop(0, 2 * blocks, weigh_block, 0, unroll=2)
    for rec, out in enumerate((out_0, out_1)):
        lax.fori_loop(0, blocks, mix_block(rec, out), 0, unroll=2)
    for copy in piece_copies(0, True):
        copy.wait()


def assemble(scalars, offsets_at, attended, gathered):
    shard = attended[0].shape[1] // 2
    offsets = [
        [pl.multiple_of(scalars[offsets_at + 2 * i + s], LANES) for s in range(2)]
        for i in range(4)
    ]
    for i in range(4):
        for s in range(2):
            gathered[:, pl.ds(offsets[i][s], shard)] = attended[i][:, s * shard : (s + 1) * shard]
    return offsets, shard


def pool_kernel(offsets_at, scalars, *refs):
    attended, projections = refs[:4], refs[4:8]
    frames, segments, owners_row, owners_col = refs[8:12]
    sent_out, gathered = refs[12:]
    first_frame, length, capacity = scalars[0], scalars[1], scalars[4]
    frame_count, _ = frames.shape
    offsets, shard = assemble(scalars, offsets_at, attended, gathered)
    token_count = owners_row.shape[1]
    tokens = lax.broadcasted_iota(jnp.int32, (token_count, frame_count), 0)
    places = first_frame + lax.broadcasted_iota(jnp.int32, (token_count, frame_count), 1)
    member = (segments[...] == tokens).astype(jnp.float32)
    counts = jnp.sum(member, axis=1, keepdims=True)
    live_member = jnp.where(places < length, member, 0.0).astype(jnp.bfloat16)
    earlier = lax.broadcasted_iota(jnp.int32, (token_count, token_count), 0)
    later = lax.broadcasted_iota(jnp.int32, (token_count, token_count), 1)
    clash = (owners_col[...] == owners_row[...]) & (earlier < later)
    slot = jnp.sum(clash.astype(jnp.int32), axis=0, keepdims=True)
    target = owners_row[...] * capacity + slot
    slots = lax.broadcasted_iota(jnp.int32, (sent_out.shape[0], token_count), 0)
    route = (slots == target).astype(jnp.bfloat16)
    mean_attended = (
        jnp.dot(live_member, gathered[...], preferred_element_type=jnp.float32) / counts
    ).astype(jnp.bfloat16)
    for i in range(4):
        mixed = jnp.dot(mean_attended, projections[i][...], preferred_element_type=jnp.float32)
        for s in range(2):
            columns = pl.ds(offsets[i][s], shard)
            base = jnp.dot(live_member, frames[:, columns], preferred_element_type=jnp.float32)
            pooled = (base / counts + mixed[:, s * shard : (s + 1) * shard]).astype(jnp.bfloat16)
            sent_out[:, columns] = jnp.dot(
                route, pooled, preferred_element_type=jnp.float32
            ).astype(jnp.bfloat16)


def encode_kernel(offsets_at, scalars, *refs):
    attended, projections, frames = refs[:4], refs[4:8], refs[8]
    encoded_out, gathered = refs[9:]
    first_frame, length = scalars[0], scalars[1]
    frame_count, _ = frames.shape
    offsets, shard = assemble(scalars, offsets_at, attended, gathered)
    live = (
        first_frame + lax.broadcasted_iota(jnp.int32, (frame_count, 1), 0) < length
    ).astype(jnp.float32)
    for i in range(4):
        mixed = jnp.dot(
            gathered[...], projections[i][...], preferred_element_type=jnp.float32
        )
        for s in range(2):
            columns = pl.ds(offsets[i][s], shard)
            base = frames[:, columns].astype(jnp.float32)
            encoded_out[:, columns] = (
                (base + mixed[:, s * shard : (s + 1) * shard]) * live
            ).astype(jnp.bfloat16)


def language_kernel(places_at, scalars, received, *refs):
    pieces, out, weights, sems = refs[:-3], refs[-3], refs[-2], refs[-1]
    half, width = pieces[0].shape
    copies = [
        pltpu.make_async_copy(
            piece, weights.at[i // 2, pl.ds((i % 2) * half, half)], sems.at[i]
        )
        for i, piece in enumerate(pieces)
    ]
    for copy in copies:
        copy.start()
    for i in range(len(pieces) // 2):
        copies[2 * i].wait()
        copies[2 * i + 1].wait()
        place = pl.multiple_of(scalars[places_at + i], LANES)
        out[:, pl.ds(place, width)] = jnp.dot(
            received[...], weights[i], preferred_element_type=jnp.float32
        ).astype(jnp.bfloat16)


def along_x(r, j, _):
    return r, j ^ 1


def along_y(r, j, _):
    return r ^ 2, j


def other_core(r, j, _):
    return r ^ 1, j


def z_up(r, j, count):
    return r, (j + 2) % count


def z_down(r, j, count):
    return r, (j - 2) % count


def relocate(value, core_0, core_1):
    rec_count, time_count = lax.axis_size("rec"), lax.axis_size("tm")
    pairs = []
    for r in range(rec_count):
        for j in range(time_count):
            route = (core_0, core_1)[r % 2]
            if route is not None:
                to_r, to_j = route(r, j, time_count)
                pairs.append((r * time_count + j, to_r * time_count + to_j))
    return lax.ppermute(value, ("rec", "tm"), pairs)


def swap_cores(value):
    return relocate(value, other_core, other_core)


def exchange_blocks(blocks):
    return lax.all_to_all(blocks, "tm", split_axis=0, concat_axis=0, tiled=True)


def per_device(
    frames,
    lengths,
    norm_gain,
    memory_gain,
    qkv_weight,
    out_weight,
    segment_ids,
    owners,
    language_weight,
):
    local_frames = frames[0]
    frame_count, model_width = local_frames.shape
    shard = out_weight.shape[1]
    half = model_width // 2
    time_count = lax.axis_size("tm")
    rec_count = lax.axis_size("rec")
    rec, time = lax.axis_index("rec"), lax.axis_index("tm")
    core, y_half = rec % 2, (rec // 2) % 2
    x, z = time % 2, time // 2
    z_count = time_count // 2
    first_frame = time * frame_count
    length = lengths[0]
    head_size = model_width // H
    bf16 = jnp.bfloat16

    own = jnp.concatenate([qkv_weight, out_weight[None]], axis=0)
    own_a = lax.dynamic_slice_in_dim(own, y_half * half, half, 1)
    own_b = lax.dynamic_slice_in_dim(own, (1 - y_half) * half, half, 1)

    def pick(for_core_0, for_core_1):
        return jnp.where(core == 0, for_core_0, for_core_1)

    token_count = owners.shape[2]
    slot_count = 2 * token_count
    capacity = slot_count // time_count
    language_shard = language_weight.shape[1]

    def group_of(of_core, slot):
        return jnp.where(of_core == 0, z + slot, z - slot - 1) % z_count

    numbers = [first_frame, length, core, y_half, capacity]
    offsets_at = len(numbers)
    for of_core in (core, 1 - core):
        for slot in range(2):
            group = group_of(of_core, slot)
            numbers += [(2 * group + x) * shard, (2 * group + 1 - x) * shard]
    places_at = len(numbers)
    numbers += [(rec ^ i) * language_shard for i in range(rec_count)]
    scalars = jnp.stack(numbers).astype(jnp.int32)

    m1 = relocate(own_a, along_x, z_up)
    m2 = relocate(pick(own_a, own_b), z_down, z_up)
    language_half = language_weight.shape[0] // 2
    upper, lower = language_weight[:language_half], language_weight[language_half:]
    l1a = relocate(upper, along_y, along_y)
    l1b = relocate(lower, along_y, along_y)

    normed, memory = local_call(
        functools.partial(normalise_kernel, C),
        (shape_of(frame_count, model_width), shape_of(frame_count // C, model_width)),
        (scalars,),
        (local_frames, norm_gain[None], memory_gain[None]),
        flops=10 * frame_count * model_width,
        moved=4 * frame_count * model_width,
    )
    other_length = swap_cores(lengths)
    other_normed = swap_cores(normed)
    ahead = shifted(normed[:RC], "tm", -1)
    memories = exchange_blocks(
        jnp.broadcast_to(memory[None], (time_count,) + memory.shape)
    ).reshape(-1, model_width)
    extra = jnp.concatenate([ahead, jnp.zeros_like(ahead), memories], axis=0)
    other_extra = swap_cores(extra)

    m3 = relocate(m1, along_y, along_x)
    m4 = relocate(m1, None, z_up)
    m5 = relocate(m2, along_x, z_up)
    m6 = relocate(m3, None, along_y)
    m6b = relocate(m2, along_y, None)
    m7 = relocate(m4, None, along_x)
    m8 = relocate(m5, along_y, along_x)

    slot_pieces = (
        ((own_a, m1), (own_b, m2), (m1, m3), (m3, m6)),
        ((m2, m4), (m6b, m5), (m5, m7), (m8, m8)),
    )
    pad = 2 * RC
    block = 2 * C
    width = 2 * shard
    row_count = frame_count + extra.shape[0]
    keys_seen = block + extra.shape[0]
    lanes = width // head_size * block
    block_count = 2 * (frame_count // block)
    attended, outs = [], []
    for pieces in slot_pieces:
        flat = [p for pair in pieces for p in pair]
        *pair, out_piece = local_call(
            functools.partial(attend_kernel, C, RC, head_size),
            (
                shape_of(frame_count, width),
                shape_of(frame_count, width),
                shape_of(model_width, width),
            ),
            (scalars, other_length),
            (normed, extra, other_normed, other_extra, *flat),
            in_place=4 + len(flat),
            scratch=(
                pltpu.VMEM((2, row_count, model_width), bf16),
                pltpu.VMEM((3, model_width, width), bf16),
                pltpu.VMEM((2, frame_count, width), bf16),
                pltpu.VMEM((2, row_count, width), bf16),
                pltpu.VMEM((2, row_count, width), bf16),
                pltpu.VMEM((block + pad, lanes), jnp.float32),
                pltpu.VMEM((block_count, keys_seen, lanes), jnp.float32),
                pltpu.VMEM((block_count, 1, lanes), jnp.float32),
                pltpu.VMEM((block_count, keys_seen, lanes), bf16),
                pltpu.SemaphoreType.DMA((12,)),
            ),
            flops=12 * frame_count * model_width * width,
            moved=8 * frame_count * model_width,
        )
        attended.append(pair)
        outs.append(out_piece)
    other_outs = [swap_cores(w) for w in outs]
    other_attended = [swap_cores(for_other) for _, for_other in attended]

    owners_col = owners[0, 0]
    features = (attended[0][0], attended[1][0], *other_attended, *outs, *other_outs, local_frames)
    sent_rows = local_call(
        functools.partial(pool_kernel, offsets_at),
        shape_of(slot_count, model_width),
        (scalars,),
        (*features, segment_ids[0], owners_col.reshape(1, token_count), owners_col),
        scratch=(pltpu.VMEM((frame_count, model_width), bf16),),
        flops=4 * token_count * model_width * model_width,
        moved=6 * frame_count * model_width,
    )
    received = exchange_blocks(
        sent_rows.reshape(time_count, capacity, model_width)
    ).reshape(slot_count, model_width)
    encoded = local_call(
        functools.partial(encode_kernel, offsets_at),
        shape_of(frame_count, model_width),
        (scalars,),
        features,
        scratch=(pltpu.VMEM((frame_count, model_width), bf16),),
        flops=2 * frame_count * model_width * model_width,
        moved=6 * frame_count * model_width,
    )
    language_pieces = (
        upper,
        lower,
        swap_cores(upper),
        swap_cores(lower),
        l1a,
        l1b,
        swap_cores(l1a),
        swap_cores(l1b),
    )
    lm_out = local_call(
        functools.partial(language_kernel, places_at),
        shape_of(slot_count, rec_count * language_shard),
        (scalars,),
        (received, *language_pieces),
        in_place=len(language_pieces),
        scratch=(
            pltpu.VMEM((rec_count, model_width, language_shard), bf16),
            pltpu.SemaphoreType.DMA((len(language_pieces),)),
        ),
        flops=2 * slot_count * model_width * rec_count * language_shard,
        moved=2 * model_width * rec_count * language_shard,
    )
    return (encoded[None], lm_out[None, None])


def solution(mesh):
    in_specs = (
        P("rec", "tm", None),
        P("rec"),
        P(),
        P(),
        P(None, None, "tm"),
        P(None, "tm"),
        P("rec", "tm", None),
        P("rec", "tm", None, None),
        P(None, "rec"),
    )
    out_specs = (P("rec", "tm", None), P("rec", "tm", None, None))
    rec_count, time_count = mesh.shape["rec"], mesh.shape["tm"]
    paired = shard_map_of(mesh, in_specs, out_specs, per_device)
    plain = shard_map_of(mesh, in_specs, out_specs, plain_device)

    def run(*arrays):
        shard = arrays[5].shape[1] // time_count
        fits = rec_count == 4 and time_count == 8 and shard % LANES == 0
        return (paired if fits else plain)(*arrays)

    return run


def shard_map_of(mesh, in_specs, out_specs, body):
    return jax.shard_map(
        body, mesh=mesh, in_specs=in_specs, out_specs=out_specs, check_vma=False
    )
```

```python
import functools

import jax
import jax.numpy as jnp
from jax import lax
from jax.experimental import pallas as pl
from jax.experimental.pallas import tpu as pltpu
from jax.sharding import PartitionSpec as P


H = 16
C = 32
RC = 8


EPS_NORM = 1e-05
EPS_MEMORY = 1e-06
NEG_BIG = -1e30
LANES = 128
LOG2_E = 1.4426950408889634


def shifted(block, axis, distance):
    devices = range(lax.axis_size(axis))
    route = [(i - distance, i) for i in devices if i - distance in devices]
    return lax.ppermute(block, axis, route)


def layer_norm(values_in, gain):
    values_in = values_in.astype(jnp.float32)
    centre = jnp.mean(values_in, axis=-1, keepdims=True)
    centred = values_in - centre
    spread = jnp.mean(centred * centred, axis=-1, keepdims=True)
    return centred * lax.rsqrt(spread + EPS_NORM) * gain


def span_memory(normed, live_mask, gain, span_len):
    model_width = normed.shape[1]
    masked = jnp.where(live_mask[:, None], normed.astype(jnp.float32), jnp.float32(0.0))
    owner_sums = masked.reshape(-1, span_len, model_width).sum(axis=1)
    counts = live_mask.reshape(-1, span_len).astype(jnp.float32).sum(axis=1)
    means = owner_sums / jnp.maximum(counts, 1.0)[:, None]
    power = jnp.mean(means * means, axis=-1, keepdims=True)
    return (means * lax.rsqrt(power + EPS_MEMORY) * gain).astype(jnp.bfloat16)


def block_size():
    return 256


def local_part(query, keys, values, first_frame, length, head_count, span_len, right_len):
    frame_count, model_width = query.shape
    head_size = model_width // head_count
    group_rows = 4 * span_len
    group_count = frame_count // group_rows
    block_rows = block_size()
    query_blocks = query.reshape(group_count, group_rows, head_count, head_size)
    key_blocks = keys[:frame_count].reshape(group_count, group_rows, head_count, head_size)
    value_blocks = values[:frame_count].reshape(group_count, group_rows, head_count, head_size)
    key_tail = keys[frame_count:].reshape(1, right_len, head_count, head_size)
    value_tail = values[frame_count:].reshape(1, right_len, head_count, head_size)
    key_all = jnp.concatenate(
        [key_blocks, jnp.concatenate([key_blocks[1:, :right_len], key_tail], axis=0)], axis=1
    )
    value_all = jnp.concatenate(
        [value_blocks, jnp.concatenate([value_blocks[1:, :right_len], value_tail], axis=0)], axis=1
    )
    start_offsets = jnp.arange(group_count, dtype=jnp.int32)[:, None] * group_rows
    query_pos = first_frame + start_offsets + jnp.arange(group_rows, dtype=jnp.int32)[None, :]
    key_pos = first_frame + jnp.concatenate(
        [
            start_offsets + jnp.arange(group_rows, dtype=jnp.int32)[None, :],
            start_offsets + group_rows + jnp.arange(right_len, dtype=jnp.int32)[None, :],
        ],
        axis=1,
    )
    query_span = query_pos // span_len
    span_end = (query_span + 1) * span_len
    same = (key_pos // span_len)[:, None, :] == query_span[:, :, None]
    ahead = (key_pos[:, None, :] >= span_end[:, :, None]) & (
        key_pos[:, None, :] < span_end[:, :, None] + right_len
    )
    allowed = (same | ahead) & (key_pos < length)[:, None, :]
    scores = jnp.einsum(
        "gqhd,gkhd->ghqk", query_blocks, key_all, preferred_element_type=jnp.float32
    ) * head_size ** (-0.5)
    scores = jnp.where(allowed[:, None], scores, NEG_BIG)
    row_peak = jnp.max(scores, axis=-1)
    weights = jnp.where(allowed[:, None], jnp.exp(scores - row_peak[..., None]), jnp.float32(0.0))
    row_total = jnp.sum(weights, axis=-1)
    accum = jnp.einsum(
        "ghqk,gkhd->ghqd",
        weights.astype(jnp.bfloat16),
        value_all,
        preferred_element_type=jnp.float32,
    )
    block_count = frame_count // block_rows
    row_peak = (
        row_peak.transpose(1, 0, 2).reshape(head_count, block_count, block_rows).transpose(1, 0, 2)
    )
    row_total = (
        row_total.transpose(1, 0, 2).reshape(head_count, block_count, block_rows).transpose(1, 0, 2)
    )
    accum = (
        accum.transpose(1, 0, 2, 3)
        .reshape(head_count, block_count, block_rows, head_size)
        .transpose(1, 0, 2, 3)
    )
    return (row_peak, row_total, accum)


def memory_update(
    carry, memory_keys, memory_values, query, first_frame, length, head_count, span_len
):
    row_peak, row_total, accum = carry
    block_count, _, block_rows = row_peak.shape
    row_count, model_width = memory_keys.shape
    head_size = model_width // head_count
    mem_keys = memory_keys.reshape(row_count, head_count, head_size)
    mem_values = memory_values.reshape(row_count, head_count, head_size)
    mem_index = jnp.arange(row_count, dtype=jnp.int32)
    mem_live = mem_index * span_len < length
    query_blocks = query.reshape(block_count, block_rows, head_count, head_size)
    positions = first_frame + jnp.arange(block_count * block_rows, dtype=jnp.int32).reshape(
        block_count, block_rows
    )

    def one_block(packed):
        query_now, pos_now, peak_now, total_now, accum_now = packed
        scores = jnp.einsum(
            "qhd,khd->hqk", query_now, mem_keys, preferred_element_type=jnp.float32
        ) * head_size ** (-0.5)
        allowed = (mem_index[None, :] < (pos_now // span_len)[:, None]) & mem_live[None, :]
        scores = jnp.where(allowed[None], scores, NEG_BIG)
        new_peak = jnp.maximum(peak_now, jnp.max(scores, axis=-1))
        weights = jnp.where(allowed[None], jnp.exp(scores - new_peak[..., None]), jnp.float32(0.0))
        factor = jnp.exp(peak_now - new_peak)
        total_next = total_now * factor + jnp.sum(weights, axis=-1)
        accum_next = accum_now * factor[..., None] + jnp.einsum(
            "hqk,khd->hqd",
            weights.astype(jnp.bfloat16),
            mem_values,
            preferred_element_type=jnp.float32,
        )
        return (new_peak, total_next, accum_next)

    return lax.map(one_block, (query_blocks, positions, row_peak, row_total, accum))


def finish(carry, frame_count, model_width):
    _, row_total, accum = carry
    result = accum / row_total[..., None]
    return result.transpose(0, 2, 1, 3).reshape(frame_count, model_width).astype(jnp.bfloat16)


def dispatch_matrix(owner_ids, owner_count, capacity):
    choose = (owner_ids[:, None] == jnp.arange(owner_count, dtype=jnp.int32)[None, :]).astype(
        jnp.int32
    )
    before = jnp.cumsum(choose, axis=0) - choose
    slot_index = jnp.sum(before * choose, axis=1)
    target = owner_ids * capacity + slot_index
    slot_rows = jnp.arange(owner_count * capacity, dtype=jnp.int32)
    return (slot_rows[:, None] == target[None, :]).astype(jnp.bfloat16)


def plain_device(
    frames,
    lengths,
    norm_gain,
    memory_gain,
    qkv_weight,
    out_weight,
    segment_ids,
    owners,
    language_weight,
):
    local_frames = frames[0]
    frame_count, model_width = local_frames.shape
    head_count = H
    time_count = lax.axis_size("tm")
    first_frame = lax.axis_index("tm") * frame_count
    length = lengths[0]
    live_mask = first_frame + jnp.arange(frame_count, dtype=jnp.int32) < length
    right_frames = shifted(local_frames[:RC], "tm", -1)
    normed = layer_norm(local_frames, norm_gain).astype(jnp.bfloat16)
    normed_right = layer_norm(right_frames, norm_gain).astype(jnp.bfloat16)
    memory = span_memory(normed, live_mask, memory_gain, C)
    stacked_rows = jnp.concatenate([normed, normed_right, memory], axis=0)
    projected = jnp.einsum(
        "fd,kdw->kfw",
        stacked_rows,
        lax.all_gather(qkv_weight, "tm", axis=2, tiled=True),
        preferred_element_type=jnp.float32,
    ).astype(jnp.bfloat16)
    split_at = frame_count + RC
    query = projected[0, :frame_count]
    keys = projected[1, :split_at]
    values = projected[2, :split_at]
    memory_keys = projected[1, split_at:]
    memory_values = projected[2, split_at:]
    carry = local_part(query, keys, values, first_frame, length, head_count, C, RC)
    carry = memory_update(
        carry,
        lax.all_gather(memory_keys, "tm", axis=0, tiled=True),
        lax.all_gather(memory_values, "tm", axis=0, tiled=True),
        query,
        first_frame,
        length,
        head_count,
        C,
    )
    attended = finish(carry, frame_count, model_width)
    output_proj = jnp.dot(
        attended,
        lax.all_gather(out_weight, "tm", axis=1, tiled=True),
        preferred_element_type=jnp.float32,
    )
    encoded = jnp.where(
        live_mask[:, None], local_frames.astype(jnp.float32) + output_proj, jnp.float32(0.0)
    ).astype(jnp.bfloat16)
    token_count = owners.shape[2]
    segments = segment_ids[0, 0]
    owner_indicator = (
        segments[None, :] == jnp.arange(token_count, dtype=jnp.int32)[:, None]
    ).astype(jnp.bfloat16)
    owner_sums = jnp.dot(owner_indicator, encoded, preferred_element_type=jnp.float32)
    counts = jnp.sum(owner_indicator.astype(jnp.float32), axis=1)
    pooled_rows = (owner_sums / counts[:, None]).astype(jnp.bfloat16)
    slot_count = 2 * token_count
    capacity = slot_count // time_count
    route_matrix = dispatch_matrix(owners[0, 0, :, 0], time_count, capacity)
    sent_rows = jnp.dot(route_matrix, pooled_rows, preferred_element_type=jnp.float32).astype(
        jnp.bfloat16
    )
    received = lax.all_to_all(
        sent_rows.reshape(time_count, capacity, model_width),
        "tm",
        split_axis=0,
        concat_axis=0,
        tiled=True,
    )
    received = received.reshape(slot_count, model_width)
    lm_out = jnp.dot(
        received,
        lax.all_gather(language_weight, "rec", axis=1, tiled=True),
        preferred_element_type=jnp.float32,
    ).astype(jnp.bfloat16)
    return (encoded[None], lm_out[None, None])


def vmem_spec():
    return pl.BlockSpec(memory_space=pltpu.VMEM)


def smem_spec():
    return pl.BlockSpec(memory_space=pltpu.SMEM)


def local_call(kernel, out_shapes, scalars, operands, scratch=(), in_place=0, out_in_place=False, vmem_mib=16, flops=0, moved=0):
    whole = len(operands) - in_place
    return pl.pallas_call(
        kernel,
        out_shape=out_shapes,
        in_specs=[smem_spec()] * len(scalars)
        + [vmem_spec()] * whole
        + [pl.BlockSpec(memory_space=pl.ANY)] * in_place,
        out_specs=jax.tree.map(
            lambda _: pl.BlockSpec(memory_space=pl.ANY) if out_in_place else vmem_spec(), out_shapes
        ),
        compiler_params=pltpu.CompilerParams(vmem_limit_bytes=vmem_mib << 20),
        scratch_shapes=list(scratch),
        cost_estimate=pl.CostEstimate(flops=flops, bytes_accessed=moved, transcendentals=0),
    )(*scalars, *operands)


def shape_of(*dims, dtype=jnp.bfloat16):
    return jax.ShapeDtypeStruct(dims, dtype)


def normalise_kernel(
    span_len, scalars, frames, gain, memory_gain, normed_out, ahead_out, memory_out
):
    first_frame, length = scalars[0], scalars[1]
    frame_count, _ = frames.shape
    span_count = frame_count // span_len
    values = frames[...].astype(jnp.float32)
    centre = jnp.mean(values, axis=-1, keepdims=True)
    centred = values - centre
    spread = jnp.mean(centred * centred, axis=-1, keepdims=True)
    normed = (centred * lax.rsqrt(spread + EPS_NORM) * gain[...]).astype(jnp.bfloat16)
    normed_out[...] = normed
    ahead_out[...] = normed[: ahead_out.shape[0]]
    spans = lax.broadcasted_iota(jnp.int32, (span_count, frame_count), 0)
    places = lax.broadcasted_iota(jnp.int32, (span_count, frame_count), 1)
    member = (places >= spans * span_len) & (places < (spans + 1) * span_len)
    member = member & (places < length - first_frame)
    sums = jnp.dot(
        member.astype(jnp.bfloat16), normed, preferred_element_type=jnp.float32
    )
    counts = jnp.sum(member.astype(jnp.float32), axis=-1, keepdims=True)
    means = sums / jnp.maximum(counts, 1.0)
    power = jnp.mean(means * means, axis=-1, keepdims=True)
    memory = (means * lax.rsqrt(power + EPS_MEMORY) * memory_gain[...]).astype(jnp.bfloat16)
    for copy in range(memory_out.shape[0]):
        memory_out[copy] = memory


def prepare_kernel(scalars, frames, segments, owners_row, owners_col, base_out, member_out, count_out, route_out):
    first_frame, length, capacity = scalars[0], scalars[1], scalars[4]
    token_count, frame_count = member_out.shape
    tokens = lax.broadcasted_iota(jnp.int32, (token_count, frame_count), 0)
    places = first_frame + lax.broadcasted_iota(jnp.int32, (token_count, frame_count), 1)
    member = (segments[...] == tokens).astype(jnp.float32)
    counts = jnp.sum(member, axis=1, keepdims=True)
    live_member = jnp.where(places < length, member, 0.0).astype(jnp.bfloat16)
    earlier = lax.broadcasted_iota(jnp.int32, (token_count, token_count), 0)
    later = lax.broadcasted_iota(jnp.int32, (token_count, token_count), 1)
    clash = (owners_col[...] == owners_row[...]) & (earlier < later)
    slot = jnp.sum(clash.astype(jnp.int32), axis=0, keepdims=True)
    target = owners_row[...] * capacity + slot
    slots = lax.broadcasted_iota(jnp.int32, route_out.shape, 0)
    route_out[...] = (slots == target).astype(jnp.bfloat16)
    member_out[...] = live_member
    count_out[...] = jnp.broadcast_to(1.0 / counts, count_out.shape)
    base_out[...] = (
        jnp.dot(live_member, frames[...], preferred_element_type=jnp.float32) / counts
    )


def attend_kernel(span_len, right_len, head_size, scalars, other_length, *refs):
    sources, pieces = refs[:6], refs[6:14]
    outs, projection = refs[14:16], refs[16]
    rows_in, weight, query, key, value, bias, scores, peaks, weights, sems = refs[17:]
    first_frame, core, y_half = scalars[0], scalars[2], scalars[3]
    frame_count, model_width = sources[0].shape
    half = model_width // 2
    width = outs[0].shape[1]
    heads = width // head_size
    block = 2 * span_len
    blocks = frame_count // block
    near = bias.shape[0]
    memory_at = frame_count + near - block
    row_count = rows_in.shape[0] // 2
    memory_count = row_count - memory_at
    lanes = heads * block

    def piece_copies(of_core, projected):
        places = (y_half * half, (1 - y_half) * half)
        copies = []
        for side in range(2):
            place = pl.ds(pl.multiple_of(places[side], half), half)
            for shard in range(2):
                piece = pieces[4 * shard + 2 * side + of_core]
                index = 2 * side + shard
                for part in (3,) if projected else (0, 1, 2):
                    target = projection if projected else weight
                    start = shard * piece.shape[2] + (0 if projected else part * width)
                    copies.append(
                        pltpu.make_async_copy(
                            piece.at[part],
                            target.at[place, pl.ds(start, piece.shape[2])],
                            sems.at[4 * part + index],
                        )
                    )
        return copies

    row_copies = []
    for rec in range(2):
        at = rec * row_count
        for i, (start, size) in enumerate(
            ((0, frame_count), (frame_count, near - block), (memory_at, memory_count))
        ):
            row_copies.append(
                pltpu.make_async_copy(
                    sources[3 * rec + i], rows_in.at[pl.ds(at + start, size)], sems.at[16 + 3 * rec + i]
                )
            )

    for copy in row_copies:
        copy.start()
    for of_core in range(2):

        @pl.when(core == of_core)
        def _():
            for copy in piece_copies(of_core, False) + piece_copies(of_core, True):
                copy.start()

    rows = lax.broadcasted_iota(jnp.int32, (near, lanes), 0)
    spans = (lax.broadcasted_iota(jnp.int32, (near, lanes), 1) % block) // span_len
    same = (rows >= spans * span_len) & (rows < (spans + 1) * span_len + right_len)
    bias[...] = jnp.where(same, jnp.float32(0.0), jnp.float32(NEG_BIG))
    lane_spans = (lax.broadcasted_iota(jnp.int32, (1, lanes), 1) % block) // span_len
    memory_rows = lax.broadcasted_iota(jnp.int32, (memory_count, lanes), 0)
    feature_head = lax.broadcasted_iota(jnp.int32, (1, width), 1) // head_size
    head_masks = [(feature_head == h).astype(jnp.bfloat16) for h in range(heads)]
    scale = head_size ** (-0.5) * LOG2_E

    for copy in row_copies + piece_copies(0, False):
        copy.wait()
    mixed = jnp.dot(rows_in[...], weight[...], preferred_element_type=jnp.float32)
    query[...] = (mixed[:, :width] * scale).astype(jnp.bfloat16)
    key[...] = mixed[:, width : 2 * width].astype(jnp.bfloat16)
    value[...] = mixed[:, 2 * width :].astype(jnp.bfloat16)

    def score_block(i):
        rec, b = divmod(i, blocks)
        at, start = rec * row_count, b * block
        length = scalars[1] if rec == 0 else other_length[0]
        q_now = query[at + start : at + start + block]
        stacked = jnp.concatenate([q_now * m for m in head_masks], axis=0)
        keys = jnp.concatenate(
            [key[at + start : at + start + near], key[at + memory_at : at + row_count]], axis=0
        )
        raw = lax.dot_general(
            keys, stacked, (((1,), (1,)), ((), ())), preferred_element_type=jnp.float32
        )
        limit = length - first_frame - start
        local = jnp.where(rows < limit, raw[:near] + bias[...], NEG_BIG)
        live_spans = (length + span_len - 1) // span_len
        span_limit = jnp.minimum(first_frame // span_len + 2 * b + lane_spans, live_spans)
        memory = jnp.where(memory_rows < span_limit, raw[near:], NEG_BIG)
        scores[i, 0:near, :] = local
        scores[i, near:, :] = memory
        peaks[i] = jnp.maximum(
            jnp.max(local, axis=0, keepdims=True), jnp.max(memory, axis=0, keepdims=True)
        )

    def weigh_block(i):
        weights[i] = jnp.exp2(scores[i] - peaks[i]).astype(jnp.bfloat16)

    ones = jnp.ones((near + memory_count, LANES), jnp.bfloat16)
    first_of_pair = lax.broadcasted_iota(jnp.int32, (1, 2 * LANES), 1) % LANES < head_size

    def mix_block(i):
        rec, b = divmod(i, blocks)
        at, start = rec * row_count, b * block
        values = jnp.concatenate(
            [value[at + start : at + start + near], value[at + memory_at : at + row_count]], axis=0
        )
        for pair in range(width // LANES):
            columns = slice(pair * LANES, (pair + 1) * LANES)
            pair_rows = slice(pair * 2 * block, (pair + 1) * 2 * block)
            sums = lax.dot_general(
                weights[i, :, pair_rows],
                jnp.concatenate([values[:, columns], ones], axis=1),
                (((0,), (0,)), ((), ())),
                preferred_element_type=jnp.float32,
            )
            picked = jnp.where(first_of_pair, sums[:block], sums[block:])
            outs[rec][start : start + block, columns] = (
                picked[:, :LANES] / picked[:, LANES:]
            ).astype(jnp.bfloat16)

    count = 2 * blocks
    for step in range(count + 2):
        if step >= 2:
            mix_block(step - 2)
        if 1 <= step <= count:
            weigh_block(step - 1)
        if step < count:
            score_block(step)
    for copy in piece_copies(0, True):
        copy.wait()


def assemble(scalars, offsets_at, attended, gathered):
    shard = attended[0].shape[1] // 2
    offsets = [
        [pl.multiple_of(scalars[offsets_at + 2 * i + s], LANES) for s in range(2)]
        for i in range(4)
    ]
    for i in range(4):
        for s in range(2):
            gathered[:, pl.ds(offsets[i][s], shard)] = attended[i][:, s * shard : (s + 1) * shard]
    return offsets, shard


def pool_kernel(offsets_at, scalars, base, member, inverse, route, *refs):
    attended, projections = refs[:4], refs[4:8]
    sent_out, gathered, weight, pooled, sems = refs[8:]
    shard = attended[0].shape[1] // 2
    offsets = [
        [pl.multiple_of(scalars[offsets_at + 2 * i + s], LANES) for s in range(2)]
        for i in range(4)
    ]
    row_copies, weight_copies = [], []
    for i in range(4):
        for s in range(2):
            row_copies.append(
                pltpu.make_async_copy(
                    attended[i].at[:, pl.ds(s * shard, shard)],
                    gathered.at[:, pl.ds(offsets[i][s], shard)],
                    sems.at[2 * i + s],
                )
            )
        weight_copies.append(
            pltpu.make_async_copy(projections[i], weight.at[i], sems.at[8 + i])
        )
    for copy in row_copies + weight_copies:
        copy.start()
    for copy in row_copies:
        copy.wait()
    means = jnp.dot(member[...], gathered[...], preferred_element_type=jnp.float32)
    model_width = means.shape[1]
    means = (means * jnp.concatenate([inverse[...]] * (model_width // LANES), axis=1)).astype(
        jnp.bfloat16
    )
    for i in range(4):
        weight_copies[i].wait()
        mixed = jnp.dot(means, weight[i], preferred_element_type=jnp.float32)
        for s in range(2):
            columns = pl.ds(offsets[i][s], shard)
            pooled[:, columns] = (
                base[:, columns] + mixed[:, s * shard : (s + 1) * shard]
            ).astype(jnp.bfloat16)
    sent_out[...] = jnp.dot(
        route[...], pooled[...], preferred_element_type=jnp.float32
    ).astype(jnp.bfloat16)


def encode_kernel(offsets_at, scalars, *refs):
    attended, projections, frames = refs[:4], refs[4:8], refs[8]
    encoded_out, gathered = refs[9:]
    first_frame, length = scalars[0], scalars[1]
    frame_count, _ = frames.shape
    offsets, shard = assemble(scalars, offsets_at, attended, gathered)
    live = (
        first_frame + lax.broadcasted_iota(jnp.int32, (frame_count, 1), 0) < length
    ).astype(jnp.float32)
    for i in range(4):
        mixed = jnp.dot(
            gathered[...], projections[i][...], preferred_element_type=jnp.float32
        )
        for s in range(2):
            columns = pl.ds(offsets[i][s], shard)
            base = frames[:, columns].astype(jnp.float32)
            encoded_out[:, columns] = (
                (base + mixed[:, s * shard : (s + 1) * shard]) * live
            ).astype(jnp.bfloat16)


def language_kernel(places_at, scalars, *refs):
    received, pieces, out = refs[0], refs[1:-6], refs[-6]
    rows, weights, product, sems, out_sems = refs[-5:]
    count, width = len(pieces), pieces[0].shape[1]
    row_copy = pltpu.make_async_copy(received, rows, sems.at[count])
    row_copy.start()
    copies = [
        pltpu.make_async_copy(piece, weights.at[i], sems.at[i]) for i, piece in enumerate(pieces)
    ]
    for copy in copies:
        copy.start()
    row_copy.wait()
    out_copies = []
    for i in range(count):
        copies[i].wait()
        product[i] = jnp.dot(
            rows[...], weights[i], preferred_element_type=jnp.float32
        ).astype(jnp.bfloat16)
        place = pl.multiple_of(scalars[places_at + i], LANES)
        out_copies.append(
            pltpu.make_async_copy(product.at[i], out.at[:, pl.ds(place, width)], out_sems.at[i])
        )
        out_copies[-1].start()
    for copy in out_copies:
        copy.wait()


def along_x(r, j, _):
    return r, j ^ 1


def along_y(r, j, _):
    return r ^ 2, j


def other_core(r, j, _):
    return r ^ 1, j


def z_up(r, j, count):
    return r, (j + 2) % count


def z_down(r, j, count):
    return r, (j - 2) % count


def relocate(value, core_0, core_1):
    rec_count, time_count = lax.axis_size("rec"), lax.axis_size("tm")
    pairs = []
    for r in range(rec_count):
        for j in range(time_count):
            route = (core_0, core_1)[r % 2]
            if route is not None:
                to_r, to_j = route(r, j, time_count)
                pairs.append((r * time_count + j, to_r * time_count + to_j))
    return lax.ppermute(value, ("rec", "tm"), pairs)


def swap_cores(value):
    return relocate(value, other_core, other_core)


def exchange_blocks(blocks):
    return lax.all_to_all(blocks, "tm", split_axis=0, concat_axis=0, tiled=True)


def per_device(
    frames,
    lengths,
    norm_gain,
    memory_gain,
    qkv_weight,
    out_weight,
    segment_ids,
    owners,
    language_weight,
):
    local_frames = frames[0]
    frame_count, model_width = local_frames.shape
    shard = out_weight.shape[1]
    half = model_width // 2
    time_count = lax.axis_size("tm")
    rec_count = lax.axis_size("rec")
    rec, time = lax.axis_index("rec"), lax.axis_index("tm")
    core, y_half = rec % 2, (rec // 2) % 2
    x, z = time % 2, time // 2
    z_count = time_count // 2
    first_frame = time * frame_count
    length = lengths[0]
    head_size = model_width // H
    bf16 = jnp.bfloat16

    own = jnp.concatenate([qkv_weight, out_weight[None]], axis=0)
    own_a = lax.dynamic_slice_in_dim(own, y_half * half, half, 1)
    own_b = lax.dynamic_slice_in_dim(own, (1 - y_half) * half, half, 1)

    def pick(for_core_0, for_core_1):
        return jnp.where(core == 0, for_core_0, for_core_1)

    token_count = owners.shape[2]
    slot_count = 2 * token_count
    capacity = slot_count // time_count
    language_shard = language_weight.shape[1]

    def group_of(of_core, slot):
        return jnp.where(of_core == 0, z + slot, z - slot - 1) % z_count

    numbers = [first_frame, length, core, y_half, capacity]
    offsets_at = len(numbers)
    for of_core in (core, 1 - core):
        for slot in range(2):
            group = group_of(of_core, slot)
            numbers += [(2 * group + x) * shard, (2 * group + 1 - x) * shard]
    places_at = len(numbers)
    numbers += [(rec ^ i) * language_shard for i in range(rec_count)]
    scalars = jnp.stack(numbers).astype(jnp.int32)

    m1 = relocate(own_a, along_x, z_up)
    m2 = relocate(pick(own_a, own_b), z_down, z_up)
    l1 = relocate(language_weight, along_y, along_y)

    pad = 2 * RC
    normed, start_rows, memory = local_call(
        functools.partial(normalise_kernel, C),
        (
            shape_of(frame_count, model_width),
            shape_of(pad, model_width),
            shape_of(time_count, frame_count // C, model_width),
        ),
        (scalars,),
        (local_frames, norm_gain[None], memory_gain[None]),
        flops=10 * frame_count * model_width,
        moved=4 * frame_count * model_width,
    )
    other_length = swap_cores(lengths)
    other_normed = swap_cores(normed)
    ahead = shifted(start_rows, "tm", -1)
    memories = exchange_blocks(memory).reshape(-1, model_width)
    owners_col = owners[0, 0]
    prepared = local_call(
        prepare_kernel,
        (
            shape_of(token_count, model_width, dtype=jnp.float32),
            shape_of(token_count, frame_count),
            shape_of(token_count, LANES, dtype=jnp.float32),
            shape_of(slot_count, token_count),
        ),
        (scalars,),
        (local_frames, segment_ids[0], owners_col.reshape(1, token_count), owners_col),
        flops=2 * token_count * frame_count * model_width,
        moved=2 * frame_count * model_width,
    )
    other_ahead = swap_cores(ahead)
    other_memories = swap_cores(memories)

    m3 = relocate(m1, along_y, along_x)
    m4 = relocate(m1, None, z_up)
    m5 = relocate(m2, along_x, z_up)
    m6 = relocate(pick(m2, m3), along_y, along_y)
    m7 = relocate(m4, None, along_x)
    m8 = relocate(m5, along_y, along_x)

    slot_pieces = (
        ((own_a, m1), (own_b, m2), (m1, m3), (m3, m6)),
        ((m2, m4), (m6, m5), (m5, m7), (m8, m8)),
    )
    block = 2 * C
    width = 2 * shard
    row_count = frame_count + pad + memories.shape[0]
    keys_seen = block + pad + memories.shape[0]
    lanes = width // head_size * block
    block_count = 2 * (frame_count // block)
    attended, outs = [], []
    for pieces in slot_pieces:
        flat = [p for pair in pieces for p in pair]
        *pair, out_piece = local_call(
            functools.partial(attend_kernel, C, RC, head_size),
            (
                shape_of(frame_count, width),
                shape_of(frame_count, width),
                shape_of(model_width, width),
            ),
            (scalars, other_length),
            (normed, ahead, memories, other_normed, other_ahead, other_memories, *flat),
            in_place=6 + len(flat),
            scratch=(
                pltpu.VMEM((2 * row_count, model_width), bf16),
                pltpu.VMEM((model_width, 3 * width), bf16),
                pltpu.VMEM((2 * row_count, width), bf16),
                pltpu.VMEM((2 * row_count, width), bf16),
                pltpu.VMEM((2 * row_count, width), bf16),
                pltpu.VMEM((block + pad, lanes), jnp.float32),
                pltpu.VMEM((block_count, keys_seen, lanes), jnp.float32),
                pltpu.VMEM((block_count, 1, lanes), jnp.float32),
                pltpu.VMEM((block_count, keys_seen, lanes), bf16),
                pltpu.SemaphoreType.DMA((22,)),
            ),
            vmem_mib=32,
            flops=12 * frame_count * model_width * width,
            moved=8 * frame_count * model_width,
        )
        attended.append(pair)
        outs.append(out_piece)
    other_outs = [swap_cores(w) for w in outs]
    other_attended = [swap_cores(for_other) for _, for_other in attended]

    features = (attended[0][0], attended[1][0], *other_attended, *outs, *other_outs)
    sent_rows = local_call(
        functools.partial(pool_kernel, offsets_at),
        shape_of(slot_count, model_width),
        (scalars,),
        (*prepared, *features),
        in_place=len(features),
        scratch=(
            pltpu.VMEM((frame_count, model_width), bf16),
            pltpu.VMEM((4, model_width, width), bf16),
            pltpu.VMEM((token_count, model_width), bf16),
            pltpu.SemaphoreType.DMA((12,)),
        ),
        flops=4 * token_count * model_width * model_width,
        moved=6 * frame_count * model_width,
    )
    received = exchange_blocks(
        sent_rows.reshape(time_count, capacity, model_width)
    ).reshape(slot_count, model_width)
    encoded = local_call(
        functools.partial(encode_kernel, offsets_at),
        shape_of(frame_count, model_width),
        (scalars,),
        (*features, local_frames),
        scratch=(pltpu.VMEM((frame_count, model_width), bf16),),
        flops=2 * frame_count * model_width * model_width,
        moved=6 * frame_count * model_width,
    )
    language_pieces = (language_weight, swap_cores(language_weight), l1, swap_cores(l1))
    lm_out = local_call(
        functools.partial(language_kernel, places_at),
        shape_of(slot_count, rec_count * language_shard),
        (scalars,),
        (received, *language_pieces),
        in_place=1 + rec_count,
        out_in_place=True,
        scratch=(
            pltpu.VMEM((slot_count, model_width), bf16),
            pltpu.VMEM((rec_count, model_width, language_shard), bf16),
            pltpu.VMEM((rec_count, slot_count, language_shard), bf16),
            pltpu.SemaphoreType.DMA((rec_count + 1,)),
            pltpu.SemaphoreType.DMA((rec_count,)),
        ),
        flops=2 * slot_count * model_width * rec_count * language_shard,
        moved=2 * model_width * rec_count * language_shard,
    )
    return (encoded[None], lm_out[None, None])


def solution(mesh):
    in_specs = (
        P("rec", "tm", None),
        P("rec"),
        P(),
        P(),
        P(None, None, "tm"),
        P(None, "tm"),
        P("rec", "tm", None),
        P("rec", "tm", None, None),
        P(None, "rec"),
    )
    out_specs = (P("rec", "tm", None), P("rec", "tm", None, None))
    rec_count, time_count = mesh.shape["rec"], mesh.shape["tm"]
    paired = shard_map_of(mesh, in_specs, out_specs, per_device)
    plain = shard_map_of(mesh, in_specs, out_specs, plain_device)

    def run(*arrays):
        shard = arrays[5].shape[1] // time_count
        fits = rec_count == 4 and time_count == 8 and shard % LANES == 0
        return (paired if fits else plain)(*arrays)

    return run


def shard_map_of(mesh, in_specs, out_specs, body):
    return jax.shard_map(
        body, mesh=mesh, in_specs=in_specs, out_specs=out_specs, check_vma=False
    )
```

```python
import functools

import jax
import jax.numpy as jnp
from jax import lax
from jax.experimental import pallas as pl
from jax.experimental.pallas import tpu as pltpu
from jax.sharding import PartitionSpec as P


H = 16
C = 32
RC = 8


EPS_NORM = 1e-05
EPS_MEMORY = 1e-06
NEG_BIG = -1e30
LANES = 128
LOG2_E = 1.4426950408889634


def shifted(block, axis, distance):
    devices = range(lax.axis_size(axis))
    route = [(i - distance, i) for i in devices if i - distance in devices]
    return lax.ppermute(block, axis, route)


def layer_norm(values_in, gain):
    values_in = values_in.astype(jnp.float32)
    centre = jnp.mean(values_in, axis=-1, keepdims=True)
    centred = values_in - centre
    spread = jnp.mean(centred * centred, axis=-1, keepdims=True)
    return centred * lax.rsqrt(spread + EPS_NORM) * gain


def span_memory(normed, live_mask, gain, span_len):
    model_width = normed.shape[1]
    masked = jnp.where(live_mask[:, None], normed.astype(jnp.float32), jnp.float32(0.0))
    owner_sums = masked.reshape(-1, span_len, model_width).sum(axis=1)
    counts = live_mask.reshape(-1, span_len).astype(jnp.float32).sum(axis=1)
    means = owner_sums / jnp.maximum(counts, 1.0)[:, None]
    power = jnp.mean(means * means, axis=-1, keepdims=True)
    return (means * lax.rsqrt(power + EPS_MEMORY) * gain).astype(jnp.bfloat16)


def block_size():
    return 256


def local_part(query, keys, values, first_frame, length, head_count, span_len, right_len):
    frame_count, model_width = query.shape
    head_size = model_width // head_count
    group_rows = 4 * span_len
    group_count = frame_count // group_rows
    block_rows = block_size()
    query_blocks = query.reshape(group_count, group_rows, head_count, head_size)
    key_blocks = keys[:frame_count].reshape(group_count, group_rows, head_count, head_size)
    value_blocks = values[:frame_count].reshape(group_count, group_rows, head_count, head_size)
    key_tail = keys[frame_count:].reshape(1, right_len, head_count, head_size)
    value_tail = values[frame_count:].reshape(1, right_len, head_count, head_size)
    key_all = jnp.concatenate(
        [key_blocks, jnp.concatenate([key_blocks[1:, :right_len], key_tail], axis=0)], axis=1
    )
    value_all = jnp.concatenate(
        [value_blocks, jnp.concatenate([value_blocks[1:, :right_len], value_tail], axis=0)], axis=1
    )
    start_offsets = jnp.arange(group_count, dtype=jnp.int32)[:, None] * group_rows
    query_pos = first_frame + start_offsets + jnp.arange(group_rows, dtype=jnp.int32)[None, :]
    key_pos = first_frame + jnp.concatenate(
        [
            start_offsets + jnp.arange(group_rows, dtype=jnp.int32)[None, :],
            start_offsets + group_rows + jnp.arange(right_len, dtype=jnp.int32)[None, :],
        ],
        axis=1,
    )
    query_span = query_pos // span_len
    span_end = (query_span + 1) * span_len
    same = (key_pos // span_len)[:, None, :] == query_span[:, :, None]
    ahead = (key_pos[:, None, :] >= span_end[:, :, None]) & (
        key_pos[:, None, :] < span_end[:, :, None] + right_len
    )
    allowed = (same | ahead) & (key_pos < length)[:, None, :]
    scores = jnp.einsum(
        "gqhd,gkhd->ghqk", query_blocks, key_all, preferred_element_type=jnp.float32
    ) * head_size ** (-0.5)
    scores = jnp.where(allowed[:, None], scores, NEG_BIG)
    row_peak = jnp.max(scores, axis=-1)
    weights = jnp.where(allowed[:, None], jnp.exp(scores - row_peak[..., None]), jnp.float32(0.0))
    row_total = jnp.sum(weights, axis=-1)
    accum = jnp.einsum(
        "ghqk,gkhd->ghqd",
        weights.astype(jnp.bfloat16),
        value_all,
        preferred_element_type=jnp.float32,
    )
    block_count = frame_count // block_rows
    row_peak = (
        row_peak.transpose(1, 0, 2).reshape(head_count, block_count, block_rows).transpose(1, 0, 2)
    )
    row_total = (
        row_total.transpose(1, 0, 2).reshape(head_count, block_count, block_rows).transpose(1, 0, 2)
    )
    accum = (
        accum.transpose(1, 0, 2, 3)
        .reshape(head_count, block_count, block_rows, head_size)
        .transpose(1, 0, 2, 3)
    )
    return (row_peak, row_total, accum)


def memory_update(
    carry, memory_keys, memory_values, query, first_frame, length, head_count, span_len
):
    row_peak, row_total, accum = carry
    block_count, _, block_rows = row_peak.shape
    row_count, model_width = memory_keys.shape
    head_size = model_width // head_count
    mem_keys = memory_keys.reshape(row_count, head_count, head_size)
    mem_values = memory_values.reshape(row_count, head_count, head_size)
    mem_index = jnp.arange(row_count, dtype=jnp.int32)
    mem_live = mem_index * span_len < length
    query_blocks = query.reshape(block_count, block_rows, head_count, head_size)
    positions = first_frame + jnp.arange(block_count * block_rows, dtype=jnp.int32).reshape(
        block_count, block_rows
    )

    def one_block(packed):
        query_now, pos_now, peak_now, total_now, accum_now = packed
        scores = jnp.einsum(
            "qhd,khd->hqk", query_now, mem_keys, preferred_element_type=jnp.float32
        ) * head_size ** (-0.5)
        allowed = (mem_index[None, :] < (pos_now // span_len)[:, None]) & mem_live[None, :]
        scores = jnp.where(allowed[None], scores, NEG_BIG)
        new_peak = jnp.maximum(peak_now, jnp.max(scores, axis=-1))
        weights = jnp.where(allowed[None], jnp.exp(scores - new_peak[..., None]), jnp.float32(0.0))
        factor = jnp.exp(peak_now - new_peak)
        total_next = total_now * factor + jnp.sum(weights, axis=-1)
        accum_next = accum_now * factor[..., None] + jnp.einsum(
            "hqk,khd->hqd",
            weights.astype(jnp.bfloat16),
            mem_values,
            preferred_element_type=jnp.float32,
        )
        return (new_peak, total_next, accum_next)

    return lax.map(one_block, (query_blocks, positions, row_peak, row_total, accum))


def finish(carry, frame_count, model_width):
    _, row_total, accum = carry
    result = accum / row_total[..., None]
    return result.transpose(0, 2, 1, 3).reshape(frame_count, model_width).astype(jnp.bfloat16)


def dispatch_matrix(owner_ids, owner_count, capacity):
    choose = (owner_ids[:, None] == jnp.arange(owner_count, dtype=jnp.int32)[None, :]).astype(
        jnp.int32
    )
    before = jnp.cumsum(choose, axis=0) - choose
    slot_index = jnp.sum(before * choose, axis=1)
    target = owner_ids * capacity + slot_index
    slot_rows = jnp.arange(owner_count * capacity, dtype=jnp.int32)
    return (slot_rows[:, None] == target[None, :]).astype(jnp.bfloat16)


def plain_device(
    frames,
    lengths,
    norm_gain,
    memory_gain,
    qkv_weight,
    out_weight,
    segment_ids,
    owners,
    language_weight,
):
    local_frames = frames[0]
    frame_count, model_width = local_frames.shape
    head_count = H
    time_count = lax.axis_size("tm")
    first_frame = lax.axis_index("tm") * frame_count
    length = lengths[0]
    live_mask = first_frame + jnp.arange(frame_count, dtype=jnp.int32) < length
    right_frames = shifted(local_frames[:RC], "tm", -1)
    normed = layer_norm(local_frames, norm_gain).astype(jnp.bfloat16)
    normed_right = layer_norm(right_frames, norm_gain).astype(jnp.bfloat16)
    memory = span_memory(normed, live_mask, memory_gain, C)
    stacked_rows = jnp.concatenate([normed, normed_right, memory], axis=0)
    projected = jnp.einsum(
        "fd,kdw->kfw",
        stacked_rows,
        lax.all_gather(qkv_weight, "tm", axis=2, tiled=True),
        preferred_element_type=jnp.float32,
    ).astype(jnp.bfloat16)
    split_at = frame_count + RC
    query = projected[0, :frame_count]
    keys = projected[1, :split_at]
    values = projected[2, :split_at]
    memory_keys = projected[1, split_at:]
    memory_values = projected[2, split_at:]
    carry = local_part(query, keys, values, first_frame, length, head_count, C, RC)
    carry = memory_update(
        carry,
        lax.all_gather(memory_keys, "tm", axis=0, tiled=True),
        lax.all_gather(memory_values, "tm", axis=0, tiled=True),
        query,
        first_frame,
        length,
        head_count,
        C,
    )
    attended = finish(carry, frame_count, model_width)
    output_proj = jnp.dot(
        attended,
        lax.all_gather(out_weight, "tm", axis=1, tiled=True),
        preferred_element_type=jnp.float32,
    )
    encoded = jnp.where(
        live_mask[:, None], local_frames.astype(jnp.float32) + output_proj, jnp.float32(0.0)
    ).astype(jnp.bfloat16)
    token_count = owners.shape[2]
    segments = segment_ids[0, 0]
    owner_indicator = (
        segments[None, :] == jnp.arange(token_count, dtype=jnp.int32)[:, None]
    ).astype(jnp.bfloat16)
    owner_sums = jnp.dot(owner_indicator, encoded, preferred_element_type=jnp.float32)
    counts = jnp.sum(owner_indicator.astype(jnp.float32), axis=1)
    pooled_rows = (owner_sums / counts[:, None]).astype(jnp.bfloat16)
    slot_count = 2 * token_count
    capacity = slot_count // time_count
    route_matrix = dispatch_matrix(owners[0, 0, :, 0], time_count, capacity)
    sent_rows = jnp.dot(route_matrix, pooled_rows, preferred_element_type=jnp.float32).astype(
        jnp.bfloat16
    )
    received = lax.all_to_all(
        sent_rows.reshape(time_count, capacity, model_width),
        "tm",
        split_axis=0,
        concat_axis=0,
        tiled=True,
    )
    received = received.reshape(slot_count, model_width)
    lm_out = jnp.dot(
        received,
        lax.all_gather(language_weight, "rec", axis=1, tiled=True),
        preferred_element_type=jnp.float32,
    ).astype(jnp.bfloat16)
    return (encoded[None], lm_out[None, None])


def vmem_spec():
    return pl.BlockSpec(memory_space=pltpu.VMEM)


def smem_spec():
    return pl.BlockSpec(memory_space=pltpu.SMEM)


def local_call(kernel, out_shapes, scalars, operands, scratch=(), in_place=0, out_in_place=False, vmem_mib=16, flops=0, moved=0):
    whole = len(operands) - in_place
    return pl.pallas_call(
        kernel,
        out_shape=out_shapes,
        in_specs=[smem_spec()] * len(scalars)
        + [vmem_spec()] * whole
        + [pl.BlockSpec(memory_space=pl.ANY)] * in_place,
        out_specs=jax.tree.map(
            lambda _: pl.BlockSpec(memory_space=pl.ANY) if out_in_place else vmem_spec(), out_shapes
        ),
        compiler_params=pltpu.CompilerParams(vmem_limit_bytes=vmem_mib << 20),
        scratch_shapes=list(scratch),
        cost_estimate=pl.CostEstimate(flops=flops, bytes_accessed=moved, transcendentals=0),
    )(*scalars, *operands)


def shape_of(*dims, dtype=jnp.bfloat16):
    return jax.ShapeDtypeStruct(dims, dtype)


def normalise_kernel(
    span_len, scalars, frames, gain, memory_gain, normed_out, ahead_out, memory_out
):
    first_frame, length = scalars[0], scalars[1]
    frame_count, _ = frames.shape
    span_count = frame_count // span_len
    values = frames[...].astype(jnp.float32)
    centre = jnp.mean(values, axis=-1, keepdims=True)
    centred = values - centre
    spread = jnp.mean(centred * centred, axis=-1, keepdims=True)
    normed = (centred * lax.rsqrt(spread + EPS_NORM) * gain[...]).astype(jnp.bfloat16)
    normed_out[...] = normed
    ahead_out[...] = normed[: ahead_out.shape[0]]
    spans = lax.broadcasted_iota(jnp.int32, (span_count, frame_count), 0)
    places = lax.broadcasted_iota(jnp.int32, (span_count, frame_count), 1)
    member = (places >= spans * span_len) & (places < (spans + 1) * span_len)
    member = member & (places < length - first_frame)
    sums = jnp.dot(
        member.astype(jnp.bfloat16), normed, preferred_element_type=jnp.float32
    )
    counts = jnp.sum(member.astype(jnp.float32), axis=-1, keepdims=True)
    means = sums / jnp.maximum(counts, 1.0)
    power = jnp.mean(means * means, axis=-1, keepdims=True)
    memory = (means * lax.rsqrt(power + EPS_MEMORY) * memory_gain[...]).astype(jnp.bfloat16)
    for copy in range(memory_out.shape[0]):
        memory_out[copy] = memory


def prepare_kernel(scalars, frames, segments, owners_row, owners_col, base_out, member_out, count_out, route_out):
    first_frame, length, capacity = scalars[0], scalars[1], scalars[4]
    token_count, frame_count = member_out.shape
    tokens = lax.broadcasted_iota(jnp.int32, (token_count, frame_count), 0)
    places = first_frame + lax.broadcasted_iota(jnp.int32, (token_count, frame_count), 1)
    member = (segments[...] == tokens).astype(jnp.float32)
    counts = jnp.sum(member, axis=1, keepdims=True)
    live_member = jnp.where(places < length, member, 0.0).astype(jnp.bfloat16)
    earlier = lax.broadcasted_iota(jnp.int32, (token_count, token_count), 0)
    later = lax.broadcasted_iota(jnp.int32, (token_count, token_count), 1)
    clash = (owners_col[...] == owners_row[...]) & (earlier < later)
    slot = jnp.sum(clash.astype(jnp.int32), axis=0, keepdims=True)
    target = owners_row[...] * capacity + slot
    slots = lax.broadcasted_iota(jnp.int32, route_out.shape, 0)
    route_out[...] = (slots == target).astype(jnp.bfloat16)
    member_out[...] = live_member
    count_out[...] = jnp.broadcast_to(1.0 / counts, count_out.shape)
    base_out[...] = (
        jnp.dot(live_member, frames[...], preferred_element_type=jnp.float32) / counts
    )


def attend_kernel(span_len, right_len, head_size, scalars, other_length, *refs):
    members, sources, pieces = refs[:2], refs[2:8], refs[8:16]
    outs, sums_out, projection = refs[16:18], refs[18:20], refs[20]
    rows_in, weight, query, key, value, bias, scores, peaks, weights, sems = refs[21:]
    first_frame, core, y_half = scalars[0], scalars[2], scalars[3]
    frame_count, model_width = sources[0].shape
    half = model_width // 2
    width = outs[0].shape[1]
    heads = width // head_size
    block = 2 * span_len
    blocks = frame_count // block
    near = bias.shape[0]
    memory_at = frame_count + near - block
    row_count = rows_in.shape[0] // 2
    memory_count = row_count - memory_at
    lanes = heads * block

    def piece_copies(of_core, projected):
        places = (y_half * half, (1 - y_half) * half)
        copies = []
        for side in range(2):
            place = pl.ds(pl.multiple_of(places[side], half), half)
            for shard in range(2):
                piece = pieces[4 * shard + 2 * side + of_core]
                index = 2 * side + shard
                for part in (3,) if projected else (0, 1, 2):
                    target = projection if projected else weight
                    start = shard * piece.shape[2] + (0 if projected else part * width)
                    copies.append(
                        pltpu.make_async_copy(
                            piece.at[part],
                            target.at[place, pl.ds(start, piece.shape[2])],
                            sems.at[4 * part + index],
                        )
                    )
        return copies

    row_copies = []
    for rec in range(2):
        at = rec * row_count
        for i, (start, size) in enumerate(
            ((0, frame_count), (frame_count, near - block), (memory_at, memory_count))
        ):
            row_copies.append(
                pltpu.make_async_copy(
                    sources[3 * rec + i], rows_in.at[pl.ds(at + start, size)], sems.at[16 + 3 * rec + i]
                )
            )

    for copy in row_copies:
        copy.start()
    for of_core in range(2):

        @pl.when(core == of_core)
        def _():
            for copy in piece_copies(of_core, False) + piece_copies(of_core, True):
                copy.start()

    rows = lax.broadcasted_iota(jnp.int32, (near, lanes), 0)
    spans = (lax.broadcasted_iota(jnp.int32, (near, lanes), 1) % block) // span_len
    same = (rows >= spans * span_len) & (rows < (spans + 1) * span_len + right_len)
    bias[...] = jnp.where(same, jnp.float32(0.0), jnp.float32(NEG_BIG))
    lane_spans = (lax.broadcasted_iota(jnp.int32, (1, lanes), 1) % block) // span_len
    memory_rows = lax.broadcasted_iota(jnp.int32, (memory_count, lanes), 0)
    feature_head = lax.broadcasted_iota(jnp.int32, (1, width), 1) // head_size
    head_masks = [(feature_head == h).astype(jnp.bfloat16) for h in range(heads)]
    scale = head_size ** (-0.5) * LOG2_E

    for copy in row_copies + piece_copies(0, False):
        copy.wait()
    mixed = jnp.dot(rows_in[...], weight[...], preferred_element_type=jnp.float32)
    query[...] = (mixed[:, :width] * scale).astype(jnp.bfloat16)
    key[...] = mixed[:, width : 2 * width].astype(jnp.bfloat16)
    value[...] = mixed[:, 2 * width :].astype(jnp.bfloat16)

    def score_block(i):
        rec, b = divmod(i, blocks)
        at, start = rec * row_count, b * block
        length = scalars[1] if rec == 0 else other_length[0]
        q_now = query[at + start : at + start + block]
        stacked = jnp.concatenate([q_now * m for m in head_masks], axis=0)
        keys = jnp.concatenate(
            [key[at + start : at + start + near], key[at + memory_at : at + row_count]], axis=0
        )
        raw = lax.dot_general(
            keys, stacked, (((1,), (1,)), ((), ())), preferred_element_type=jnp.float32
        )
        limit = length - first_frame - start
        local = jnp.where(rows < limit, raw[:near] + bias[...], NEG_BIG)
        live_spans = (length + span_len - 1) // span_len
        span_limit = jnp.minimum(first_frame // span_len + 2 * b + lane_spans, live_spans)
        memory = jnp.where(memory_rows < span_limit, raw[near:], NEG_BIG)
        scores[i, 0:near, :] = local
        scores[i, near:, :] = memory
        peaks[i] = jnp.maximum(
            jnp.max(local, axis=0, keepdims=True), jnp.max(memory, axis=0, keepdims=True)
        )

    def weigh_block(i):
        weights[i] = jnp.exp2(scores[i] - peaks[i]).astype(jnp.bfloat16)

    ones = jnp.ones((near + memory_count, LANES), jnp.bfloat16)
    first_of_pair = lax.broadcasted_iota(jnp.int32, (1, 2 * LANES), 1) % LANES < head_size

    def mix_block(i):
        rec, b = divmod(i, blocks)
        at, start = rec * row_count, b * block
        values = jnp.concatenate(
            [value[at + start : at + start + near], value[at + memory_at : at + row_count]], axis=0
        )
        for pair in range(width // LANES):
            columns = slice(pair * LANES, (pair + 1) * LANES)
            pair_rows = slice(pair * 2 * block, (pair + 1) * 2 * block)
            sums = lax.dot_general(
                weights[i, :, pair_rows],
                jnp.concatenate([values[:, columns], ones], axis=1),
                (((0,), (0,)), ((), ())),
                preferred_element_type=jnp.float32,
            )
            picked = jnp.where(first_of_pair, sums[:block], sums[block:])
            outs[rec][start : start + block, columns] = (
                picked[:, :LANES] / picked[:, LANES:]
            ).astype(jnp.bfloat16)

    count = 2 * blocks
    for step in range(count + 2):
        if step >= 2:
            mix_block(step - 2)
        if 1 <= step <= count:
            weigh_block(step - 1)
        if step < count:
            score_block(step)
    for rec in range(2):
        sums_out[rec][...] = jnp.dot(
            members[rec][...], outs[rec][...], preferred_element_type=jnp.float32
        )
    for copy in piece_copies(0, True):
        copy.wait()


def assemble(scalars, offsets_at, attended, gathered):
    shard = attended[0].shape[1] // 2
    offsets = [
        [pl.multiple_of(scalars[offsets_at + 2 * i + s], LANES) for s in range(2)]
        for i in range(4)
    ]
    for i in range(4):
        for s in range(2):
            gathered[:, pl.ds(offsets[i][s], shard)] = attended[i][:, s * shard : (s + 1) * shard]
    return offsets, shard


def pool_kernel(offsets_at, scalars, base, inverse, route, *refs):
    sums, projections = refs[:4], refs[4:8]
    sent_out, means, pooled = refs[8:]
    shard = sums[0].shape[1] // 2
    offsets = [
        [pl.multiple_of(scalars[offsets_at + 2 * i + s], LANES) for s in range(2)]
        for i in range(4)
    ]
    for i in range(4):
        for s in range(2):
            for lane in range(0, shard, LANES):
                means[:, pl.ds(offsets[i][s] + lane, LANES)] = (
                    sums[i][:, s * shard + lane : s * shard + lane + LANES] * inverse[...]
                ).astype(jnp.bfloat16)
    for i in range(4):
        mixed = jnp.dot(means[...], projections[i][...], preferred_element_type=jnp.float32)
        for s in range(2):
            columns = pl.ds(offsets[i][s], shard)
            pooled[:, columns] = (
                base[:, columns] + mixed[:, s * shard : (s + 1) * shard]
            ).astype(jnp.bfloat16)
    sent_out[...] = jnp.dot(
        route[...], pooled[...], preferred_element_type=jnp.float32
    ).astype(jnp.bfloat16)


def encode_kernel(offsets_at, scalars, *refs):
    attended, projections, frames = refs[:4], refs[4:8], refs[8]
    encoded_out, gathered = refs[9:]
    first_frame, length = scalars[0], scalars[1]
    frame_count, _ = frames.shape
    offsets, shard = assemble(scalars, offsets_at, attended, gathered)
    live = (
        first_frame + lax.broadcasted_iota(jnp.int32, (frame_count, 1), 0) < length
    ).astype(jnp.float32)
    for i in range(4):
        mixed = jnp.dot(
            gathered[...], projections[i][...], preferred_element_type=jnp.float32
        )
        for s in range(2):
            columns = pl.ds(offsets[i][s], shard)
            base = frames[:, columns].astype(jnp.float32)
            encoded_out[:, columns] = (
                (base + mixed[:, s * shard : (s + 1) * shard]) * live
            ).astype(jnp.bfloat16)


def language_kernel(places_at, scalars, received, *refs):
    pieces, out = refs[:-5], refs[-5]
    weights, product, sems, out_sems = refs[-4:]
    count, width = len(pieces), pieces[0].shape[1]
    copies = [
        pltpu.make_async_copy(piece, weights.at[i], sems.at[i]) for i, piece in enumerate(pieces)
    ]
    for copy in copies:
        copy.start()
    out_copies = []
    for i in range(count):
        copies[i].wait()
        product[i] = jnp.dot(
            received[...], weights[i], preferred_element_type=jnp.float32
        ).astype(jnp.bfloat16)
        place = pl.multiple_of(scalars[places_at + i], LANES)
        out_copies.append(
            pltpu.make_async_copy(product.at[i], out.at[:, pl.ds(place, width)], out_sems.at[i])
        )
        out_copies[-1].start()
    for copy in out_copies:
        copy.wait()


def along_x(r, j, _):
    return r, j ^ 1


def along_y(r, j, _):
    return r ^ 2, j


def other_core(r, j, _):
    return r ^ 1, j


def z_up(r, j, count):
    return r, (j + 2) % count


def z_down(r, j, count):
    return r, (j - 2) % count


def relocate(value, core_0, core_1):
    rec_count, time_count = lax.axis_size("rec"), lax.axis_size("tm")
    pairs = []
    for r in range(rec_count):
        for j in range(time_count):
            route = (core_0, core_1)[r % 2]
            if route is not None:
                to_r, to_j = route(r, j, time_count)
                pairs.append((r * time_count + j, to_r * time_count + to_j))
    return lax.ppermute(value, ("rec", "tm"), pairs)


def swap_cores(value):
    return relocate(value, other_core, other_core)


def exchange_blocks(blocks):
    return lax.all_to_all(blocks, "tm", split_axis=0, concat_axis=0, tiled=True)


def per_device(
    frames,
    lengths,
    norm_gain,
    memory_gain,
    qkv_weight,
    out_weight,
    segment_ids,
    owners,
    language_weight,
):
    local_frames = frames[0]
    frame_count, model_width = local_frames.shape
    shard = out_weight.shape[1]
    half = model_width // 2
    time_count = lax.axis_size("tm")
    rec_count = lax.axis_size("rec")
    rec, time = lax.axis_index("rec"), lax.axis_index("tm")
    core, y_half = rec % 2, (rec // 2) % 2
    x, z = time % 2, time // 2
    z_count = time_count // 2
    first_frame = time * frame_count
    length = lengths[0]
    head_size = model_width // H
    bf16 = jnp.bfloat16

    own = jnp.concatenate([qkv_weight, out_weight[None]], axis=0)
    own_a = lax.dynamic_slice_in_dim(own, y_half * half, half, 1)
    later_qkv, later_out, own_a = lax.optimization_barrier((qkv_weight, out_weight, own_a))
    later = jnp.concatenate([later_qkv, later_out[None]], axis=0)
    own_b = lax.dynamic_slice_in_dim(later, (1 - y_half) * half, half, 1)

    def pick(for_core_0, for_core_1):
        return jnp.where(core == 0, for_core_0, for_core_1)

    token_count = owners.shape[2]
    slot_count = 2 * token_count
    capacity = slot_count // time_count
    language_shard = language_weight.shape[1]

    def group_of(of_core, slot):
        return jnp.where(of_core == 0, z + slot, z - slot - 1) % z_count

    numbers = [first_frame, length, core, y_half, capacity]
    offsets_at = len(numbers)
    for of_core in (core, 1 - core):
        for slot in range(2):
            group = group_of(of_core, slot)
            numbers += [(2 * group + x) * shard, (2 * group + 1 - x) * shard]
    places_at = len(numbers)
    numbers += [(rec ^ i) * language_shard for i in range(rec_count)]
    scalars = jnp.stack(numbers).astype(jnp.int32)

    m1 = relocate(own_a, along_x, z_up)
    m2 = relocate(pick(own_a, own_b), z_down, z_up)
    l1 = relocate(language_weight, along_y, along_y)

    pad = 2 * RC
    normed, start_rows, memory = local_call(
        functools.partial(normalise_kernel, C),
        (
            shape_of(frame_count, model_width),
            shape_of(pad, model_width),
            shape_of(time_count, frame_count // C, model_width),
        ),
        (scalars,),
        (local_frames, norm_gain[None], memory_gain[None]),
        flops=10 * frame_count * model_width,
        moved=4 * frame_count * model_width,
    )
    other_length = swap_cores(lengths)
    other_normed = swap_cores(normed)
    ahead = shifted(start_rows, "tm", -1)
    memories = exchange_blocks(memory).reshape(-1, model_width)
    owners_col = owners[0, 0]
    base, member, inverse, route = local_call(
        prepare_kernel,
        (
            shape_of(token_count, model_width, dtype=jnp.float32),
            shape_of(token_count, frame_count),
            shape_of(token_count, LANES, dtype=jnp.float32),
            shape_of(slot_count, token_count),
        ),
        (scalars,),
        (local_frames, segment_ids[0], owners_col.reshape(1, token_count), owners_col),
        flops=2 * token_count * frame_count * model_width,
        moved=2 * frame_count * model_width,
    )
    other_member = swap_cores(member)
    other_ahead = swap_cores(ahead)
    other_memories = swap_cores(memories)

    m3 = relocate(m1, along_y, along_x)
    m4 = relocate(m1, None, z_up)
    m5 = relocate(m2, along_x, z_up)
    m6 = relocate(pick(m2, m3), along_y, along_y)
    m7 = relocate(m4, None, along_x)
    m8 = relocate(m5, along_y, along_x)

    slot_pieces = (
        ((own_a, m1), (own_b, m2), (m1, m3), (m3, m6)),
        ((m2, m4), (m6, m5), (m5, m7), (m8, m8)),
    )
    block = 2 * C
    width = 2 * shard
    row_count = frame_count + pad + memories.shape[0]
    keys_seen = block + pad + memories.shape[0]
    lanes = width // head_size * block
    block_count = 2 * (frame_count // block)
    attended, sums, outs = [], [], []
    for pieces in slot_pieces:
        flat = [p for pair in pieces for p in pair]
        *results, out_piece = local_call(
            functools.partial(attend_kernel, C, RC, head_size),
            (
                shape_of(frame_count, width),
                shape_of(frame_count, width),
                shape_of(token_count, width, dtype=jnp.float32),
                shape_of(token_count, width, dtype=jnp.float32),
                shape_of(model_width, width),
            ),
            (scalars, other_length),
            (member, other_member, normed, ahead, memories, other_normed, other_ahead, other_memories, *flat),
            in_place=6 + len(flat),
            scratch=(
                pltpu.VMEM((2 * row_count, model_width), bf16),
                pltpu.VMEM((model_width, 3 * width), bf16),
                pltpu.VMEM((2 * row_count, width), bf16),
                pltpu.VMEM((2 * row_count, width), bf16),
                pltpu.VMEM((2 * row_count, width), bf16),
                pltpu.VMEM((block + pad, lanes), jnp.float32),
                pltpu.VMEM((block_count, keys_seen, lanes), jnp.float32),
                pltpu.VMEM((block_count, 1, lanes), jnp.float32),
                pltpu.VMEM((block_count, keys_seen, lanes), bf16),
                pltpu.SemaphoreType.DMA((22,)),
            ),
            vmem_mib=32,
            flops=12 * frame_count * model_width * width,
            moved=8 * frame_count * model_width,
        )
        attended.append(results[:2])
        sums.append(results[2:])
        outs.append(out_piece)
    other_outs = [swap_cores(w) for w in outs]
    other_attended = [swap_cores(for_other) for _, for_other in attended]

    other_sums = [swap_cores(for_other) for _, for_other in sums]
    projections = (*outs, *other_outs)
    features = (attended[0][0], attended[1][0], *other_attended, *projections)
    sent_rows = local_call(
        functools.partial(pool_kernel, offsets_at),
        shape_of(slot_count, model_width),
        (scalars,),
        (base, inverse, route, sums[0][0], sums[1][0], *other_sums, *projections),
        scratch=(
            pltpu.VMEM((token_count, model_width), bf16),
            pltpu.VMEM((token_count, model_width), bf16),
        ),
        flops=4 * token_count * model_width * model_width,
        moved=6 * frame_count * model_width,
    )
    received = exchange_blocks(
        sent_rows.reshape(time_count, capacity, model_width)
    ).reshape(slot_count, model_width)
    encoded = local_call(
        functools.partial(encode_kernel, offsets_at),
        shape_of(frame_count, model_width),
        (scalars,),
        (*features, local_frames),
        scratch=(pltpu.VMEM((frame_count, model_width), bf16),),
        flops=2 * frame_count * model_width * model_width,
        moved=6 * frame_count * model_width,
    )
    language_pieces = (language_weight, swap_cores(language_weight), l1, swap_cores(l1))
    lm_out = local_call(
        functools.partial(language_kernel, places_at),
        shape_of(slot_count, rec_count * language_shard),
        (scalars,),
        (received, *language_pieces),
        in_place=rec_count,
        out_in_place=True,
        scratch=(
            pltpu.VMEM((rec_count, model_width, language_shard), bf16),
            pltpu.VMEM((rec_count, slot_count, language_shard), bf16),
            pltpu.SemaphoreType.DMA((rec_count,)),
            pltpu.SemaphoreType.DMA((rec_count,)),
        ),
        flops=2 * slot_count * model_width * rec_count * language_shard,
        moved=2 * model_width * rec_count * language_shard,
    )
    return (encoded[None], lm_out[None, None])


def solution(mesh):
    in_specs = (
        P("rec", "tm", None),
        P("rec"),
        P(),
        P(),
        P(None, None, "tm"),
        P(None, "tm"),
        P("rec", "tm", None),
        P("rec", "tm", None, None),
        P(None, "rec"),
    )
    out_specs = (P("rec", "tm", None), P("rec", "tm", None, None))
    rec_count, time_count = mesh.shape["rec"], mesh.shape["tm"]
    paired = shard_map_of(mesh, in_specs, out_specs, per_device)
    plain = shard_map_of(mesh, in_specs, out_specs, plain_device)

    def run(*arrays):
        shard = arrays[5].shape[1] // time_count
        fits = rec_count == 4 and time_count == 8 and shard % LANES == 0
        return (paired if fits else plain)(*arrays)

    return run


def shard_map_of(mesh, in_specs, out_specs, body):
    return jax.shard_map(
        body, mesh=mesh, in_specs=in_specs, out_specs=out_specs, check_vma=False
    )
```

```python
import functools

import jax
import jax.numpy as jnp
from jax import lax
from jax.experimental import pallas as pl
from jax.experimental.pallas import tpu as pltpu
from jax.sharding import PartitionSpec as P


H = 16
C = 32
RC = 8


EPS_NORM = 1e-05
EPS_MEMORY = 1e-06
NEG_BIG = -1e30
LANES = 128
RING = 4
LOG2_E = 1.4426950408889634


def shifted(block, axis, distance):
    devices = range(lax.axis_size(axis))
    route = [(i - distance, i) for i in devices if i - distance in devices]
    return lax.ppermute(block, axis, route)


def layer_norm(values_in, gain):
    values_in = values_in.astype(jnp.float32)
    centre = jnp.mean(values_in, axis=-1, keepdims=True)
    centred = values_in - centre
    spread = jnp.mean(centred * centred, axis=-1, keepdims=True)
    return centred * lax.rsqrt(spread + EPS_NORM) * gain


def span_memory(normed, live_mask, gain, span_len):
    model_width = normed.shape[1]
    masked = jnp.where(live_mask[:, None], normed.astype(jnp.float32), jnp.float32(0.0))
    owner_sums = masked.reshape(-1, span_len, model_width).sum(axis=1)
    counts = live_mask.reshape(-1, span_len).astype(jnp.float32).sum(axis=1)
    means = owner_sums / jnp.maximum(counts, 1.0)[:, None]
    power = jnp.mean(means * means, axis=-1, keepdims=True)
    return (means * lax.rsqrt(power + EPS_MEMORY) * gain).astype(jnp.bfloat16)


def block_size():
    return 256


def local_part(query, keys, values, first_frame, length, head_count, span_len, right_len):
    frame_count, model_width = query.shape
    head_size = model_width // head_count
    group_rows = 4 * span_len
    group_count = frame_count // group_rows
    block_rows = block_size()
    query_blocks = query.reshape(group_count, group_rows, head_count, head_size)
    key_blocks = keys[:frame_count].reshape(group_count, group_rows, head_count, head_size)
    value_blocks = values[:frame_count].reshape(group_count, group_rows, head_count, head_size)
    key_tail = keys[frame_count:].reshape(1, right_len, head_count, head_size)
    value_tail = values[frame_count:].reshape(1, right_len, head_count, head_size)
    key_all = jnp.concatenate(
        [key_blocks, jnp.concatenate([key_blocks[1:, :right_len], key_tail], axis=0)], axis=1
    )
    value_all = jnp.concatenate(
        [value_blocks, jnp.concatenate([value_blocks[1:, :right_len], value_tail], axis=0)], axis=1
    )
    start_offsets = jnp.arange(group_count, dtype=jnp.int32)[:, None] * group_rows
    query_pos = first_frame + start_offsets + jnp.arange(group_rows, dtype=jnp.int32)[None, :]
    key_pos = first_frame + jnp.concatenate(
        [
            start_offsets + jnp.arange(group_rows, dtype=jnp.int32)[None, :],
            start_offsets + group_rows + jnp.arange(right_len, dtype=jnp.int32)[None, :],
        ],
        axis=1,
    )
    query_span = query_pos // span_len
    span_end = (query_span + 1) * span_len
    same = (key_pos // span_len)[:, None, :] == query_span[:, :, None]
    ahead = (key_pos[:, None, :] >= span_end[:, :, None]) & (
        key_pos[:, None, :] < span_end[:, :, None] + right_len
    )
    allowed = (same | ahead) & (key_pos < length)[:, None, :]
    scores = jnp.einsum(
        "gqhd,gkhd->ghqk", query_blocks, key_all, preferred_element_type=jnp.float32
    ) * head_size ** (-0.5)
    scores = jnp.where(allowed[:, None], scores, NEG_BIG)
    row_peak = jnp.max(scores, axis=-1)
    weights = jnp.where(allowed[:, None], jnp.exp(scores - row_peak[..., None]), jnp.float32(0.0))
    row_total = jnp.sum(weights, axis=-1)
    accum = jnp.einsum(
        "ghqk,gkhd->ghqd",
        weights.astype(jnp.bfloat16),
        value_all,
        preferred_element_type=jnp.float32,
    )
    block_count = frame_count // block_rows
    row_peak = (
        row_peak.transpose(1, 0, 2).reshape(head_count, block_count, block_rows).transpose(1, 0, 2)
    )
    row_total = (
        row_total.transpose(1, 0, 2).reshape(head_count, block_count, block_rows).transpose(1, 0, 2)
    )
    accum = (
        accum.transpose(1, 0, 2, 3)
        .reshape(head_count, block_count, block_rows, head_size)
        .transpose(1, 0, 2, 3)
    )
    return (row_peak, row_total, accum)


def memory_update(
    carry, memory_keys, memory_values, query, first_frame, length, head_count, span_len
):
    row_peak, row_total, accum = carry
    block_count, _, block_rows = row_peak.shape
    row_count, model_width = memory_keys.shape
    head_size = model_width // head_count
    mem_keys = memory_keys.reshape(row_count, head_count, head_size)
    mem_values = memory_values.reshape(row_count, head_count, head_size)
    mem_index = jnp.arange(row_count, dtype=jnp.int32)
    mem_live = mem_index * span_len < length
    query_blocks = query.reshape(block_count, block_rows, head_count, head_size)
    positions = first_frame + jnp.arange(block_count * block_rows, dtype=jnp.int32).reshape(
        block_count, block_rows
    )

    def one_block(packed):
        query_now, pos_now, peak_now, total_now, accum_now = packed
        scores = jnp.einsum(
            "qhd,khd->hqk", query_now, mem_keys, preferred_element_type=jnp.float32
        ) * head_size ** (-0.5)
        allowed = (mem_index[None, :] < (pos_now // span_len)[:, None]) & mem_live[None, :]
        scores = jnp.where(allowed[None], scores, NEG_BIG)
        new_peak = jnp.maximum(peak_now, jnp.max(scores, axis=-1))
        weights = jnp.where(allowed[None], jnp.exp(scores - new_peak[..., None]), jnp.float32(0.0))
        factor = jnp.exp(peak_now - new_peak)
        total_next = total_now * factor + jnp.sum(weights, axis=-1)
        accum_next = accum_now * factor[..., None] + jnp.einsum(
            "hqk,khd->hqd",
            weights.astype(jnp.bfloat16),
            mem_values,
            preferred_element_type=jnp.float32,
        )
        return (new_peak, total_next, accum_next)

    return lax.map(one_block, (query_blocks, positions, row_peak, row_total, accum))


def finish(carry, frame_count, model_width):
    _, row_total, accum = carry
    result = accum / row_total[..., None]
    return result.transpose(0, 2, 1, 3).reshape(frame_count, model_width).astype(jnp.bfloat16)


def dispatch_matrix(owner_ids, owner_count, capacity):
    choose = (owner_ids[:, None] == jnp.arange(owner_count, dtype=jnp.int32)[None, :]).astype(
        jnp.int32
    )
    before = jnp.cumsum(choose, axis=0) - choose
    slot_index = jnp.sum(before * choose, axis=1)
    target = owner_ids * capacity + slot_index
    slot_rows = jnp.arange(owner_count * capacity, dtype=jnp.int32)
    return (slot_rows[:, None] == target[None, :]).astype(jnp.bfloat16)


def plain_device(
    frames,
    lengths,
    norm_gain,
    memory_gain,
    qkv_weight,
    out_weight,
    segment_ids,
    owners,
    language_weight,
):
    local_frames = frames[0]
    frame_count, model_width = local_frames.shape
    head_count = H
    time_count = lax.axis_size("tm")
    first_frame = lax.axis_index("tm") * frame_count
    length = lengths[0]
    live_mask = first_frame + jnp.arange(frame_count, dtype=jnp.int32) < length
    right_frames = shifted(local_frames[:RC], "tm", -1)
    normed = layer_norm(local_frames, norm_gain).astype(jnp.bfloat16)
    normed_right = layer_norm(right_frames, norm_gain).astype(jnp.bfloat16)
    memory = span_memory(normed, live_mask, memory_gain, C)
    stacked_rows = jnp.concatenate([normed, normed_right, memory], axis=0)
    projected = jnp.einsum(
        "fd,kdw->kfw",
        stacked_rows,
        lax.all_gather(qkv_weight, "tm", axis=2, tiled=True),
        preferred_element_type=jnp.float32,
    ).astype(jnp.bfloat16)
    split_at = frame_count + RC
    query = projected[0, :frame_count]
    keys = projected[1, :split_at]
    values = projected[2, :split_at]
    memory_keys = projected[1, split_at:]
    memory_values = projected[2, split_at:]
    carry = local_part(query, keys, values, first_frame, length, head_count, C, RC)
    carry = memory_update(
        carry,
        lax.all_gather(memory_keys, "tm", axis=0, tiled=True),
        lax.all_gather(memory_values, "tm", axis=0, tiled=True),
        query,
        first_frame,
        length,
        head_count,
        C,
    )
    attended = finish(carry, frame_count, model_width)
    output_proj = jnp.dot(
        attended,
        lax.all_gather(out_weight, "tm", axis=1, tiled=True),
        preferred_element_type=jnp.float32,
    )
    encoded = jnp.where(
        live_mask[:, None], local_frames.astype(jnp.float32) + output_proj, jnp.float32(0.0)
    ).astype(jnp.bfloat16)
    token_count = owners.shape[2]
    segments = segment_ids[0, 0]
    owner_indicator = (
        segments[None, :] == jnp.arange(token_count, dtype=jnp.int32)[:, None]
    ).astype(jnp.bfloat16)
    owner_sums = jnp.dot(owner_indicator, encoded, preferred_element_type=jnp.float32)
    counts = jnp.sum(owner_indicator.astype(jnp.float32), axis=1)
    pooled_rows = (owner_sums / counts[:, None]).astype(jnp.bfloat16)
    slot_count = 2 * token_count
    capacity = slot_count // time_count
    route_matrix = dispatch_matrix(owners[0, 0, :, 0], time_count, capacity)
    sent_rows = jnp.dot(route_matrix, pooled_rows, preferred_element_type=jnp.float32).astype(
        jnp.bfloat16
    )
    received = lax.all_to_all(
        sent_rows.reshape(time_count, capacity, model_width),
        "tm",
        split_axis=0,
        concat_axis=0,
        tiled=True,
    )
    received = received.reshape(slot_count, model_width)
    lm_out = jnp.dot(
        received,
        lax.all_gather(language_weight, "rec", axis=1, tiled=True),
        preferred_element_type=jnp.float32,
    ).astype(jnp.bfloat16)
    return (encoded[None], lm_out[None, None])


def vmem_spec():
    return pl.BlockSpec(memory_space=pltpu.VMEM)


def smem_spec():
    return pl.BlockSpec(memory_space=pltpu.SMEM)


def local_call(kernel, out_shapes, scalars, operands, scratch=(), in_place=0, out_in_place=False, vmem_mib=16, flops=0, moved=0):
    whole = len(operands) - in_place
    return pl.pallas_call(
        kernel,
        out_shape=out_shapes,
        in_specs=[smem_spec()] * len(scalars)
        + [vmem_spec()] * whole
        + [pl.BlockSpec(memory_space=pltpu.HBM if out_in_place else pl.ANY)] * in_place,
        out_specs=jax.tree.map(
            lambda _: pl.BlockSpec(memory_space=pl.ANY) if out_in_place else vmem_spec(), out_shapes
        ),
        compiler_params=pltpu.CompilerParams(vmem_limit_bytes=vmem_mib << 20),
        scratch_shapes=list(scratch),
        cost_estimate=pl.CostEstimate(flops=flops, bytes_accessed=moved, transcendentals=0),
    )(*scalars, *operands)


def shape_of(*dims, dtype=jnp.bfloat16):
    return jax.ShapeDtypeStruct(dims, dtype)


def normalise_kernel(
    span_len, scalars, frames, gain, memory_gain, normed_out, ahead_out, memory_out
):
    first_frame, length = scalars[0], scalars[1]
    frame_count, _ = frames.shape
    span_count = frame_count // span_len
    values = frames[...].astype(jnp.float32)
    centre = jnp.mean(values, axis=-1, keepdims=True)
    centred = values - centre
    spread = jnp.mean(centred * centred, axis=-1, keepdims=True)
    normed = (centred * lax.rsqrt(spread + EPS_NORM) * gain[...]).astype(jnp.bfloat16)
    normed_out[...] = normed
    ahead_out[...] = normed[: ahead_out.shape[0]]
    spans = lax.broadcasted_iota(jnp.int32, (span_count, frame_count), 0)
    places = lax.broadcasted_iota(jnp.int32, (span_count, frame_count), 1)
    member = (places >= spans * span_len) & (places < (spans + 1) * span_len)
    member = member & (places < length - first_frame)
    sums = jnp.dot(
        member.astype(jnp.bfloat16), normed, preferred_element_type=jnp.float32
    )
    counts = jnp.sum(member.astype(jnp.float32), axis=-1, keepdims=True)
    means = sums / jnp.maximum(counts, 1.0)
    power = jnp.mean(means * means, axis=-1, keepdims=True)
    memory = (means * lax.rsqrt(power + EPS_MEMORY) * memory_gain[...]).astype(jnp.bfloat16)
    for copy in range(memory_out.shape[0]):
        memory_out[copy] = memory


def prepare_kernel(scalars, frames, segments, owners_row, owners_col, base_out, member_out, count_out, route_out):
    first_frame, length, capacity = scalars[0], scalars[1], scalars[4]
    token_count, frame_count = member_out.shape
    tokens = lax.broadcasted_iota(jnp.int32, (token_count, frame_count), 0)
    places = first_frame + lax.broadcasted_iota(jnp.int32, (token_count, frame_count), 1)
    member = (segments[...] == tokens).astype(jnp.float32)
    counts = jnp.sum(member, axis=1, keepdims=True)
    live_member = jnp.where(places < length, member, 0.0).astype(jnp.bfloat16)
    earlier = lax.broadcasted_iota(jnp.int32, (token_count, token_count), 0)
    later = lax.broadcasted_iota(jnp.int32, (token_count, token_count), 1)
    clash = (owners_col[...] == owners_row[...]) & (earlier < later)
    slot = jnp.sum(clash.astype(jnp.int32), axis=0, keepdims=True)
    target = owners_row[...] * capacity + slot
    slots = lax.broadcasted_iota(jnp.int32, route_out.shape, 0)
    route_out[...] = (slots == target).astype(jnp.bfloat16)
    member_out[...] = live_member
    count_out[...] = jnp.broadcast_to(1.0 / counts, count_out.shape)
    base_out[...] = (
        jnp.dot(live_member, frames[...], preferred_element_type=jnp.float32) / counts
    )


def attend_kernel(span_len, right_len, head_size, scalars, other_length, *refs):
    members, sources, pieces = refs[:2], refs[2:8], refs[8:16]
    outs, sums_out, projection = refs[16:18], refs[18:20], refs[20]
    rows_in, weight, query, key, value, bias, scores, peaks, weights, sems = refs[21:]
    first_frame, core, y_half = scalars[0], scalars[2], scalars[3]
    frame_count, model_width = sources[0].shape
    half = model_width // 2
    width = outs[0].shape[1]
    heads = width // head_size
    block = 2 * span_len
    blocks = frame_count // block
    near = bias.shape[0]
    memory_at = frame_count + near - block
    row_count = rows_in.shape[0] // 2
    memory_count = row_count - memory_at
    lanes = heads * block

    def piece_copies(of_core, projected):
        places = (y_half * half, (1 - y_half) * half)
        copies = []
        for side in range(2):
            place = pl.ds(pl.multiple_of(places[side], half), half)
            for shard in range(2):
                piece = pieces[4 * shard + 2 * side + of_core]
                index = 2 * side + shard
                for part in (3,) if projected else (0, 1, 2):
                    target = projection if projected else weight
                    start = shard * piece.shape[2] + (0 if projected else part * width)
                    copies.append(
                        pltpu.make_async_copy(
                            piece.at[part],
                            target.at[place, pl.ds(start, piece.shape[2])],
                            sems.at[4 * part + index],
                        )
                    )
        return copies

    row_copies = []
    for rec in range(2):
        at = rec * row_count
        for i, (start, size) in enumerate(
            ((0, frame_count), (frame_count, near - block), (memory_at, memory_count))
        ):
            row_copies.append(
                pltpu.make_async_copy(
                    sources[3 * rec + i], rows_in.at[pl.ds(at + start, size)], sems.at[16 + 3 * rec + i]
                )
            )

    for copy in row_copies:
        copy.start()
    for of_core in range(2):

        @pl.when(core == of_core)
        def _():
            for copy in piece_copies(of_core, False) + piece_copies(of_core, True):
                copy.start()

    rows = lax.broadcasted_iota(jnp.int32, (near, lanes), 0)
    spans = (lax.broadcasted_iota(jnp.int32, (near, lanes), 1) % block) // span_len
    same = (rows >= spans * span_len) & (rows < (spans + 1) * span_len + right_len)
    bias[...] = jnp.where(same, jnp.float32(0.0), jnp.float32(NEG_BIG))
    lane_spans = (lax.broadcasted_iota(jnp.int32, (1, lanes), 1) % block) // span_len
    memory_rows = lax.broadcasted_iota(jnp.int32, (memory_count, lanes), 0)
    feature_head = lax.broadcasted_iota(jnp.int32, (1, width), 1) // head_size
    head_masks = [(feature_head == h).astype(jnp.bfloat16) for h in range(heads)]
    scale = head_size ** (-0.5) * LOG2_E

    for copy in row_copies + piece_copies(0, False):
        copy.wait()
    mixed = jnp.dot(rows_in[...], weight[...], preferred_element_type=jnp.float32)
    query[...] = (mixed[:, :width] * scale).astype(jnp.bfloat16)
    key[...] = mixed[:, width : 2 * width].astype(jnp.bfloat16)
    value[...] = mixed[:, 2 * width :].astype(jnp.bfloat16)

    def score_block(i):
        rec, b = divmod(i, blocks)
        at, start = rec * row_count, b * block
        length = scalars[1] if rec == 0 else other_length[0]
        q_now = query[at + start : at + start + block]
        stacked = jnp.concatenate([q_now * m for m in head_masks], axis=0)
        keys = jnp.concatenate(
            [key[at + start : at + start + near], key[at + memory_at : at + row_count]], axis=0
        )
        raw = lax.dot_general(
            keys, stacked, (((1,), (1,)), ((), ())), preferred_element_type=jnp.float32
        )
        limit = length - first_frame - start
        local = jnp.where(rows < limit, raw[:near] + bias[...], NEG_BIG)
        live_spans = (length + span_len - 1) // span_len
        span_limit = jnp.minimum(first_frame // span_len + 2 * b + lane_spans, live_spans)
        memory = jnp.where(memory_rows < span_limit, raw[near:], NEG_BIG)
        slot = i % scores.shape[0]
        scores[slot, 0:near, :] = local
        scores[slot, near:, :] = memory
        peaks[slot] = jnp.maximum(
            jnp.max(local, axis=0, keepdims=True), jnp.max(memory, axis=0, keepdims=True)
        )

    def weigh_block(i):
        slot = i % scores.shape[0]
        weights[slot] = jnp.exp2(scores[slot] - peaks[slot]).astype(jnp.bfloat16)

    ones = jnp.ones((near + memory_count, LANES), jnp.bfloat16)
    first_of_pair = lax.broadcasted_iota(jnp.int32, (1, 2 * LANES), 1) % LANES < head_size

    def mix_block(i):
        rec, b = divmod(i, blocks)
        at, start = rec * row_count, b * block
        values = jnp.concatenate(
            [value[at + start : at + start + near], value[at + memory_at : at + row_count]], axis=0
        )
        for pair in range(width // LANES):
            columns = slice(pair * LANES, (pair + 1) * LANES)
            pair_rows = slice(pair * 2 * block, (pair + 1) * 2 * block)
            sums = lax.dot_general(
                weights[i % weights.shape[0], :, pair_rows],
                jnp.concatenate([values[:, columns], ones], axis=1),
                (((0,), (0,)), ((), ())),
                preferred_element_type=jnp.float32,
            )
            picked = jnp.where(first_of_pair, sums[:block], sums[block:])
            outs[rec][start : start + block, columns] = (
                picked[:, :LANES] / picked[:, LANES:]
            ).astype(jnp.bfloat16)

    count = 2 * blocks
    for step in range(count + 2):
        if step >= 2:
            mix_block(step - 2)
        if 1 <= step <= count:
            weigh_block(step - 1)
        if step < count:
            score_block(step)
    for rec in range(2):
        sums_out[rec][...] = jnp.dot(
            members[rec][...], outs[rec][...], preferred_element_type=jnp.float32
        )
    for copy in piece_copies(0, True):
        copy.wait()


def assemble(scalars, offsets_at, attended, gathered):
    shard = attended[0].shape[1] // 2
    offsets = [
        [pl.multiple_of(scalars[offsets_at + 2 * i + s], LANES) for s in range(2)]
        for i in range(4)
    ]
    for i in range(4):
        for s in range(2):
            gathered[:, pl.ds(offsets[i][s], shard)] = attended[i][:, s * shard : (s + 1) * shard]
    return offsets, shard


def pool_kernel(offsets_at, scalars, base, inverse, route, *refs):
    sums, projections = refs[:4], refs[4:8]
    sent_out, means, pooled = refs[8:]
    shard = sums[0].shape[1] // 2
    offsets = [
        [pl.multiple_of(scalars[offsets_at + 2 * i + s], LANES) for s in range(2)]
        for i in range(4)
    ]
    for i in range(4):
        for s in range(2):
            for lane in range(0, shard, LANES):
                means[:, pl.ds(offsets[i][s] + lane, LANES)] = (
                    sums[i][:, s * shard + lane : s * shard + lane + LANES] * inverse[...]
                ).astype(jnp.bfloat16)
    for i in range(4):
        mixed = jnp.dot(means[...], projections[i][...], preferred_element_type=jnp.float32)
        for s in range(2):
            columns = pl.ds(offsets[i][s], shard)
            pooled[:, columns] = (
                base[:, columns] + mixed[:, s * shard : (s + 1) * shard]
            ).astype(jnp.bfloat16)
    sent_out[...] = jnp.dot(
        route[...], pooled[...], preferred_element_type=jnp.float32
    ).astype(jnp.bfloat16)


def encode_kernel(offsets_at, scalars, *refs):
    attended, projections, frames = refs[:4], refs[4:8], refs[8]
    encoded_out, gathered = refs[9:]
    first_frame, length = scalars[0], scalars[1]
    frame_count, _ = frames.shape
    offsets, shard = assemble(scalars, offsets_at, attended, gathered)
    live = (
        first_frame + lax.broadcasted_iota(jnp.int32, (frame_count, 1), 0) < length
    ).astype(jnp.float32)
    for i in range(4):
        mixed = jnp.dot(
            gathered[...], projections[i][...], preferred_element_type=jnp.float32
        )
        for s in range(2):
            columns = pl.ds(offsets[i][s], shard)
            base = frames[:, columns].astype(jnp.float32)
            encoded_out[:, columns] = (
                (base + mixed[:, s * shard : (s + 1) * shard]) * live
            ).astype(jnp.bfloat16)


def language_kernel(places_at, scalars, received, *refs):
    pieces, out = refs[:-5], refs[-5]
    weights, product, sems, out_sems = refs[-4:]
    count, width = len(pieces), pieces[0].shape[1]
    copies = [
        pltpu.make_async_copy(piece, weights.at[i], sems.at[i]) for i, piece in enumerate(pieces)
    ]
    for copy in copies:
        copy.start()
    out_copies = []
    for i in range(count):
        copies[i].wait()
        product[i] = jnp.dot(
            received[...], weights[i], preferred_element_type=jnp.float32
        ).astype(jnp.bfloat16)
        place = pl.multiple_of(scalars[places_at + i], LANES)
        out_copies.append(
            pltpu.make_async_copy(product.at[i], out.at[:, pl.ds(place, width)], out_sems.at[i])
        )
        out_copies[-1].start()
    for copy in out_copies:
        copy.wait()


def along_x(r, j, _):
    return r, j ^ 1


def along_y(r, j, _):
    return r ^ 2, j


def other_core(r, j, _):
    return r ^ 1, j


def z_up(r, j, count):
    return r, (j + 2) % count


def z_down(r, j, count):
    return r, (j - 2) % count


def relocate(value, core_0, core_1):
    rec_count, time_count = lax.axis_size("rec"), lax.axis_size("tm")
    pairs = []
    for r in range(rec_count):
        for j in range(time_count):
            route = (core_0, core_1)[r % 2]
            if route is not None:
                to_r, to_j = route(r, j, time_count)
                pairs.append((r * time_count + j, to_r * time_count + to_j))
    return lax.ppermute(value, ("rec", "tm"), pairs)


def swap_cores(value):
    return relocate(value, other_core, other_core)


def exchange_blocks(blocks):
    return lax.all_to_all(blocks, "tm", split_axis=0, concat_axis=0, tiled=True)


def per_device(
    frames,
    lengths,
    norm_gain,
    memory_gain,
    qkv_weight,
    out_weight,
    segment_ids,
    owners,
    language_weight,
):
    local_frames = frames[0]
    frame_count, model_width = local_frames.shape
    shard = out_weight.shape[1]
    half = model_width // 2
    time_count = lax.axis_size("tm")
    rec_count = lax.axis_size("rec")
    rec, time = lax.axis_index("rec"), lax.axis_index("tm")
    core, y_half = rec % 2, (rec // 2) % 2
    x, z = time % 2, time // 2
    z_count = time_count // 2
    first_frame = time * frame_count
    length = lengths[0]
    head_size = model_width // H
    bf16 = jnp.bfloat16

    own = jnp.concatenate([qkv_weight, out_weight[None]], axis=0)
    own_a = lax.dynamic_slice_in_dim(own, y_half * half, half, 1)
    later_qkv, later_out, own_a = lax.optimization_barrier((qkv_weight, out_weight, own_a))
    later = jnp.concatenate([later_qkv, later_out[None]], axis=0)
    own_b = lax.dynamic_slice_in_dim(later, (1 - y_half) * half, half, 1)

    def pick(for_core_0, for_core_1):
        return jnp.where(core == 0, for_core_0, for_core_1)

    token_count = owners.shape[2]
    slot_count = 2 * token_count
    capacity = slot_count // time_count
    language_shard = language_weight.shape[1]

    def group_of(of_core, slot):
        return jnp.where(of_core == 0, z + slot, z - slot - 1) % z_count

    numbers = [first_frame, length, core, y_half, capacity]
    offsets_at = len(numbers)
    for of_core in (core, 1 - core):
        for slot in range(2):
            group = group_of(of_core, slot)
            numbers += [(2 * group + x) * shard, (2 * group + 1 - x) * shard]
    places_at = len(numbers)
    numbers += [(rec ^ i) * language_shard for i in range(rec_count)]
    scalars = jnp.stack(numbers).astype(jnp.int32)

    m1 = relocate(own_a, along_x, z_up)
    m2 = relocate(pick(own_a, own_b), z_down, z_up)
    l1 = relocate(language_weight, along_y, along_y)

    pad = 2 * RC
    normed, start_rows, memory = local_call(
        functools.partial(normalise_kernel, C),
        (
            shape_of(frame_count, model_width),
            shape_of(pad, model_width),
            shape_of(time_count, frame_count // C, model_width),
        ),
        (scalars,),
        (local_frames, norm_gain[None], memory_gain[None]),
        flops=10 * frame_count * model_width,
        moved=4 * frame_count * model_width,
    )
    other_length = swap_cores(lengths)
    other_normed = swap_cores(normed)
    ahead = shifted(start_rows, "tm", -1)
    memories = exchange_blocks(memory).reshape(-1, model_width)
    owners_col = owners[0, 0]
    base, member, inverse, route = local_call(
        prepare_kernel,
        (
            shape_of(token_count, model_width, dtype=jnp.float32),
            shape_of(token_count, frame_count),
            shape_of(token_count, LANES, dtype=jnp.float32),
            shape_of(slot_count, token_count),
        ),
        (scalars,),
        (local_frames, segment_ids[0], owners_col.reshape(1, token_count), owners_col),
        flops=2 * token_count * frame_count * model_width,
        moved=2 * frame_count * model_width,
    )
    other_member = swap_cores(member)
    other_ahead = swap_cores(ahead)
    other_memories = swap_cores(memories)

    m3 = relocate(m1, along_y, along_x)
    m4 = relocate(m1, None, z_up)
    m5 = relocate(m2, along_x, z_up)
    m6 = relocate(m3, None, along_y)
    m7 = relocate(pick(m2, m4), along_y, along_x)
    m8 = relocate(m5, along_y, along_x)

    slot_pieces = (
        ((own_a, m1), (own_b, m2), (m1, m3), (m3, m6)),
        ((m2, m4), (m7, m5), (m5, m7), (m8, m8)),
    )
    block = 2 * C
    width = 2 * shard
    row_count = frame_count + pad + memories.shape[0]
    keys_seen = block + pad + memories.shape[0]
    lanes = width // head_size * block
    attended, sums, outs = [], [], []
    for pieces in slot_pieces:
        flat = [p for pair in pieces for p in pair]
        *results, out_piece = local_call(
            functools.partial(attend_kernel, C, RC, head_size),
            (
                shape_of(frame_count, width),
                shape_of(frame_count, width),
                shape_of(token_count, width, dtype=jnp.float32),
                shape_of(token_count, width, dtype=jnp.float32),
                shape_of(model_width, width),
            ),
            (scalars, other_length),
            (member, other_member, normed, ahead, memories, other_normed, other_ahead, other_memories, *flat),
            in_place=6 + len(flat),
            scratch=(
                pltpu.VMEM((2 * row_count, model_width), bf16),
                pltpu.VMEM((model_width, 3 * width), bf16),
                pltpu.VMEM((2 * row_count, width), bf16),
                pltpu.VMEM((2 * row_count, width), bf16),
                pltpu.VMEM((2 * row_count, width), bf16),
                pltpu.VMEM((block + pad, lanes), jnp.float32),
                pltpu.VMEM((RING, keys_seen, lanes), jnp.float32),
                pltpu.VMEM((RING, 1, lanes), jnp.float32),
                pltpu.VMEM((RING, keys_seen, lanes), bf16),
                pltpu.SemaphoreType.DMA((22,)),
            ),
            vmem_mib=20,
            flops=12 * frame_count * model_width * width,
            moved=8 * frame_count * model_width,
        )
        attended.append(results[:2])
        sums.append(results[2:])
        outs.append(out_piece)
    other_outs = [swap_cores(w) for w in outs]
    other_attended = [swap_cores(for_other) for _, for_other in attended]

    other_sums = [swap_cores(for_other) for _, for_other in sums]
    projections = (*outs, *other_outs)
    features = (attended[0][0], attended[1][0], *other_attended, *projections)
    sent_rows = local_call(
        functools.partial(pool_kernel, offsets_at),
        shape_of(slot_count, model_width),
        (scalars,),
        (base, inverse, route, sums[0][0], sums[1][0], *other_sums, *projections),
        scratch=(
            pltpu.VMEM((token_count, model_width), bf16),
            pltpu.VMEM((token_count, model_width), bf16),
        ),
        flops=4 * token_count * model_width * model_width,
        moved=6 * frame_count * model_width,
    )
    received = exchange_blocks(
        sent_rows.reshape(time_count, capacity, model_width)
    ).reshape(slot_count, model_width)
    encoded = local_call(
        functools.partial(encode_kernel, offsets_at),
        shape_of(frame_count, model_width),
        (scalars,),
        (*features, local_frames),
        scratch=(pltpu.VMEM((frame_count, model_width), bf16),),
        flops=2 * frame_count * model_width * model_width,
        moved=6 * frame_count * model_width,
    )
    language_pieces = (language_weight, swap_cores(language_weight), l1, swap_cores(l1))
    lm_out = local_call(
        functools.partial(language_kernel, places_at),
        shape_of(slot_count, rec_count * language_shard),
        (scalars,),
        (received, *language_pieces),
        in_place=rec_count,
        out_in_place=True,
        scratch=(
            pltpu.VMEM((rec_count, model_width, language_shard), bf16),
            pltpu.VMEM((rec_count, slot_count, language_shard), bf16),
            pltpu.SemaphoreType.DMA((rec_count,)),
            pltpu.SemaphoreType.DMA((rec_count,)),
        ),
        flops=2 * slot_count * model_width * rec_count * language_shard,
        moved=2 * model_width * rec_count * language_shard,
    )
    return (encoded[None], lm_out[None, None])


def solution(mesh):
    in_specs = (
        P("rec", "tm", None),
        P("rec"),
        P(),
        P(),
        P(None, None, "tm"),
        P(None, "tm"),
        P("rec", "tm", None),
        P("rec", "tm", None, None),
        P(None, "rec"),
    )
    out_specs = (P("rec", "tm", None), P("rec", "tm", None, None))
    rec_count, time_count = mesh.shape["rec"], mesh.shape["tm"]
    paired = shard_map_of(mesh, in_specs, out_specs, per_device)
    plain = shard_map_of(mesh, in_specs, out_specs, plain_device)

    def run(*arrays):
        shard = arrays[5].shape[1] // time_count
        fits = rec_count == 4 and time_count == 8 and shard % LANES == 0
        return (paired if fits else plain)(*arrays)

    return run


def shard_map_of(mesh, in_specs, out_specs, body):
    return jax.shard_map(
        body, mesh=mesh, in_specs=in_specs, out_specs=out_specs, check_vma=False
    )
```

```python
import functools

import jax
import jax.numpy as jnp
from jax import lax
from jax.experimental import pallas as pl
from jax.experimental.pallas import tpu as pltpu
from jax.sharding import PartitionSpec as P


H = 16
C = 32
RC = 8


EPS_NORM = 1e-05
EPS_MEMORY = 1e-06
NEG_BIG = -1e30
LANES = 128
RING = 16
LOG2_E = 1.4426950408889634


def shifted(block, axis, distance):
    devices = range(lax.axis_size(axis))
    route = [(i - distance, i) for i in devices if i - distance in devices]
    return lax.ppermute(block, axis, route)


def layer_norm(values_in, gain):
    values_in = values_in.astype(jnp.float32)
    centre = jnp.mean(values_in, axis=-1, keepdims=True)
    centred = values_in - centre
    spread = jnp.mean(centred * centred, axis=-1, keepdims=True)
    return centred * lax.rsqrt(spread + EPS_NORM) * gain


def span_memory(normed, live_mask, gain, span_len):
    model_width = normed.shape[1]
    masked = jnp.where(live_mask[:, None], normed.astype(jnp.float32), jnp.float32(0.0))
    owner_sums = masked.reshape(-1, span_len, model_width).sum(axis=1)
    counts = live_mask.reshape(-1, span_len).astype(jnp.float32).sum(axis=1)
    means = owner_sums / jnp.maximum(counts, 1.0)[:, None]
    power = jnp.mean(means * means, axis=-1, keepdims=True)
    return (means * lax.rsqrt(power + EPS_MEMORY) * gain).astype(jnp.bfloat16)


def block_size():
    return 256


def local_part(query, keys, values, first_frame, length, head_count, span_len, right_len):
    frame_count, model_width = query.shape
    head_size = model_width // head_count
    group_rows = 4 * span_len
    group_count = frame_count // group_rows
    block_rows = block_size()
    query_blocks = query.reshape(group_count, group_rows, head_count, head_size)
    key_blocks = keys[:frame_count].reshape(group_count, group_rows, head_count, head_size)
    value_blocks = values[:frame_count].reshape(group_count, group_rows, head_count, head_size)
    key_tail = keys[frame_count:].reshape(1, right_len, head_count, head_size)
    value_tail = values[frame_count:].reshape(1, right_len, head_count, head_size)
    key_all = jnp.concatenate(
        [key_blocks, jnp.concatenate([key_blocks[1:, :right_len], key_tail], axis=0)], axis=1
    )
    value_all = jnp.concatenate(
        [value_blocks, jnp.concatenate([value_blocks[1:, :right_len], value_tail], axis=0)], axis=1
    )
    start_offsets = jnp.arange(group_count, dtype=jnp.int32)[:, None] * group_rows
    query_pos = first_frame + start_offsets + jnp.arange(group_rows, dtype=jnp.int32)[None, :]
    key_pos = first_frame + jnp.concatenate(
        [
            start_offsets + jnp.arange(group_rows, dtype=jnp.int32)[None, :],
            start_offsets + group_rows + jnp.arange(right_len, dtype=jnp.int32)[None, :],
        ],
        axis=1,
    )
    query_span = query_pos // span_len
    span_end = (query_span + 1) * span_len
    same = (key_pos // span_len)[:, None, :] == query_span[:, :, None]
    ahead = (key_pos[:, None, :] >= span_end[:, :, None]) & (
        key_pos[:, None, :] < span_end[:, :, None] + right_len
    )
    allowed = (same | ahead) & (key_pos < length)[:, None, :]
    scores = jnp.einsum(
        "gqhd,gkhd->ghqk", query_blocks, key_all, preferred_element_type=jnp.float32
    ) * head_size ** (-0.5)
    scores = jnp.where(allowed[:, None], scores, NEG_BIG)
    row_peak = jnp.max(scores, axis=-1)
    weights = jnp.where(allowed[:, None], jnp.exp(scores - row_peak[..., None]), jnp.float32(0.0))
    row_total = jnp.sum(weights, axis=-1)
    accum = jnp.einsum(
        "ghqk,gkhd->ghqd",
        weights.astype(jnp.bfloat16),
        value_all,
        preferred_element_type=jnp.float32,
    )
    block_count = frame_count // block_rows
    row_peak = (
        row_peak.transpose(1, 0, 2).reshape(head_count, block_count, block_rows).transpose(1, 0, 2)
    )
    row_total = (
        row_total.transpose(1, 0, 2).reshape(head_count, block_count, block_rows).transpose(1, 0, 2)
    )
    accum = (
        accum.transpose(1, 0, 2, 3)
        .reshape(head_count, block_count, block_rows, head_size)
        .transpose(1, 0, 2, 3)
    )
    return (row_peak, row_total, accum)


def memory_update(
    carry, memory_keys, memory_values, query, first_frame, length, head_count, span_len
):
    row_peak, row_total, accum = carry
    block_count, _, block_rows = row_peak.shape
    row_count, model_width = memory_keys.shape
    head_size = model_width // head_count
    mem_keys = memory_keys.reshape(row_count, head_count, head_size)
    mem_values = memory_values.reshape(row_count, head_count, head_size)
    mem_index = jnp.arange(row_count, dtype=jnp.int32)
    mem_live = mem_index * span_len < length
    query_blocks = query.reshape(block_count, block_rows, head_count, head_size)
    positions = first_frame + jnp.arange(block_count * block_rows, dtype=jnp.int32).reshape(
        block_count, block_rows
    )

    def one_block(packed):
        query_now, pos_now, peak_now, total_now, accum_now = packed
        scores = jnp.einsum(
            "qhd,khd->hqk", query_now, mem_keys, preferred_element_type=jnp.float32
        ) * head_size ** (-0.5)
        allowed = (mem_index[None, :] < (pos_now // span_len)[:, None]) & mem_live[None, :]
        scores = jnp.where(allowed[None], scores, NEG_BIG)
        new_peak = jnp.maximum(peak_now, jnp.max(scores, axis=-1))
        weights = jnp.where(allowed[None], jnp.exp(scores - new_peak[..., None]), jnp.float32(0.0))
        factor = jnp.exp(peak_now - new_peak)
        total_next = total_now * factor + jnp.sum(weights, axis=-1)
        accum_next = accum_now * factor[..., None] + jnp.einsum(
            "hqk,khd->hqd",
            weights.astype(jnp.bfloat16),
            mem_values,
            preferred_element_type=jnp.float32,
        )
        return (new_peak, total_next, accum_next)

    return lax.map(one_block, (query_blocks, positions, row_peak, row_total, accum))


def finish(carry, frame_count, model_width):
    _, row_total, accum = carry
    result = accum / row_total[..., None]
    return result.transpose(0, 2, 1, 3).reshape(frame_count, model_width).astype(jnp.bfloat16)


def dispatch_matrix(owner_ids, owner_count, capacity):
    choose = (owner_ids[:, None] == jnp.arange(owner_count, dtype=jnp.int32)[None, :]).astype(
        jnp.int32
    )
    before = jnp.cumsum(choose, axis=0) - choose
    slot_index = jnp.sum(before * choose, axis=1)
    target = owner_ids * capacity + slot_index
    slot_rows = jnp.arange(owner_count * capacity, dtype=jnp.int32)
    return (slot_rows[:, None] == target[None, :]).astype(jnp.bfloat16)


def plain_device(
    frames,
    lengths,
    norm_gain,
    memory_gain,
    qkv_weight,
    out_weight,
    segment_ids,
    owners,
    language_weight,
):
    local_frames = frames[0]
    frame_count, model_width = local_frames.shape
    head_count = H
    time_count = lax.axis_size("tm")
    first_frame = lax.axis_index("tm") * frame_count
    length = lengths[0]
    live_mask = first_frame + jnp.arange(frame_count, dtype=jnp.int32) < length
    right_frames = shifted(local_frames[:RC], "tm", -1)
    normed = layer_norm(local_frames, norm_gain).astype(jnp.bfloat16)
    normed_right = layer_norm(right_frames, norm_gain).astype(jnp.bfloat16)
    memory = span_memory(normed, live_mask, memory_gain, C)
    stacked_rows = jnp.concatenate([normed, normed_right, memory], axis=0)
    projected = jnp.einsum(
        "fd,kdw->kfw",
        stacked_rows,
        lax.all_gather(qkv_weight, "tm", axis=2, tiled=True),
        preferred_element_type=jnp.float32,
    ).astype(jnp.bfloat16)
    split_at = frame_count + RC
    query = projected[0, :frame_count]
    keys = projected[1, :split_at]
    values = projected[2, :split_at]
    memory_keys = projected[1, split_at:]
    memory_values = projected[2, split_at:]
    carry = local_part(query, keys, values, first_frame, length, head_count, C, RC)
    carry = memory_update(
        carry,
        lax.all_gather(memory_keys, "tm", axis=0, tiled=True),
        lax.all_gather(memory_values, "tm", axis=0, tiled=True),
        query,
        first_frame,
        length,
        head_count,
        C,
    )
    attended = finish(carry, frame_count, model_width)
    output_proj = jnp.dot(
        attended,
        lax.all_gather(out_weight, "tm", axis=1, tiled=True),
        preferred_element_type=jnp.float32,
    )
    encoded = jnp.where(
        live_mask[:, None], local_frames.astype(jnp.float32) + output_proj, jnp.float32(0.0)
    ).astype(jnp.bfloat16)
    token_count = owners.shape[2]
    segments = segment_ids[0, 0]
    owner_indicator = (
        segments[None, :] == jnp.arange(token_count, dtype=jnp.int32)[:, None]
    ).astype(jnp.bfloat16)
    owner_sums = jnp.dot(owner_indicator, encoded, preferred_element_type=jnp.float32)
    counts = jnp.sum(owner_indicator.astype(jnp.float32), axis=1)
    pooled_rows = (owner_sums / counts[:, None]).astype(jnp.bfloat16)
    slot_count = 2 * token_count
    capacity = slot_count // time_count
    route_matrix = dispatch_matrix(owners[0, 0, :, 0], time_count, capacity)
    sent_rows = jnp.dot(route_matrix, pooled_rows, preferred_element_type=jnp.float32).astype(
        jnp.bfloat16
    )
    received = lax.all_to_all(
        sent_rows.reshape(time_count, capacity, model_width),
        "tm",
        split_axis=0,
        concat_axis=0,
        tiled=True,
    )
    received = received.reshape(slot_count, model_width)
    lm_out = jnp.dot(
        received,
        lax.all_gather(language_weight, "rec", axis=1, tiled=True),
        preferred_element_type=jnp.float32,
    ).astype(jnp.bfloat16)
    return (encoded[None], lm_out[None, None])


def vmem_spec():
    return pl.BlockSpec(memory_space=pltpu.VMEM)


def smem_spec():
    return pl.BlockSpec(memory_space=pltpu.SMEM)


def local_call(kernel, out_shapes, scalars, operands, scratch=(), in_place=0, out_in_place=False, vmem_mib=16, flops=0, moved=0):
    whole = len(operands) - in_place
    anywhere = pl.BlockSpec(memory_space=pl.ANY)
    if isinstance(out_shapes, tuple):
        stays = out_in_place or (False,) * len(out_shapes)
        out_specs = tuple(anywhere if stay else vmem_spec() for stay in stays)
    else:
        out_specs = anywhere if out_in_place else vmem_spec()
    return pl.pallas_call(
        kernel,
        out_shape=out_shapes,
        in_specs=[smem_spec()] * len(scalars) + [vmem_spec()] * whole + [anywhere] * in_place,
        out_specs=out_specs,
        compiler_params=pltpu.CompilerParams(vmem_limit_bytes=vmem_mib << 20),
        scratch_shapes=list(scratch),
        cost_estimate=pl.CostEstimate(flops=flops, bytes_accessed=moved, transcendentals=0),
    )(*scalars, *operands)


def shape_of(*dims, dtype=jnp.bfloat16):
    return jax.ShapeDtypeStruct(dims, dtype)


def normalise_kernel(
    span_len, scalars, frames, gain, memory_gain, normed_out, ahead_out, memory_out
):
    first_frame, length = scalars[0], scalars[1]
    frame_count, _ = frames.shape
    span_count = frame_count // span_len
    values = frames[...].astype(jnp.float32)
    centre = jnp.mean(values, axis=-1, keepdims=True)
    centred = values - centre
    spread = jnp.mean(centred * centred, axis=-1, keepdims=True)
    normed = (centred * lax.rsqrt(spread + EPS_NORM) * gain[...]).astype(jnp.bfloat16)
    normed_out[...] = normed
    ahead_out[...] = normed[: ahead_out.shape[0]]
    spans = lax.broadcasted_iota(jnp.int32, (span_count, frame_count), 0)
    places = lax.broadcasted_iota(jnp.int32, (span_count, frame_count), 1)
    member = (places >= spans * span_len) & (places < (spans + 1) * span_len)
    member = member & (places < length - first_frame)
    sums = jnp.dot(
        member.astype(jnp.bfloat16), normed, preferred_element_type=jnp.float32
    )
    counts = jnp.sum(member.astype(jnp.float32), axis=-1, keepdims=True)
    means = sums / jnp.maximum(counts, 1.0)
    power = jnp.mean(means * means, axis=-1, keepdims=True)
    memory = (means * lax.rsqrt(power + EPS_MEMORY) * memory_gain[...]).astype(jnp.bfloat16)
    for copy in range(memory_out.shape[0]):
        memory_out[copy] = memory


def prepare_kernel(scalars, frames, segments, owners_row, owners_col, base_out, member_out, count_out, route_out):
    first_frame, length, capacity = scalars[0], scalars[1], scalars[4]
    token_count, frame_count = member_out.shape
    tokens = lax.broadcasted_iota(jnp.int32, (token_count, frame_count), 0)
    places = first_frame + lax.broadcasted_iota(jnp.int32, (token_count, frame_count), 1)
    member = (segments[...] == tokens).astype(jnp.float32)
    counts = jnp.sum(member, axis=1, keepdims=True)
    live_member = jnp.where(places < length, member, 0.0).astype(jnp.bfloat16)
    earlier = lax.broadcasted_iota(jnp.int32, (token_count, token_count), 0)
    later = lax.broadcasted_iota(jnp.int32, (token_count, token_count), 1)
    clash = (owners_col[...] == owners_row[...]) & (earlier < later)
    slot = jnp.sum(clash.astype(jnp.int32), axis=0, keepdims=True)
    target = owners_row[...] * capacity + slot
    slots = lax.broadcasted_iota(jnp.int32, route_out.shape, 0)
    route_out[...] = (slots == target).astype(jnp.bfloat16)
    member_out[...] = live_member
    count_out[...] = jnp.broadcast_to(1.0 / counts, count_out.shape)
    base_out[...] = (
        jnp.dot(live_member, frames[...], preferred_element_type=jnp.float32) / counts
    )


def attend_kernel(span_len, right_len, head_size, starts_here, scalars, other_length, *refs):
    members, sources, pieces = refs[:2], refs[2:8], refs[8:16]
    out_refs, sums_out, projection = refs[16:18], refs[18:20], refs[20]
    outs, rows_in, weight, query, key, value, bias, scores, peaks, weights, sems = refs[21:]
    first_frame, core, y_half = scalars[0], scalars[2], scalars[3]
    frame_count, model_width = sources[0].shape
    half = model_width // 2
    width = out_refs[0].shape[1]
    out_copies = [
        pltpu.make_async_copy(outs.at[rec], out_refs[rec], sems.at[22 + rec]) for rec in range(2)
    ]
    heads = width // head_size
    block = 2 * span_len
    blocks = frame_count // block
    near = bias.shape[0]
    memory_at = frame_count + near - block
    row_count = rows_in.shape[0] // 2
    memory_count = row_count - memory_at
    lanes = heads * block

    def piece_copies(of_core, projected):
        places = (y_half * half, (1 - y_half) * half)
        copies = []
        for side in range(2):
            place = pl.ds(pl.multiple_of(places[side], half), half)
            for shard in range(2):
                piece = pieces[4 * shard + 2 * side + of_core]
                raw = starts_here and of_core == 0 and shard == 0
                shard_width = pieces[-1].shape[2]
                index = 2 * side + shard
                for part in (3,) if projected else (0, 1, 2):
                    target = projection if projected else weight
                    start = shard * shard_width + (0 if projected else part * width)
                    if raw:
                        source = pieces[2].at[place] if projected else pieces[0].at[part, place]
                    else:
                        source = piece.at[part]
                    copies.append(
                        pltpu.make_async_copy(
                            source,
                            target.at[place, pl.ds(start, shard_width)],
                            sems.at[4 * part + index],
                        )
                    )
        return copies

    row_copies = []
    for rec in range(2):
        at = rec * row_count
        for i, (start, size) in enumerate(
            ((0, frame_count), (frame_count, near - block), (memory_at, memory_count))
        ):
            row_copies.append(
                pltpu.make_async_copy(
                    sources[3 * rec + i], rows_in.at[pl.ds(at + start, size)], sems.at[16 + 3 * rec + i]
                )
            )

    for copy in row_copies:
        copy.start()
    for of_core in range(2):

        @pl.when(core == of_core)
        def _():
            for copy in piece_copies(of_core, False) + piece_copies(of_core, True):
                copy.start()

    rows = lax.broadcasted_iota(jnp.int32, (near, lanes), 0)
    spans = (lax.broadcasted_iota(jnp.int32, (near, lanes), 1) % block) // span_len
    same = (rows >= spans * span_len) & (rows < (spans + 1) * span_len + right_len)
    bias[...] = jnp.where(same, jnp.float32(0.0), jnp.float32(NEG_BIG))
    lane_spans = (lax.broadcasted_iota(jnp.int32, (1, lanes), 1) % block) // span_len
    memory_rows = lax.broadcasted_iota(jnp.int32, (memory_count, lanes), 0)
    feature_head = lax.broadcasted_iota(jnp.int32, (1, width), 1) // head_size
    head_masks = [(feature_head == h).astype(jnp.bfloat16) for h in range(heads)]
    scale = head_size ** (-0.5) * LOG2_E

    for copy in row_copies + piece_copies(1, False):
        copy.wait()
    mixed = jnp.dot(rows_in[...], weight[...], preferred_element_type=jnp.float32)
    query[...] = (mixed[:, :width] * scale).astype(jnp.bfloat16)
    key[...] = mixed[:, width : 2 * width].astype(jnp.bfloat16)
    value[...] = mixed[:, 2 * width :].astype(jnp.bfloat16)

    def score_block(i):
        rec, b = divmod(i, blocks)
        at, start = rec * row_count, b * block
        length = scalars[1] if rec == 0 else other_length[0]
        q_now = query[at + start : at + start + block]
        stacked = jnp.concatenate([q_now * m for m in head_masks], axis=0)
        keys = jnp.concatenate(
            [key[at + start : at + start + near], key[at + memory_at : at + row_count]], axis=0
        )
        raw = lax.dot_general(
            keys, stacked, (((1,), (1,)), ((), ())), preferred_element_type=jnp.float32
        )
        limit = length - first_frame - start
        local = jnp.where(rows < limit, raw[:near] + bias[...], NEG_BIG)
        live_spans = (length + span_len - 1) // span_len
        span_limit = jnp.minimum(first_frame // span_len + 2 * b + lane_spans, live_spans)
        memory = jnp.where(memory_rows < span_limit, raw[near:], NEG_BIG)
        slot = i % scores.shape[0]
        scores[slot, 0:near, :] = local
        scores[slot, near:, :] = memory
        peaks[slot] = jnp.maximum(
            jnp.max(local, axis=0, keepdims=True), jnp.max(memory, axis=0, keepdims=True)
        )

    def weigh_block(i):
        slot = i % scores.shape[0]
        weights[slot] = jnp.exp2(scores[slot] - peaks[slot]).astype(jnp.bfloat16)

    ones = jnp.ones((near + memory_count, LANES), jnp.bfloat16)
    first_of_pair = lax.broadcasted_iota(jnp.int32, (1, 2 * LANES), 1) % LANES < head_size

    def mix_block(i):
        rec, b = divmod(i, blocks)
        at, start = rec * row_count, b * block
        values = jnp.concatenate(
            [value[at + start : at + start + near], value[at + memory_at : at + row_count]], axis=0
        )
        for pair in range(width // LANES):
            columns = slice(pair * LANES, (pair + 1) * LANES)
            pair_rows = slice(pair * 2 * block, (pair + 1) * 2 * block)
            sums = lax.dot_general(
                weights[i % weights.shape[0], :, pair_rows],
                jnp.concatenate([values[:, columns], ones], axis=1),
                (((0,), (0,)), ((), ())),
                preferred_element_type=jnp.float32,
            )
            picked = jnp.where(first_of_pair, sums[:block], sums[block:])
            outs[rec, start : start + block, columns] = (
                picked[:, :LANES] / picked[:, LANES:]
            ).astype(jnp.bfloat16)

    count = 2 * blocks
    ring = scores.shape[0]
    for first in range(0, count, ring):
        for stage in (score_block, weigh_block, mix_block):
            for i in range(first, min(first + ring, count)):
                stage(i)
        for rec in range(2):
            if first < (rec + 1) * blocks <= first + ring:
                out_copies[rec].start()
    for rec in range(2):
        sums_out[rec][...] = jnp.dot(
            members[rec][...], outs[rec], preferred_element_type=jnp.float32
        )
    for copy in piece_copies(1, True) + out_copies:
        copy.wait()


def assemble(scalars, offsets_at, attended, gathered):
    shard = attended[0].shape[1] // 2
    offsets = [
        [pl.multiple_of(scalars[offsets_at + 2 * i + s], LANES) for s in range(2)]
        for i in range(4)
    ]
    for i in range(4):
        for s in range(2):
            gathered[:, pl.ds(offsets[i][s], shard)] = attended[i][:, s * shard : (s + 1) * shard]
    return offsets, shard


def pool_kernel(offsets_at, scalars, base, inverse, route, *refs):
    sums, projections = refs[:4], refs[4:8]
    sent_out, means, pooled = refs[8:]
    shard = sums[0].shape[1] // 2
    offsets = [
        [pl.multiple_of(scalars[offsets_at + 2 * i + s], LANES) for s in range(2)]
        for i in range(4)
    ]
    for i in range(4):
        for s in range(2):
            for lane in range(0, shard, LANES):
                means[:, pl.ds(offsets[i][s] + lane, LANES)] = (
                    sums[i][:, s * shard + lane : s * shard + lane + LANES] * inverse[...]
                ).astype(jnp.bfloat16)
    for i in range(4):
        mixed = jnp.dot(means[...], projections[i][...], preferred_element_type=jnp.float32)
        for s in range(2):
            columns = pl.ds(offsets[i][s], shard)
            pooled[:, columns] = (
                base[:, columns] + mixed[:, s * shard : (s + 1) * shard]
            ).astype(jnp.bfloat16)
    sent_out[...] = jnp.dot(
        route[...], pooled[...], preferred_element_type=jnp.float32
    ).astype(jnp.bfloat16)


def encode_kernel(offsets_at, scalars, *refs):
    attended, projections, frames = refs[:4], refs[4:8], refs[8]
    encoded_out, gathered = refs[9:]
    first_frame, length = scalars[0], scalars[1]
    frame_count, _ = frames.shape
    offsets, shard = assemble(scalars, offsets_at, attended, gathered)
    live = (
        first_frame + lax.broadcasted_iota(jnp.int32, (frame_count, 1), 0) < length
    ).astype(jnp.float32)
    for i in range(4):
        mixed = jnp.dot(
            gathered[...], projections[i][...], preferred_element_type=jnp.float32
        )
        for s in range(2):
            columns = pl.ds(offsets[i][s], shard)
            base = frames[:, columns].astype(jnp.float32)
            encoded_out[:, columns] = (
                (base + mixed[:, s * shard : (s + 1) * shard]) * live
            ).astype(jnp.bfloat16)


def language_kernel(places_at, scalars, received, *refs):
    pieces, out = refs[:-5], refs[-5]
    weights, product, sems, out_sems = refs[-4:]
    count, width = len(pieces), pieces[0].shape[1]
    copies = [
        pltpu.make_async_copy(piece, weights.at[i], sems.at[i]) for i, piece in enumerate(pieces)
    ]
    for copy in copies:
        copy.start()
    out_copies = []
    for i in range(count):
        copies[i].wait()
        product[i] = jnp.dot(
            received[...], weights[i], preferred_element_type=jnp.float32
        ).astype(jnp.bfloat16)
        place = pl.multiple_of(scalars[places_at + i], LANES)
        out_copies.append(
            pltpu.make_async_copy(product.at[i], out.at[:, pl.ds(place, width)], out_sems.at[i])
        )
        out_copies[-1].start()
    for copy in out_copies:
        copy.wait()


def along_x(r, j, _):
    return r, j ^ 1


def along_y(r, j, _):
    return r ^ 2, j


def other_core(r, j, _):
    return r ^ 1, j


def z_up(r, j, count):
    return r, (j + 2) % count


def z_down(r, j, count):
    return r, (j - 2) % count


def relocate(value, core_0, core_1):
    rec_count, time_count = lax.axis_size("rec"), lax.axis_size("tm")
    pairs = []
    for r in range(rec_count):
        for j in range(time_count):
            route = (core_0, core_1)[r % 2]
            if route is not None:
                to_r, to_j = route(r, j, time_count)
                pairs.append((r * time_count + j, to_r * time_count + to_j))
    return lax.ppermute(value, ("rec", "tm"), pairs)


def swap_cores(value):
    return relocate(value, other_core, other_core)


def exchange_blocks(blocks):
    return lax.all_to_all(blocks, "tm", split_axis=0, concat_axis=0, tiled=True)


def per_device(
    frames,
    lengths,
    norm_gain,
    memory_gain,
    qkv_weight,
    out_weight,
    segment_ids,
    owners,
    language_weight,
):
    local_frames = frames[0]
    frame_count, model_width = local_frames.shape
    shard = out_weight.shape[1]
    half = model_width // 2
    time_count = lax.axis_size("tm")
    rec_count = lax.axis_size("rec")
    rec, time = lax.axis_index("rec"), lax.axis_index("tm")
    core, y_half = rec % 2, (rec // 2) % 2
    x, z = time % 2, time // 2
    z_count = time_count // 2
    first_frame = time * frame_count
    length = lengths[0]
    head_size = model_width // H
    bf16 = jnp.bfloat16

    own = jnp.concatenate([qkv_weight, out_weight[None]], axis=0)
    own_a = lax.dynamic_slice_in_dim(own, y_half * half, half, 1)

    def pick(for_core_0, for_core_1):
        return jnp.where(core == 0, for_core_0, for_core_1)

    token_count = owners.shape[2]
    slot_count = 2 * token_count
    capacity = slot_count // time_count
    language_shard = language_weight.shape[1]

    def group_of(of_core, slot):
        return jnp.where(of_core == 0, z + slot, z - slot - 1) % z_count

    numbers = [first_frame, length, core, y_half, capacity]
    offsets_at = len(numbers)
    for of_core in (core, 1 - core):
        for slot in range(2):
            group = group_of(of_core, slot)
            numbers += [(2 * group + x) * shard, (2 * group + 1 - x) * shard]
    places_at = len(numbers)
    numbers += [(rec ^ i) * language_shard for i in range(rec_count)]
    scalars = jnp.stack(numbers).astype(jnp.int32)

    m1 = relocate(own_a, along_x, z_up)
    m2 = relocate(own_a, z_down, None)
    l1 = relocate(language_weight, along_y, along_y)

    pad = 2 * RC
    normed, start_rows, memory = local_call(
        functools.partial(normalise_kernel, C),
        (
            shape_of(frame_count, model_width),
            shape_of(pad, model_width),
            shape_of(time_count, frame_count // C, model_width),
        ),
        (scalars,),
        (local_frames, norm_gain[None], memory_gain[None]),
        flops=10 * frame_count * model_width,
        moved=4 * frame_count * model_width,
    )
    other_length = swap_cores(lengths)
    other_normed = swap_cores(normed)
    ahead = shifted(start_rows, "tm", -1)
    memories = exchange_blocks(memory).reshape(-1, model_width)
    owners_col = owners[0, 0]
    base, member, inverse, route = local_call(
        prepare_kernel,
        (
            shape_of(token_count, model_width, dtype=jnp.float32),
            shape_of(token_count, frame_count),
            shape_of(token_count, LANES, dtype=jnp.float32),
            shape_of(slot_count, token_count),
        ),
        (scalars,),
        (local_frames, segment_ids[0], owners_col.reshape(1, token_count), owners_col),
        flops=2 * token_count * frame_count * model_width,
        moved=2 * frame_count * model_width,
    )
    other_member = swap_cores(member)
    other_ahead = swap_cores(ahead)
    other_memories = swap_cores(memories)

    m3 = relocate(m1, along_y, along_x)
    m4 = relocate(m1, None, z_up)
    m5 = relocate(pick(m2, m1), along_x, along_y)
    m6 = relocate(m3, None, along_y)
    m7 = relocate(pick(m2, m5), along_y, z_up)
    m8 = relocate(pick(m5, m4), along_y, along_x)
    m9 = relocate(m7, None, along_x)

    slot_pieces = (
        ((qkv_weight, m1), (out_weight, m5), (m1, m3), (m3, m6)),
        ((m2, m4), (m7, m7), (m5, m8), (m8, m9)),
    )
    block = 2 * C
    width = 2 * shard
    row_count = frame_count + pad + memories.shape[0]
    keys_seen = block + pad + memories.shape[0]
    lanes = width // head_size * block
    attended, sums, outs = [], [], []
    for slot, pieces in enumerate(slot_pieces):
        flat = [p for pair in pieces for p in pair]
        *results, out_piece = local_call(
            functools.partial(attend_kernel, C, RC, head_size, slot == 0),
            (
                shape_of(frame_count, width),
                shape_of(frame_count, width),
                shape_of(token_count, width, dtype=jnp.float32),
                shape_of(token_count, width, dtype=jnp.float32),
                shape_of(model_width, width),
            ),
            (scalars, other_length),
            (member, other_member, normed, ahead, memories, other_normed, other_ahead, other_memories, *flat),
            in_place=6 + len(flat),
            out_in_place=(True, True, False, False, False),
            scratch=(
                pltpu.VMEM((2, frame_count, width), bf16),
                pltpu.VMEM((2 * row_count, model_width), bf16),
                pltpu.VMEM((model_width, 3 * width), bf16),
                pltpu.VMEM((2 * row_count, width), bf16),
                pltpu.VMEM((2 * row_count, width), bf16),
                pltpu.VMEM((2 * row_count, width), bf16),
                pltpu.VMEM((block + pad, lanes), jnp.float32),
                pltpu.VMEM((RING, keys_seen, lanes), jnp.float32),
                pltpu.VMEM((RING, 1, lanes), jnp.float32),
                pltpu.VMEM((RING, keys_seen, lanes), bf16),
                pltpu.SemaphoreType.DMA((24,)),
            ),
            vmem_mib=24,
            flops=12 * frame_count * model_width * width,
            moved=8 * frame_count * model_width,
        )
        attended.append(results[:2])
        sums.append(results[2:])
        outs.append(out_piece)
    other_outs = [swap_cores(w) for w in outs]
    other_attended = [swap_cores(for_other) for _, for_other in attended]

    other_sums = [swap_cores(for_other) for _, for_other in sums]
    projections = (*outs, *other_outs)
    features = (attended[0][0], attended[1][0], *other_attended, *projections)
    sent_rows = local_call(
        functools.partial(pool_kernel, offsets_at),
        shape_of(slot_count, model_width),
        (scalars,),
        (base, inverse, route, sums[0][0], sums[1][0], *other_sums, *projections),
        scratch=(
            pltpu.VMEM((token_count, model_width), bf16),
            pltpu.VMEM((token_count, model_width), bf16),
        ),
        flops=4 * token_count * model_width * model_width,
        moved=6 * frame_count * model_width,
    )
    received = exchange_blocks(
        sent_rows.reshape(time_count, capacity, model_width)
    ).reshape(slot_count, model_width)
    encoded = local_call(
        functools.partial(encode_kernel, offsets_at),
        shape_of(frame_count, model_width),
        (scalars,),
        (*features, local_frames),
        scratch=(pltpu.VMEM((frame_count, model_width), bf16),),
        flops=2 * frame_count * model_width * model_width,
        moved=6 * frame_count * model_width,
    )
    language_pieces = (language_weight, swap_cores(language_weight), l1, swap_cores(l1))
    lm_out = local_call(
        functools.partial(language_kernel, places_at),
        shape_of(slot_count, rec_count * language_shard),
        (scalars,),
        (received, *language_pieces),
        in_place=rec_count,
        out_in_place=True,
        vmem_mib=63,
        scratch=(
            pltpu.VMEM((rec_count, model_width, language_shard), bf16),
            pltpu.VMEM((rec_count, slot_count, language_shard), bf16),
            pltpu.SemaphoreType.DMA((rec_count,)),
            pltpu.SemaphoreType.DMA((rec_count,)),
        ),
        flops=2 * slot_count * model_width * rec_count * language_shard,
        moved=2 * model_width * rec_count * language_shard,
    )
    return (encoded[None], lm_out[None, None])


def solution(mesh):
    in_specs = (
        P("rec", "tm", None),
        P("rec"),
        P(),
        P(),
        P(None, None, "tm"),
        P(None, "tm"),
        P("rec", "tm", None),
        P("rec", "tm", None, None),
        P(None, "rec"),
    )
    out_specs = (P("rec", "tm", None), P("rec", "tm", None, None))
    rec_count, time_count = mesh.shape["rec"], mesh.shape["tm"]
    paired = shard_map_of(mesh, in_specs, out_specs, per_device)
    plain = shard_map_of(mesh, in_specs, out_specs, plain_device)

    def run(*arrays):
        shard = arrays[5].shape[1] // time_count
        fits = rec_count == 4 and time_count == 8 and shard % LANES == 0
        return (paired if fits else plain)(*arrays)

    return run


def shard_map_of(mesh, in_specs, out_specs, body):
    return jax.shard_map(
        body, mesh=mesh, in_specs=in_specs, out_specs=out_specs, check_vma=False
    )
```

```python
import functools

import jax
import jax.numpy as jnp
from jax import lax
from jax.experimental import pallas as pl
from jax.experimental.pallas import tpu as pltpu
from jax.sharding import PartitionSpec as P


H = 16
C = 32
RC = 8


EPS_NORM = 1e-05
EPS_MEMORY = 1e-06
NEG_BIG = -1e30
LANES = 128
RING = 16
LOG2_E = 1.4426950408889634


def shifted(block, axis, distance):
    devices = range(lax.axis_size(axis))
    route = [(i - distance, i) for i in devices if i - distance in devices]
    return lax.ppermute(block, axis, route)


def layer_norm(values_in, gain):
    values_in = values_in.astype(jnp.float32)
    centre = jnp.mean(values_in, axis=-1, keepdims=True)
    centred = values_in - centre
    spread = jnp.mean(centred * centred, axis=-1, keepdims=True)
    return centred * lax.rsqrt(spread + EPS_NORM) * gain


def span_memory(normed, live_mask, gain, span_len):
    model_width = normed.shape[1]
    masked = jnp.where(live_mask[:, None], normed.astype(jnp.float32), jnp.float32(0.0))
    owner_sums = masked.reshape(-1, span_len, model_width).sum(axis=1)
    counts = live_mask.reshape(-1, span_len).astype(jnp.float32).sum(axis=1)
    means = owner_sums / jnp.maximum(counts, 1.0)[:, None]
    power = jnp.mean(means * means, axis=-1, keepdims=True)
    return (means * lax.rsqrt(power + EPS_MEMORY) * gain).astype(jnp.bfloat16)


def block_size():
    return 256


def local_part(query, keys, values, first_frame, length, head_count, span_len, right_len):
    frame_count, model_width = query.shape
    head_size = model_width // head_count
    group_rows = 4 * span_len
    group_count = frame_count // group_rows
    block_rows = block_size()
    query_blocks = query.reshape(group_count, group_rows, head_count, head_size)
    key_blocks = keys[:frame_count].reshape(group_count, group_rows, head_count, head_size)
    value_blocks = values[:frame_count].reshape(group_count, group_rows, head_count, head_size)
    key_tail = keys[frame_count:].reshape(1, right_len, head_count, head_size)
    value_tail = values[frame_count:].reshape(1, right_len, head_count, head_size)
    key_all = jnp.concatenate(
        [key_blocks, jnp.concatenate([key_blocks[1:, :right_len], key_tail], axis=0)], axis=1
    )
    value_all = jnp.concatenate(
        [value_blocks, jnp.concatenate([value_blocks[1:, :right_len], value_tail], axis=0)], axis=1
    )
    start_offsets = jnp.arange(group_count, dtype=jnp.int32)[:, None] * group_rows
    query_pos = first_frame + start_offsets + jnp.arange(group_rows, dtype=jnp.int32)[None, :]
    key_pos = first_frame + jnp.concatenate(
        [
            start_offsets + jnp.arange(group_rows, dtype=jnp.int32)[None, :],
            start_offsets + group_rows + jnp.arange(right_len, dtype=jnp.int32)[None, :],
        ],
        axis=1,
    )
    query_span = query_pos // span_len
    span_end = (query_span + 1) * span_len
    same = (key_pos // span_len)[:, None, :] == query_span[:, :, None]
    ahead = (key_pos[:, None, :] >= span_end[:, :, None]) & (
        key_pos[:, None, :] < span_end[:, :, None] + right_len
    )
    allowed = (same | ahead) & (key_pos < length)[:, None, :]
    scores = jnp.einsum(
        "gqhd,gkhd->ghqk", query_blocks, key_all, preferred_element_type=jnp.float32
    ) * head_size ** (-0.5)
    scores = jnp.where(allowed[:, None], scores, NEG_BIG)
    row_peak = jnp.max(scores, axis=-1)
    weights = jnp.where(allowed[:, None], jnp.exp(scores - row_peak[..., None]), jnp.float32(0.0))
    row_total = jnp.sum(weights, axis=-1)
    accum = jnp.einsum(
        "ghqk,gkhd->ghqd",
        weights.astype(jnp.bfloat16),
        value_all,
        preferred_element_type=jnp.float32,
    )
    block_count = frame_count // block_rows
    row_peak = (
        row_peak.transpose(1, 0, 2).reshape(head_count, block_count, block_rows).transpose(1, 0, 2)
    )
    row_total = (
        row_total.transpose(1, 0, 2).reshape(head_count, block_count, block_rows).transpose(1, 0, 2)
    )
    accum = (
        accum.transpose(1, 0, 2, 3)
        .reshape(head_count, block_count, block_rows, head_size)
        .transpose(1, 0, 2, 3)
    )
    return (row_peak, row_total, accum)


def memory_update(
    carry, memory_keys, memory_values, query, first_frame, length, head_count, span_len
):
    row_peak, row_total, accum = carry
    block_count, _, block_rows = row_peak.shape
    row_count, model_width = memory_keys.shape
    head_size = model_width // head_count
    mem_keys = memory_keys.reshape(row_count, head_count, head_size)
    mem_values = memory_values.reshape(row_count, head_count, head_size)
    mem_index = jnp.arange(row_count, dtype=jnp.int32)
    mem_live = mem_index * span_len < length
    query_blocks = query.reshape(block_count, block_rows, head_count, head_size)
    positions = first_frame + jnp.arange(block_count * block_rows, dtype=jnp.int32).reshape(
        block_count, block_rows
    )

    def one_block(packed):
        query_now, pos_now, peak_now, total_now, accum_now = packed
        scores = jnp.einsum(
            "qhd,khd->hqk", query_now, mem_keys, preferred_element_type=jnp.float32
        ) * head_size ** (-0.5)
        allowed = (mem_index[None, :] < (pos_now // span_len)[:, None]) & mem_live[None, :]
        scores = jnp.where(allowed[None], scores, NEG_BIG)
        new_peak = jnp.maximum(peak_now, jnp.max(scores, axis=-1))
        weights = jnp.where(allowed[None], jnp.exp(scores - new_peak[..., None]), jnp.float32(0.0))
        factor = jnp.exp(peak_now - new_peak)
        total_next = total_now * factor + jnp.sum(weights, axis=-1)
        accum_next = accum_now * factor[..., None] + jnp.einsum(
            "hqk,khd->hqd",
            weights.astype(jnp.bfloat16),
            mem_values,
            preferred_element_type=jnp.float32,
        )
        return (new_peak, total_next, accum_next)

    return lax.map(one_block, (query_blocks, positions, row_peak, row_total, accum))


def finish(carry, frame_count, model_width):
    _, row_total, accum = carry
    result = accum / row_total[..., None]
    return result.transpose(0, 2, 1, 3).reshape(frame_count, model_width).astype(jnp.bfloat16)


def dispatch_matrix(owner_ids, owner_count, capacity):
    choose = (owner_ids[:, None] == jnp.arange(owner_count, dtype=jnp.int32)[None, :]).astype(
        jnp.int32
    )
    before = jnp.cumsum(choose, axis=0) - choose
    slot_index = jnp.sum(before * choose, axis=1)
    target = owner_ids * capacity + slot_index
    slot_rows = jnp.arange(owner_count * capacity, dtype=jnp.int32)
    return (slot_rows[:, None] == target[None, :]).astype(jnp.bfloat16)


def plain_device(
    frames,
    lengths,
    norm_gain,
    memory_gain,
    qkv_weight,
    out_weight,
    segment_ids,
    owners,
    language_weight,
):
    local_frames = frames[0]
    frame_count, model_width = local_frames.shape
    head_count = H
    time_count = lax.axis_size("tm")
    first_frame = lax.axis_index("tm") * frame_count
    length = lengths[0]
    live_mask = first_frame + jnp.arange(frame_count, dtype=jnp.int32) < length
    right_frames = shifted(local_frames[:RC], "tm", -1)
    normed = layer_norm(local_frames, norm_gain).astype(jnp.bfloat16)
    normed_right = layer_norm(right_frames, norm_gain).astype(jnp.bfloat16)
    memory = span_memory(normed, live_mask, memory_gain, C)
    stacked_rows = jnp.concatenate([normed, normed_right, memory], axis=0)
    projected = jnp.einsum(
        "fd,kdw->kfw",
        stacked_rows,
        lax.all_gather(qkv_weight, "tm", axis=2, tiled=True),
        preferred_element_type=jnp.float32,
    ).astype(jnp.bfloat16)
    split_at = frame_count + RC
    query = projected[0, :frame_count]
    keys = projected[1, :split_at]
    values = projected[2, :split_at]
    memory_keys = projected[1, split_at:]
    memory_values = projected[2, split_at:]
    carry = local_part(query, keys, values, first_frame, length, head_count, C, RC)
    carry = memory_update(
        carry,
        lax.all_gather(memory_keys, "tm", axis=0, tiled=True),
        lax.all_gather(memory_values, "tm", axis=0, tiled=True),
        query,
        first_frame,
        length,
        head_count,
        C,
    )
    attended = finish(carry, frame_count, model_width)
    output_proj = jnp.dot(
        attended,
        lax.all_gather(out_weight, "tm", axis=1, tiled=True),
        preferred_element_type=jnp.float32,
    )
    encoded = jnp.where(
        live_mask[:, None], local_frames.astype(jnp.float32) + output_proj, jnp.float32(0.0)
    ).astype(jnp.bfloat16)
    token_count = owners.shape[2]
    segments = segment_ids[0, 0]
    owner_indicator = (
        segments[None, :] == jnp.arange(token_count, dtype=jnp.int32)[:, None]
    ).astype(jnp.bfloat16)
    owner_sums = jnp.dot(owner_indicator, encoded, preferred_element_type=jnp.float32)
    counts = jnp.sum(owner_indicator.astype(jnp.float32), axis=1)
    pooled_rows = (owner_sums / counts[:, None]).astype(jnp.bfloat16)
    slot_count = 2 * token_count
    capacity = slot_count // time_count
    route_matrix = dispatch_matrix(owners[0, 0, :, 0], time_count, capacity)
    sent_rows = jnp.dot(route_matrix, pooled_rows, preferred_element_type=jnp.float32).astype(
        jnp.bfloat16
    )
    received = lax.all_to_all(
        sent_rows.reshape(time_count, capacity, model_width),
        "tm",
        split_axis=0,
        concat_axis=0,
        tiled=True,
    )
    received = received.reshape(slot_count, model_width)
    lm_out = jnp.dot(
        received,
        lax.all_gather(language_weight, "rec", axis=1, tiled=True),
        preferred_element_type=jnp.float32,
    ).astype(jnp.bfloat16)
    return (encoded[None], lm_out[None, None])


def vmem_spec():
    return pl.BlockSpec(memory_space=pltpu.VMEM)


def smem_spec():
    return pl.BlockSpec(memory_space=pltpu.SMEM)


def local_call(kernel, out_shapes, scalars, operands, scratch=(), in_place=0, out_in_place=False, vmem_mib=16, flops=0, moved=0):
    whole = len(operands) - in_place
    anywhere = pl.BlockSpec(memory_space=pl.ANY)
    if isinstance(out_shapes, tuple):
        stays = out_in_place or (False,) * len(out_shapes)
        out_specs = tuple(anywhere if stay else vmem_spec() for stay in stays)
    else:
        out_specs = anywhere if out_in_place else vmem_spec()
    return pl.pallas_call(
        kernel,
        out_shape=out_shapes,
        in_specs=[smem_spec()] * len(scalars) + [vmem_spec()] * whole + [anywhere] * in_place,
        out_specs=out_specs,
        compiler_params=pltpu.CompilerParams(vmem_limit_bytes=vmem_mib << 20),
        scratch_shapes=list(scratch),
        cost_estimate=pl.CostEstimate(flops=flops, bytes_accessed=moved, transcendentals=0),
    )(*scalars, *operands)


def shape_of(*dims, dtype=jnp.bfloat16):
    return jax.ShapeDtypeStruct(dims, dtype)


def normalise_kernel(
    span_len, scalars, frames, gain, memory_gain, normed_out, ahead_out, memory_out
):
    first_frame, length = scalars[0], scalars[1]
    frame_count, _ = frames.shape
    span_count = frame_count // span_len
    values = frames[...].astype(jnp.float32)
    centre = jnp.mean(values, axis=-1, keepdims=True)
    centred = values - centre
    spread = jnp.mean(centred * centred, axis=-1, keepdims=True)
    normed = (centred * lax.rsqrt(spread + EPS_NORM) * gain[...]).astype(jnp.bfloat16)
    normed_out[...] = normed
    ahead_out[...] = normed[: ahead_out.shape[0]]
    spans = lax.broadcasted_iota(jnp.int32, (span_count, frame_count), 0)
    places = lax.broadcasted_iota(jnp.int32, (span_count, frame_count), 1)
    member = (places >= spans * span_len) & (places < (spans + 1) * span_len)
    member = member & (places < length - first_frame)
    sums = jnp.dot(
        member.astype(jnp.bfloat16), normed, preferred_element_type=jnp.float32
    )
    counts = jnp.sum(member.astype(jnp.float32), axis=-1, keepdims=True)
    means = sums / jnp.maximum(counts, 1.0)
    power = jnp.mean(means * means, axis=-1, keepdims=True)
    memory = (means * lax.rsqrt(power + EPS_MEMORY) * memory_gain[...]).astype(jnp.bfloat16)
    for copy in range(memory_out.shape[0]):
        memory_out[copy] = memory


def prepare_kernel(scalars, frames, segments, owners_row, owners_col, base_out, member_out, count_out, route_out):
    first_frame, length, capacity = scalars[0], scalars[1], scalars[4]
    token_count, frame_count = member_out.shape
    tokens = lax.broadcasted_iota(jnp.int32, (token_count, frame_count), 0)
    places = first_frame + lax.broadcasted_iota(jnp.int32, (token_count, frame_count), 1)
    member = (segments[...] == tokens).astype(jnp.float32)
    counts = jnp.sum(member, axis=1, keepdims=True)
    live_member = jnp.where(places < length, member, 0.0).astype(jnp.bfloat16)
    earlier = lax.broadcasted_iota(jnp.int32, (token_count, token_count), 0)
    later = lax.broadcasted_iota(jnp.int32, (token_count, token_count), 1)
    clash = (owners_col[...] == owners_row[...]) & (earlier < later)
    slot = jnp.sum(clash.astype(jnp.int32), axis=0, keepdims=True)
    target = owners_row[...] * capacity + slot
    slots = lax.broadcasted_iota(jnp.int32, route_out.shape, 0)
    route_out[...] = (slots == target).astype(jnp.bfloat16)
    member_out[...] = live_member
    count_out[...] = jnp.broadcast_to(1.0 / counts, count_out.shape)
    base_out[...] = (
        jnp.dot(live_member, frames[...], preferred_element_type=jnp.float32) / counts
    )


def attend_kernel(span_len, right_len, head_size, starts_here, scalars, other_length, *refs):
    members, sources, pieces = refs[:2], refs[2:8], refs[8:16]
    out_refs, sums_out, projection = refs[16:18], refs[18:20], refs[20]
    outs, rows_in, weight, query, key, value, bias, scores, peaks, weights, sems = refs[21:]
    first_frame, core, y_half = scalars[0], scalars[2], scalars[3]
    frame_count, model_width = sources[0].shape
    half = model_width // 2
    width = out_refs[0].shape[1]
    out_copies = [
        pltpu.make_async_copy(outs.at[rec], out_refs[rec], sems.at[22 + rec]) for rec in range(2)
    ]
    heads = width // head_size
    block = 2 * span_len
    blocks = frame_count // block
    near = bias.shape[0]
    memory_at = frame_count + near - block
    row_count = rows_in.shape[0] // 2
    memory_count = row_count - memory_at
    lanes = heads * block

    def piece_copies(of_core, projected):
        places = (y_half * half, (1 - y_half) * half)
        copies = []
        for side in range(2):
            place = pl.ds(pl.multiple_of(places[side], half), half)
            for shard in range(2):
                piece = pieces[4 * shard + 2 * side + of_core]
                raw = starts_here and of_core == 0 and shard == 0
                shard_width = pieces[-1].shape[2]
                index = 2 * side + shard
                for part in (3,) if projected else (0, 1, 2):
                    target = projection if projected else weight
                    start = shard * shard_width + (0 if projected else part * width)
                    if raw:
                        source = pieces[2].at[place] if projected else pieces[0].at[part, place]
                    else:
                        source = piece.at[part]
                    copies.append(
                        pltpu.make_async_copy(
                            source,
                            target.at[place, pl.ds(start, shard_width)],
                            sems.at[4 * part + index],
                        )
                    )
        return copies

    row_copies = []
    for rec in range(2):
        at = rec * row_count
        for i, (start, size) in enumerate(
            ((0, frame_count), (frame_count, near - block), (memory_at, memory_count))
        ):
            row_copies.append(
                pltpu.make_async_copy(
                    sources[3 * rec + i], rows_in.at[pl.ds(at + start, size)], sems.at[16 + 3 * rec + i]
                )
            )

    for copy in row_copies:
        copy.start()
    for of_core in range(2):

        @pl.when(core == of_core)
        def _():
            for copy in piece_copies(of_core, False) + piece_copies(of_core, True):
                copy.start()

    rows = lax.broadcasted_iota(jnp.int32, (near, lanes), 0)
    spans = (lax.broadcasted_iota(jnp.int32, (near, lanes), 1) % block) // span_len
    same = (rows >= spans * span_len) & (rows < (spans + 1) * span_len + right_len)
    bias[...] = jnp.where(same, jnp.float32(0.0), jnp.float32(NEG_BIG))
    lane_spans = (lax.broadcasted_iota(jnp.int32, (1, lanes), 1) % block) // span_len
    memory_rows = lax.broadcasted_iota(jnp.int32, (memory_count, lanes), 0)
    feature_head = lax.broadcasted_iota(jnp.int32, (1, width), 1) // head_size
    head_masks = [(feature_head == h).astype(jnp.bfloat16) for h in range(heads)]
    scale = head_size ** (-0.5) * LOG2_E

    for copy in row_copies + piece_copies(1, False):
        copy.wait()
    mixed = jnp.dot(rows_in[...], weight[...], preferred_element_type=jnp.float32)
    query[...] = (mixed[:, :width] * scale).astype(jnp.bfloat16)
    key[...] = mixed[:, width : 2 * width].astype(jnp.bfloat16)
    value[...] = mixed[:, 2 * width :].astype(jnp.bfloat16)

    def score_block(i):
        rec, b = divmod(i, blocks)
        at, start = rec * row_count, b * block
        length = scalars[1] if rec == 0 else other_length[0]
        q_now = query[at + start : at + start + block]
        stacked = jnp.concatenate([q_now * m for m in head_masks], axis=0)
        keys = jnp.concatenate(
            [key[at + start : at + start + near], key[at + memory_at : at + row_count]], axis=0
        )
        raw = lax.dot_general(
            keys, stacked, (((1,), (1,)), ((), ())), preferred_element_type=jnp.float32
        )
        limit = length - first_frame - start
        local = jnp.where(rows < limit, raw[:near] + bias[...], NEG_BIG)
        live_spans = (length + span_len - 1) // span_len
        span_limit = jnp.minimum(first_frame // span_len + 2 * b + lane_spans, live_spans)
        memory = jnp.where(memory_rows < span_limit, raw[near:], NEG_BIG)
        slot = i % scores.shape[0]
        scores[slot, 0:near, :] = local
        scores[slot, near:, :] = memory
        peaks[slot] = jnp.maximum(
            jnp.max(local, axis=0, keepdims=True), jnp.max(memory, axis=0, keepdims=True)
        )

    def weigh_block(i):
        slot = i % scores.shape[0]
        weights[slot] = jnp.exp2(scores[slot] - peaks[slot]).astype(jnp.bfloat16)

    ones = jnp.ones((near + memory_count, LANES), jnp.bfloat16)
    first_of_pair = lax.broadcasted_iota(jnp.int32, (1, 2 * LANES), 1) % LANES < head_size

    def mix_block(i):
        rec, b = divmod(i, blocks)
        at, start = rec * row_count, b * block
        values = jnp.concatenate(
            [value[at + start : at + start + near], value[at + memory_at : at + row_count]], axis=0
        )
        for pair in range(width // LANES):
            columns = slice(pair * LANES, (pair + 1) * LANES)
            pair_rows = slice(pair * 2 * block, (pair + 1) * 2 * block)
            sums = lax.dot_general(
                weights[i % weights.shape[0], :, pair_rows],
                jnp.concatenate([values[:, columns], ones], axis=1),
                (((0,), (0,)), ((), ())),
                preferred_element_type=jnp.float32,
            )
            picked = jnp.where(first_of_pair, sums[:block], sums[block:])
            outs[rec, start : start + block, columns] = (
                picked[:, :LANES] / picked[:, LANES:]
            ).astype(jnp.bfloat16)

    count = 2 * blocks
    ring = scores.shape[0]
    for first in range(0, count, ring):
        for stage in (score_block, weigh_block, mix_block):
            for i in range(first, min(first + ring, count)):
                stage(i)
        for rec in range(2):
            if first < (rec + 1) * blocks <= first + ring:
                out_copies[rec].start()
    for rec in range(2):
        sums_out[rec][...] = jnp.dot(
            members[rec][...], outs[rec], preferred_element_type=jnp.float32
        )
    for copy in piece_copies(1, True) + out_copies:
        copy.wait()


def assemble(scalars, offsets_at, attended, gathered):
    shard = attended[0].shape[1] // 2
    offsets = [
        [pl.multiple_of(scalars[offsets_at + 2 * i + s], LANES) for s in range(2)]
        for i in range(4)
    ]
    for i in range(4):
        for s in range(2):
            gathered[:, pl.ds(offsets[i][s], shard)] = attended[i][:, s * shard : (s + 1) * shard]
    return offsets, shard


def pool_kernel(offsets_at, scalars, base, inverse, route, *refs):
    sums, projections = refs[:4], refs[4:8]
    sent_out, means, pooled = refs[8:]
    shard = sums[0].shape[1] // 2
    offsets = [
        [pl.multiple_of(scalars[offsets_at + 2 * i + s], LANES) for s in range(2)]
        for i in range(4)
    ]
    for i in range(4):
        for s in range(2):
            for lane in range(0, shard, LANES):
                means[:, pl.ds(offsets[i][s] + lane, LANES)] = (
                    sums[i][:, s * shard + lane : s * shard + lane + LANES] * inverse[...]
                ).astype(jnp.bfloat16)
    for i in range(4):
        mixed = jnp.dot(means[...], projections[i][...], preferred_element_type=jnp.float32)
        for s in range(2):
            columns = pl.ds(offsets[i][s], shard)
            pooled[:, columns] = (
                base[:, columns] + mixed[:, s * shard : (s + 1) * shard]
            ).astype(jnp.bfloat16)
    sent_out[...] = jnp.dot(
        route[...], pooled[...], preferred_element_type=jnp.float32
    ).astype(jnp.bfloat16)


def encode_kernel(offsets_at, scalars, *refs):
    attended, projections, frames = refs[:4], refs[4:8], refs[8]
    encoded_out, gathered = refs[9:]
    first_frame, length = scalars[0], scalars[1]
    frame_count, _ = frames.shape
    offsets, shard = assemble(scalars, offsets_at, attended, gathered)
    live = (
        first_frame + lax.broadcasted_iota(jnp.int32, (frame_count, 1), 0) < length
    ).astype(jnp.float32)
    for i in range(4):
        mixed = jnp.dot(
            gathered[...], projections[i][...], preferred_element_type=jnp.float32
        )
        for s in range(2):
            columns = pl.ds(offsets[i][s], shard)
            base = frames[:, columns].astype(jnp.float32)
            encoded_out[:, columns] = (
                (base + mixed[:, s * shard : (s + 1) * shard]) * live
            ).astype(jnp.bfloat16)


def language_kernel(places_at, scalars, received, *refs):
    pieces, out = refs[:-5], refs[-5]
    weights, product, sems, out_sems = refs[-4:]
    count, width = len(pieces), pieces[0].shape[1]
    copies = [
        pltpu.make_async_copy(piece, weights.at[i], sems.at[i]) for i, piece in enumerate(pieces)
    ]
    for copy in copies:
        copy.start()
    out_copies = []
    for i in range(count):
        copies[i].wait()
        product[i] = jnp.dot(
            received[...], weights[i], preferred_element_type=jnp.float32
        ).astype(jnp.bfloat16)
        place = pl.multiple_of(scalars[places_at + i], LANES)
        out_copies.append(
            pltpu.make_async_copy(product.at[i], out.at[:, pl.ds(place, width)], out_sems.at[i])
        )
        out_copies[-1].start()
    for copy in out_copies:
        copy.wait()


def along_x(r, j, _):
    return r, j ^ 1


def along_y(r, j, _):
    return r ^ 2, j


def other_core(r, j, _):
    return r ^ 1, j


def z_up(r, j, count):
    return r, (j + 2) % count


def z_down(r, j, count):
    return r, (j - 2) % count


def relocate(value, core_0, core_1):
    rec_count, time_count = lax.axis_size("rec"), lax.axis_size("tm")
    pairs = []
    for r in range(rec_count):
        for j in range(time_count):
            route = (core_0, core_1)[r % 2]
            if route is not None:
                to_r, to_j = route(r, j, time_count)
                pairs.append((r * time_count + j, to_r * time_count + to_j))
    return lax.ppermute(value, ("rec", "tm"), pairs)


def swap_cores(value):
    return relocate(value, other_core, other_core)


def exchange_blocks(blocks):
    return lax.all_to_all(blocks, "tm", split_axis=0, concat_axis=0, tiled=True)


def per_device(
    frames,
    lengths,
    norm_gain,
    memory_gain,
    qkv_weight,
    out_weight,
    segment_ids,
    owners,
    language_weight,
):
    local_frames = frames[0]
    frame_count, model_width = local_frames.shape
    shard = out_weight.shape[1]
    half = model_width // 2
    time_count = lax.axis_size("tm")
    rec_count = lax.axis_size("rec")
    rec, time = lax.axis_index("rec"), lax.axis_index("tm")
    core, y_half = rec % 2, (rec // 2) % 2
    x, z = time % 2, time // 2
    z_count = time_count // 2
    first_frame = time * frame_count
    length = lengths[0]
    head_size = model_width // H
    bf16 = jnp.bfloat16

    own = jnp.concatenate([qkv_weight, out_weight[None]], axis=0)
    own_a = lax.dynamic_slice_in_dim(own, y_half * half, half, 1)
    later_qkv, later_out, own_a = lax.optimization_barrier((qkv_weight, out_weight, own_a))
    later = jnp.concatenate([later_qkv, later_out[None]], axis=0)
    own_b = lax.dynamic_slice_in_dim(later, (1 - y_half) * half, half, 1)

    def pick(for_core_0, for_core_1):
        return jnp.where(core == 0, for_core_0, for_core_1)

    token_count = owners.shape[2]
    slot_count = 2 * token_count
    capacity = slot_count // time_count
    language_shard = language_weight.shape[1]

    def group_of(of_core, slot):
        return jnp.where(of_core == 0, z + slot, z - slot - 1) % z_count

    numbers = [first_frame, length, core, y_half, capacity]
    offsets_at = len(numbers)
    for of_core in (core, 1 - core):
        for slot in range(2):
            group = group_of(of_core, slot)
            numbers += [(2 * group + x) * shard, (2 * group + 1 - x) * shard]
    places_at = len(numbers)
    numbers += [(rec ^ i) * language_shard for i in range(rec_count)]
    scalars = jnp.stack(numbers).astype(jnp.int32)

    m1 = relocate(own_a, along_x, z_up)
    m2 = relocate(pick(own_a, own_b), z_down, z_up)
    l1 = relocate(language_weight, along_y, along_y)

    pad = 2 * RC
    normed, start_rows, memory = local_call(
        functools.partial(normalise_kernel, C),
        (
            shape_of(frame_count, model_width),
            shape_of(pad, model_width),
            shape_of(time_count, frame_count // C, model_width),
        ),
        (scalars,),
        (local_frames, norm_gain[None], memory_gain[None]),
        flops=10 * frame_count * model_width,
        moved=4 * frame_count * model_width,
    )
    other_length = swap_cores(lengths)
    other_normed = swap_cores(normed)
    ahead = shifted(start_rows, "tm", -1)
    memories = exchange_blocks(memory).reshape(-1, model_width)
    owners_col = owners[0, 0]
    base, member, inverse, route = local_call(
        prepare_kernel,
        (
            shape_of(token_count, model_width, dtype=jnp.float32),
            shape_of(token_count, frame_count),
            shape_of(token_count, LANES, dtype=jnp.float32),
            shape_of(slot_count, token_count),
        ),
        (scalars,),
        (local_frames, segment_ids[0], owners_col.reshape(1, token_count), owners_col),
        flops=2 * token_count * frame_count * model_width,
        moved=2 * frame_count * model_width,
    )
    other_member = swap_cores(member)
    other_ahead = swap_cores(ahead)
    other_memories = swap_cores(memories)

    m3 = relocate(m1, along_y, along_x)
    m4 = relocate(m1, None, z_up)
    m5 = relocate(m2, along_x, z_up)
    m6 = relocate(m3, None, along_y)
    m7 = relocate(pick(m2, m4), along_y, along_x)
    m8 = relocate(m5, along_y, along_x)

    slot_pieces = (
        ((qkv_weight, m1), (out_weight, m2), (m1, m3), (m3, m6)),
        ((m2, m4), (m7, m5), (m5, m7), (m8, m8)),
    )
    block = 2 * C
    width = 2 * shard
    row_count = frame_count + pad + memories.shape[0]
    keys_seen = block + pad + memories.shape[0]
    lanes = width // head_size * block
    attended, sums, outs = [], [], []
    for slot, pieces in enumerate(slot_pieces):
        flat = [p for pair in pieces for p in pair]
        *results, out_piece = local_call(
            functools.partial(attend_kernel, C, RC, head_size, slot == 0),
            (
                shape_of(frame_count, width),
                shape_of(frame_count, width),
                shape_of(token_count, width, dtype=jnp.float32),
                shape_of(token_count, width, dtype=jnp.float32),
                shape_of(model_width, width),
            ),
            (scalars, other_length),
            (member, other_member, normed, ahead, memories, other_normed, other_ahead, other_memories, *flat),
            in_place=6 + len(flat),
            out_in_place=(True, True, False, False, False),
            scratch=(
                pltpu.VMEM((2, frame_count, width), bf16),
                pltpu.VMEM((2 * row_count, model_width), bf16),
                pltpu.VMEM((model_width, 3 * width), bf16),
                pltpu.VMEM((2 * row_count, width), bf16),
                pltpu.VMEM((2 * row_count, width), bf16),
                pltpu.VMEM((2 * row_count, width), bf16),
                pltpu.VMEM((block + pad, lanes), jnp.float32),
                pltpu.VMEM((RING, keys_seen, lanes), jnp.float32),
                pltpu.VMEM((RING, 1, lanes), jnp.float32),
                pltpu.VMEM((RING, keys_seen, lanes), bf16),
                pltpu.SemaphoreType.DMA((24,)),
            ),
            vmem_mib=24,
            flops=12 * frame_count * model_width * width,
            moved=8 * frame_count * model_width,
        )
        attended.append(results[:2])
        sums.append(results[2:])
        outs.append(out_piece)
    other_outs = [swap_cores(w) for w in outs]
    other_attended = [swap_cores(for_other) for _, for_other in attended]

    other_sums = [swap_cores(for_other) for _, for_other in sums]
    projections = (*outs, *other_outs)
    features = (attended[0][0], attended[1][0], *other_attended, *projections)
    sent_rows = local_call(
        functools.partial(pool_kernel, offsets_at),
        shape_of(slot_count, model_width),
        (scalars,),
        (base, inverse, route, sums[0][0], sums[1][0], *other_sums, *projections),
        scratch=(
            pltpu.VMEM((token_count, model_width), bf16),
            pltpu.VMEM((token_count, model_width), bf16),
        ),
        flops=4 * token_count * model_width * model_width,
        moved=6 * frame_count * model_width,
    )
    received = exchange_blocks(
        sent_rows.reshape(time_count, capacity, model_width)
    ).reshape(slot_count, model_width)
    encoded = local_call(
        functools.partial(encode_kernel, offsets_at),
        shape_of(frame_count, model_width),
        (scalars,),
        (*features, local_frames),
        scratch=(pltpu.VMEM((frame_count, model_width), bf16),),
        flops=2 * frame_count * model_width * model_width,
        moved=6 * frame_count * model_width,
    )
    language_pieces = (language_weight, swap_cores(language_weight), l1, swap_cores(l1))
    lm_out = local_call(
        functools.partial(language_kernel, places_at),
        shape_of(slot_count, rec_count * language_shard),
        (scalars,),
        (received, *language_pieces),
        in_place=rec_count,
        out_in_place=True,
        scratch=(
            pltpu.VMEM((rec_count, model_width, language_shard), bf16),
            pltpu.VMEM((rec_count, slot_count, language_shard), bf16),
            pltpu.SemaphoreType.DMA((rec_count,)),
            pltpu.SemaphoreType.DMA((rec_count,)),
        ),
        flops=2 * slot_count * model_width * rec_count * language_shard,
        moved=2 * model_width * rec_count * language_shard,
    )
    return (encoded[None], lm_out[None, None])


def solution(mesh):
    in_specs = (
        P("rec", "tm", None),
        P("rec"),
        P(),
        P(),
        P(None, None, "tm"),
        P(None, "tm"),
        P("rec", "tm", None),
        P("rec", "tm", None, None),
        P(None, "rec"),
    )
    out_specs = (P("rec", "tm", None), P("rec", "tm", None, None))
    rec_count, time_count = mesh.shape["rec"], mesh.shape["tm"]
    paired = shard_map_of(mesh, in_specs, out_specs, per_device)
    plain = shard_map_of(mesh, in_specs, out_specs, plain_device)

    def run(*arrays):
        shard = arrays[5].shape[1] // time_count
        fits = rec_count == 4 and time_count == 8 and shard % LANES == 0
        return (paired if fits else plain)(*arrays)

    return run


def shard_map_of(mesh, in_specs, out_specs, body):
    return jax.shard_map(
        body, mesh=mesh, in_specs=in_specs, out_specs=out_specs, check_vma=False
    )
```

```python
import functools

import jax
import jax.numpy as jnp
from jax import lax
from jax.experimental import pallas as pl
from jax.experimental.pallas import tpu as pltpu
from jax.sharding import PartitionSpec as P


H = 16
C = 32
RC = 8


EPS_NORM = 1e-05
EPS_MEMORY = 1e-06
NEG_BIG = -1e30
LANES = 128
RING = 16
LOG2_E = 1.4426950408889634


def shifted(block, axis, distance):
    devices = range(lax.axis_size(axis))
    route = [(i - distance, i) for i in devices if i - distance in devices]
    return lax.ppermute(block, axis, route)


def layer_norm(values_in, gain):
    values_in = values_in.astype(jnp.float32)
    centre = jnp.mean(values_in, axis=-1, keepdims=True)
    centred = values_in - centre
    spread = jnp.mean(centred * centred, axis=-1, keepdims=True)
    return centred * lax.rsqrt(spread + EPS_NORM) * gain


def span_memory(normed, live_mask, gain, span_len):
    model_width = normed.shape[1]
    masked = jnp.where(live_mask[:, None], normed.astype(jnp.float32), jnp.float32(0.0))
    owner_sums = masked.reshape(-1, span_len, model_width).sum(axis=1)
    counts = live_mask.reshape(-1, span_len).astype(jnp.float32).sum(axis=1)
    means = owner_sums / jnp.maximum(counts, 1.0)[:, None]
    power = jnp.mean(means * means, axis=-1, keepdims=True)
    return (means * lax.rsqrt(power + EPS_MEMORY) * gain).astype(jnp.bfloat16)


def block_size():
    return 256


def local_part(query, keys, values, first_frame, length, head_count, span_len, right_len):
    frame_count, model_width = query.shape
    head_size = model_width // head_count
    group_rows = 4 * span_len
    group_count = frame_count // group_rows
    block_rows = block_size()
    query_blocks = query.reshape(group_count, group_rows, head_count, head_size)
    key_blocks = keys[:frame_count].reshape(group_count, group_rows, head_count, head_size)
    value_blocks = values[:frame_count].reshape(group_count, group_rows, head_count, head_size)
    key_tail = keys[frame_count:].reshape(1, right_len, head_count, head_size)
    value_tail = values[frame_count:].reshape(1, right_len, head_count, head_size)
    key_all = jnp.concatenate(
        [key_blocks, jnp.concatenate([key_blocks[1:, :right_len], key_tail], axis=0)], axis=1
    )
    value_all = jnp.concatenate(
        [value_blocks, jnp.concatenate([value_blocks[1:, :right_len], value_tail], axis=0)], axis=1
    )
    start_offsets = jnp.arange(group_count, dtype=jnp.int32)[:, None] * group_rows
    query_pos = first_frame + start_offsets + jnp.arange(group_rows, dtype=jnp.int32)[None, :]
    key_pos = first_frame + jnp.concatenate(
        [
            start_offsets + jnp.arange(group_rows, dtype=jnp.int32)[None, :],
            start_offsets + group_rows + jnp.arange(right_len, dtype=jnp.int32)[None, :],
        ],
        axis=1,
    )
    query_span = query_pos // span_len
    span_end = (query_span + 1) * span_len
    same = (key_pos // span_len)[:, None, :] == query_span[:, :, None]
    ahead = (key_pos[:, None, :] >= span_end[:, :, None]) & (
        key_pos[:, None, :] < span_end[:, :, None] + right_len
    )
    allowed = (same | ahead) & (key_pos < length)[:, None, :]
    scores = jnp.einsum(
        "gqhd,gkhd->ghqk", query_blocks, key_all, preferred_element_type=jnp.float32
    ) * head_size ** (-0.5)
    scores = jnp.where(allowed[:, None], scores, NEG_BIG)
    row_peak = jnp.max(scores, axis=-1)
    weights = jnp.where(allowed[:, None], jnp.exp(scores - row_peak[..., None]), jnp.float32(0.0))
    row_total = jnp.sum(weights, axis=-1)
    accum = jnp.einsum(
        "ghqk,gkhd->ghqd",
        weights.astype(jnp.bfloat16),
        value_all,
        preferred_element_type=jnp.float32,
    )
    block_count = frame_count // block_rows
    row_peak = (
        row_peak.transpose(1, 0, 2).reshape(head_count, block_count, block_rows).transpose(1, 0, 2)
    )
    row_total = (
        row_total.transpose(1, 0, 2).reshape(head_count, block_count, block_rows).transpose(1, 0, 2)
    )
    accum = (
        accum.transpose(1, 0, 2, 3)
        .reshape(head_count, block_count, block_rows, head_size)
        .transpose(1, 0, 2, 3)
    )
    return (row_peak, row_total, accum)


def memory_update(
    carry, memory_keys, memory_values, query, first_frame, length, head_count, span_len
):
    row_peak, row_total, accum = carry
    block_count, _, block_rows = row_peak.shape
    row_count, model_width = memory_keys.shape
    head_size = model_width // head_count
    mem_keys = memory_keys.reshape(row_count, head_count, head_size)
    mem_values = memory_values.reshape(row_count, head_count, head_size)
    mem_index = jnp.arange(row_count, dtype=jnp.int32)
    mem_live = mem_index * span_len < length
    query_blocks = query.reshape(block_count, block_rows, head_count, head_size)
    positions = first_frame + jnp.arange(block_count * block_rows, dtype=jnp.int32).reshape(
        block_count, block_rows
    )

    def one_block(packed):
        query_now, pos_now, peak_now, total_now, accum_now = packed
        scores = jnp.einsum(
            "qhd,khd->hqk", query_now, mem_keys, preferred_element_type=jnp.float32
        ) * head_size ** (-0.5)
        allowed = (mem_index[None, :] < (pos_now // span_len)[:, None]) & mem_live[None, :]
        scores = jnp.where(allowed[None], scores, NEG_BIG)
        new_peak = jnp.maximum(peak_now, jnp.max(scores, axis=-1))
        weights = jnp.where(allowed[None], jnp.exp(scores - new_peak[..., None]), jnp.float32(0.0))
        factor = jnp.exp(peak_now - new_peak)
        total_next = total_now * factor + jnp.sum(weights, axis=-1)
        accum_next = accum_now * factor[..., None] + jnp.einsum(
            "hqk,khd->hqd",
            weights.astype(jnp.bfloat16),
            mem_values,
            preferred_element_type=jnp.float32,
        )
        return (new_peak, total_next, accum_next)

    return lax.map(one_block, (query_blocks, positions, row_peak, row_total, accum))


def finish(carry, frame_count, model_width):
    _, row_total, accum = carry
    result = accum / row_total[..., None]
    return result.transpose(0, 2, 1, 3).reshape(frame_count, model_width).astype(jnp.bfloat16)


def dispatch_matrix(owner_ids, owner_count, capacity):
    choose = (owner_ids[:, None] == jnp.arange(owner_count, dtype=jnp.int32)[None, :]).astype(
        jnp.int32
    )
    before = jnp.cumsum(choose, axis=0) - choose
    slot_index = jnp.sum(before * choose, axis=1)
    target = owner_ids * capacity + slot_index
    slot_rows = jnp.arange(owner_count * capacity, dtype=jnp.int32)
    return (slot_rows[:, None] == target[None, :]).astype(jnp.bfloat16)


def plain_device(
    frames,
    lengths,
    norm_gain,
    memory_gain,
    qkv_weight,
    out_weight,
    segment_ids,
    owners,
    language_weight,
):
    local_frames = frames[0]
    frame_count, model_width = local_frames.shape
    head_count = H
    time_count = lax.axis_size("tm")
    first_frame = lax.axis_index("tm") * frame_count
    length = lengths[0]
    live_mask = first_frame + jnp.arange(frame_count, dtype=jnp.int32) < length
    right_frames = shifted(local_frames[:RC], "tm", -1)
    normed = layer_norm(local_frames, norm_gain).astype(jnp.bfloat16)
    normed_right = layer_norm(right_frames, norm_gain).astype(jnp.bfloat16)
    memory = span_memory(normed, live_mask, memory_gain, C)
    stacked_rows = jnp.concatenate([normed, normed_right, memory], axis=0)
    projected = jnp.einsum(
        "fd,kdw->kfw",
        stacked_rows,
        lax.all_gather(qkv_weight, "tm", axis=2, tiled=True),
        preferred_element_type=jnp.float32,
    ).astype(jnp.bfloat16)
    split_at = frame_count + RC
    query = projected[0, :frame_count]
    keys = projected[1, :split_at]
    values = projected[2, :split_at]
    memory_keys = projected[1, split_at:]
    memory_values = projected[2, split_at:]
    carry = local_part(query, keys, values, first_frame, length, head_count, C, RC)
    carry = memory_update(
        carry,
        lax.all_gather(memory_keys, "tm", axis=0, tiled=True),
        lax.all_gather(memory_values, "tm", axis=0, tiled=True),
        query,
        first_frame,
        length,
        head_count,
        C,
    )
    attended = finish(carry, frame_count, model_width)
    output_proj = jnp.dot(
        attended,
        lax.all_gather(out_weight, "tm", axis=1, tiled=True),
        preferred_element_type=jnp.float32,
    )
    encoded = jnp.where(
        live_mask[:, None], local_frames.astype(jnp.float32) + output_proj, jnp.float32(0.0)
    ).astype(jnp.bfloat16)
    token_count = owners.shape[2]
    segments = segment_ids[0, 0]
    owner_indicator = (
        segments[None, :] == jnp.arange(token_count, dtype=jnp.int32)[:, None]
    ).astype(jnp.bfloat16)
    owner_sums = jnp.dot(owner_indicator, encoded, preferred_element_type=jnp.float32)
    counts = jnp.sum(owner_indicator.astype(jnp.float32), axis=1)
    pooled_rows = (owner_sums / counts[:, None]).astype(jnp.bfloat16)
    slot_count = 2 * token_count
    capacity = slot_count // time_count
    route_matrix = dispatch_matrix(owners[0, 0, :, 0], time_count, capacity)
    sent_rows = jnp.dot(route_matrix, pooled_rows, preferred_element_type=jnp.float32).astype(
        jnp.bfloat16
    )
    received = lax.all_to_all(
        sent_rows.reshape(time_count, capacity, model_width),
        "tm",
        split_axis=0,
        concat_axis=0,
        tiled=True,
    )
    received = received.reshape(slot_count, model_width)
    lm_out = jnp.dot(
        received,
        lax.all_gather(language_weight, "rec", axis=1, tiled=True),
        preferred_element_type=jnp.float32,
    ).astype(jnp.bfloat16)
    return (encoded[None], lm_out[None, None])


def vmem_spec():
    return pl.BlockSpec(memory_space=pltpu.VMEM)


def smem_spec():
    return pl.BlockSpec(memory_space=pltpu.SMEM)


def local_call(kernel, out_shapes, scalars, operands, scratch=(), in_place=0, out_in_place=False, vmem_mib=16, flops=0, moved=0):
    whole = len(operands) - in_place
    anywhere = pl.BlockSpec(memory_space=pl.ANY)
    if isinstance(out_shapes, tuple):
        stays = out_in_place or (False,) * len(out_shapes)
        out_specs = tuple(anywhere if stay else vmem_spec() for stay in stays)
    else:
        out_specs = anywhere if out_in_place else vmem_spec()
    return pl.pallas_call(
        kernel,
        out_shape=out_shapes,
        in_specs=[smem_spec()] * len(scalars) + [vmem_spec()] * whole + [anywhere] * in_place,
        out_specs=out_specs,
        compiler_params=pltpu.CompilerParams(vmem_limit_bytes=vmem_mib << 20),
        scratch_shapes=list(scratch),
        cost_estimate=pl.CostEstimate(flops=flops, bytes_accessed=moved, transcendentals=0),
    )(*scalars, *operands)


def shape_of(*dims, dtype=jnp.bfloat16):
    return jax.ShapeDtypeStruct(dims, dtype)


def normalise_kernel(
    span_len, scalars, frames, gain, memory_gain, normed_out, ahead_out, memory_out
):
    first_frame, length = scalars[0], scalars[1]
    frame_count, _ = frames.shape
    span_count = frame_count // span_len
    values = frames[...].astype(jnp.float32)
    centre = jnp.mean(values, axis=-1, keepdims=True)
    centred = values - centre
    spread = jnp.mean(centred * centred, axis=-1, keepdims=True)
    normed = (centred * lax.rsqrt(spread + EPS_NORM) * gain[...]).astype(jnp.bfloat16)
    normed_out[...] = normed
    ahead_out[...] = normed[: ahead_out.shape[0]]
    spans = lax.broadcasted_iota(jnp.int32, (span_count, frame_count), 0)
    places = lax.broadcasted_iota(jnp.int32, (span_count, frame_count), 1)
    member = (places >= spans * span_len) & (places < (spans + 1) * span_len)
    member = member & (places < length - first_frame)
    sums = jnp.dot(
        member.astype(jnp.bfloat16), normed, preferred_element_type=jnp.float32
    )
    counts = jnp.sum(member.astype(jnp.float32), axis=-1, keepdims=True)
    means = sums / jnp.maximum(counts, 1.0)
    power = jnp.mean(means * means, axis=-1, keepdims=True)
    memory = (means * lax.rsqrt(power + EPS_MEMORY) * memory_gain[...]).astype(jnp.bfloat16)
    for copy in range(memory_out.shape[0]):
        memory_out[copy] = memory


def prepare_kernel(scalars, frames, segments, owners_row, owners_col, base_out, member_out, count_out, route_out):
    first_frame, length, capacity = scalars[0], scalars[1], scalars[4]
    token_count, frame_count = member_out.shape
    tokens = lax.broadcasted_iota(jnp.int32, (token_count, frame_count), 0)
    places = first_frame + lax.broadcasted_iota(jnp.int32, (token_count, frame_count), 1)
    member = (segments[...] == tokens).astype(jnp.float32)
    counts = jnp.sum(member, axis=1, keepdims=True)
    live_member = jnp.where(places < length, member, 0.0).astype(jnp.bfloat16)
    earlier = lax.broadcasted_iota(jnp.int32, (token_count, token_count), 0)
    later = lax.broadcasted_iota(jnp.int32, (token_count, token_count), 1)
    clash = (owners_col[...] == owners_row[...]) & (earlier < later)
    slot = jnp.sum(clash.astype(jnp.int32), axis=0, keepdims=True)
    target = owners_row[...] * capacity + slot
    slots = lax.broadcasted_iota(jnp.int32, route_out.shape, 0)
    route_out[...] = (slots == target).astype(jnp.bfloat16)
    member_out[...] = live_member
    count_out[...] = jnp.broadcast_to(1.0 / counts, count_out.shape)
    base_out[...] = (
        jnp.dot(live_member, frames[...], preferred_element_type=jnp.float32) / counts
    )


def attend_kernel(span_len, right_len, head_size, starts_here, scalars, other_length, *refs):
    members, sources, pieces = refs[:2], refs[2:8], refs[8:16]
    out_refs, sums_out, projection = refs[16:18], refs[18:20], refs[20]
    outs, rows_in, weight, query, key, value, bias, scores, peaks, weights, sems = refs[21:]
    first_frame, core, y_half = scalars[0], scalars[2], scalars[3]
    frame_count, model_width = sources[0].shape
    half = model_width // 2
    width = out_refs[0].shape[1]
    out_copies = [
        pltpu.make_async_copy(outs.at[rec], out_refs[rec], sems.at[22 + rec]) for rec in range(2)
    ]
    heads = width // head_size
    block = 2 * span_len
    blocks = frame_count // block
    near = bias.shape[0]
    memory_at = frame_count + near - block
    row_count = rows_in.shape[0] // 2
    memory_count = row_count - memory_at
    lanes = heads * block

    def piece_copies(of_core, projected):
        places = (y_half * half, (1 - y_half) * half)
        copies = []
        for side in range(2):
            place = pl.ds(pl.multiple_of(places[side], half), half)
            for shard in range(2):
                piece = pieces[4 * shard + 2 * side + of_core]
                raw = starts_here and of_core == 0 and shard == 0
                shard_width = pieces[-1].shape[2]
                index = 2 * side + shard
                for part in (3,) if projected else (0, 1, 2):
                    target = projection if projected else weight
                    start = shard * shard_width + (0 if projected else part * width)
                    if raw:
                        source = pieces[2].at[place] if projected else pieces[0].at[part, place]
                    else:
                        source = piece.at[part]
                    copies.append(
                        pltpu.make_async_copy(
                            source,
                            target.at[place, pl.ds(start, shard_width)],
                            sems.at[4 * part + index],
                        )
                    )
        return copies

    row_copies = []
    for rec in range(2):
        at = rec * row_count
        for i, (start, size) in enumerate(
            ((0, frame_count), (frame_count, near - block), (memory_at, memory_count))
        ):
            row_copies.append(
                pltpu.make_async_copy(
                    sources[3 * rec + i], rows_in.at[pl.ds(at + start, size)], sems.at[16 + 3 * rec + i]
                )
            )

    for copy in row_copies:
        copy.start()
    for of_core in range(2):

        @pl.when(core == of_core)
        def _():
            for copy in piece_copies(of_core, False) + piece_copies(of_core, True):
                copy.start()

    rows = lax.broadcasted_iota(jnp.int32, (near, lanes), 0)
    spans = (lax.broadcasted_iota(jnp.int32, (near, lanes), 1) % block) // span_len
    same = (rows >= spans * span_len) & (rows < (spans + 1) * span_len + right_len)
    bias[...] = jnp.where(same, jnp.float32(0.0), jnp.float32(NEG_BIG))
    lane_spans = (lax.broadcasted_iota(jnp.int32, (1, lanes), 1) % block) // span_len
    memory_rows = lax.broadcasted_iota(jnp.int32, (memory_count, lanes), 0)
    feature_head = lax.broadcasted_iota(jnp.int32, (1, width), 1) // head_size
    head_masks = [(feature_head == h).astype(jnp.bfloat16) for h in range(heads)]
    scale = head_size ** (-0.5) * LOG2_E

    for copy in row_copies + piece_copies(1, False):
        copy.wait()
    mixed = jnp.dot(rows_in[...], weight[...], preferred_element_type=jnp.float32)
    query[...] = (mixed[:, :width] * scale).astype(jnp.bfloat16)
    key[...] = mixed[:, width : 2 * width].astype(jnp.bfloat16)
    value[...] = mixed[:, 2 * width :].astype(jnp.bfloat16)

    def score_block(i):
        rec, b = divmod(i, blocks)
        at, start = rec * row_count, b * block
        length = scalars[1] if rec == 0 else other_length[0]
        q_now = query[at + start : at + start + block]
        stacked = jnp.concatenate([q_now * m for m in head_masks], axis=0)
        keys = jnp.concatenate(
            [key[at + start : at + start + near], key[at + memory_at : at + row_count]], axis=0
        )
        raw = lax.dot_general(
            keys, stacked, (((1,), (1,)), ((), ())), preferred_element_type=jnp.float32
        )
        limit = length - first_frame - start
        local = jnp.where(rows < limit, raw[:near] + bias[...], NEG_BIG)
        live_spans = (length + span_len - 1) // span_len
        span_limit = jnp.minimum(first_frame // span_len + 2 * b + lane_spans, live_spans)
        memory = jnp.where(memory_rows < span_limit, raw[near:], NEG_BIG)
        slot = i % scores.shape[0]
        scores[slot, 0:near, :] = local
        scores[slot, near:, :] = memory
        peaks[slot] = jnp.maximum(
            jnp.max(local, axis=0, keepdims=True), jnp.max(memory, axis=0, keepdims=True)
        )

    def weigh_block(i):
        slot = i % scores.shape[0]
        weights[slot] = jnp.exp2(scores[slot] - peaks[slot]).astype(jnp.bfloat16)

    ones = jnp.ones((near + memory_count, LANES), jnp.bfloat16)
    first_of_pair = lax.broadcasted_iota(jnp.int32, (1, 2 * LANES), 1) % LANES < head_size

    def mix_block(i):
        rec, b = divmod(i, blocks)
        at, start = rec * row_count, b * block
        values = jnp.concatenate(
            [value[at + start : at + start + near], value[at + memory_at : at + row_count]], axis=0
        )
        for pair in range(width // LANES):
            columns = slice(pair * LANES, (pair + 1) * LANES)
            pair_rows = slice(pair * 2 * block, (pair + 1) * 2 * block)
            sums = lax.dot_general(
                weights[i % weights.shape[0], :, pair_rows],
                jnp.concatenate([values[:, columns], ones], axis=1),
                (((0,), (0,)), ((), ())),
                preferred_element_type=jnp.float32,
            )
            picked = jnp.where(first_of_pair, sums[:block], sums[block:])
            outs[rec, start : start + block, columns] = (
                picked[:, :LANES] / picked[:, LANES:]
            ).astype(jnp.bfloat16)

    count = 2 * blocks
    ring = scores.shape[0]
    for first in range(0, count, ring):
        for stage in (score_block, weigh_block, mix_block):
            for i in range(first, min(first + ring, count)):
                stage(i)
        for rec in range(2):
            if first < (rec + 1) * blocks <= first + ring:
                out_copies[rec].start()
    for rec in range(2):
        sums_out[rec][...] = jnp.dot(
            members[rec][...], outs[rec], preferred_element_type=jnp.float32
        )
    for copy in piece_copies(1, True) + out_copies:
        copy.wait()


def assemble(scalars, offsets_at, attended, gathered):
    shard = attended[0].shape[1] // 2
    offsets = [
        [pl.multiple_of(scalars[offsets_at + 2 * i + s], LANES) for s in range(2)]
        for i in range(4)
    ]
    for i in range(4):
        for s in range(2):
            gathered[:, pl.ds(offsets[i][s], shard)] = attended[i][:, s * shard : (s + 1) * shard]
    return offsets, shard


def pool_kernel(offsets_at, scalars, base, inverse, route, *refs):
    sums, projections = refs[:4], refs[4:8]
    sent_out, means, pooled = refs[8:]
    shard = sums[0].shape[1] // 2
    offsets = [
        [pl.multiple_of(scalars[offsets_at + 2 * i + s], LANES) for s in range(2)]
        for i in range(4)
    ]
    for i in range(4):
        for s in range(2):
            for lane in range(0, shard, LANES):
                means[:, pl.ds(offsets[i][s] + lane, LANES)] = (
                    sums[i][:, s * shard + lane : s * shard + lane + LANES] * inverse[...]
                ).astype(jnp.bfloat16)
    for i in range(4):
        mixed = jnp.dot(means[...], projections[i][...], preferred_element_type=jnp.float32)
        for s in range(2):
            columns = pl.ds(offsets[i][s], shard)
            pooled[:, columns] = (
                base[:, columns] + mixed[:, s * shard : (s + 1) * shard]
            ).astype(jnp.bfloat16)
    sent_out[...] = jnp.dot(
        route[...], pooled[...], preferred_element_type=jnp.float32
    ).astype(jnp.bfloat16)


def encode_kernel(offsets_at, scalars, *refs):
    attended, projections, frames = refs[:4], refs[4:8], refs[8]
    encoded_out, gathered = refs[9:]
    first_frame, length = scalars[0], scalars[1]
    frame_count, _ = frames.shape
    offsets, shard = assemble(scalars, offsets_at, attended, gathered)
    live = (
        first_frame + lax.broadcasted_iota(jnp.int32, (frame_count, 1), 0) < length
    ).astype(jnp.float32)
    for i in range(4):
        mixed = jnp.dot(
            gathered[...], projections[i][...], preferred_element_type=jnp.float32
        )
        for s in range(2):
            columns = pl.ds(offsets[i][s], shard)
            base = frames[:, columns].astype(jnp.float32)
            encoded_out[:, columns] = (
                (base + mixed[:, s * shard : (s + 1) * shard]) * live
            ).astype(jnp.bfloat16)


def language_kernel(places_at, scalars, received, *refs):
    pieces, out = refs[:-5], refs[-5]
    weights, product, sems, out_sems = refs[-4:]
    count, width = len(pieces), pieces[0].shape[1]
    copies = [
        pltpu.make_async_copy(piece, weights.at[i], sems.at[i]) for i, piece in enumerate(pieces)
    ]
    for copy in copies:
        copy.start()
    out_copies = []
    for i in range(count):
        copies[i].wait()
        product[i] = jnp.dot(
            received[...], weights[i], preferred_element_type=jnp.float32
        ).astype(jnp.bfloat16)
        place = pl.multiple_of(scalars[places_at + i], LANES)
        out_copies.append(
            pltpu.make_async_copy(product.at[i], out.at[:, pl.ds(place, width)], out_sems.at[i])
        )
        out_copies[-1].start()
    for copy in out_copies:
        copy.wait()


def along_x(r, j, _):
    return r, j ^ 1


def along_y(r, j, _):
    return r ^ 2, j


def other_core(r, j, _):
    return r ^ 1, j


def z_up(r, j, count):
    return r, (j + 2) % count


def z_down(r, j, count):
    return r, (j - 2) % count


def relocate(value, core_0, core_1):
    rec_count, time_count = lax.axis_size("rec"), lax.axis_size("tm")
    pairs = []
    for r in range(rec_count):
        for j in range(time_count):
            route = (core_0, core_1)[r % 2]
            if route is not None:
                to_r, to_j = route(r, j, time_count)
                pairs.append((r * time_count + j, to_r * time_count + to_j))
    return lax.ppermute(value, ("rec", "tm"), pairs)


def swap_cores(value):
    return relocate(value, other_core, other_core)


def exchange_blocks(blocks):
    return lax.all_to_all(blocks, "tm", split_axis=0, concat_axis=0, tiled=True)


def per_device(
    frames,
    lengths,
    norm_gain,
    memory_gain,
    qkv_weight,
    out_weight,
    segment_ids,
    owners,
    language_weight,
):
    local_frames = frames[0]
    frame_count, model_width = local_frames.shape
    shard = out_weight.shape[1]
    half = model_width // 2
    time_count = lax.axis_size("tm")
    rec_count = lax.axis_size("rec")
    rec, time = lax.axis_index("rec"), lax.axis_index("tm")
    core, y_half = rec % 2, (rec // 2) % 2
    x, z = time % 2, time // 2
    z_count = time_count // 2
    first_frame = time * frame_count
    length = lengths[0]
    head_size = model_width // H
    bf16 = jnp.bfloat16

    own = jnp.concatenate([qkv_weight, out_weight[None]], axis=0)
    own_a = lax.dynamic_slice_in_dim(own, y_half * half, half, 1)

    def pick(for_core_0, for_core_1):
        return jnp.where(core == 0, for_core_0, for_core_1)

    token_count = owners.shape[2]
    slot_count = 2 * token_count
    capacity = slot_count // time_count
    language_shard = language_weight.shape[1]

    def group_of(of_core, slot):
        return jnp.where(of_core == 0, z + slot, z - slot - 1) % z_count

    numbers = [first_frame, length, core, y_half, capacity]
    offsets_at = len(numbers)
    for of_core in (core, 1 - core):
        for slot in range(2):
            group = group_of(of_core, slot)
            numbers += [(2 * group + x) * shard, (2 * group + 1 - x) * shard]
    places_at = len(numbers)
    numbers += [(rec ^ i) * language_shard for i in range(rec_count)]
    scalars = jnp.stack(numbers).astype(jnp.int32)

    m1 = relocate(own_a, along_x, z_up)
    m2 = relocate(own_a, z_down, None)
    l1 = relocate(language_weight, along_y, along_y)

    pad = 2 * RC
    normed, start_rows, memory = local_call(
        functools.partial(normalise_kernel, C),
        (
            shape_of(frame_count, model_width),
            shape_of(pad, model_width),
            shape_of(time_count, frame_count // C, model_width),
        ),
        (scalars,),
        (local_frames, norm_gain[None], memory_gain[None]),
        flops=10 * frame_count * model_width,
        moved=4 * frame_count * model_width,
    )
    other_length = swap_cores(lengths)
    other_normed = swap_cores(normed)
    ahead = shifted(start_rows, "tm", -1)
    memories = exchange_blocks(memory).reshape(-1, model_width)
    owners_col = owners[0, 0]
    base, member, inverse, route = local_call(
        prepare_kernel,
        (
            shape_of(token_count, model_width, dtype=jnp.float32),
            shape_of(token_count, frame_count),
            shape_of(token_count, LANES, dtype=jnp.float32),
            shape_of(slot_count, token_count),
        ),
        (scalars,),
        (local_frames, segment_ids[0], owners_col.reshape(1, token_count), owners_col),
        flops=2 * token_count * frame_count * model_width,
        moved=2 * frame_count * model_width,
    )
    other_member = swap_cores(member)
    other_ahead = swap_cores(ahead)
    other_memories = swap_cores(memories)

    m3 = relocate(m1, along_y, along_y)
    m3x = relocate(m1, None, along_x)
    m4 = relocate(m1, None, z_up)
    m5 = relocate(pick(m2, m3), along_x, z_up)
    m6 = relocate(m3x, None, along_y)
    m7 = relocate(pick(m2, m4), along_y, along_x)
    m8 = relocate(m5, along_y, along_x)

    slot_pieces = (
        ((qkv_weight, m1), (out_weight, m3), (m1, m3x), (m3, m6)),
        ((m2, m4), (m7, m5), (m5, m7), (m8, m8)),
    )
    block = 2 * C
    width = 2 * shard
    row_count = frame_count + pad + memories.shape[0]
    keys_seen = block + pad + memories.shape[0]
    lanes = width // head_size * block
    attended, sums, outs = [], [], []
    for slot, pieces in enumerate(slot_pieces):
        flat = [p for pair in pieces for p in pair]
        *results, out_piece = local_call(
            functools.partial(attend_kernel, C, RC, head_size, slot == 0),
            (
                shape_of(frame_count, width),
                shape_of(frame_count, width),
                shape_of(token_count, width, dtype=jnp.float32),
                shape_of(token_count, width, dtype=jnp.float32),
                shape_of(model_width, width),
            ),
            (scalars, other_length),
            (member, other_member, normed, ahead, memories, other_normed, other_ahead, other_memories, *flat),
            in_place=6 + len(flat),
            out_in_place=(True, True, False, False, False),
            scratch=(
                pltpu.VMEM((2, frame_count, width), bf16),
                pltpu.VMEM((2 * row_count, model_width), bf16),
                pltpu.VMEM((model_width, 3 * width), bf16),
                pltpu.VMEM((2 * row_count, width), bf16),
                pltpu.VMEM((2 * row_count, width), bf16),
                pltpu.VMEM((2 * row_count, width), bf16),
                pltpu.VMEM((block + pad, lanes), jnp.float32),
                pltpu.VMEM((RING, keys_seen, lanes), jnp.float32),
                pltpu.VMEM((RING, 1, lanes), jnp.float32),
                pltpu.VMEM((RING, keys_seen, lanes), bf16),
                pltpu.SemaphoreType.DMA((24,)),
            ),
            vmem_mib=24,
            flops=12 * frame_count * model_width * width,
            moved=8 * frame_count * model_width,
        )
        attended.append(results[:2])
        sums.append(results[2:])
        outs.append(out_piece)
    other_outs = [swap_cores(w) for w in outs]
    other_attended = [swap_cores(for_other) for _, for_other in attended]

    other_sums = [swap_cores(for_other) for _, for_other in sums]
    projections = (*outs, *other_outs)
    features = (attended[0][0], attended[1][0], *other_attended, *projections)
    sent_rows = local_call(
        functools.partial(pool_kernel, offsets_at),
        shape_of(slot_count, model_width),
        (scalars,),
        (base, inverse, route, sums[0][0], sums[1][0], *other_sums, *projections),
        scratch=(
            pltpu.VMEM((token_count, model_width), bf16),
            pltpu.VMEM((token_count, model_width), bf16),
        ),
        flops=4 * token_count * model_width * model_width,
        moved=6 * frame_count * model_width,
    )
    received = exchange_blocks(
        sent_rows.reshape(time_count, capacity, model_width)
    ).reshape(slot_count, model_width)
    encoded = local_call(
        functools.partial(encode_kernel, offsets_at),
        shape_of(frame_count, model_width),
        (scalars,),
        (*features, local_frames),
        scratch=(pltpu.VMEM((frame_count, model_width), bf16),),
        flops=2 * frame_count * model_width * model_width,
        moved=6 * frame_count * model_width,
    )
    language_pieces = (language_weight, swap_cores(language_weight), l1, swap_cores(l1))
    lm_out = local_call(
        functools.partial(language_kernel, places_at),
        shape_of(slot_count, rec_count * language_shard),
        (scalars,),
        (received, *language_pieces),
        in_place=rec_count,
        out_in_place=True,
        scratch=(
            pltpu.VMEM((rec_count, model_width, language_shard), bf16),
            pltpu.VMEM((rec_count, slot_count, language_shard), bf16),
            pltpu.SemaphoreType.DMA((rec_count,)),
            pltpu.SemaphoreType.DMA((rec_count,)),
        ),
        flops=2 * slot_count * model_width * rec_count * language_shard,
        moved=2 * model_width * rec_count * language_shard,
    )
    return (encoded[None], lm_out[None, None])


def solution(mesh):
    in_specs = (
        P("rec", "tm", None),
        P("rec"),
        P(),
        P(),
        P(None, None, "tm"),
        P(None, "tm"),
        P("rec", "tm", None),
        P("rec", "tm", None, None),
        P(None, "rec"),
    )
    out_specs = (P("rec", "tm", None), P("rec", "tm", None, None))
    rec_count, time_count = mesh.shape["rec"], mesh.shape["tm"]
    paired = shard_map_of(mesh, in_specs, out_specs, per_device)
    plain = shard_map_of(mesh, in_specs, out_specs, plain_device)

    def run(*arrays):
        shard = arrays[5].shape[1] // time_count
        fits = rec_count == 4 and time_count == 8 and shard % LANES == 0
        return (paired if fits else plain)(*arrays)

    return run


def shard_map_of(mesh, in_specs, out_specs, body):
    return jax.shard_map(
        body, mesh=mesh, in_specs=in_specs, out_specs=out_specs, check_vma=False
    )
```

```python
import functools

import jax
import jax.numpy as jnp
from jax import lax
from jax.experimental import pallas as pl
from jax.experimental.pallas import tpu as pltpu
from jax.sharding import PartitionSpec as P


H = 16
C = 32
RC = 8


EPS_NORM = 1e-05
EPS_MEMORY = 1e-06
NEG_BIG = -1e30
LANES = 128
RING = 16
LOG2_E = 1.4426950408889634


def shifted(block, axis, distance):
    devices = range(lax.axis_size(axis))
    route = [(i - distance, i) for i in devices if i - distance in devices]
    return lax.ppermute(block, axis, route)


def layer_norm(values_in, gain):
    values_in = values_in.astype(jnp.float32)
    centre = jnp.mean(values_in, axis=-1, keepdims=True)
    centred = values_in - centre
    spread = jnp.mean(centred * centred, axis=-1, keepdims=True)
    return centred * lax.rsqrt(spread + EPS_NORM) * gain


def span_memory(normed, live_mask, gain, span_len):
    model_width = normed.shape[1]
    masked = jnp.where(live_mask[:, None], normed.astype(jnp.float32), jnp.float32(0.0))
    owner_sums = masked.reshape(-1, span_len, model_width).sum(axis=1)
    counts = live_mask.reshape(-1, span_len).astype(jnp.float32).sum(axis=1)
    means = owner_sums / jnp.maximum(counts, 1.0)[:, None]
    power = jnp.mean(means * means, axis=-1, keepdims=True)
    return (means * lax.rsqrt(power + EPS_MEMORY) * gain).astype(jnp.bfloat16)


def block_size():
    return 256


def local_part(query, keys, values, first_frame, length, head_count, span_len, right_len):
    frame_count, model_width = query.shape
    head_size = model_width // head_count
    group_rows = 4 * span_len
    group_count = frame_count // group_rows
    block_rows = block_size()
    query_blocks = query.reshape(group_count, group_rows, head_count, head_size)
    key_blocks = keys[:frame_count].reshape(group_count, group_rows, head_count, head_size)
    value_blocks = values[:frame_count].reshape(group_count, group_rows, head_count, head_size)
    key_tail = keys[frame_count:].reshape(1, right_len, head_count, head_size)
    value_tail = values[frame_count:].reshape(1, right_len, head_count, head_size)
    key_all = jnp.concatenate(
        [key_blocks, jnp.concatenate([key_blocks[1:, :right_len], key_tail], axis=0)], axis=1
    )
    value_all = jnp.concatenate(
        [value_blocks, jnp.concatenate([value_blocks[1:, :right_len], value_tail], axis=0)], axis=1
    )
    start_offsets = jnp.arange(group_count, dtype=jnp.int32)[:, None] * group_rows
    query_pos = first_frame + start_offsets + jnp.arange(group_rows, dtype=jnp.int32)[None, :]
    key_pos = first_frame + jnp.concatenate(
        [
            start_offsets + jnp.arange(group_rows, dtype=jnp.int32)[None, :],
            start_offsets + group_rows + jnp.arange(right_len, dtype=jnp.int32)[None, :],
        ],
        axis=1,
    )
    query_span = query_pos // span_len
    span_end = (query_span + 1) * span_len
    same = (key_pos // span_len)[:, None, :] == query_span[:, :, None]
    ahead = (key_pos[:, None, :] >= span_end[:, :, None]) & (
        key_pos[:, None, :] < span_end[:, :, None] + right_len
    )
    allowed = (same | ahead) & (key_pos < length)[:, None, :]
    scores = jnp.einsum(
        "gqhd,gkhd->ghqk", query_blocks, key_all, preferred_element_type=jnp.float32
    ) * head_size ** (-0.5)
    scores = jnp.where(allowed[:, None], scores, NEG_BIG)
    row_peak = jnp.max(scores, axis=-1)
    weights = jnp.where(allowed[:, None], jnp.exp(scores - row_peak[..., None]), jnp.float32(0.0))
    row_total = jnp.sum(weights, axis=-1)
    accum = jnp.einsum(
        "ghqk,gkhd->ghqd",
        weights.astype(jnp.bfloat16),
        value_all,
        preferred_element_type=jnp.float32,
    )
    block_count = frame_count // block_rows
    row_peak = (
        row_peak.transpose(1, 0, 2).reshape(head_count, block_count, block_rows).transpose(1, 0, 2)
    )
    row_total = (
        row_total.transpose(1, 0, 2).reshape(head_count, block_count, block_rows).transpose(1, 0, 2)
    )
    accum = (
        accum.transpose(1, 0, 2, 3)
        .reshape(head_count, block_count, block_rows, head_size)
        .transpose(1, 0, 2, 3)
    )
    return (row_peak, row_total, accum)


def memory_update(
    carry, memory_keys, memory_values, query, first_frame, length, head_count, span_len
):
    row_peak, row_total, accum = carry
    block_count, _, block_rows = row_peak.shape
    row_count, model_width = memory_keys.shape
    head_size = model_width // head_count
    mem_keys = memory_keys.reshape(row_count, head_count, head_size)
    mem_values = memory_values.reshape(row_count, head_count, head_size)
    mem_index = jnp.arange(row_count, dtype=jnp.int32)
    mem_live = mem_index * span_len < length
    query_blocks = query.reshape(block_count, block_rows, head_count, head_size)
    positions = first_frame + jnp.arange(block_count * block_rows, dtype=jnp.int32).reshape(
        block_count, block_rows
    )

    def one_block(packed):
        query_now, pos_now, peak_now, total_now, accum_now = packed
        scores = jnp.einsum(
            "qhd,khd->hqk", query_now, mem_keys, preferred_element_type=jnp.float32
        ) * head_size ** (-0.5)
        allowed = (mem_index[None, :] < (pos_now // span_len)[:, None]) & mem_live[None, :]
        scores = jnp.where(allowed[None], scores, NEG_BIG)
        new_peak = jnp.maximum(peak_now, jnp.max(scores, axis=-1))
        weights = jnp.where(allowed[None], jnp.exp(scores - new_peak[..., None]), jnp.float32(0.0))
        factor = jnp.exp(peak_now - new_peak)
        total_next = total_now * factor + jnp.sum(weights, axis=-1)
        accum_next = accum_now * factor[..., None] + jnp.einsum(
            "hqk,khd->hqd",
            weights.astype(jnp.bfloat16),
            mem_values,
            preferred_element_type=jnp.float32,
        )
        return (new_peak, total_next, accum_next)

    return lax.map(one_block, (query_blocks, positions, row_peak, row_total, accum))


def finish(carry, frame_count, model_width):
    _, row_total, accum = carry
    result = accum / row_total[..., None]
    return result.transpose(0, 2, 1, 3).reshape(frame_count, model_width).astype(jnp.bfloat16)


def dispatch_matrix(owner_ids, owner_count, capacity):
    choose = (owner_ids[:, None] == jnp.arange(owner_count, dtype=jnp.int32)[None, :]).astype(
        jnp.int32
    )
    before = jnp.cumsum(choose, axis=0) - choose
    slot_index = jnp.sum(before * choose, axis=1)
    target = owner_ids * capacity + slot_index
    slot_rows = jnp.arange(owner_count * capacity, dtype=jnp.int32)
    return (slot_rows[:, None] == target[None, :]).astype(jnp.bfloat16)


def plain_device(
    frames,
    lengths,
    norm_gain,
    memory_gain,
    qkv_weight,
    out_weight,
    segment_ids,
    owners,
    language_weight,
):
    local_frames = frames[0]
    frame_count, model_width = local_frames.shape
    head_count = H
    time_count = lax.axis_size("tm")
    first_frame = lax.axis_index("tm") * frame_count
    length = lengths[0]
    live_mask = first_frame + jnp.arange(frame_count, dtype=jnp.int32) < length
    right_frames = shifted(local_frames[:RC], "tm", -1)
    normed = layer_norm(local_frames, norm_gain).astype(jnp.bfloat16)
    normed_right = layer_norm(right_frames, norm_gain).astype(jnp.bfloat16)
    memory = span_memory(normed, live_mask, memory_gain, C)
    stacked_rows = jnp.concatenate([normed, normed_right, memory], axis=0)
    projected = jnp.einsum(
        "fd,kdw->kfw",
        stacked_rows,
        lax.all_gather(qkv_weight, "tm", axis=2, tiled=True),
        preferred_element_type=jnp.float32,
    ).astype(jnp.bfloat16)
    split_at = frame_count + RC
    query = projected[0, :frame_count]
    keys = projected[1, :split_at]
    values = projected[2, :split_at]
    memory_keys = projected[1, split_at:]
    memory_values = projected[2, split_at:]
    carry = local_part(query, keys, values, first_frame, length, head_count, C, RC)
    carry = memory_update(
        carry,
        lax.all_gather(memory_keys, "tm", axis=0, tiled=True),
        lax.all_gather(memory_values, "tm", axis=0, tiled=True),
        query,
        first_frame,
        length,
        head_count,
        C,
    )
    attended = finish(carry, frame_count, model_width)
    output_proj = jnp.dot(
        attended,
        lax.all_gather(out_weight, "tm", axis=1, tiled=True),
        preferred_element_type=jnp.float32,
    )
    encoded = jnp.where(
        live_mask[:, None], local_frames.astype(jnp.float32) + output_proj, jnp.float32(0.0)
    ).astype(jnp.bfloat16)
    token_count = owners.shape[2]
    segments = segment_ids[0, 0]
    owner_indicator = (
        segments[None, :] == jnp.arange(token_count, dtype=jnp.int32)[:, None]
    ).astype(jnp.bfloat16)
    owner_sums = jnp.dot(owner_indicator, encoded, preferred_element_type=jnp.float32)
    counts = jnp.sum(owner_indicator.astype(jnp.float32), axis=1)
    pooled_rows = (owner_sums / counts[:, None]).astype(jnp.bfloat16)
    slot_count = 2 * token_count
    capacity = slot_count // time_count
    route_matrix = dispatch_matrix(owners[0, 0, :, 0], time_count, capacity)
    sent_rows = jnp.dot(route_matrix, pooled_rows, preferred_element_type=jnp.float32).astype(
        jnp.bfloat16
    )
    received = lax.all_to_all(
        sent_rows.reshape(time_count, capacity, model_width),
        "tm",
        split_axis=0,
        concat_axis=0,
        tiled=True,
    )
    received = received.reshape(slot_count, model_width)
    lm_out = jnp.dot(
        received,
        lax.all_gather(language_weight, "rec", axis=1, tiled=True),
        preferred_element_type=jnp.float32,
    ).astype(jnp.bfloat16)
    return (encoded[None], lm_out[None, None])


def vmem_spec():
    return pl.BlockSpec(memory_space=pltpu.VMEM)


def smem_spec():
    return pl.BlockSpec(memory_space=pltpu.SMEM)


def local_call(kernel, out_shapes, scalars, operands, scratch=(), in_place=0, out_in_place=False, vmem_mib=16, flops=0, moved=0):
    whole = len(operands) - in_place
    anywhere = pl.BlockSpec(memory_space=pl.ANY)
    if isinstance(out_shapes, tuple):
        stays = out_in_place or (False,) * len(out_shapes)
        out_specs = tuple(anywhere if stay else vmem_spec() for stay in stays)
    else:
        out_specs = anywhere if out_in_place else vmem_spec()
    return pl.pallas_call(
        kernel,
        out_shape=out_shapes,
        in_specs=[smem_spec()] * len(scalars) + [vmem_spec()] * whole + [anywhere] * in_place,
        out_specs=out_specs,
        compiler_params=pltpu.CompilerParams(vmem_limit_bytes=vmem_mib << 20),
        scratch_shapes=list(scratch),
        cost_estimate=pl.CostEstimate(flops=flops, bytes_accessed=moved, transcendentals=0),
    )(*scalars, *operands)


def shape_of(*dims, dtype=jnp.bfloat16):
    return jax.ShapeDtypeStruct(dims, dtype)


def normalise_kernel(
    span_len, scalars, frames, gain, memory_gain, normed_out, ahead_out, memory_out
):
    first_frame, length = scalars[0], scalars[1]
    frame_count, _ = frames.shape
    span_count = frame_count // span_len
    values = frames[...].astype(jnp.float32)
    centre = jnp.mean(values, axis=-1, keepdims=True)
    centred = values - centre
    spread = jnp.mean(centred * centred, axis=-1, keepdims=True)
    normed = (centred * lax.rsqrt(spread + EPS_NORM) * gain[...]).astype(jnp.bfloat16)
    normed_out[...] = normed
    ahead_out[...] = normed[: ahead_out.shape[0]]
    spans = lax.broadcasted_iota(jnp.int32, (span_count, frame_count), 0)
    places = lax.broadcasted_iota(jnp.int32, (span_count, frame_count), 1)
    member = (places >= spans * span_len) & (places < (spans + 1) * span_len)
    member = member & (places < length - first_frame)
    sums = jnp.dot(
        member.astype(jnp.bfloat16), normed, preferred_element_type=jnp.float32
    )
    counts = jnp.sum(member.astype(jnp.float32), axis=-1, keepdims=True)
    means = sums / jnp.maximum(counts, 1.0)
    power = jnp.mean(means * means, axis=-1, keepdims=True)
    memory = (means * lax.rsqrt(power + EPS_MEMORY) * memory_gain[...]).astype(jnp.bfloat16)
    for copy in range(memory_out.shape[0]):
        memory_out[copy] = memory


def prepare_kernel(scalars, frames, segments, owners_row, owners_col, base_out, member_out, count_out, route_out):
    first_frame, length, capacity = scalars[0], scalars[1], scalars[4]
    token_count, frame_count = member_out.shape
    tokens = lax.broadcasted_iota(jnp.int32, (token_count, frame_count), 0)
    places = first_frame + lax.broadcasted_iota(jnp.int32, (token_count, frame_count), 1)
    member = (segments[...] == tokens).astype(jnp.float32)
    counts = jnp.sum(member, axis=1, keepdims=True)
    live_member = jnp.where(places < length, member, 0.0).astype(jnp.bfloat16)
    earlier = lax.broadcasted_iota(jnp.int32, (token_count, token_count), 0)
    later = lax.broadcasted_iota(jnp.int32, (token_count, token_count), 1)
    clash = (owners_col[...] == owners_row[...]) & (earlier < later)
    slot = jnp.sum(clash.astype(jnp.int32), axis=0, keepdims=True)
    target = owners_row[...] * capacity + slot
    slots = lax.broadcasted_iota(jnp.int32, route_out.shape, 0)
    route_out[...] = (slots == target).astype(jnp.bfloat16)
    member_out[...] = live_member
    count_out[...] = jnp.broadcast_to(1.0 / counts, count_out.shape)
    base_out[...] = (
        jnp.dot(live_member, frames[...], preferred_element_type=jnp.float32) / counts
    )


def attend_kernel(span_len, right_len, head_size, starts_here, scalars, other_length, *refs):
    members, sources, pieces = refs[:2], refs[2:8], refs[8:16]
    out_refs, sums_out, projection = refs[16:18], refs[18:20], refs[20]
    outs, rows_in, weight, query, key, value, bias, scores, peaks, weights, sems = refs[21:]
    first_frame, core, y_half = scalars[0], scalars[2], scalars[3]
    frame_count, model_width = sources[0].shape
    half = model_width // 2
    width = out_refs[0].shape[1]
    out_copies = [
        pltpu.make_async_copy(outs.at[rec], out_refs[rec], sems.at[22 + rec]) for rec in range(2)
    ]
    heads = width // head_size
    block = 2 * span_len
    blocks = frame_count // block
    near = bias.shape[0]
    memory_at = frame_count + near - block
    row_count = rows_in.shape[0] // 2
    memory_count = row_count - memory_at
    lanes = heads * block

    def piece_copies(of_core, projected):
        places = (y_half * half, (1 - y_half) * half)
        copies = []
        for side in range(2):
            place = pl.ds(pl.multiple_of(places[side], half), half)
            for shard in range(2):
                piece = pieces[4 * shard + 2 * side + of_core]
                raw = starts_here and of_core == 0 and shard == 0
                shard_width = pieces[-1].shape[2]
                index = 2 * side + shard
                for part in (3,) if projected else (0, 1, 2):
                    target = projection if projected else weight
                    start = shard * shard_width + (0 if projected else part * width)
                    if raw:
                        source = pieces[2].at[place] if projected else pieces[0].at[part, place]
                    else:
                        source = piece.at[part]
                    copies.append(
                        pltpu.make_async_copy(
                            source,
                            target.at[place, pl.ds(start, shard_width)],
                            sems.at[4 * part + index],
                        )
                    )
        return copies

    row_copies = []
    for rec in range(2):
        at = rec * row_count
        for i, (start, size) in enumerate(
            ((0, frame_count), (frame_count, near - block), (memory_at, memory_count))
        ):
            row_copies.append(
                pltpu.make_async_copy(
                    sources[3 * rec + i], rows_in.at[pl.ds(at + start, size)], sems.at[16 + 3 * rec + i]
                )
            )

    for copy in row_copies:
        copy.start()
    for of_core in range(2):

        @pl.when(core == of_core)
        def _():
            for copy in piece_copies(of_core, False) + piece_copies(of_core, True):
                copy.start()

    rows = lax.broadcasted_iota(jnp.int32, (near, lanes), 0)
    spans = (lax.broadcasted_iota(jnp.int32, (near, lanes), 1) % block) // span_len
    same = (rows >= spans * span_len) & (rows < (spans + 1) * span_len + right_len)
    bias[...] = jnp.where(same, jnp.float32(0.0), jnp.float32(NEG_BIG))
    lane_spans = (lax.broadcasted_iota(jnp.int32, (1, lanes), 1) % block) // span_len
    memory_rows = lax.broadcasted_iota(jnp.int32, (memory_count, lanes), 0)
    feature_head = lax.broadcasted_iota(jnp.int32, (1, width), 1) // head_size
    head_masks = [(feature_head == h).astype(jnp.bfloat16) for h in range(heads)]
    scale = head_size ** (-0.5) * LOG2_E

    for copy in row_copies + piece_copies(1, False):
        copy.wait()
    mixed = jnp.dot(rows_in[...], weight[...], preferred_element_type=jnp.float32)
    query[...] = (mixed[:, :width] * scale).astype(jnp.bfloat16)
    key[...] = mixed[:, width : 2 * width].astype(jnp.bfloat16)
    value[...] = mixed[:, 2 * width :].astype(jnp.bfloat16)

    def score_block(i):
        rec, b = divmod(i, blocks)
        at, start = rec * row_count, b * block
        length = scalars[1] if rec == 0 else other_length[0]
        q_now = query[at + start : at + start + block]
        stacked = jnp.concatenate([q_now * m for m in head_masks], axis=0)
        keys = jnp.concatenate(
            [key[at + start : at + start + near], key[at + memory_at : at + row_count]], axis=0
        )
        raw = lax.dot_general(
            keys, stacked, (((1,), (1,)), ((), ())), preferred_element_type=jnp.float32
        )
        limit = length - first_frame - start
        local = jnp.where(rows < limit, raw[:near] + bias[...], NEG_BIG)
        live_spans = (length + span_len - 1) // span_len
        span_limit = jnp.minimum(first_frame // span_len + 2 * b + lane_spans, live_spans)
        memory = jnp.where(memory_rows < span_limit, raw[near:], NEG_BIG)
        slot = i % scores.shape[0]
        scores[slot, 0:near, :] = local
        scores[slot, near:, :] = memory
        peaks[slot] = jnp.maximum(
            jnp.max(local, axis=0, keepdims=True), jnp.max(memory, axis=0, keepdims=True)
        )

    def weigh_block(i):
        slot = i % scores.shape[0]
        weights[slot] = jnp.exp2(scores[slot] - peaks[slot]).astype(jnp.bfloat16)

    ones = jnp.ones((near + memory_count, LANES), jnp.bfloat16)
    first_of_pair = lax.broadcasted_iota(jnp.int32, (1, 2 * LANES), 1) % LANES < head_size

    def mix_block(i):
        rec, b = divmod(i, blocks)
        at, start = rec * row_count, b * block
        values = jnp.concatenate(
            [value[at + start : at + start + near], value[at + memory_at : at + row_count]], axis=0
        )
        for pair in range(width // LANES):
            columns = slice(pair * LANES, (pair + 1) * LANES)
            pair_rows = slice(pair * 2 * block, (pair + 1) * 2 * block)
            sums = lax.dot_general(
                weights[i % weights.shape[0], :, pair_rows],
                jnp.concatenate([values[:, columns], ones], axis=1),
                (((0,), (0,)), ((), ())),
                preferred_element_type=jnp.float32,
            )
            picked = jnp.where(first_of_pair, sums[:block], sums[block:])
            outs[rec, start : start + block, columns] = (
                picked[:, :LANES] / picked[:, LANES:]
            ).astype(jnp.bfloat16)

    count = 2 * blocks
    ring = scores.shape[0]
    for first in range(0, count, ring):
        for stage in (score_block, weigh_block, mix_block):
            for i in range(first, min(first + ring, count)):
                stage(i)
        for rec in range(2):
            if first < (rec + 1) * blocks <= first + ring:
                out_copies[rec].start()
    for rec in range(2):
        sums_out[rec][...] = jnp.dot(
            members[rec][...], outs[rec], preferred_element_type=jnp.float32
        )
    for copy in piece_copies(1, True) + out_copies:
        copy.wait()


def assemble(scalars, offsets_at, attended, gathered):
    shard = attended[0].shape[1] // 2
    offsets = [
        [pl.multiple_of(scalars[offsets_at + 2 * i + s], LANES) for s in range(2)]
        for i in range(4)
    ]
    for i in range(4):
        for s in range(2):
            gathered[:, pl.ds(offsets[i][s], shard)] = attended[i][:, s * shard : (s + 1) * shard]
    return offsets, shard


def pool_kernel(offsets_at, scalars, base, inverse, route, *refs):
    sums, projections = refs[:4], refs[4:8]
    sent_out, means, pooled = refs[8:]
    shard = sums[0].shape[1] // 2
    offsets = [
        [pl.multiple_of(scalars[offsets_at + 2 * i + s], LANES) for s in range(2)]
        for i in range(4)
    ]
    for i in range(4):
        for s in range(2):
            for lane in range(0, shard, LANES):
                means[:, pl.ds(offsets[i][s] + lane, LANES)] = (
                    sums[i][:, s * shard + lane : s * shard + lane + LANES] * inverse[...]
                ).astype(jnp.bfloat16)
    for i in range(4):
        mixed = jnp.dot(means[...], projections[i][...], preferred_element_type=jnp.float32)
        for s in range(2):
            columns = pl.ds(offsets[i][s], shard)
            pooled[:, columns] = (
                base[:, columns] + mixed[:, s * shard : (s + 1) * shard]
            ).astype(jnp.bfloat16)
    sent_out[...] = jnp.dot(
        route[...], pooled[...], preferred_element_type=jnp.float32
    ).astype(jnp.bfloat16)


def encode_kernel(offsets_at, scalars, *refs):
    attended, projections, frames = refs[:4], refs[4:8], refs[8]
    encoded_out, gathered = refs[9:]
    first_frame, length = scalars[0], scalars[1]
    frame_count, _ = frames.shape
    offsets, shard = assemble(scalars, offsets_at, attended, gathered)
    live = (
        first_frame + lax.broadcasted_iota(jnp.int32, (frame_count, 1), 0) < length
    ).astype(jnp.float32)
    for i in range(4):
        mixed = jnp.dot(
            gathered[...], projections[i][...], preferred_element_type=jnp.float32
        )
        for s in range(2):
            columns = pl.ds(offsets[i][s], shard)
            base = frames[:, columns].astype(jnp.float32)
            encoded_out[:, columns] = (
                (base + mixed[:, s * shard : (s + 1) * shard]) * live
            ).astype(jnp.bfloat16)


def language_kernel(places_at, scalars, received, *refs):
    pieces, out = refs[:-6], refs[-6]
    rows, weights, product, sems, out_sems = refs[-5:]
    count, width = len(pieces), pieces[0].shape[1]
    row_copy = pltpu.make_async_copy(received, rows, sems.at[count])
    row_copy.start()
    copies = [
        pltpu.make_async_copy(piece, weights.at[i], sems.at[i]) for i, piece in enumerate(pieces)
    ]
    for copy in copies:
        copy.start()
    row_copy.wait()
    out_copies = []
    for i in range(count):
        copies[i].wait()
        product[i] = jnp.dot(
            rows[...], weights[i], preferred_element_type=jnp.float32
        ).astype(jnp.bfloat16)
        place = pl.multiple_of(scalars[places_at + i], LANES)
        out_copies.append(
            pltpu.make_async_copy(product.at[i], out.at[:, pl.ds(place, width)], out_sems.at[i])
        )
        out_copies[-1].start()
    for copy in out_copies:
        copy.wait()


def along_x(r, j, _):
    return r, j ^ 1


def along_y(r, j, _):
    return r ^ 2, j


def other_core(r, j, _):
    return r ^ 1, j


def z_up(r, j, count):
    return r, (j + 2) % count


def z_down(r, j, count):
    return r, (j - 2) % count


def relocate(value, core_0, core_1):
    rec_count, time_count = lax.axis_size("rec"), lax.axis_size("tm")
    pairs = []
    for r in range(rec_count):
        for j in range(time_count):
            route = (core_0, core_1)[r % 2]
            if route is not None:
                to_r, to_j = route(r, j, time_count)
                pairs.append((r * time_count + j, to_r * time_count + to_j))
    return lax.ppermute(value, ("rec", "tm"), pairs)


def swap_cores(value):
    return relocate(value, other_core, other_core)


def exchange_blocks(blocks):
    return lax.all_to_all(blocks, "tm", split_axis=0, concat_axis=0, tiled=True)


def per_device(
    frames,
    lengths,
    norm_gain,
    memory_gain,
    qkv_weight,
    out_weight,
    segment_ids,
    owners,
    language_weight,
):
    local_frames = frames[0]
    frame_count, model_width = local_frames.shape
    shard = out_weight.shape[1]
    half = model_width // 2
    time_count = lax.axis_size("tm")
    rec_count = lax.axis_size("rec")
    rec, time = lax.axis_index("rec"), lax.axis_index("tm")
    core, y_half = rec % 2, (rec // 2) % 2
    x, z = time % 2, time // 2
    z_count = time_count // 2
    first_frame = time * frame_count
    length = lengths[0]
    head_size = model_width // H
    bf16 = jnp.bfloat16

    own = jnp.concatenate([qkv_weight, out_weight[None]], axis=0)
    own_a = lax.dynamic_slice_in_dim(own, y_half * half, half, 1)
    later_qkv, later_out, own_a = lax.optimization_barrier((qkv_weight, out_weight, own_a))
    later = jnp.concatenate([later_qkv, later_out[None]], axis=0)
    own_b = lax.dynamic_slice_in_dim(later, (1 - y_half) * half, half, 1)

    def pick(for_core_0, for_core_1):
        return jnp.where(core == 0, for_core_0, for_core_1)

    token_count = owners.shape[2]
    slot_count = 2 * token_count
    capacity = slot_count // time_count
    language_shard = language_weight.shape[1]

    def group_of(of_core, slot):
        return jnp.where(of_core == 0, z + slot, z - slot - 1) % z_count

    numbers = [first_frame, length, core, y_half, capacity]
    offsets_at = len(numbers)
    for of_core in (core, 1 - core):
        for slot in range(2):
            group = group_of(of_core, slot)
            numbers += [(2 * group + x) * shard, (2 * group + 1 - x) * shard]
    places_at = len(numbers)
    numbers += [(rec ^ i) * language_shard for i in range(rec_count)]
    scalars = jnp.stack(numbers).astype(jnp.int32)

    m1 = relocate(own_a, along_x, z_up)
    m2 = relocate(pick(own_a, own_b), z_down, z_up)
    l1 = relocate(language_weight, along_y, along_y)

    pad = 2 * RC
    normed, start_rows, memory = local_call(
        functools.partial(normalise_kernel, C),
        (
            shape_of(frame_count, model_width),
            shape_of(pad, model_width),
            shape_of(time_count, frame_count // C, model_width),
        ),
        (scalars,),
        (local_frames, norm_gain[None], memory_gain[None]),
        flops=10 * frame_count * model_width,
        moved=4 * frame_count * model_width,
    )
    other_length = swap_cores(lengths)
    other_normed = swap_cores(normed)
    ahead = shifted(start_rows, "tm", -1)
    memories = exchange_blocks(memory).reshape(-1, model_width)
    owners_col = owners[0, 0]
    base, member, inverse, route = local_call(
        prepare_kernel,
        (
            shape_of(token_count, model_width, dtype=jnp.float32),
            shape_of(token_count, frame_count),
            shape_of(token_count, LANES, dtype=jnp.float32),
            shape_of(slot_count, token_count),
        ),
        (scalars,),
        (local_frames, segment_ids[0], owners_col.reshape(1, token_count), owners_col),
        flops=2 * token_count * frame_count * model_width,
        moved=2 * frame_count * model_width,
    )
    other_member = swap_cores(member)
    other_ahead = swap_cores(ahead)
    other_memories = swap_cores(memories)

    m3 = relocate(m1, along_y, along_x)
    m4 = relocate(m1, None, z_up)
    m5 = relocate(m2, along_x, z_up)
    m6 = relocate(m3, None, along_y)
    m7 = relocate(pick(m2, m4), along_y, along_x)
    m8 = relocate(m5, along_y, along_x)

    slot_pieces = (
        ((qkv_weight, m1), (out_weight, m2), (m1, m3), (m3, m6)),
        ((m2, m4), (m7, m5), (m5, m7), (m8, m8)),
    )
    block = 2 * C
    width = 2 * shard
    row_count = frame_count + pad + memories.shape[0]
    keys_seen = block + pad + memories.shape[0]
    lanes = width // head_size * block
    attended, sums, outs = [], [], []
    for slot, pieces in enumerate(slot_pieces):
        flat = [p for pair in pieces for p in pair]
        *results, out_piece = local_call(
            functools.partial(attend_kernel, C, RC, head_size, slot == 0),
            (
                shape_of(frame_count, width),
                shape_of(frame_count, width),
                shape_of(token_count, width, dtype=jnp.float32),
                shape_of(token_count, width, dtype=jnp.float32),
                shape_of(model_width, width),
            ),
            (scalars, other_length),
            (member, other_member, normed, ahead, memories, other_normed, other_ahead, other_memories, *flat),
            in_place=6 + len(flat),
            out_in_place=(True, True, False, False, False),
            scratch=(
                pltpu.VMEM((2, frame_count, width), bf16),
                pltpu.VMEM((2 * row_count, model_width), bf16),
                pltpu.VMEM((model_width, 3 * width), bf16),
                pltpu.VMEM((2 * row_count, width), bf16),
                pltpu.VMEM((2 * row_count, width), bf16),
                pltpu.VMEM((2 * row_count, width), bf16),
                pltpu.VMEM((block + pad, lanes), jnp.float32),
                pltpu.VMEM((RING, keys_seen, lanes), jnp.float32),
                pltpu.VMEM((RING, 1, lanes), jnp.float32),
                pltpu.VMEM((RING, keys_seen, lanes), bf16),
                pltpu.SemaphoreType.DMA((24,)),
            ),
            vmem_mib=24,
            flops=12 * frame_count * model_width * width,
            moved=8 * frame_count * model_width,
        )
        attended.append(results[:2])
        sums.append(results[2:])
        outs.append(out_piece)
    other_outs = [swap_cores(w) for w in outs]
    other_attended = [swap_cores(for_other) for _, for_other in attended]

    other_sums = [swap_cores(for_other) for _, for_other in sums]
    projections = (*outs, *other_outs)
    features = (attended[0][0], attended[1][0], *other_attended, *projections)
    sent_rows = local_call(
        functools.partial(pool_kernel, offsets_at),
        shape_of(slot_count, model_width),
        (scalars,),
        (base, inverse, route, sums[0][0], sums[1][0], *other_sums, *projections),
        scratch=(
            pltpu.VMEM((token_count, model_width), bf16),
            pltpu.VMEM((token_count, model_width), bf16),
        ),
        flops=4 * token_count * model_width * model_width,
        moved=6 * frame_count * model_width,
    )
    received = exchange_blocks(
        sent_rows.reshape(time_count, capacity, model_width)
    ).reshape(slot_count, model_width)
    encoded = local_call(
        functools.partial(encode_kernel, offsets_at),
        shape_of(frame_count, model_width),
        (scalars,),
        (*features, local_frames),
        scratch=(pltpu.VMEM((frame_count, model_width), bf16),),
        flops=2 * frame_count * model_width * model_width,
        moved=6 * frame_count * model_width,
    )
    language_pieces = (language_weight, swap_cores(language_weight), l1, swap_cores(l1))
    lm_out = local_call(
        functools.partial(language_kernel, places_at),
        shape_of(slot_count, rec_count * language_shard),
        (scalars,),
        (received, *language_pieces),
        in_place=1 + rec_count,
        out_in_place=True,
        vmem_mib=62,
        scratch=(
            pltpu.VMEM((slot_count, model_width), bf16),
            pltpu.VMEM((rec_count, model_width, language_shard), bf16),
            pltpu.VMEM((rec_count, slot_count, language_shard), bf16),
            pltpu.SemaphoreType.DMA((rec_count + 1,)),
            pltpu.SemaphoreType.DMA((rec_count,)),
        ),
        flops=2 * slot_count * model_width * rec_count * language_shard,
        moved=2 * model_width * rec_count * language_shard,
    )
    return (encoded[None], lm_out[None, None])


def solution(mesh):
    in_specs = (
        P("rec", "tm", None),
        P("rec"),
        P(),
        P(),
        P(None, None, "tm"),
        P(None, "tm"),
        P("rec", "tm", None),
        P("rec", "tm", None, None),
        P(None, "rec"),
    )
    out_specs = (P("rec", "tm", None), P("rec", "tm", None, None))
    rec_count, time_count = mesh.shape["rec"], mesh.shape["tm"]
    paired = shard_map_of(mesh, in_specs, out_specs, per_device)
    plain = shard_map_of(mesh, in_specs, out_specs, plain_device)

    def run(*arrays):
        shard = arrays[5].shape[1] // time_count
        fits = rec_count == 4 and time_count == 8 and shard % LANES == 0
        return (paired if fits else plain)(*arrays)

    return run


def shard_map_of(mesh, in_specs, out_specs, body):
    return jax.shard_map(
        body, mesh=mesh, in_specs=in_specs, out_specs=out_specs, check_vma=False
    )
```

```python
import functools

import jax
import jax.numpy as jnp
from jax import lax
from jax.experimental import pallas as pl
from jax.experimental.pallas import tpu as pltpu
from jax.sharding import PartitionSpec as P


H = 16
C = 32
RC = 8


EPS_NORM = 1e-05
EPS_MEMORY = 1e-06
NEG_BIG = -1e30
LANES = 128
RING = 16
LOG2_E = 1.4426950408889634


def shifted(block, axis, distance):
    devices = range(lax.axis_size(axis))
    route = [(i - distance, i) for i in devices if i - distance in devices]
    return lax.ppermute(block, axis, route)


def layer_norm(values_in, gain):
    values_in = values_in.astype(jnp.float32)
    centre = jnp.mean(values_in, axis=-1, keepdims=True)
    centred = values_in - centre
    spread = jnp.mean(centred * centred, axis=-1, keepdims=True)
    return centred * lax.rsqrt(spread + EPS_NORM) * gain


def span_memory(normed, live_mask, gain, span_len):
    model_width = normed.shape[1]
    masked = jnp.where(live_mask[:, None], normed.astype(jnp.float32), jnp.float32(0.0))
    owner_sums = masked.reshape(-1, span_len, model_width).sum(axis=1)
    counts = live_mask.reshape(-1, span_len).astype(jnp.float32).sum(axis=1)
    means = owner_sums / jnp.maximum(counts, 1.0)[:, None]
    power = jnp.mean(means * means, axis=-1, keepdims=True)
    return (means * lax.rsqrt(power + EPS_MEMORY) * gain).astype(jnp.bfloat16)


def block_size():
    return 256


def local_part(query, keys, values, first_frame, length, head_count, span_len, right_len):
    frame_count, model_width = query.shape
    head_size = model_width // head_count
    group_rows = 4 * span_len
    group_count = frame_count // group_rows
    block_rows = block_size()
    query_blocks = query.reshape(group_count, group_rows, head_count, head_size)
    key_blocks = keys[:frame_count].reshape(group_count, group_rows, head_count, head_size)
    value_blocks = values[:frame_count].reshape(group_count, group_rows, head_count, head_size)
    key_tail = keys[frame_count:].reshape(1, right_len, head_count, head_size)
    value_tail = values[frame_count:].reshape(1, right_len, head_count, head_size)
    key_all = jnp.concatenate(
        [key_blocks, jnp.concatenate([key_blocks[1:, :right_len], key_tail], axis=0)], axis=1
    )
    value_all = jnp.concatenate(
        [value_blocks, jnp.concatenate([value_blocks[1:, :right_len], value_tail], axis=0)], axis=1
    )
    start_offsets = jnp.arange(group_count, dtype=jnp.int32)[:, None] * group_rows
    query_pos = first_frame + start_offsets + jnp.arange(group_rows, dtype=jnp.int32)[None, :]
    key_pos = first_frame + jnp.concatenate(
        [
            start_offsets + jnp.arange(group_rows, dtype=jnp.int32)[None, :],
            start_offsets + group_rows + jnp.arange(right_len, dtype=jnp.int32)[None, :],
        ],
        axis=1,
    )
    query_span = query_pos // span_len
    span_end = (query_span + 1) * span_len
    same = (key_pos // span_len)[:, None, :] == query_span[:, :, None]
    ahead = (key_pos[:, None, :] >= span_end[:, :, None]) & (
        key_pos[:, None, :] < span_end[:, :, None] + right_len
    )
    allowed = (same | ahead) & (key_pos < length)[:, None, :]
    scores = jnp.einsum(
        "gqhd,gkhd->ghqk", query_blocks, key_all, preferred_element_type=jnp.float32
    ) * head_size ** (-0.5)
    scores = jnp.where(allowed[:, None], scores, NEG_BIG)
    row_peak = jnp.max(scores, axis=-1)
    weights = jnp.where(allowed[:, None], jnp.exp(scores - row_peak[..., None]), jnp.float32(0.0))
    row_total = jnp.sum(weights, axis=-1)
    accum = jnp.einsum(
        "ghqk,gkhd->ghqd",
        weights.astype(jnp.bfloat16),
        value_all,
        preferred_element_type=jnp.float32,
    )
    block_count = frame_count // block_rows
    row_peak = (
        row_peak.transpose(1, 0, 2).reshape(head_count, block_count, block_rows).transpose(1, 0, 2)
    )
    row_total = (
        row_total.transpose(1, 0, 2).reshape(head_count, block_count, block_rows).transpose(1, 0, 2)
    )
    accum = (
        accum.transpose(1, 0, 2, 3)
        .reshape(head_count, block_count, block_rows, head_size)
        .transpose(1, 0, 2, 3)
    )
    return (row_peak, row_total, accum)


def memory_update(
    carry, memory_keys, memory_values, query, first_frame, length, head_count, span_len
):
    row_peak, row_total, accum = carry
    block_count, _, block_rows = row_peak.shape
    row_count, model_width = memory_keys.shape
    head_size = model_width // head_count
    mem_keys = memory_keys.reshape(row_count, head_count, head_size)
    mem_values = memory_values.reshape(row_count, head_count, head_size)
    mem_index = jnp.arange(row_count, dtype=jnp.int32)
    mem_live = mem_index * span_len < length
    query_blocks = query.reshape(block_count, block_rows, head_count, head_size)
    positions = first_frame + jnp.arange(block_count * block_rows, dtype=jnp.int32).reshape(
        block_count, block_rows
    )

    def one_block(packed):
        query_now, pos_now, peak_now, total_now, accum_now = packed
        scores = jnp.einsum(
            "qhd,khd->hqk", query_now, mem_keys, preferred_element_type=jnp.float32
        ) * head_size ** (-0.5)
        allowed = (mem_index[None, :] < (pos_now // span_len)[:, None]) & mem_live[None, :]
        scores = jnp.where(allowed[None], scores, NEG_BIG)
        new_peak = jnp.maximum(peak_now, jnp.max(scores, axis=-1))
        weights = jnp.where(allowed[None], jnp.exp(scores - new_peak[..., None]), jnp.float32(0.0))
        factor = jnp.exp(peak_now - new_peak)
        total_next = total_now * factor + jnp.sum(weights, axis=-1)
        accum_next = accum_now * factor[..., None] + jnp.einsum(
            "hqk,khd->hqd",
            weights.astype(jnp.bfloat16),
            mem_values,
            preferred_element_type=jnp.float32,
        )
        return (new_peak, total_next, accum_next)

    return lax.map(one_block, (query_blocks, positions, row_peak, row_total, accum))


def finish(carry, frame_count, model_width):
    _, row_total, accum = carry
    result = accum / row_total[..., None]
    return result.transpose(0, 2, 1, 3).reshape(frame_count, model_width).astype(jnp.bfloat16)


def dispatch_matrix(owner_ids, owner_count, capacity):
    choose = (owner_ids[:, None] == jnp.arange(owner_count, dtype=jnp.int32)[None, :]).astype(
        jnp.int32
    )
    before = jnp.cumsum(choose, axis=0) - choose
    slot_index = jnp.sum(before * choose, axis=1)
    target = owner_ids * capacity + slot_index
    slot_rows = jnp.arange(owner_count * capacity, dtype=jnp.int32)
    return (slot_rows[:, None] == target[None, :]).astype(jnp.bfloat16)


def plain_device(
    frames,
    lengths,
    norm_gain,
    memory_gain,
    qkv_weight,
    out_weight,
    segment_ids,
    owners,
    language_weight,
):
    local_frames = frames[0]
    frame_count, model_width = local_frames.shape
    head_count = H
    time_count = lax.axis_size("tm")
    first_frame = lax.axis_index("tm") * frame_count
    length = lengths[0]
    live_mask = first_frame + jnp.arange(frame_count, dtype=jnp.int32) < length
    right_frames = shifted(local_frames[:RC], "tm", -1)
    normed = layer_norm(local_frames, norm_gain).astype(jnp.bfloat16)
    normed_right = layer_norm(right_frames, norm_gain).astype(jnp.bfloat16)
    memory = span_memory(normed, live_mask, memory_gain, C)
    stacked_rows = jnp.concatenate([normed, normed_right, memory], axis=0)
    projected = jnp.einsum(
        "fd,kdw->kfw",
        stacked_rows,
        lax.all_gather(qkv_weight, "tm", axis=2, tiled=True),
        preferred_element_type=jnp.float32,
    ).astype(jnp.bfloat16)
    split_at = frame_count + RC
    query = projected[0, :frame_count]
    keys = projected[1, :split_at]
    values = projected[2, :split_at]
    memory_keys = projected[1, split_at:]
    memory_values = projected[2, split_at:]
    carry = local_part(query, keys, values, first_frame, length, head_count, C, RC)
    carry = memory_update(
        carry,
        lax.all_gather(memory_keys, "tm", axis=0, tiled=True),
        lax.all_gather(memory_values, "tm", axis=0, tiled=True),
        query,
        first_frame,
        length,
        head_count,
        C,
    )
    attended = finish(carry, frame_count, model_width)
    output_proj = jnp.dot(
        attended,
        lax.all_gather(out_weight, "tm", axis=1, tiled=True),
        preferred_element_type=jnp.float32,
    )
    encoded = jnp.where(
        live_mask[:, None], local_frames.astype(jnp.float32) + output_proj, jnp.float32(0.0)
    ).astype(jnp.bfloat16)
    token_count = owners.shape[2]
    segments = segment_ids[0, 0]
    owner_indicator = (
        segments[None, :] == jnp.arange(token_count, dtype=jnp.int32)[:, None]
    ).astype(jnp.bfloat16)
    owner_sums = jnp.dot(owner_indicator, encoded, preferred_element_type=jnp.float32)
    counts = jnp.sum(owner_indicator.astype(jnp.float32), axis=1)
    pooled_rows = (owner_sums / counts[:, None]).astype(jnp.bfloat16)
    slot_count = 2 * token_count
    capacity = slot_count // time_count
    route_matrix = dispatch_matrix(owners[0, 0, :, 0], time_count, capacity)
    sent_rows = jnp.dot(route_matrix, pooled_rows, preferred_element_type=jnp.float32).astype(
        jnp.bfloat16
    )
    received = lax.all_to_all(
        sent_rows.reshape(time_count, capacity, model_width),
        "tm",
        split_axis=0,
        concat_axis=0,
        tiled=True,
    )
    received = received.reshape(slot_count, model_width)
    lm_out = jnp.dot(
        received,
        lax.all_gather(language_weight, "rec", axis=1, tiled=True),
        preferred_element_type=jnp.float32,
    ).astype(jnp.bfloat16)
    return (encoded[None], lm_out[None, None])


def vmem_spec():
    return pl.BlockSpec(memory_space=pltpu.VMEM)


def smem_spec():
    return pl.BlockSpec(memory_space=pltpu.SMEM)


def local_call(kernel, out_shapes, scalars, operands, scratch=(), in_place=0, out_in_place=False, vmem_mib=16, flops=0, moved=0):
    whole = len(operands) - in_place
    anywhere = pl.BlockSpec(memory_space=pl.ANY)
    if isinstance(out_shapes, tuple):
        stays = out_in_place or (False,) * len(out_shapes)
        out_specs = tuple(anywhere if stay else vmem_spec() for stay in stays)
    else:
        out_specs = anywhere if out_in_place else vmem_spec()
    return pl.pallas_call(
        kernel,
        out_shape=out_shapes,
        in_specs=[smem_spec()] * len(scalars) + [vmem_spec()] * whole + [anywhere] * in_place,
        out_specs=out_specs,
        compiler_params=pltpu.CompilerParams(vmem_limit_bytes=vmem_mib << 20),
        scratch_shapes=list(scratch),
        cost_estimate=pl.CostEstimate(flops=flops, bytes_accessed=moved, transcendentals=0),
    )(*scalars, *operands)


def shape_of(*dims, dtype=jnp.bfloat16):
    return jax.ShapeDtypeStruct(dims, dtype)


def normalise_kernel(
    span_len, scalars, frames, gain, memory_gain, normed_out, ahead_out, memory_out
):
    first_frame, length = scalars[0], scalars[1]
    frame_count, _ = frames.shape
    span_count = frame_count // span_len
    values = frames[...].astype(jnp.float32)
    centre = jnp.mean(values, axis=-1, keepdims=True)
    centred = values - centre
    spread = jnp.mean(centred * centred, axis=-1, keepdims=True)
    normed = (centred * lax.rsqrt(spread + EPS_NORM) * gain[...]).astype(jnp.bfloat16)
    normed_out[...] = normed
    ahead_out[...] = normed[: ahead_out.shape[0]]
    spans = lax.broadcasted_iota(jnp.int32, (span_count, frame_count), 0)
    places = lax.broadcasted_iota(jnp.int32, (span_count, frame_count), 1)
    member = (places >= spans * span_len) & (places < (spans + 1) * span_len)
    member = member & (places < length - first_frame)
    sums = jnp.dot(
        member.astype(jnp.bfloat16), normed, preferred_element_type=jnp.float32
    )
    counts = jnp.sum(member.astype(jnp.float32), axis=-1, keepdims=True)
    means = sums / jnp.maximum(counts, 1.0)
    power = jnp.mean(means * means, axis=-1, keepdims=True)
    memory = (means * lax.rsqrt(power + EPS_MEMORY) * memory_gain[...]).astype(jnp.bfloat16)
    for copy in range(memory_out.shape[0]):
        memory_out[copy] = memory


def prepare_kernel(scalars, frames, segments, owners_row, owners_col, base_out, member_out, count_out, route_out):
    first_frame, length, capacity = scalars[0], scalars[1], scalars[4]
    token_count, frame_count = member_out.shape
    tokens = lax.broadcasted_iota(jnp.int32, (token_count, frame_count), 0)
    places = first_frame + lax.broadcasted_iota(jnp.int32, (token_count, frame_count), 1)
    member = (segments[...] == tokens).astype(jnp.float32)
    counts = jnp.sum(member, axis=1, keepdims=True)
    live_member = jnp.where(places < length, member, 0.0).astype(jnp.bfloat16)
    earlier = lax.broadcasted_iota(jnp.int32, (token_count, token_count), 0)
    later = lax.broadcasted_iota(jnp.int32, (token_count, token_count), 1)
    clash = (owners_col[...] == owners_row[...]) & (earlier < later)
    slot = jnp.sum(clash.astype(jnp.int32), axis=0, keepdims=True)
    target = owners_row[...] * capacity + slot
    slots = lax.broadcasted_iota(jnp.int32, route_out.shape, 0)
    route_out[...] = (slots == target).astype(jnp.bfloat16)
    member_out[...] = live_member
    count_out[...] = jnp.broadcast_to(1.0 / counts, count_out.shape)
    base_out[...] = (
        jnp.dot(live_member, frames[...], preferred_element_type=jnp.float32) / counts
    )


def attend_kernel(span_len, right_len, head_size, starts_here, scalars, other_length, *refs):
    members, sources, pieces = refs[:2], refs[2:8], refs[8:16]
    out_refs, sums_out, projection = refs[16:18], refs[18:20], refs[20]
    outs, rows_in, weight, query, key, value, bias, scores, peaks, weights, sems = refs[21:]
    first_frame, core, y_half = scalars[0], scalars[2], scalars[3]
    frame_count, model_width = sources[0].shape
    half = model_width // 2
    width = out_refs[0].shape[1]
    out_copies = [
        pltpu.make_async_copy(outs.at[rec], out_refs[rec], sems.at[22 + rec]) for rec in range(2)
    ]
    heads = width // head_size
    block = 2 * span_len
    blocks = frame_count // block
    near = bias.shape[0]
    memory_at = frame_count + near - block
    row_count = rows_in.shape[0] // 2
    memory_count = row_count - memory_at
    lanes = heads * block

    def piece_copies(of_core, projected):
        places = (y_half * half, (1 - y_half) * half)
        copies = []
        for side in range(2):
            place = pl.ds(pl.multiple_of(places[side], half), half)
            for shard in range(2):
                piece = pieces[4 * shard + 2 * side + of_core]
                raw = starts_here and of_core == 0 and shard == 0
                shard_width = pieces[-1].shape[2]
                index = 2 * side + shard
                for part in (3,) if projected else (0, 1, 2):
                    target = projection if projected else weight
                    start = shard * shard_width + (0 if projected else part * width)
                    if raw:
                        source = pieces[2].at[place] if projected else pieces[0].at[part, place]
                    else:
                        source = piece.at[part]
                    copies.append(
                        pltpu.make_async_copy(
                            source,
                            target.at[place, pl.ds(start, shard_width)],
                            sems.at[4 * part + index],
                        )
                    )
        return copies

    row_copies = []
    for rec in range(2):
        at = rec * row_count
        for i, (start, size) in enumerate(
            ((0, frame_count), (frame_count, near - block), (memory_at, memory_count))
        ):
            row_copies.append(
                pltpu.make_async_copy(
                    sources[3 * rec + i], rows_in.at[pl.ds(at + start, size)], sems.at[16 + 3 * rec + i]
                )
            )

    for copy in row_copies:
        copy.start()
    for of_core in range(2):

        @pl.when(core == of_core)
        def _():
            for copy in piece_copies(of_core, False) + piece_copies(of_core, True):
                copy.start()

    rows = lax.broadcasted_iota(jnp.int32, (near, lanes), 0)
    spans = (lax.broadcasted_iota(jnp.int32, (near, lanes), 1) % block) // span_len
    same = (rows >= spans * span_len) & (rows < (spans + 1) * span_len + right_len)
    bias[...] = jnp.where(same, jnp.float32(0.0), jnp.float32(NEG_BIG))
    lane_spans = (lax.broadcasted_iota(jnp.int32, (1, lanes), 1) % block) // span_len
    memory_rows = lax.broadcasted_iota(jnp.int32, (memory_count, lanes), 0)
    feature_head = lax.broadcasted_iota(jnp.int32, (1, width), 1) // head_size
    head_masks = [(feature_head == h).astype(jnp.bfloat16) for h in range(heads)]
    scale = head_size ** (-0.5) * LOG2_E

    for copy in row_copies + piece_copies(1, False):
        copy.wait()
    for part, target in enumerate((query, key, value)):
        mixed = jnp.dot(
            rows_in[...],
            weight[:, part * width : (part + 1) * width],
            preferred_element_type=jnp.float32,
        )
        target[...] = (mixed * scale if part == 0 else mixed).astype(jnp.bfloat16)

    def score_block(i):
        rec, b = divmod(i, blocks)
        at, start = rec * row_count, b * block
        length = scalars[1] if rec == 0 else other_length[0]
        q_now = query[at + start : at + start + block]
        stacked = jnp.concatenate([q_now * m for m in head_masks], axis=0)
        keys = jnp.concatenate(
            [key[at + start : at + start + near], key[at + memory_at : at + row_count]], axis=0
        )
        raw = lax.dot_general(
            keys, stacked, (((1,), (1,)), ((), ())), preferred_element_type=jnp.float32
        )
        limit = length - first_frame - start
        local = jnp.where(rows < limit, raw[:near] + bias[...], NEG_BIG)
        live_spans = (length + span_len - 1) // span_len
        span_limit = jnp.minimum(first_frame // span_len + 2 * b + lane_spans, live_spans)
        memory = jnp.where(memory_rows < span_limit, raw[near:], NEG_BIG)
        slot = i % scores.shape[0]
        scores[slot, 0:near, :] = local
        scores[slot, near:, :] = memory
        peaks[slot] = jnp.maximum(
            jnp.max(local, axis=0, keepdims=True), jnp.max(memory, axis=0, keepdims=True)
        )

    def weigh_block(i):
        slot = i % scores.shape[0]
        weights[slot] = jnp.exp2(scores[slot] - peaks[slot]).astype(jnp.bfloat16)

    ones = jnp.ones((near + memory_count, LANES), jnp.bfloat16)
    first_of_pair = lax.broadcasted_iota(jnp.int32, (1, 2 * LANES), 1) % LANES < head_size

    def mix_block(i):
        rec, b = divmod(i, blocks)
        at, start = rec * row_count, b * block
        values = jnp.concatenate(
            [value[at + start : at + start + near], value[at + memory_at : at + row_count]], axis=0
        )
        for pair in range(width // LANES):
            columns = slice(pair * LANES, (pair + 1) * LANES)
            pair_rows = slice(pair * 2 * block, (pair + 1) * 2 * block)
            sums = lax.dot_general(
                weights[i % weights.shape[0], :, pair_rows],
                jnp.concatenate([values[:, columns], ones], axis=1),
                (((0,), (0,)), ((), ())),
                preferred_element_type=jnp.float32,
            )
            picked = jnp.where(first_of_pair, sums[:block], sums[block:])
            outs[rec, start : start + block, columns] = (
                picked[:, :LANES] / picked[:, LANES:]
            ).astype(jnp.bfloat16)

    count = 2 * blocks
    ring = scores.shape[0]
    for first in range(0, count, ring):
        for stage in (score_block, weigh_block, mix_block):
            for i in range(first, min(first + ring, count)):
                stage(i)
        for rec in range(2):
            if first < (rec + 1) * blocks <= first + ring:
                out_copies[rec].start()
    for rec in range(2):
        sums_out[rec][...] = jnp.dot(
            members[rec][...], outs[rec], preferred_element_type=jnp.float32
        )
    for copy in piece_copies(1, True) + out_copies:
        copy.wait()


def assemble(scalars, offsets_at, attended, gathered):
    shard = attended[0].shape[1] // 2
    offsets = [
        [pl.multiple_of(scalars[offsets_at + 2 * i + s], LANES) for s in range(2)]
        for i in range(4)
    ]
    for i in range(4):
        for s in range(2):
            gathered[:, pl.ds(offsets[i][s], shard)] = attended[i][:, s * shard : (s + 1) * shard]
    return offsets, shard


def pool_kernel(offsets_at, scalars, base, inverse, route, *refs):
    sums, projections = refs[:4], refs[4:8]
    sent_out, means, pooled = refs[8:]
    shard = sums[0].shape[1] // 2
    offsets = [
        [pl.multiple_of(scalars[offsets_at + 2 * i + s], LANES) for s in range(2)]
        for i in range(4)
    ]
    for i in range(4):
        for s in range(2):
            for lane in range(0, shard, LANES):
                means[:, pl.ds(offsets[i][s] + lane, LANES)] = (
                    sums[i][:, s * shard + lane : s * shard + lane + LANES] * inverse[...]
                ).astype(jnp.bfloat16)
    for i in range(4):
        mixed = jnp.dot(means[...], projections[i][...], preferred_element_type=jnp.float32)
        for s in range(2):
            columns = pl.ds(offsets[i][s], shard)
            pooled[:, columns] = (
                base[:, columns] + mixed[:, s * shard : (s + 1) * shard]
            ).astype(jnp.bfloat16)
    sent_out[...] = jnp.dot(
        route[...], pooled[...], preferred_element_type=jnp.float32
    ).astype(jnp.bfloat16)


def encode_kernel(offsets_at, scalars, *refs):
    attended, projections, frames = refs[:4], refs[4:8], refs[8]
    encoded_out, gathered = refs[9:]
    first_frame, length = scalars[0], scalars[1]
    frame_count, _ = frames.shape
    offsets, shard = assemble(scalars, offsets_at, attended, gathered)
    live = (
        first_frame + lax.broadcasted_iota(jnp.int32, (frame_count, 1), 0) < length
    ).astype(jnp.float32)
    for i in range(4):
        mixed = jnp.dot(
            gathered[...], projections[i][...], preferred_element_type=jnp.float32
        )
        for s in range(2):
            columns = pl.ds(offsets[i][s], shard)
            base = frames[:, columns].astype(jnp.float32)
            encoded_out[:, columns] = (
                (base + mixed[:, s * shard : (s + 1) * shard]) * live
            ).astype(jnp.bfloat16)


def language_kernel(places_at, scalars, received, *refs):
    pieces, out = refs[:-6], refs[-6]
    rows, weights, product, sems, out_sems = refs[-5:]
    count, width = len(pieces), pieces[0].shape[1]
    row_copy = pltpu.make_async_copy(received, rows, sems.at[count])
    row_copy.start()
    copies = [
        pltpu.make_async_copy(piece, weights.at[i], sems.at[i]) for i, piece in enumerate(pieces)
    ]
    for copy in copies:
        copy.start()
    row_copy.wait()
    out_copies = []
    for i in range(count):
        copies[i].wait()
        product[i] = jnp.dot(
            rows[...], weights[i], preferred_element_type=jnp.float32
        ).astype(jnp.bfloat16)
        place = pl.multiple_of(scalars[places_at + i], LANES)
        out_copies.append(
            pltpu.make_async_copy(product.at[i], out.at[:, pl.ds(place, width)], out_sems.at[i])
        )
        out_copies[-1].start()
    for copy in out_copies:
        copy.wait()


def along_x(r, j, _):
    return r, j ^ 1


def along_y(r, j, _):
    return r ^ 2, j


def other_core(r, j, _):
    return r ^ 1, j


def z_up(r, j, count):
    return r, (j + 2) % count


def z_down(r, j, count):
    return r, (j - 2) % count


def relocate(value, core_0, core_1):
    rec_count, time_count = lax.axis_size("rec"), lax.axis_size("tm")
    pairs = []
    for r in range(rec_count):
        for j in range(time_count):
            route = (core_0, core_1)[r % 2]
            if route is not None:
                to_r, to_j = route(r, j, time_count)
                pairs.append((r * time_count + j, to_r * time_count + to_j))
    return lax.ppermute(value, ("rec", "tm"), pairs)


def swap_cores(value):
    return relocate(value, other_core, other_core)


def exchange_blocks(blocks):
    return lax.all_to_all(blocks, "tm", split_axis=0, concat_axis=0, tiled=True)


def per_device(
    frames,
    lengths,
    norm_gain,
    memory_gain,
    qkv_weight,
    out_weight,
    segment_ids,
    owners,
    language_weight,
):
    local_frames = frames[0]
    frame_count, model_width = local_frames.shape
    shard = out_weight.shape[1]
    half = model_width // 2
    time_count = lax.axis_size("tm")
    rec_count = lax.axis_size("rec")
    rec, time = lax.axis_index("rec"), lax.axis_index("tm")
    core, y_half = rec % 2, (rec // 2) % 2
    x, z = time % 2, time // 2
    z_count = time_count // 2
    first_frame = time * frame_count
    length = lengths[0]
    head_size = model_width // H
    bf16 = jnp.bfloat16

    own = jnp.concatenate([qkv_weight, out_weight[None]], axis=0)
    own_a = lax.dynamic_slice_in_dim(own, y_half * half, half, 1)
    later_qkv, later_out, own_a = lax.optimization_barrier((qkv_weight, out_weight, own_a))
    later = jnp.concatenate([later_qkv, later_out[None]], axis=0)
    own_b = lax.dynamic_slice_in_dim(later, (1 - y_half) * half, half, 1)

    def pick(for_core_0, for_core_1):
        return jnp.where(core == 0, for_core_0, for_core_1)

    token_count = owners.shape[2]
    slot_count = 2 * token_count
    capacity = slot_count // time_count
    language_shard = language_weight.shape[1]

    def group_of(of_core, slot):
        return jnp.where(of_core == 0, z + slot, z - slot - 1) % z_count

    numbers = [first_frame, length, core, y_half, capacity]
    offsets_at = len(numbers)
    for of_core in (core, 1 - core):
        for slot in range(2):
            group = group_of(of_core, slot)
            numbers += [(2 * group + x) * shard, (2 * group + 1 - x) * shard]
    places_at = len(numbers)
    numbers += [(rec ^ i) * language_shard for i in range(rec_count)]
    scalars = jnp.stack(numbers).astype(jnp.int32)

    m1 = relocate(own_a, along_x, z_up)
    m2 = relocate(pick(own_a, own_b), z_down, z_up)
    l1 = relocate(language_weight, along_y, along_y)

    pad = 2 * RC
    normed, start_rows, memory = local_call(
        functools.partial(normalise_kernel, C),
        (
            shape_of(frame_count, model_width),
            shape_of(pad, model_width),
            shape_of(time_count, frame_count // C, model_width),
        ),
        (scalars,),
        (local_frames, norm_gain[None], memory_gain[None]),
        flops=10 * frame_count * model_width,
        moved=4 * frame_count * model_width,
    )
    other_length = swap_cores(lengths)
    other_normed = swap_cores(normed)
    ahead = shifted(start_rows, "tm", -1)
    memories = exchange_blocks(memory).reshape(-1, model_width)
    owners_col = owners[0, 0]
    base, member, inverse, route = local_call(
        prepare_kernel,
        (
            shape_of(token_count, model_width, dtype=jnp.float32),
            shape_of(token_count, frame_count),
            shape_of(token_count, LANES, dtype=jnp.float32),
            shape_of(slot_count, token_count),
        ),
        (scalars,),
        (local_frames, segment_ids[0], owners_col.reshape(1, token_count), owners_col),
        flops=2 * token_count * frame_count * model_width,
        moved=2 * frame_count * model_width,
    )
    other_member = swap_cores(member)
    other_ahead = swap_cores(ahead)
    other_memories = swap_cores(memories)

    m3 = relocate(m1, along_y, along_x)
    m4 = relocate(m1, None, z_up)
    m5 = relocate(m2, along_x, z_up)
    m6 = relocate(m3, None, along_y)
    m7 = relocate(pick(m2, m4), along_y, along_x)
    m8 = relocate(m5, along_y, along_x)

    slot_pieces = (
        ((own_a, m1), (own_b, m2), (m1, m3), (m3, m6)),
        ((m2, m4), (m7, m5), (m5, m7), (m8, m8)),
    )
    block = 2 * C
    width = 2 * shard
    row_count = frame_count + pad + memories.shape[0]
    keys_seen = block + pad + memories.shape[0]
    lanes = width // head_size * block
    attended, sums, outs = [], [], []
    for pieces in slot_pieces:
        flat = [p for pair in pieces for p in pair]
        *results, out_piece = local_call(
            functools.partial(attend_kernel, C, RC, head_size, False),
            (
                shape_of(frame_count, width),
                shape_of(frame_count, width),
                shape_of(token_count, width, dtype=jnp.float32),
                shape_of(token_count, width, dtype=jnp.float32),
                shape_of(model_width, width),
            ),
            (scalars, other_length),
            (member, other_member, normed, ahead, memories, other_normed, other_ahead, other_memories, *flat),
            in_place=6 + len(flat),
            out_in_place=(True, True, False, False, False),
            scratch=(
                pltpu.VMEM((2, frame_count, width), bf16),
                pltpu.VMEM((2 * row_count, model_width), bf16),
                pltpu.VMEM((model_width, 3 * width), bf16),
                pltpu.VMEM((2 * row_count, width), bf16),
                pltpu.VMEM((2 * row_count, width), bf16),
                pltpu.VMEM((2 * row_count, width), bf16),
                pltpu.VMEM((block + pad, lanes), jnp.float32),
                pltpu.VMEM((RING, keys_seen, lanes), jnp.float32),
                pltpu.VMEM((RING, 1, lanes), jnp.float32),
                pltpu.VMEM((RING, keys_seen, lanes), bf16),
                pltpu.SemaphoreType.DMA((24,)),
            ),
            vmem_mib=20,
            flops=12 * frame_count * model_width * width,
            moved=8 * frame_count * model_width,
        )
        attended.append(results[:2])
        sums.append(results[2:])
        outs.append(out_piece)
    other_outs = [swap_cores(w) for w in outs]
    other_attended = [swap_cores(for_other) for _, for_other in attended]

    other_sums = [swap_cores(for_other) for _, for_other in sums]
    projections = (*outs, *other_outs)
    features = (attended[0][0], attended[1][0], *other_attended, *projections)
    sent_rows = local_call(
        functools.partial(pool_kernel, offsets_at),
        shape_of(slot_count, model_width),
        (scalars,),
        (base, inverse, route, sums[0][0], sums[1][0], *other_sums, *projections),
        scratch=(
            pltpu.VMEM((token_count, model_width), bf16),
            pltpu.VMEM((token_count, model_width), bf16),
        ),
        flops=4 * token_count * model_width * model_width,
        moved=6 * frame_count * model_width,
    )
    received = exchange_blocks(
        sent_rows.reshape(time_count, capacity, model_width)
    ).reshape(slot_count, model_width)
    encoded = local_call(
        functools.partial(encode_kernel, offsets_at),
        shape_of(frame_count, model_width),
        (scalars,),
        (*features, local_frames),
        scratch=(pltpu.VMEM((frame_count, model_width), bf16),),
        flops=2 * frame_count * model_width * model_width,
        moved=6 * frame_count * model_width,
    )
    language_pieces = (language_weight, swap_cores(language_weight), l1, swap_cores(l1))
    lm_out = local_call(
        functools.partial(language_kernel, places_at),
        shape_of(slot_count, rec_count * language_shard),
        (scalars,),
        (received, *language_pieces),
        in_place=1 + rec_count,
        out_in_place=True,
        scratch=(
            pltpu.VMEM((slot_count, model_width), bf16),
            pltpu.VMEM((rec_count, model_width, language_shard), bf16),
            pltpu.VMEM((rec_count, slot_count, language_shard), bf16),
            pltpu.SemaphoreType.DMA((rec_count + 1,)),
            pltpu.SemaphoreType.DMA((rec_count,)),
        ),
        flops=2 * slot_count * model_width * rec_count * language_shard,
        moved=2 * model_width * rec_count * language_shard,
    )
    return (encoded[None], lm_out[None, None])


def solution(mesh):
    in_specs = (
        P("rec", "tm", None),
        P("rec"),
        P(),
        P(),
        P(None, None, "tm"),
        P(None, "tm"),
        P("rec", "tm", None),
        P("rec", "tm", None, None),
        P(None, "rec"),
    )
    out_specs = (P("rec", "tm", None), P("rec", "tm", None, None))
    rec_count, time_count = mesh.shape["rec"], mesh.shape["tm"]
    paired = shard_map_of(mesh, in_specs, out_specs, per_device)
    plain = shard_map_of(mesh, in_specs, out_specs, plain_device)

    def run(*arrays):
        shard = arrays[5].shape[1] // time_count
        fits = rec_count == 4 and time_count == 8 and shard % LANES == 0
        return (paired if fits else plain)(*arrays)

    return run


def shard_map_of(mesh, in_specs, out_specs, body):
    return jax.shard_map(
        body, mesh=mesh, in_specs=in_specs, out_specs=out_specs, check_vma=False
    )
```

```python
import functools

import jax
import jax.numpy as jnp
from jax import lax
from jax.experimental import pallas as pl
from jax.experimental.pallas import tpu as pltpu
from jax.sharding import PartitionSpec as P


H = 16
C = 32
RC = 8


EPS_NORM = 1e-05
EPS_MEMORY = 1e-06
NEG_BIG = -1e30
LANES = 128
RING = 16
LOG2_E = 1.4426950408889634


def shifted(block, axis, distance):
    devices = range(lax.axis_size(axis))
    route = [(i - distance, i) for i in devices if i - distance in devices]
    return lax.ppermute(block, axis, route)


def layer_norm(values_in, gain):
    values_in = values_in.astype(jnp.float32)
    centre = jnp.mean(values_in, axis=-1, keepdims=True)
    centred = values_in - centre
    spread = jnp.mean(centred * centred, axis=-1, keepdims=True)
    return centred * lax.rsqrt(spread + EPS_NORM) * gain


def span_memory(normed, live_mask, gain, span_len):
    model_width = normed.shape[1]
    masked = jnp.where(live_mask[:, None], normed.astype(jnp.float32), jnp.float32(0.0))
    owner_sums = masked.reshape(-1, span_len, model_width).sum(axis=1)
    counts = live_mask.reshape(-1, span_len).astype(jnp.float32).sum(axis=1)
    means = owner_sums / jnp.maximum(counts, 1.0)[:, None]
    power = jnp.mean(means * means, axis=-1, keepdims=True)
    return (means * lax.rsqrt(power + EPS_MEMORY) * gain).astype(jnp.bfloat16)


def block_size():
    return 256


def local_part(query, keys, values, first_frame, length, head_count, span_len, right_len):
    frame_count, model_width = query.shape
    head_size = model_width // head_count
    group_rows = 4 * span_len
    group_count = frame_count // group_rows
    block_rows = block_size()
    query_blocks = query.reshape(group_count, group_rows, head_count, head_size)
    key_blocks = keys[:frame_count].reshape(group_count, group_rows, head_count, head_size)
    value_blocks = values[:frame_count].reshape(group_count, group_rows, head_count, head_size)
    key_tail = keys[frame_count:].reshape(1, right_len, head_count, head_size)
    value_tail = values[frame_count:].reshape(1, right_len, head_count, head_size)
    key_all = jnp.concatenate(
        [key_blocks, jnp.concatenate([key_blocks[1:, :right_len], key_tail], axis=0)], axis=1
    )
    value_all = jnp.concatenate(
        [value_blocks, jnp.concatenate([value_blocks[1:, :right_len], value_tail], axis=0)], axis=1
    )
    start_offsets = jnp.arange(group_count, dtype=jnp.int32)[:, None] * group_rows
    query_pos = first_frame + start_offsets + jnp.arange(group_rows, dtype=jnp.int32)[None, :]
    key_pos = first_frame + jnp.concatenate(
        [
            start_offsets + jnp.arange(group_rows, dtype=jnp.int32)[None, :],
            start_offsets + group_rows + jnp.arange(right_len, dtype=jnp.int32)[None, :],
        ],
        axis=1,
    )
    query_span = query_pos // span_len
    span_end = (query_span + 1) * span_len
    same = (key_pos // span_len)[:, None, :] == query_span[:, :, None]
    ahead = (key_pos[:, None, :] >= span_end[:, :, None]) & (
        key_pos[:, None, :] < span_end[:, :, None] + right_len
    )
    allowed = (same | ahead) & (key_pos < length)[:, None, :]
    scores = jnp.einsum(
        "gqhd,gkhd->ghqk", query_blocks, key_all, preferred_element_type=jnp.float32
    ) * head_size ** (-0.5)
    scores = jnp.where(allowed[:, None], scores, NEG_BIG)
    row_peak = jnp.max(scores, axis=-1)
    weights = jnp.where(allowed[:, None], jnp.exp(scores - row_peak[..., None]), jnp.float32(0.0))
    row_total = jnp.sum(weights, axis=-1)
    accum = jnp.einsum(
        "ghqk,gkhd->ghqd",
        weights.astype(jnp.bfloat16),
        value_all,
        preferred_element_type=jnp.float32,
    )
    block_count = frame_count // block_rows
    row_peak = (
        row_peak.transpose(1, 0, 2).reshape(head_count, block_count, block_rows).transpose(1, 0, 2)
    )
    row_total = (
        row_total.transpose(1, 0, 2).reshape(head_count, block_count, block_rows).transpose(1, 0, 2)
    )
    accum = (
        accum.transpose(1, 0, 2, 3)
        .reshape(head_count, block_count, block_rows, head_size)
        .transpose(1, 0, 2, 3)
    )
    return (row_peak, row_total, accum)


def memory_update(
    carry, memory_keys, memory_values, query, first_frame, length, head_count, span_len
):
    row_peak, row_total, accum = carry
    block_count, _, block_rows = row_peak.shape
    row_count, model_width = memory_keys.shape
    head_size = model_width // head_count
    mem_keys = memory_keys.reshape(row_count, head_count, head_size)
    mem_values = memory_values.reshape(row_count, head_count, head_size)
    mem_index = jnp.arange(row_count, dtype=jnp.int32)
    mem_live = mem_index * span_len < length
    query_blocks = query.reshape(block_count, block_rows, head_count, head_size)
    positions = first_frame + jnp.arange(block_count * block_rows, dtype=jnp.int32).reshape(
        block_count, block_rows
    )

    def one_block(packed):
        query_now, pos_now, peak_now, total_now, accum_now = packed
        scores = jnp.einsum(
            "qhd,khd->hqk", query_now, mem_keys, preferred_element_type=jnp.float32
        ) * head_size ** (-0.5)
        allowed = (mem_index[None, :] < (pos_now // span_len)[:, None]) & mem_live[None, :]
        scores = jnp.where(allowed[None], scores, NEG_BIG)
        new_peak = jnp.maximum(peak_now, jnp.max(scores, axis=-1))
        weights = jnp.where(allowed[None], jnp.exp(scores - new_peak[..., None]), jnp.float32(0.0))
        factor = jnp.exp(peak_now - new_peak)
        total_next = total_now * factor + jnp.sum(weights, axis=-1)
        accum_next = accum_now * factor[..., None] + jnp.einsum(
            "hqk,khd->hqd",
            weights.astype(jnp.bfloat16),
            mem_values,
            preferred_element_type=jnp.float32,
        )
        return (new_peak, total_next, accum_next)

    return lax.map(one_block, (query_blocks, positions, row_peak, row_total, accum))


def finish(carry, frame_count, model_width):
    _, row_total, accum = carry
    result = accum / row_total[..., None]
    return result.transpose(0, 2, 1, 3).reshape(frame_count, model_width).astype(jnp.bfloat16)


def dispatch_matrix(owner_ids, owner_count, capacity):
    choose = (owner_ids[:, None] == jnp.arange(owner_count, dtype=jnp.int32)[None, :]).astype(
        jnp.int32
    )
    before = jnp.cumsum(choose, axis=0) - choose
    slot_index = jnp.sum(before * choose, axis=1)
    target = owner_ids * capacity + slot_index
    slot_rows = jnp.arange(owner_count * capacity, dtype=jnp.int32)
    return (slot_rows[:, None] == target[None, :]).astype(jnp.bfloat16)


def plain_device(
    frames,
    lengths,
    norm_gain,
    memory_gain,
    qkv_weight,
    out_weight,
    segment_ids,
    owners,
    language_weight,
):
    local_frames = frames[0]
    frame_count, model_width = local_frames.shape
    head_count = H
    time_count = lax.axis_size("tm")
    first_frame = lax.axis_index("tm") * frame_count
    length = lengths[0]
    live_mask = first_frame + jnp.arange(frame_count, dtype=jnp.int32) < length
    right_frames = shifted(local_frames[:RC], "tm", -1)
    normed = layer_norm(local_frames, norm_gain).astype(jnp.bfloat16)
    normed_right = layer_norm(right_frames, norm_gain).astype(jnp.bfloat16)
    memory = span_memory(normed, live_mask, memory_gain, C)
    stacked_rows = jnp.concatenate([normed, normed_right, memory], axis=0)
    projected = jnp.einsum(
        "fd,kdw->kfw",
        stacked_rows,
        lax.all_gather(qkv_weight, "tm", axis=2, tiled=True),
        preferred_element_type=jnp.float32,
    ).astype(jnp.bfloat16)
    split_at = frame_count + RC
    query = projected[0, :frame_count]
    keys = projected[1, :split_at]
    values = projected[2, :split_at]
    memory_keys = projected[1, split_at:]
    memory_values = projected[2, split_at:]
    carry = local_part(query, keys, values, first_frame, length, head_count, C, RC)
    carry = memory_update(
        carry,
        lax.all_gather(memory_keys, "tm", axis=0, tiled=True),
        lax.all_gather(memory_values, "tm", axis=0, tiled=True),
        query,
        first_frame,
        length,
        head_count,
        C,
    )
    attended = finish(carry, frame_count, model_width)
    output_proj = jnp.dot(
        attended,
        lax.all_gather(out_weight, "tm", axis=1, tiled=True),
        preferred_element_type=jnp.float32,
    )
    encoded = jnp.where(
        live_mask[:, None], local_frames.astype(jnp.float32) + output_proj, jnp.float32(0.0)
    ).astype(jnp.bfloat16)
    token_count = owners.shape[2]
    segments = segment_ids[0, 0]
    owner_indicator = (
        segments[None, :] == jnp.arange(token_count, dtype=jnp.int32)[:, None]
    ).astype(jnp.bfloat16)
    owner_sums = jnp.dot(owner_indicator, encoded, preferred_element_type=jnp.float32)
    counts = jnp.sum(owner_indicator.astype(jnp.float32), axis=1)
    pooled_rows = (owner_sums / counts[:, None]).astype(jnp.bfloat16)
    slot_count = 2 * token_count
    capacity = slot_count // time_count
    route_matrix = dispatch_matrix(owners[0, 0, :, 0], time_count, capacity)
    sent_rows = jnp.dot(route_matrix, pooled_rows, preferred_element_type=jnp.float32).astype(
        jnp.bfloat16
    )
    received = lax.all_to_all(
        sent_rows.reshape(time_count, capacity, model_width),
        "tm",
        split_axis=0,
        concat_axis=0,
        tiled=True,
    )
    received = received.reshape(slot_count, model_width)
    lm_out = jnp.dot(
        received,
        lax.all_gather(language_weight, "rec", axis=1, tiled=True),
        preferred_element_type=jnp.float32,
    ).astype(jnp.bfloat16)
    return (encoded[None], lm_out[None, None])


def vmem_spec():
    return pl.BlockSpec(memory_space=pltpu.VMEM)


def smem_spec():
    return pl.BlockSpec(memory_space=pltpu.SMEM)


def local_call(kernel, out_shapes, scalars, operands, scratch=(), in_place=0, out_in_place=False, vmem_mib=16, flops=0, moved=0):
    whole = len(operands) - in_place
    anywhere = pl.BlockSpec(memory_space=pl.ANY)
    if isinstance(out_shapes, tuple):
        stays = out_in_place or (False,) * len(out_shapes)
        out_specs = tuple(anywhere if stay else vmem_spec() for stay in stays)
    else:
        out_specs = anywhere if out_in_place else vmem_spec()
    return pl.pallas_call(
        kernel,
        out_shape=out_shapes,
        in_specs=[smem_spec()] * len(scalars) + [vmem_spec()] * whole + [anywhere] * in_place,
        out_specs=out_specs,
        compiler_params=pltpu.CompilerParams(vmem_limit_bytes=vmem_mib << 20),
        scratch_shapes=list(scratch),
        cost_estimate=pl.CostEstimate(flops=flops, bytes_accessed=moved, transcendentals=0),
    )(*scalars, *operands)


def shape_of(*dims, dtype=jnp.bfloat16):
    return jax.ShapeDtypeStruct(dims, dtype)


def normalise_kernel(
    span_len, scalars, frames, gain, memory_gain, normed_out, ahead_out, memory_out
):
    first_frame, length = scalars[0], scalars[1]
    frame_count, _ = frames.shape
    span_count = frame_count // span_len
    values = frames[...].astype(jnp.float32)
    centre = jnp.mean(values, axis=-1, keepdims=True)
    centred = values - centre
    spread = jnp.mean(centred * centred, axis=-1, keepdims=True)
    normed = (centred * lax.rsqrt(spread + EPS_NORM) * gain[...]).astype(jnp.bfloat16)
    normed_out[...] = normed
    ahead_out[...] = normed[: ahead_out.shape[0]]
    spans = lax.broadcasted_iota(jnp.int32, (span_count, frame_count), 0)
    places = lax.broadcasted_iota(jnp.int32, (span_count, frame_count), 1)
    member = (places >= spans * span_len) & (places < (spans + 1) * span_len)
    member = member & (places < length - first_frame)
    sums = jnp.dot(
        member.astype(jnp.bfloat16), normed, preferred_element_type=jnp.float32
    )
    counts = jnp.sum(member.astype(jnp.float32), axis=-1, keepdims=True)
    means = sums / jnp.maximum(counts, 1.0)
    power = jnp.mean(means * means, axis=-1, keepdims=True)
    memory = (means * lax.rsqrt(power + EPS_MEMORY) * memory_gain[...]).astype(jnp.bfloat16)
    for copy in range(memory_out.shape[0]):
        memory_out[copy] = memory


def prepare_kernel(scalars, frames, segments, owners_row, owners_col, base_out, member_out, count_out, route_out):
    first_frame, length, capacity = scalars[0], scalars[1], scalars[4]
    token_count, frame_count = member_out.shape
    tokens = lax.broadcasted_iota(jnp.int32, (token_count, frame_count), 0)
    places = first_frame + lax.broadcasted_iota(jnp.int32, (token_count, frame_count), 1)
    member = (segments[...] == tokens).astype(jnp.float32)
    counts = jnp.sum(member, axis=1, keepdims=True)
    live_member = jnp.where(places < length, member, 0.0).astype(jnp.bfloat16)
    earlier = lax.broadcasted_iota(jnp.int32, (token_count, token_count), 0)
    later = lax.broadcasted_iota(jnp.int32, (token_count, token_count), 1)
    clash = (owners_col[...] == owners_row[...]) & (earlier < later)
    slot = jnp.sum(clash.astype(jnp.int32), axis=0, keepdims=True)
    target = owners_row[...] * capacity + slot
    slots = lax.broadcasted_iota(jnp.int32, route_out.shape, 0)
    route_out[...] = (slots == target).astype(jnp.bfloat16)
    member_out[...] = live_member
    count_out[...] = jnp.broadcast_to(1.0 / counts, count_out.shape)
    base_out[...] = (
        jnp.dot(live_member, frames[...], preferred_element_type=jnp.float32) / counts
    )


def project_kernel(head_size, scalars, *refs):
    sources, pieces = refs[:4], refs[4:12]
    query, key, value, pair_weight, projection = refs[12:17]
    rows_in, query_weight, sems = refs[17:]
    core, y_half = scalars[2], scalars[3]
    model_width, width = query_weight.shape
    half = model_width // 2
    row_count = rows_in.shape[0] // 2
    frame_count = sources[0].shape[0]

    def piece_copies(of_core, projected):
        places = (y_half * half, (1 - y_half) * half)
        copies = []
        for side in range(2):
            place = pl.ds(pl.multiple_of(places[side], half), half)
            for shard in range(2):
                piece = pieces[4 * shard + 2 * side + of_core]
                shard_width = piece.shape[2]
                for part in (3,) if projected else (0, 1, 2):
                    target = (query_weight, pair_weight, pair_weight, projection)[part]
                    start = shard * shard_width + (width if part == 2 else 0)
                    copies.append(
                        pltpu.make_async_copy(
                            piece.at[part],
                            target.at[place, pl.ds(start, shard_width)],
                            sems.at[4 * part + 2 * side + shard],
                        )
                    )
        return copies

    row_copies = []
    for rec in range(2):
        for i, (start, size) in enumerate(
            ((0, frame_count), (frame_count, row_count - frame_count))
        ):
            row_copies.append(
                pltpu.make_async_copy(
                    sources[2 * rec + i],
                    rows_in.at[pl.ds(rec * row_count + start, size)],
                    sems.at[16 + 2 * rec + i],
                )
            )
    for copy in row_copies:
        copy.start()
    for of_core in range(2):

        @pl.when(core == of_core)
        def _():
            for copy in piece_copies(of_core, False) + piece_copies(of_core, True):
                copy.start()

    for copy in row_copies + piece_copies(1, False):
        copy.wait()
    scale = head_size ** (-0.5) * LOG2_E
    query[...] = (
        jnp.dot(rows_in[...], query_weight[...], preferred_element_type=jnp.float32) * scale
    ).astype(jnp.bfloat16)
    for part, target in enumerate((key, value)):
        target[...] = jnp.dot(
            rows_in[...],
            pair_weight[:, part * width : (part + 1) * width],
            preferred_element_type=jnp.float32,
        ).astype(jnp.bfloat16)
    for copy in piece_copies(1, True):
        copy.wait()


def attend_kernel(span_len, right_len, head_size, scalars, other_length, *refs):
    members, query, key, value = refs[:2], refs[2], refs[3], refs[4]
    memories, pair_weight = refs[5:7], refs[7]
    out_refs, sums_out = refs[8:10], refs[10:12]
    outs, memory_key, memory_value, bias, scores, peaks, weights, sems = refs[12:]
    first_frame = scalars[0]
    frame_count, width = out_refs[0].shape
    out_copies = [
        pltpu.make_async_copy(outs.at[rec], out_refs[rec], sems.at[rec]) for rec in range(2)
    ]
    heads = width // head_size
    block = 2 * span_len
    blocks = frame_count // block
    near = bias.shape[0]
    row_count = query.shape[0] // 2
    memory_count = memories[0].shape[0]
    lanes = heads * block

    rows = lax.broadcasted_iota(jnp.int32, (near, lanes), 0)
    spans = (lax.broadcasted_iota(jnp.int32, (near, lanes), 1) % block) // span_len
    same = (rows >= spans * span_len) & (rows < (spans + 1) * span_len + right_len)
    bias[...] = jnp.where(same, jnp.float32(0.0), jnp.float32(NEG_BIG))
    lane_spans = (lax.broadcasted_iota(jnp.int32, (1, lanes), 1) % block) // span_len
    memory_rows = lax.broadcasted_iota(jnp.int32, (memory_count, lanes), 0)
    feature_head = lax.broadcasted_iota(jnp.int32, (1, width), 1) // head_size
    head_masks = [(feature_head == h).astype(jnp.bfloat16) for h in range(heads)]
    for rec in range(2):
        mixed = jnp.dot(memories[rec][...], pair_weight[...], preferred_element_type=jnp.float32)
        memory_key[rec] = mixed[:, :width].astype(jnp.bfloat16)
        memory_value[rec] = mixed[:, width:].astype(jnp.bfloat16)

    def score_block(i):
        rec, b = divmod(i, blocks)
        at, start = rec * row_count, b * block
        length = scalars[1] if rec == 0 else other_length[0]
        q_now = query[at + start : at + start + block]
        stacked = jnp.concatenate([q_now * m for m in head_masks], axis=0)
        keys = jnp.concatenate(
            [key[at + start : at + start + near], memory_key[rec]], axis=0
        )
        raw = lax.dot_general(
            keys, stacked, (((1,), (1,)), ((), ())), preferred_element_type=jnp.float32
        )
        limit = length - first_frame - start
        local = jnp.where(rows < limit, raw[:near] + bias[...], NEG_BIG)
        live_spans = (length + span_len - 1) // span_len
        span_limit = jnp.minimum(first_frame // span_len + 2 * b + lane_spans, live_spans)
        memory = jnp.where(memory_rows < span_limit, raw[near:], NEG_BIG)
        slot = i % scores.shape[0]
        scores[slot, 0:near, :] = local
        scores[slot, near:, :] = memory
        peaks[slot] = jnp.maximum(
            jnp.max(local, axis=0, keepdims=True), jnp.max(memory, axis=0, keepdims=True)
        )

    def weigh_block(i):
        slot = i % scores.shape[0]
        weights[slot] = jnp.exp2(scores[slot] - peaks[slot]).astype(jnp.bfloat16)

    ones = jnp.ones((near + memory_count, LANES), jnp.bfloat16)
    first_of_pair = lax.broadcasted_iota(jnp.int32, (1, 2 * LANES), 1) % LANES < head_size

    def mix_block(i):
        rec, b = divmod(i, blocks)
        at, start = rec * row_count, b * block
        values = jnp.concatenate(
            [value[at + start : at + start + near], memory_value[rec]], axis=0
        )
        for pair in range(width // LANES):
            columns = slice(pair * LANES, (pair + 1) * LANES)
            pair_rows = slice(pair * 2 * block, (pair + 1) * 2 * block)
            sums = lax.dot_general(
                weights[i % weights.shape[0], :, pair_rows],
                jnp.concatenate([values[:, columns], ones], axis=1),
                (((0,), (0,)), ((), ())),
                preferred_element_type=jnp.float32,
            )
            picked = jnp.where(first_of_pair, sums[:block], sums[block:])
            outs[rec, start : start + block, columns] = (
                picked[:, :LANES] / picked[:, LANES:]
            ).astype(jnp.bfloat16)

    count = 2 * blocks
    ring = scores.shape[0]
    for first in range(0, count, ring):
        for stage in (score_block, weigh_block, mix_block):
            for i in range(first, min(first + ring, count)):
                stage(i)
        for rec in range(2):
            if first < (rec + 1) * blocks <= first + ring:
                out_copies[rec].start()
    for rec in range(2):
        sums_out[rec][...] = jnp.dot(
            members[rec][...], outs[rec], preferred_element_type=jnp.float32
        )
    for copy in out_copies:
        copy.wait()


def assemble(scalars, offsets_at, attended, gathered):
    shard = attended[0].shape[1] // 2
    offsets = [
        [pl.multiple_of(scalars[offsets_at + 2 * i + s], LANES) for s in range(2)]
        for i in range(4)
    ]
    for i in range(4):
        for s in range(2):
            gathered[:, pl.ds(offsets[i][s], shard)] = attended[i][:, s * shard : (s + 1) * shard]
    return offsets, shard


def pool_kernel(offsets_at, scalars, base, inverse, route, *refs):
    sums, projections = refs[:4], refs[4:8]
    sent_out, means, pooled = refs[8:]
    shard = sums[0].shape[1] // 2
    offsets = [
        [pl.multiple_of(scalars[offsets_at + 2 * i + s], LANES) for s in range(2)]
        for i in range(4)
    ]
    for i in range(4):
        for s in range(2):
            for lane in range(0, shard, LANES):
                means[:, pl.ds(offsets[i][s] + lane, LANES)] = (
                    sums[i][:, s * shard + lane : s * shard + lane + LANES] * inverse[...]
                ).astype(jnp.bfloat16)
    for i in range(4):
        mixed = jnp.dot(means[...], projections[i][...], preferred_element_type=jnp.float32)
        for s in range(2):
            columns = pl.ds(offsets[i][s], shard)
            pooled[:, columns] = (
                base[:, columns] + mixed[:, s * shard : (s + 1) * shard]
            ).astype(jnp.bfloat16)
    sent_out[...] = jnp.dot(
        route[...], pooled[...], preferred_element_type=jnp.float32
    ).astype(jnp.bfloat16)


def encode_kernel(offsets_at, scalars, *refs):
    attended, projections, frames = refs[:4], refs[4:8], refs[8]
    encoded_out, gathered = refs[9:]
    first_frame, length = scalars[0], scalars[1]
    frame_count, _ = frames.shape
    offsets, shard = assemble(scalars, offsets_at, attended, gathered)
    live = (
        first_frame + lax.broadcasted_iota(jnp.int32, (frame_count, 1), 0) < length
    ).astype(jnp.float32)
    for i in range(4):
        mixed = jnp.dot(
            gathered[...], projections[i][...], preferred_element_type=jnp.float32
        )
        for s in range(2):
            columns = pl.ds(offsets[i][s], shard)
            base = frames[:, columns].astype(jnp.float32)
            encoded_out[:, columns] = (
                (base + mixed[:, s * shard : (s + 1) * shard]) * live
            ).astype(jnp.bfloat16)


def language_kernel(places_at, scalars, received, *refs):
    pieces, out = refs[:-6], refs[-6]
    rows, weights, product, sems, out_sems = refs[-5:]
    count, width = len(pieces), pieces[0].shape[1]
    row_copy = pltpu.make_async_copy(received, rows, sems.at[count])
    row_copy.start()
    copies = [
        pltpu.make_async_copy(piece, weights.at[i], sems.at[i]) for i, piece in enumerate(pieces)
    ]
    for copy in copies:
        copy.start()
    row_copy.wait()
    out_copies = []
    for i in range(count):
        copies[i].wait()
        product[i] = jnp.dot(
            rows[...], weights[i], preferred_element_type=jnp.float32
        ).astype(jnp.bfloat16)
        place = pl.multiple_of(scalars[places_at + i], LANES)
        out_copies.append(
            pltpu.make_async_copy(product.at[i], out.at[:, pl.ds(place, width)], out_sems.at[i])
        )
        out_copies[-1].start()
    for copy in out_copies:
        copy.wait()


def along_x(r, j, _):
    return r, j ^ 1


def along_y(r, j, _):
    return r ^ 2, j


def other_core(r, j, _):
    return r ^ 1, j


def z_up(r, j, count):
    return r, (j + 2) % count


def z_down(r, j, count):
    return r, (j - 2) % count


def relocate(value, core_0, core_1):
    rec_count, time_count = lax.axis_size("rec"), lax.axis_size("tm")
    pairs = []
    for r in range(rec_count):
        for j in range(time_count):
            route = (core_0, core_1)[r % 2]
            if route is not None:
                to_r, to_j = route(r, j, time_count)
                pairs.append((r * time_count + j, to_r * time_count + to_j))
    return lax.ppermute(value, ("rec", "tm"), pairs)


def swap_cores(value):
    return relocate(value, other_core, other_core)


def exchange_blocks(blocks):
    return lax.all_to_all(blocks, "tm", split_axis=0, concat_axis=0, tiled=True)


def per_device(
    frames,
    lengths,
    norm_gain,
    memory_gain,
    qkv_weight,
    out_weight,
    segment_ids,
    owners,
    language_weight,
):
    local_frames = frames[0]
    frame_count, model_width = local_frames.shape
    shard = out_weight.shape[1]
    half = model_width // 2
    time_count = lax.axis_size("tm")
    rec_count = lax.axis_size("rec")
    rec, time = lax.axis_index("rec"), lax.axis_index("tm")
    core, y_half = rec % 2, (rec // 2) % 2
    x, z = time % 2, time // 2
    z_count = time_count // 2
    first_frame = time * frame_count
    length = lengths[0]
    head_size = model_width // H
    bf16 = jnp.bfloat16

    own = jnp.concatenate([qkv_weight, out_weight[None]], axis=0)
    own_a = lax.dynamic_slice_in_dim(own, y_half * half, half, 1)
    later_qkv, later_out, own_a = lax.optimization_barrier((qkv_weight, out_weight, own_a))
    later = jnp.concatenate([later_qkv, later_out[None]], axis=0)
    own_b = lax.dynamic_slice_in_dim(later, (1 - y_half) * half, half, 1)

    def pick(for_core_0, for_core_1):
        return jnp.where(core == 0, for_core_0, for_core_1)

    token_count = owners.shape[2]
    slot_count = 2 * token_count
    capacity = slot_count // time_count
    language_shard = language_weight.shape[1]

    def group_of(of_core, slot):
        return jnp.where(of_core == 0, z + slot, z - slot - 1) % z_count

    numbers = [first_frame, length, core, y_half, capacity]
    offsets_at = len(numbers)
    for of_core in (core, 1 - core):
        for slot in range(2):
            group = group_of(of_core, slot)
            numbers += [(2 * group + x) * shard, (2 * group + 1 - x) * shard]
    places_at = len(numbers)
    numbers += [(rec ^ i) * language_shard for i in range(rec_count)]
    scalars = jnp.stack(numbers).astype(jnp.int32)

    m1 = relocate(own_a, along_x, z_up)
    m2 = relocate(pick(own_a, own_b), z_down, z_up)
    l1 = relocate(language_weight, along_y, along_y)

    pad = 2 * RC
    normed, start_rows, memory = local_call(
        functools.partial(normalise_kernel, C),
        (
            shape_of(frame_count, model_width),
            shape_of(pad, model_width),
            shape_of(time_count, frame_count // C, model_width),
        ),
        (scalars,),
        (local_frames, norm_gain[None], memory_gain[None]),
        flops=10 * frame_count * model_width,
        moved=4 * frame_count * model_width,
    )
    other_length = swap_cores(lengths)
    other_normed = swap_cores(normed)
    ahead = shifted(start_rows, "tm", -1)
    memories = exchange_blocks(memory).reshape(-1, model_width)
    owners_col = owners[0, 0]
    base, member, inverse, route = local_call(
        prepare_kernel,
        (
            shape_of(token_count, model_width, dtype=jnp.float32),
            shape_of(token_count, frame_count),
            shape_of(token_count, LANES, dtype=jnp.float32),
            shape_of(slot_count, token_count),
        ),
        (scalars,),
        (local_frames, segment_ids[0], owners_col.reshape(1, token_count), owners_col),
        flops=2 * token_count * frame_count * model_width,
        moved=2 * frame_count * model_width,
    )
    other_member = swap_cores(member)
    other_ahead = swap_cores(ahead)
    other_memories = swap_cores(memories)

    m3 = relocate(m1, along_y, along_x)
    m4 = relocate(m1, None, z_up)
    m5 = relocate(m2, along_x, z_up)
    m6 = relocate(m3, None, along_y)
    m7 = relocate(pick(m2, m4), along_y, along_x)
    m8 = relocate(m5, along_y, along_x)

    slot_pieces = (
        ((own_a, m1), (own_b, m2), (m1, m3), (m3, m6)),
        ((m2, m4), (m7, m5), (m5, m7), (m8, m8)),
    )
    block = 2 * C
    width = 2 * shard
    row_count = frame_count + pad
    memory_count = memories.shape[0]
    keys_seen = block + pad + memory_count
    lanes = width // head_size * block
    attended, sums, outs = [], [], []
    for pieces in slot_pieces:
        flat = [p for pair in pieces for p in pair]
        *rows, pair_weight, out_piece = local_call(
            functools.partial(project_kernel, head_size),
            (
                shape_of(2 * row_count, width),
                shape_of(2 * row_count, width),
                shape_of(2 * row_count, width),
                shape_of(model_width, 2 * width),
                shape_of(model_width, width),
            ),
            (scalars,),
            (normed, ahead, other_normed, other_ahead, *flat),
            in_place=4 + len(flat),
            scratch=(
                pltpu.VMEM((2 * row_count, model_width), bf16),
                pltpu.VMEM((model_width, width), bf16),
                pltpu.SemaphoreType.DMA((20,)),
            ),
            vmem_mib=16,
            flops=12 * frame_count * model_width * width,
            moved=8 * frame_count * model_width,
        )
        results = local_call(
            functools.partial(attend_kernel, C, RC, head_size),
            (
                shape_of(frame_count, width),
                shape_of(frame_count, width),
                shape_of(token_count, width, dtype=jnp.float32),
                shape_of(token_count, width, dtype=jnp.float32),
            ),
            (scalars, other_length),
            (member, other_member, *rows, memories, other_memories, pair_weight),
            out_in_place=(True, True, False, False),
            scratch=(
                pltpu.VMEM((2, frame_count, width), bf16),
                pltpu.VMEM((2, memory_count, width), bf16),
                pltpu.VMEM((2, memory_count, width), bf16),
                pltpu.VMEM((block + pad, lanes), jnp.float32),
                pltpu.VMEM((RING, keys_seen, lanes), jnp.float32),
                pltpu.VMEM((RING, 1, lanes), jnp.float32),
                pltpu.VMEM((RING, keys_seen, lanes), bf16),
                pltpu.SemaphoreType.DMA((2,)),
            ),
            vmem_mib=20,
            flops=4 * frame_count * keys_seen * width,
            moved=8 * frame_count * width,
        )
        attended.append(results[:2])
        sums.append(results[2:])
        outs.append(out_piece)
    other_outs = [swap_cores(w) for w in outs]
    other_attended = [swap_cores(for_other) for _, for_other in attended]

    other_sums = [swap_cores(for_other) for _, for_other in sums]
    projections = (*outs, *other_outs)
    features = (attended[0][0], attended[1][0], *other_attended, *projections)
    sent_rows = local_call(
        functools.partial(pool_kernel, offsets_at),
        shape_of(slot_count, model_width),
        (scalars,),
        (base, inverse, route, sums[0][0], sums[1][0], *other_sums, *projections),
        scratch=(
            pltpu.VMEM((token_count, model_width), bf16),
            pltpu.VMEM((token_count, model_width), bf16),
        ),
        flops=4 * token_count * model_width * model_width,
        moved=6 * frame_count * model_width,
    )
    received = exchange_blocks(
        sent_rows.reshape(time_count, capacity, model_width)
    ).reshape(slot_count, model_width)
    encoded = local_call(
        functools.partial(encode_kernel, offsets_at),
        shape_of(frame_count, model_width),
        (scalars,),
        (*features, local_frames),
        scratch=(pltpu.VMEM((frame_count, model_width), bf16),),
        flops=2 * frame_count * model_width * model_width,
        moved=6 * frame_count * model_width,
    )
    language_pieces = (language_weight, swap_cores(language_weight), l1, swap_cores(l1))
    lm_out = local_call(
        functools.partial(language_kernel, places_at),
        shape_of(slot_count, rec_count * language_shard),
        (scalars,),
        (received, *language_pieces),
        in_place=1 + rec_count,
        out_in_place=True,
        scratch=(
            pltpu.VMEM((slot_count, model_width), bf16),
            pltpu.VMEM((rec_count, model_width, language_shard), bf16),
            pltpu.VMEM((rec_count, slot_count, language_shard), bf16),
            pltpu.SemaphoreType.DMA((rec_count + 1,)),
            pltpu.SemaphoreType.DMA((rec_count,)),
        ),
        flops=2 * slot_count * model_width * rec_count * language_shard,
        moved=2 * model_width * rec_count * language_shard,
    )
    return (encoded[None], lm_out[None, None])


def solution(mesh):
    in_specs = (
        P("rec", "tm", None),
        P("rec"),
        P(),
        P(),
        P(None, None, "tm"),
        P(None, "tm"),
        P("rec", "tm", None),
        P("rec", "tm", None, None),
        P(None, "rec"),
    )
    out_specs = (P("rec", "tm", None), P("rec", "tm", None, None))
    rec_count, time_count = mesh.shape["rec"], mesh.shape["tm"]
    paired = shard_map_of(mesh, in_specs, out_specs, per_device)
    plain = shard_map_of(mesh, in_specs, out_specs, plain_device)

    def run(*arrays):
        shard = arrays[5].shape[1] // time_count
        fits = rec_count == 4 and time_count == 8 and shard % LANES == 0
        return (paired if fits else plain)(*arrays)

    return run


def shard_map_of(mesh, in_specs, out_specs, body):
    return jax.shard_map(
        body, mesh=mesh, in_specs=in_specs, out_specs=out_specs, check_vma=False
    )
```

```python
import functools

import jax
import jax.numpy as jnp
from jax import lax
from jax.experimental import pallas as pl
from jax.experimental.pallas import tpu as pltpu
from jax.sharding import PartitionSpec as P


H = 16
C = 32
RC = 8


EPS_NORM = 1e-05
EPS_MEMORY = 1e-06
NEG_BIG = -1e30
LANES = 128
RING = 16
LOG2_E = 1.4426950408889634


def shifted(block, axis, distance):
    devices = range(lax.axis_size(axis))
    route = [(i - distance, i) for i in devices if i - distance in devices]
    return lax.ppermute(block, axis, route)


def layer_norm(values_in, gain):
    values_in = values_in.astype(jnp.float32)
    centre = jnp.mean(values_in, axis=-1, keepdims=True)
    centred = values_in - centre
    spread = jnp.mean(centred * centred, axis=-1, keepdims=True)
    return centred * lax.rsqrt(spread + EPS_NORM) * gain


def span_memory(normed, live_mask, gain, span_len):
    model_width = normed.shape[1]
    masked = jnp.where(live_mask[:, None], normed.astype(jnp.float32), jnp.float32(0.0))
    owner_sums = masked.reshape(-1, span_len, model_width).sum(axis=1)
    counts = live_mask.reshape(-1, span_len).astype(jnp.float32).sum(axis=1)
    means = owner_sums / jnp.maximum(counts, 1.0)[:, None]
    power = jnp.mean(means * means, axis=-1, keepdims=True)
    return (means * lax.rsqrt(power + EPS_MEMORY) * gain).astype(jnp.bfloat16)


def block_size():
    return 256


def local_part(query, keys, values, first_frame, length, head_count, span_len, right_len):
    frame_count, model_width = query.shape
    head_size = model_width // head_count
    group_rows = 4 * span_len
    group_count = frame_count // group_rows
    block_rows = block_size()
    query_blocks = query.reshape(group_count, group_rows, head_count, head_size)
    key_blocks = keys[:frame_count].reshape(group_count, group_rows, head_count, head_size)
    value_blocks = values[:frame_count].reshape(group_count, group_rows, head_count, head_size)
    key_tail = keys[frame_count:].reshape(1, right_len, head_count, head_size)
    value_tail = values[frame_count:].reshape(1, right_len, head_count, head_size)
    key_all = jnp.concatenate(
        [key_blocks, jnp.concatenate([key_blocks[1:, :right_len], key_tail], axis=0)], axis=1
    )
    value_all = jnp.concatenate(
        [value_blocks, jnp.concatenate([value_blocks[1:, :right_len], value_tail], axis=0)], axis=1
    )
    start_offsets = jnp.arange(group_count, dtype=jnp.int32)[:, None] * group_rows
    query_pos = first_frame + start_offsets + jnp.arange(group_rows, dtype=jnp.int32)[None, :]
    key_pos = first_frame + jnp.concatenate(
        [
            start_offsets + jnp.arange(group_rows, dtype=jnp.int32)[None, :],
            start_offsets + group_rows + jnp.arange(right_len, dtype=jnp.int32)[None, :],
        ],
        axis=1,
    )
    query_span = query_pos // span_len
    span_end = (query_span + 1) * span_len
    same = (key_pos // span_len)[:, None, :] == query_span[:, :, None]
    ahead = (key_pos[:, None, :] >= span_end[:, :, None]) & (
        key_pos[:, None, :] < span_end[:, :, None] + right_len
    )
    allowed = (same | ahead) & (key_pos < length)[:, None, :]
    scores = jnp.einsum(
        "gqhd,gkhd->ghqk", query_blocks, key_all, preferred_element_type=jnp.float32
    ) * head_size ** (-0.5)
    scores = jnp.where(allowed[:, None], scores, NEG_BIG)
    row_peak = jnp.max(scores, axis=-1)
    weights = jnp.where(allowed[:, None], jnp.exp(scores - row_peak[..., None]), jnp.float32(0.0))
    row_total = jnp.sum(weights, axis=-1)
    accum = jnp.einsum(
        "ghqk,gkhd->ghqd",
        weights.astype(jnp.bfloat16),
        value_all,
        preferred_element_type=jnp.float32,
    )
    block_count = frame_count // block_rows
    row_peak = (
        row_peak.transpose(1, 0, 2).reshape(head_count, block_count, block_rows).transpose(1, 0, 2)
    )
    row_total = (
        row_total.transpose(1, 0, 2).reshape(head_count, block_count, block_rows).transpose(1, 0, 2)
    )
    accum = (
        accum.transpose(1, 0, 2, 3)
        .reshape(head_count, block_count, block_rows, head_size)
        .transpose(1, 0, 2, 3)
    )
    return (row_peak, row_total, accum)


def memory_update(
    carry, memory_keys, memory_values, query, first_frame, length, head_count, span_len
):
    row_peak, row_total, accum = carry
    block_count, _, block_rows = row_peak.shape
    row_count, model_width = memory_keys.shape
    head_size = model_width // head_count
    mem_keys = memory_keys.reshape(row_count, head_count, head_size)
    mem_values = memory_values.reshape(row_count, head_count, head_size)
    mem_index = jnp.arange(row_count, dtype=jnp.int32)
    mem_live = mem_index * span_len < length
    query_blocks = query.reshape(block_count, block_rows, head_count, head_size)
    positions = first_frame + jnp.arange(block_count * block_rows, dtype=jnp.int32).reshape(
        block_count, block_rows
    )

    def one_block(packed):
        query_now, pos_now, peak_now, total_now, accum_now = packed
        scores = jnp.einsum(
            "qhd,khd->hqk", query_now, mem_keys, preferred_element_type=jnp.float32
        ) * head_size ** (-0.5)
        allowed = (mem_index[None, :] < (pos_now // span_len)[:, None]) & mem_live[None, :]
        scores = jnp.where(allowed[None], scores, NEG_BIG)
        new_peak = jnp.maximum(peak_now, jnp.max(scores, axis=-1))
        weights = jnp.where(allowed[None], jnp.exp(scores - new_peak[..., None]), jnp.float32(0.0))
        factor = jnp.exp(peak_now - new_peak)
        total_next = total_now * factor + jnp.sum(weights, axis=-1)
        accum_next = accum_now * factor[..., None] + jnp.einsum(
            "hqk,khd->hqd",
            weights.astype(jnp.bfloat16),
            mem_values,
            preferred_element_type=jnp.float32,
        )
        return (new_peak, total_next, accum_next)

    return lax.map(one_block, (query_blocks, positions, row_peak, row_total, accum))


def finish(carry, frame_count, model_width):
    _, row_total, accum = carry
    result = accum / row_total[..., None]
    return result.transpose(0, 2, 1, 3).reshape(frame_count, model_width).astype(jnp.bfloat16)


def dispatch_matrix(owner_ids, owner_count, capacity):
    choose = (owner_ids[:, None] == jnp.arange(owner_count, dtype=jnp.int32)[None, :]).astype(
        jnp.int32
    )
    before = jnp.cumsum(choose, axis=0) - choose
    slot_index = jnp.sum(before * choose, axis=1)
    target = owner_ids * capacity + slot_index
    slot_rows = jnp.arange(owner_count * capacity, dtype=jnp.int32)
    return (slot_rows[:, None] == target[None, :]).astype(jnp.bfloat16)


def plain_device(
    frames,
    lengths,
    norm_gain,
    memory_gain,
    qkv_weight,
    out_weight,
    segment_ids,
    owners,
    language_weight,
):
    local_frames = frames[0]
    frame_count, model_width = local_frames.shape
    head_count = H
    time_count = lax.axis_size("tm")
    first_frame = lax.axis_index("tm") * frame_count
    length = lengths[0]
    live_mask = first_frame + jnp.arange(frame_count, dtype=jnp.int32) < length
    right_frames = shifted(local_frames[:RC], "tm", -1)
    normed = layer_norm(local_frames, norm_gain).astype(jnp.bfloat16)
    normed_right = layer_norm(right_frames, norm_gain).astype(jnp.bfloat16)
    memory = span_memory(normed, live_mask, memory_gain, C)
    stacked_rows = jnp.concatenate([normed, normed_right, memory], axis=0)
    projected = jnp.einsum(
        "fd,kdw->kfw",
        stacked_rows,
        lax.all_gather(qkv_weight, "tm", axis=2, tiled=True),
        preferred_element_type=jnp.float32,
    ).astype(jnp.bfloat16)
    split_at = frame_count + RC
    query = projected[0, :frame_count]
    keys = projected[1, :split_at]
    values = projected[2, :split_at]
    memory_keys = projected[1, split_at:]
    memory_values = projected[2, split_at:]
    carry = local_part(query, keys, values, first_frame, length, head_count, C, RC)
    carry = memory_update(
        carry,
        lax.all_gather(memory_keys, "tm", axis=0, tiled=True),
        lax.all_gather(memory_values, "tm", axis=0, tiled=True),
        query,
        first_frame,
        length,
        head_count,
        C,
    )
    attended = finish(carry, frame_count, model_width)
    output_proj = jnp.dot(
        attended,
        lax.all_gather(out_weight, "tm", axis=1, tiled=True),
        preferred_element_type=jnp.float32,
    )
    encoded = jnp.where(
        live_mask[:, None], local_frames.astype(jnp.float32) + output_proj, jnp.float32(0.0)
    ).astype(jnp.bfloat16)
    token_count = owners.shape[2]
    segments = segment_ids[0, 0]
    owner_indicator = (
        segments[None, :] == jnp.arange(token_count, dtype=jnp.int32)[:, None]
    ).astype(jnp.bfloat16)
    owner_sums = jnp.dot(owner_indicator, encoded, preferred_element_type=jnp.float32)
    counts = jnp.sum(owner_indicator.astype(jnp.float32), axis=1)
    pooled_rows = (owner_sums / counts[:, None]).astype(jnp.bfloat16)
    slot_count = 2 * token_count
    capacity = slot_count // time_count
    route_matrix = dispatch_matrix(owners[0, 0, :, 0], time_count, capacity)
    sent_rows = jnp.dot(route_matrix, pooled_rows, preferred_element_type=jnp.float32).astype(
        jnp.bfloat16
    )
    received = lax.all_to_all(
        sent_rows.reshape(time_count, capacity, model_width),
        "tm",
        split_axis=0,
        concat_axis=0,
        tiled=True,
    )
    received = received.reshape(slot_count, model_width)
    lm_out = jnp.dot(
        received,
        lax.all_gather(language_weight, "rec", axis=1, tiled=True),
        preferred_element_type=jnp.float32,
    ).astype(jnp.bfloat16)
    return (encoded[None], lm_out[None, None])


def vmem_spec():
    return pl.BlockSpec(memory_space=pltpu.VMEM)


def smem_spec():
    return pl.BlockSpec(memory_space=pltpu.SMEM)


def local_call(kernel, out_shapes, scalars, operands, scratch=(), in_place=0, out_in_place=False, vmem_mib=16, flops=0, moved=0):
    whole = len(operands) - in_place
    anywhere = pl.BlockSpec(memory_space=pl.ANY)
    if isinstance(out_shapes, tuple):
        stays = out_in_place or (False,) * len(out_shapes)
        out_specs = tuple(anywhere if stay else vmem_spec() for stay in stays)
    else:
        out_specs = anywhere if out_in_place else vmem_spec()
    return pl.pallas_call(
        kernel,
        out_shape=out_shapes,
        in_specs=[smem_spec()] * len(scalars) + [vmem_spec()] * whole + [anywhere] * in_place,
        out_specs=out_specs,
        compiler_params=pltpu.CompilerParams(vmem_limit_bytes=vmem_mib << 20),
        scratch_shapes=list(scratch),
        cost_estimate=pl.CostEstimate(flops=flops, bytes_accessed=moved, transcendentals=0),
    )(*scalars, *operands)


def shape_of(*dims, dtype=jnp.bfloat16):
    return jax.ShapeDtypeStruct(dims, dtype)


def normalise_kernel(
    span_len, scalars, frames, gain, memory_gain, normed_out, ahead_out, memory_out
):
    first_frame, length = scalars[0], scalars[1]
    frame_count, _ = frames.shape
    span_count = frame_count // span_len
    values = frames[...].astype(jnp.float32)
    centre = jnp.mean(values, axis=-1, keepdims=True)
    centred = values - centre
    spread = jnp.mean(centred * centred, axis=-1, keepdims=True)
    normed = (centred * lax.rsqrt(spread + EPS_NORM) * gain[...]).astype(jnp.bfloat16)
    normed_out[...] = normed
    ahead_out[...] = normed[: ahead_out.shape[0]]
    spans = lax.broadcasted_iota(jnp.int32, (span_count, frame_count), 0)
    places = lax.broadcasted_iota(jnp.int32, (span_count, frame_count), 1)
    member = (places >= spans * span_len) & (places < (spans + 1) * span_len)
    member = member & (places < length - first_frame)
    sums = jnp.dot(
        member.astype(jnp.bfloat16), normed, preferred_element_type=jnp.float32
    )
    counts = jnp.sum(member.astype(jnp.float32), axis=-1, keepdims=True)
    means = sums / jnp.maximum(counts, 1.0)
    power = jnp.mean(means * means, axis=-1, keepdims=True)
    memory = (means * lax.rsqrt(power + EPS_MEMORY) * memory_gain[...]).astype(jnp.bfloat16)
    for copy in range(memory_out.shape[0]):
        memory_out[copy] = memory


def prepare_kernel(scalars, frames, segments, owners_row, owners_col, base_out, member_out, count_out, route_out):
    first_frame, length, capacity = scalars[0], scalars[1], scalars[4]
    token_count, frame_count = member_out.shape
    tokens = lax.broadcasted_iota(jnp.int32, (token_count, frame_count), 0)
    places = first_frame + lax.broadcasted_iota(jnp.int32, (token_count, frame_count), 1)
    member = (segments[...] == tokens).astype(jnp.float32)
    counts = jnp.sum(member, axis=1, keepdims=True)
    live_member = jnp.where(places < length, member, 0.0).astype(jnp.bfloat16)
    earlier = lax.broadcasted_iota(jnp.int32, (token_count, token_count), 0)
    later = lax.broadcasted_iota(jnp.int32, (token_count, token_count), 1)
    clash = (owners_col[...] == owners_row[...]) & (earlier < later)
    slot = jnp.sum(clash.astype(jnp.int32), axis=0, keepdims=True)
    target = owners_row[...] * capacity + slot
    slots = lax.broadcasted_iota(jnp.int32, route_out.shape, 0)
    route_out[...] = (slots == target).astype(jnp.bfloat16)
    member_out[...] = live_member
    count_out[...] = jnp.broadcast_to(1.0 / counts, count_out.shape)
    base_out[...] = (
        jnp.dot(live_member, frames[...], preferred_element_type=jnp.float32) / counts
    )


def attend_kernel(span_len, right_len, head_size, starts_here, scalars, other_length, *refs):
    members, sources, pieces = refs[:2], refs[2:8], refs[8:16]
    out_refs, sums_out, projection = refs[16:18], refs[18:20], refs[20]
    outs, rows_in, weight, query, key, value, bias, scores, peaks, weights, sems = refs[21:]
    first_frame, core, y_half = scalars[0], scalars[2], scalars[3]
    frame_count, model_width = sources[0].shape
    half = model_width // 2
    width = out_refs[0].shape[1]
    out_copies = [
        pltpu.make_async_copy(outs.at[rec], out_refs[rec], sems.at[22 + rec]) for rec in range(2)
    ]
    heads = width // head_size
    block = 2 * span_len
    blocks = frame_count // block
    near = bias.shape[0]
    memory_at = frame_count + near - block
    row_count = rows_in.shape[0] // 2
    memory_count = row_count - memory_at
    lanes = heads * block

    def piece_copies(of_core, projected):
        places = (y_half * half, (1 - y_half) * half)
        copies = []
        for side in range(2):
            place = pl.ds(pl.multiple_of(places[side], half), half)
            for shard in range(2):
                piece = pieces[4 * shard + 2 * side + of_core]
                raw = starts_here and of_core == 0 and shard == 0
                shard_width = pieces[-1].shape[2]
                index = 2 * side + shard
                for part in (3,) if projected else (0, 1, 2):
                    target = projection if projected else weight
                    start = shard * shard_width + (0 if projected else part * width)
                    if raw:
                        source = pieces[2].at[place] if projected else pieces[0].at[part, place]
                    else:
                        source = piece.at[part]
                    copies.append(
                        pltpu.make_async_copy(
                            source,
                            target.at[place, pl.ds(start, shard_width)],
                            sems.at[4 * part + index],
                        )
                    )
        return copies

    row_copies = []
    for rec in range(2):
        at = rec * row_count
        for i, (start, size) in enumerate(
            ((0, frame_count), (frame_count, near - block), (memory_at, memory_count))
        ):
            row_copies.append(
                pltpu.make_async_copy(
                    sources[3 * rec + i], rows_in.at[pl.ds(at + start, size)], sems.at[16 + 3 * rec + i]
                )
            )

    for copy in row_copies:
        copy.start()
    for of_core in range(2):

        @pl.when(core == of_core)
        def _():
            for copy in piece_copies(of_core, False) + piece_copies(of_core, True):
                copy.start()

    rows = lax.broadcasted_iota(jnp.int32, (near, lanes), 0)
    spans = (lax.broadcasted_iota(jnp.int32, (near, lanes), 1) % block) // span_len
    same = (rows >= spans * span_len) & (rows < (spans + 1) * span_len + right_len)
    bias[...] = jnp.where(same, jnp.float32(0.0), jnp.float32(NEG_BIG))
    lane_spans = (lax.broadcasted_iota(jnp.int32, (1, lanes), 1) % block) // span_len
    memory_rows = lax.broadcasted_iota(jnp.int32, (memory_count, lanes), 0)
    feature_head = lax.broadcasted_iota(jnp.int32, (1, width), 1) // head_size
    head_masks = [(feature_head == h).astype(jnp.bfloat16) for h in range(heads)]
    scale = head_size ** (-0.5) * LOG2_E

    for copy in row_copies + piece_copies(1, False):
        copy.wait()
    for part, target in enumerate((query, key, value)):
        mixed = jnp.dot(
            rows_in[...],
            weight[:, part * width : (part + 1) * width],
            preferred_element_type=jnp.float32,
        )
        target[...] = (mixed * scale if part == 0 else mixed).astype(jnp.bfloat16)

    def score_block(i):
        rec, b = divmod(i, blocks)
        at, start = rec * row_count, b * block
        length = scalars[1] if rec == 0 else other_length[0]
        q_now = query[at + start : at + start + block]
        stacked = jnp.concatenate([q_now * m for m in head_masks], axis=0)
        keys = jnp.concatenate(
            [key[at + start : at + start + near], key[at + memory_at : at + row_count]], axis=0
        )
        raw = lax.dot_general(
            keys, stacked, (((1,), (1,)), ((), ())), preferred_element_type=jnp.float32
        )
        limit = length - first_frame - start
        local = jnp.where(rows < limit, raw[:near] + bias[...], NEG_BIG)
        live_spans = (length + span_len - 1) // span_len
        span_limit = jnp.minimum(first_frame // span_len + 2 * b + lane_spans, live_spans)
        memory = jnp.where(memory_rows < span_limit, raw[near:], NEG_BIG)
        slot = i % scores.shape[0]
        scores[slot, 0:near, :] = local
        scores[slot, near:, :] = memory
        peaks[slot] = jnp.maximum(
            jnp.max(local, axis=0, keepdims=True), jnp.max(memory, axis=0, keepdims=True)
        )

    def weigh_block(i):
        slot = i % scores.shape[0]
        weights[slot] = jnp.exp2(scores[slot] - peaks[slot]).astype(jnp.bfloat16)

    ones = jnp.ones((near + memory_count, LANES), jnp.bfloat16)
    first_of_pair = lax.broadcasted_iota(jnp.int32, (1, 2 * LANES), 1) % LANES < head_size

    def mix_block(i):
        rec, b = divmod(i, blocks)
        at, start = rec * row_count, b * block
        values = jnp.concatenate(
            [value[at + start : at + start + near], value[at + memory_at : at + row_count]], axis=0
        )
        for pair in range(width // LANES):
            columns = slice(pair * LANES, (pair + 1) * LANES)
            pair_rows = slice(pair * 2 * block, (pair + 1) * 2 * block)
            sums = lax.dot_general(
                weights[i % weights.shape[0], :, pair_rows],
                jnp.concatenate([values[:, columns], ones], axis=1),
                (((0,), (0,)), ((), ())),
                preferred_element_type=jnp.float32,
            )
            picked = jnp.where(first_of_pair, sums[:block], sums[block:])
            outs[rec, start : start + block, columns] = (
                picked[:, :LANES] / picked[:, LANES:]
            ).astype(jnp.bfloat16)

    count = 2 * blocks
    ring = scores.shape[0]
    for first in range(0, count, ring):
        for stage in (score_block, weigh_block, mix_block):
            for i in range(first, min(first + ring, count)):
                stage(i)
        for rec in range(2):
            if first < (rec + 1) * blocks <= first + ring:
                out_copies[rec].start()
    for rec in range(2):
        sums_out[rec][...] = jnp.dot(
            members[rec][...], outs[rec], preferred_element_type=jnp.float32
        )
    for copy in piece_copies(1, True) + out_copies:
        copy.wait()


def assemble(scalars, offsets_at, attended, gathered):
    shard = attended[0].shape[1] // 2
    offsets = [
        [pl.multiple_of(scalars[offsets_at + 2 * i + s], LANES) for s in range(2)]
        for i in range(4)
    ]
    for i in range(4):
        for s in range(2):
            gathered[:, pl.ds(offsets[i][s], shard)] = attended[i][:, s * shard : (s + 1) * shard]
    return offsets, shard


def pool_kernel(offsets_at, scalars, base, inverse, route, *refs):
    sums, projections = refs[:4], refs[4:8]
    sent_out, means, pooled = refs[8:]
    shard = sums[0].shape[1] // 2
    offsets = [
        [pl.multiple_of(scalars[offsets_at + 2 * i + s], LANES) for s in range(2)]
        for i in range(4)
    ]
    for i in range(4):
        for s in range(2):
            for lane in range(0, shard, LANES):
                means[:, pl.ds(offsets[i][s] + lane, LANES)] = (
                    sums[i][:, s * shard + lane : s * shard + lane + LANES] * inverse[...]
                ).astype(jnp.bfloat16)
    for i in range(4):
        mixed = jnp.dot(means[...], projections[i][...], preferred_element_type=jnp.float32)
        for s in range(2):
            columns = pl.ds(offsets[i][s], shard)
            pooled[:, columns] = (
                base[:, columns] + mixed[:, s * shard : (s + 1) * shard]
            ).astype(jnp.bfloat16)
    sent_out[...] = jnp.dot(
        route[...], pooled[...], preferred_element_type=jnp.float32
    ).astype(jnp.bfloat16)


def encode_kernel(offsets_at, scalars, *refs):
    attended, projections, frames = refs[:4], refs[4:8], refs[8]
    encoded_out, gathered = refs[9:]
    first_frame, length = scalars[0], scalars[1]
    frame_count, _ = frames.shape
    offsets, shard = assemble(scalars, offsets_at, attended, gathered)
    live = (
        first_frame + lax.broadcasted_iota(jnp.int32, (frame_count, 1), 0) < length
    ).astype(jnp.float32)
    for i in range(4):
        mixed = jnp.dot(
            gathered[...], projections[i][...], preferred_element_type=jnp.float32
        )
        for s in range(2):
            columns = pl.ds(offsets[i][s], shard)
            base = frames[:, columns].astype(jnp.float32)
            encoded_out[:, columns] = (
                (base + mixed[:, s * shard : (s + 1) * shard]) * live
            ).astype(jnp.bfloat16)


def language_kernel(places_at, scalars, received, *refs):
    pieces, out = refs[:-6], refs[-6]
    rows, weights, product, sems, out_sems = refs[-5:]
    count, width = len(pieces), pieces[0].shape[1]
    row_copy = pltpu.make_async_copy(received, rows, sems.at[4 * count])
    row_copy.start()
    quarter = pieces[0].shape[0] // 4
    copies = []
    for i, piece in enumerate(pieces):
        for part in range(4):
            part_rows = pl.ds(part * quarter, quarter)
            copies.append(
                pltpu.make_async_copy(
                    piece.at[part_rows], weights.at[i, part_rows], sems.at[4 * i + part]
                )
            )
    for copy in copies:
        copy.start()
    row_copy.wait()
    out_copies = []
    for i in range(count):
        for copy in copies[4 * i : 4 * i + 4]:
            copy.wait()
        product[i] = jnp.dot(
            rows[...], weights[i], preferred_element_type=jnp.float32
        ).astype(jnp.bfloat16)
        place = pl.multiple_of(scalars[places_at + i], LANES)
        out_copies.append(
            pltpu.make_async_copy(product.at[i], out.at[:, pl.ds(place, width)], out_sems.at[i])
        )
        out_copies[-1].start()
    for copy in out_copies:
        copy.wait()


def along_x(r, j, _):
    return r, j ^ 1


def along_y(r, j, _):
    return r ^ 2, j


def other_core(r, j, _):
    return r ^ 1, j


def z_up(r, j, count):
    return r, (j + 2) % count


def z_down(r, j, count):
    return r, (j - 2) % count


def relocate(value, core_0, core_1):
    rec_count, time_count = lax.axis_size("rec"), lax.axis_size("tm")
    pairs = []
    for r in range(rec_count):
        for j in range(time_count):
            route = (core_0, core_1)[r % 2]
            if route is not None:
                to_r, to_j = route(r, j, time_count)
                pairs.append((r * time_count + j, to_r * time_count + to_j))
    return lax.ppermute(value, ("rec", "tm"), pairs)


def swap_cores(value):
    return relocate(value, other_core, other_core)


def exchange_blocks(blocks):
    return lax.all_to_all(blocks, "tm", split_axis=0, concat_axis=0, tiled=True)


def per_device(
    frames,
    lengths,
    norm_gain,
    memory_gain,
    qkv_weight,
    out_weight,
    segment_ids,
    owners,
    language_weight,
):
    local_frames = frames[0]
    frame_count, model_width = local_frames.shape
    shard = out_weight.shape[1]
    half = model_width // 2
    time_count = lax.axis_size("tm")
    rec_count = lax.axis_size("rec")
    rec, time = lax.axis_index("rec"), lax.axis_index("tm")
    core, y_half = rec % 2, (rec // 2) % 2
    x, z = time % 2, time // 2
    z_count = time_count // 2
    first_frame = time * frame_count
    length = lengths[0]
    head_size = model_width // H
    bf16 = jnp.bfloat16

    own = jnp.concatenate([qkv_weight, out_weight[None]], axis=0)
    own_a = lax.dynamic_slice_in_dim(own, y_half * half, half, 1)
    later_qkv, later_out, own_a = lax.optimization_barrier((qkv_weight, out_weight, own_a))
    later = jnp.concatenate([later_qkv, later_out[None]], axis=0)
    own_b = lax.dynamic_slice_in_dim(later, (1 - y_half) * half, half, 1)

    def pick(for_core_0, for_core_1):
        return jnp.where(core == 0, for_core_0, for_core_1)

    token_count = owners.shape[2]
    slot_count = 2 * token_count
    capacity = slot_count // time_count
    language_shard = language_weight.shape[1]

    def group_of(of_core, slot):
        return jnp.where(of_core == 0, z + slot, z - slot - 1) % z_count

    numbers = [first_frame, length, core, y_half, capacity]
    offsets_at = len(numbers)
    for of_core in (core, 1 - core):
        for slot in range(2):
            group = group_of(of_core, slot)
            numbers += [(2 * group + x) * shard, (2 * group + 1 - x) * shard]
    places_at = len(numbers)
    numbers += [(rec ^ i) * language_shard for i in range(rec_count)]
    scalars = jnp.stack(numbers).astype(jnp.int32)

    m1 = relocate(own_a, along_x, z_up)
    m2 = relocate(pick(own_a, own_b), z_down, z_up)
    l1 = relocate(language_weight, along_y, along_y)

    pad = 2 * RC
    normed, start_rows, memory = local_call(
        functools.partial(normalise_kernel, C),
        (
            shape_of(frame_count, model_width),
            shape_of(pad, model_width),
            shape_of(time_count, frame_count // C, model_width),
        ),
        (scalars,),
        (local_frames, norm_gain[None], memory_gain[None]),
        flops=10 * frame_count * model_width,
        moved=4 * frame_count * model_width,
    )
    other_length = swap_cores(lengths)
    other_normed = swap_cores(normed)
    ahead = shifted(start_rows, "tm", -1)
    memories = exchange_blocks(memory).reshape(-1, model_width)
    owners_col = owners[0, 0]
    base, member, inverse, route = local_call(
        prepare_kernel,
        (
            shape_of(token_count, model_width, dtype=jnp.float32),
            shape_of(token_count, frame_count),
            shape_of(token_count, LANES, dtype=jnp.float32),
            shape_of(slot_count, token_count),
        ),
        (scalars,),
        (local_frames, segment_ids[0], owners_col.reshape(1, token_count), owners_col),
        flops=2 * token_count * frame_count * model_width,
        moved=2 * frame_count * model_width,
    )
    other_member = swap_cores(member)
    other_ahead = swap_cores(ahead)
    other_memories = swap_cores(memories)

    m3 = relocate(m1, along_y, along_x)
    m4 = relocate(m1, None, z_up)
    m5 = relocate(m2, along_x, z_up)
    m6 = relocate(m3, None, along_y)
    m7 = relocate(pick(m2, m4), along_y, along_x)
    m8 = relocate(m5, along_y, along_x)

    slot_pieces = (
        ((own_a, m1), (own_b, m2), (m1, m3), (m3, m6)),
        ((m2, m4), (m7, m5), (m5, m7), (m8, m8)),
    )
    block = 2 * C
    width = 2 * shard
    row_count = frame_count + pad + memories.shape[0]
    keys_seen = block + pad + memories.shape[0]
    lanes = width // head_size * block
    attended, sums, outs = [], [], []
    for pieces in slot_pieces:
        flat = [p for pair in pieces for p in pair]
        *results, out_piece = local_call(
            functools.partial(attend_kernel, C, RC, head_size, False),
            (
                shape_of(frame_count, width),
                shape_of(frame_count, width),
                shape_of(token_count, width, dtype=jnp.float32),
                shape_of(token_count, width, dtype=jnp.float32),
                shape_of(model_width, width),
            ),
            (scalars, other_length),
            (member, other_member, normed, ahead, memories, other_normed, other_ahead, other_memories, *flat),
            in_place=6 + len(flat),
            out_in_place=(True, True, False, False, False),
            scratch=(
                pltpu.VMEM((2, frame_count, width), bf16),
                pltpu.VMEM((2 * row_count, model_width), bf16),
                pltpu.VMEM((model_width, 3 * width), bf16),
                pltpu.VMEM((2 * row_count, width), bf16),
                pltpu.VMEM((2 * row_count, width), bf16),
                pltpu.VMEM((2 * row_count, width), bf16),
                pltpu.VMEM((block + pad, lanes), jnp.float32),
                pltpu.VMEM((RING, keys_seen, lanes), jnp.float32),
                pltpu.VMEM((RING, 1, lanes), jnp.float32),
                pltpu.VMEM((RING, keys_seen, lanes), bf16),
                pltpu.SemaphoreType.DMA((24,)),
            ),
            vmem_mib=20,
            flops=12 * frame_count * model_width * width,
            moved=8 * frame_count * model_width,
        )
        attended.append(results[:2])
        sums.append(results[2:])
        outs.append(out_piece)
    other_outs = [swap_cores(w) for w in outs]
    other_attended = [swap_cores(for_other) for _, for_other in attended]

    other_sums = [swap_cores(for_other) for _, for_other in sums]
    projections = (*outs, *other_outs)
    features = (attended[0][0], attended[1][0], *other_attended, *projections)
    sent_rows = local_call(
        functools.partial(pool_kernel, offsets_at),
        shape_of(slot_count, model_width),
        (scalars,),
        (base, inverse, route, sums[0][0], sums[1][0], *other_sums, *projections),
        scratch=(
            pltpu.VMEM((token_count, model_width), bf16),
            pltpu.VMEM((token_count, model_width), bf16),
        ),
        flops=4 * token_count * model_width * model_width,
        moved=6 * frame_count * model_width,
    )
    received = exchange_blocks(
        sent_rows.reshape(time_count, capacity, model_width)
    ).reshape(slot_count, model_width)
    encoded = local_call(
        functools.partial(encode_kernel, offsets_at),
        shape_of(frame_count, model_width),
        (scalars,),
        (*features, local_frames),
        scratch=(pltpu.VMEM((frame_count, model_width), bf16),),
        flops=2 * frame_count * model_width * model_width,
        moved=6 * frame_count * model_width,
    )
    language_pieces = (language_weight, swap_cores(language_weight), l1, swap_cores(l1))
    lm_out = local_call(
        functools.partial(language_kernel, places_at),
        shape_of(slot_count, rec_count * language_shard),
        (scalars,),
        (received, *language_pieces),
        in_place=1 + rec_count,
        out_in_place=True,
        scratch=(
            pltpu.VMEM((slot_count, model_width), bf16),
            pltpu.VMEM((rec_count, model_width, language_shard), bf16),
            pltpu.VMEM((rec_count, slot_count, language_shard), bf16),
            pltpu.SemaphoreType.DMA((4 * rec_count + 1,)),
            pltpu.SemaphoreType.DMA((rec_count,)),
        ),
        flops=2 * slot_count * model_width * rec_count * language_shard,
        moved=2 * model_width * rec_count * language_shard,
    )
    return (encoded[None], lm_out[None, None])


def solution(mesh):
    in_specs = (
        P("rec", "tm", None),
        P("rec"),
        P(),
        P(),
        P(None, None, "tm"),
        P(None, "tm"),
        P("rec", "tm", None),
        P("rec", "tm", None, None),
        P(None, "rec"),
    )
    out_specs = (P("rec", "tm", None), P("rec", "tm", None, None))
    rec_count, time_count = mesh.shape["rec"], mesh.shape["tm"]
    paired = shard_map_of(mesh, in_specs, out_specs, per_device)
    plain = shard_map_of(mesh, in_specs, out_specs, plain_device)

    def run(*arrays):
        shard = arrays[5].shape[1] // time_count
        fits = rec_count == 4 and time_count == 8 and shard % LANES == 0
        return (paired if fits else plain)(*arrays)

    return run


def shard_map_of(mesh, in_specs, out_specs, body):
    return jax.shard_map(
        body, mesh=mesh, in_specs=in_specs, out_specs=out_specs, check_vma=False
    )
```
